32 devices in a mesh: section: 2 (over core), dp: 4 (over z), expert: 4 (over y, x).
Axes of the slice: x: 2, y: 2, z: 4, core: 2. Of those that a mesh axis runs over, the one named last changes fastest.
Arguments:
- boundary_in: float32 [2, 2, 16, 197, 768], P('section', None, ('dp', 'expert')), may hold values from -6 to 6
- routes: int32 [2, 2, 16, 197, 2], P('section', None, ('dp', 'expert')), may hold values from 0 to 7, as said below
- capacity_slots: int32 [2, 2, 16, 197, 2], P('section', None, ('dp', 'expert')), may hold values from 0 to 40, as said below
- ln_gain: bfloat16 [2, 2, 768], P('section', None, ('dp', 'expert')), may hold values from 0.5 to 1.5
- ln_bias: bfloat16 [2, 2, 768], P('section', None, ('dp', 'expert')), may hold values from -3 to 3
- w_qkv: bfloat16 [2, 768, 2304], P('section', ('dp', 'expert')), may hold values from -0.21875 to 0.21875
- w_out: bfloat16 [2, 768, 768], P('section', ('dp', 'expert')), may hold values from -1.25 to 1.25
- w_router: bfloat16 [2, 768, 8], P('section', ('dp', 'expert')), may hold values from -0.21875 to 0.21875
- w_up: bfloat16 [2, 8, 768, 3072], P('section', 'expert', None, 'dp'), may hold values from -0.21875 to 0.21875
- w_down: bfloat16 [2, 8, 3072, 768], P('section', 'expert', 'dp'), may hold values from -0.109375 to 0.109375
Outputs:
- boundary_out: float32 [2, 2, 16, 197, 768], P('section', None, ('dp', 'expert'))
- grad_ln_gain: float32 [2, 2, 768], P('section', None, ('dp', 'expert'))
- grad_ln_bias: float32 [2, 2, 768], P('section', None, ('dp', 'expert'))
- grad_qkv: float32 [2, 768, 2304], P('section', ('dp', 'expert'))
- grad_out: float32 [2, 768, 768], P('section', ('dp', 'expert'))
- grad_router: float32 [2, 768, 8], P('section', ('dp', 'expert'))
- grad_up: float32 [2, 8, 768, 3072], P('section', 'expert', None, 'dp')
- grad_down: float32 [2, 8, 3072, 768], P('section', 'expert', 'dp')
The draws below stay inside these ranges and needn't reach their ends.
Inputs may be any that keep to these rules, and one draw needn't show every extreme that they name: `routes`: each token names two different experts of the 8. In every block (the 1 images of one micro-batch on one device of dp+expert, each layer apart) some expert is named by 40 or more tokens. `capacity_slots`: within a block, the kept choices of one expert hold the slots 0, 1, 2, ... without gaps or repeats; the value 40 marks a dropped choice, and every block drops at least one choice.
All inputs are finite; a program needn't handle non-finite values.
Results may differ from the reference program's by a relative error of at most 0.02.
Values may be sent and summed in bfloat16 or wider, within the bound.
A program may use at most 256 MiB of HBM per device.

```python
import math
import jax
import jax.numpy as jnp
from jax import lax

D = 768
HEADS = 12
HEAD_DIM = 64
FF = 3072
SEQ = 197
MB = 2
IMG_DEV = 1
LAYERS = 2
EXPERTS = 8
IMAGES = 16
CAP = 40


def routing(key):
    key_list = jax.random.split(jax.random.fold_in(key, 11), 5)
    block_count = IMAGES // IMG_DEV
    block_rows = IMG_DEV * SEQ
    shape = (LAYERS, MB, block_count, block_rows)
    weights = jax.random.randint(key_list[0], (LAYERS, EXPERTS), 1, 9, dtype=jnp.int32)
    bounds = jnp.cumsum(weights, axis=1)
    totals = bounds[:, -1]
    draws = jax.random.randint(key_list[1], shape, 0, 1 << 20, dtype=jnp.int32)
    target = draws % totals[:, None, None, None]
    first_ids = jnp.sum((target[..., None] >= bounds[:, None, None, None, :]).astype(jnp.int32), axis=-1)
    heavy = jax.random.randint(key_list[2], (LAYERS,), 0, EXPERTS, dtype=jnp.int32)
    position = jnp.arange(block_rows, dtype=jnp.int32)
    first_ids = jnp.where(position < CAP, heavy[:, None, None, None], first_ids)
    offsets = jax.random.randint(key_list[3], shape, 1, EXPERTS, dtype=jnp.int32)
    second_ids = (first_ids + offsets) % EXPERTS
    chosen = jnp.stack([first_ids, second_ids], axis=-1)
    flat = chosen.reshape(LAYERS, MB, block_count, 2 * block_rows)
    ranking = jax.random.randint(key_list[4], flat.shape, 0, 1 << 16, dtype=jnp.int32) * (2 * block_rows)
    ranking = ranking + jnp.arange(2 * block_rows, dtype=jnp.int32)
    order = jnp.argsort(ranking, axis=-1, stable=True)
    ordered = jnp.take_along_axis(flat, order, axis=-1)
    hits = (ordered[..., None] == jnp.arange(EXPERTS, dtype=jnp.int32)).astype(jnp.int32)
    before = jnp.cumsum(hits, axis=-2) - hits
    rank_sorted = jnp.sum(before * hits, axis=-1)
    inverse = jnp.argsort(order, axis=-1, stable=True)
    ranks = jnp.take_along_axis(rank_sorted, inverse, axis=-1)
    slot_values = jnp.minimum(ranks, CAP)
    return (chosen.reshape(LAYERS, MB, IMAGES, SEQ, 2), slot_values.reshape(LAYERS, MB, IMAGES, SEQ, 2))


def draw_routes(key, part):
    return routing(key)[0]


def draw_capacity_slots(key, part):
    return routing(key)[1]


def block_scale(stream_key, extent, cuts, least, largest):
    loudness, own = 1.0, jax.random.fold_in(stream_key, 6)
    for dim, shards_of in cuts:
        steps = jnp.exp(jax.random.uniform(jax.random.fold_in(own, dim), (shards_of,), jnp.float32, least / len(cuts), largest / len(cuts)))
        loudness = loudness * jnp.repeat(steps, extent[dim] // shards_of).reshape([-1 if axis == dim else 1 for axis in range(len(extent))])
    return loudness


def scatter_about(own_key, extent, scale, reach, pieces=(), held_as=jnp.bfloat16):
    drawn = jax.random.normal(own_key, extent, jnp.float32) * scale
    if len(pieces) > 0:
        drawn = block_scale(own_key, extent, pieces, -0.22, 0.18) * drawn
    return jnp.clip(drawn, min=-reach, max=reach).astype(held_as)


def setup_inputs(seed: int = 0) -> dict:
    streams_of = jax.random.split(jax.random.key(seed), 11)
    return {
        "boundary_in": scatter_about(streams_of[0], (2, MB, IMAGES, SEQ, D), 1.0, 6.0, ((0, 2), (2, 16)), jnp.float32),
        "routes": draw_routes(jax.random.fold_in(streams_of[10], 71), 0),
        "capacity_slots": draw_capacity_slots(jax.random.fold_in(streams_of[10], 71), 0),
        "ln_gain": jnp.clip(1.0 + 0.1 * jax.random.normal(streams_of[3], (LAYERS, 2, D), jnp.float32), 0.5, 1.5).astype(jnp.bfloat16),
        "ln_bias": scatter_about(streams_of[4], (LAYERS, 2, D), 0.5, 3.0, ((0, 2), (2, 16))),
        "w_qkv": scatter_about(streams_of[5], (LAYERS, D, 3 * D), D ** -0.5, 0.21875, ((0, 2), (1, 16))),
        "w_out": scatter_about(streams_of[6], (LAYERS, D, D), (D // 32) ** -0.5, 1.25, ((0, 2), (1, 16))),
        "w_router": scatter_about(streams_of[7], (LAYERS, D, EXPERTS), D ** -0.5, 0.21875, ((0, 2), (1, 16))),
        "w_up": scatter_about(streams_of[8], (LAYERS, EXPERTS, D, FF), D ** -0.5, 0.21875, ((0, 2), (1, 4), (3, 4))),
        "w_down": scatter_about(streams_of[9], (LAYERS, EXPERTS, FF, D), FF ** -0.5, 0.109375, ((0, 2), (1, 4), (2, 4))),
    }


EPS = 1e-06
SQRT_HALF = 0.7071067811865476
INV_ROOT_TAU = 0.3989422804014327

def norm_forward(values, gain_row, shift_row):
    centred = values - lax.optimization_barrier(jnp.mean(values, axis=-1, keepdims=True))
    variance = lax.optimization_barrier(jnp.mean(centred * centred, axis=-1, keepdims=True))
    inverse = lax.rsqrt(variance + EPS)
    unit_rows = centred * inverse
    return (unit_rows * gain_row + shift_row, unit_rows, inverse)

def norm_backward(d_normed, unit_rows, inverse, gain_row):
    d_gain = lax.optimization_barrier(jnp.sum(d_normed * unit_rows, axis=0))
    d_shift = lax.optimization_barrier(jnp.sum(d_normed, axis=0))
    scaled = d_normed * gain_row
    d_values = inverse * (scaled - lax.optimization_barrier(jnp.mean(scaled, axis=-1, keepdims=True)) - unit_rows * lax.optimization_barrier(jnp.mean(scaled * unit_rows, axis=-1, keepdims=True)))
    return (d_values, d_gain, d_shift)

def gelu_slope(pre_act):
    return 0.5 * (1.0 + lax.erf(pre_act * SQRT_HALF)) + pre_act * jnp.exp(-0.5 * pre_act * pre_act) * INV_ROOT_TAU

def split_heads(qkv_rows, image_count):
    feature_count = qkv_rows.shape[1] // 3
    return [qkv_rows[:, part_index * feature_count:(part_index + 1) * feature_count].astype(jnp.float32).reshape(image_count, SEQ, HEADS, HEAD_DIM) for part_index in range(3)]

def attend_forward(qkv_rows, image_count):
    queries, key_rows, value_rows = split_heads(qkv_rows, image_count)
    scale_factor = 1.0 / math.sqrt(HEAD_DIM)
    scores = jnp.einsum('bqhd,bkhd->bhqk', queries, key_rows) * scale_factor
    log_totals = jnp.log(lax.optimization_barrier(jnp.sum(jnp.exp(scores), axis=-1)))
    probs_half = jnp.exp(scores - log_totals[..., None]).astype(jnp.bfloat16)
    attended = jnp.einsum('bhqk,bkhd->bqhd', probs_half.astype(jnp.float32), value_rows)
    return (attended.astype(jnp.bfloat16).reshape(-1, HEADS * HEAD_DIM), log_totals)

def attend_backward(qkv_rows, log_totals, d_attended, image_count):
    queries, key_rows, value_rows = split_heads(qkv_rows, image_count)
    scale_factor = 1.0 / math.sqrt(HEAD_DIM)
    scores = jnp.einsum('bqhd,bkhd->bhqk', queries, key_rows) * scale_factor
    probs = jnp.exp(scores - log_totals[..., None])
    probs_half = probs.astype(jnp.bfloat16).astype(jnp.float32)
    d_heads = d_attended.astype(jnp.float32).reshape(image_count, SEQ, HEADS, HEAD_DIM)
    d_values = jnp.einsum('bhqk,bqhd->bkhd', probs_half, d_heads)
    d_probs = jnp.einsum('bqhd,bkhd->bhqk', d_heads, value_rows)
    row_dot = lax.optimization_barrier(jnp.sum(probs * d_probs, axis=-1, keepdims=True))
    d_scores = (probs * (d_probs - row_dot) * scale_factor).astype(jnp.bfloat16).astype(jnp.float32)
    d_queries = jnp.einsum('bhqk,bkhd->bqhd', d_scores, key_rows)
    d_keys = jnp.einsum('bhqk,bqhd->bkhd', d_scores, queries)
    feature_count = HEADS * HEAD_DIM
    joined = jnp.concatenate([d_queries.reshape(-1, feature_count), d_keys.reshape(-1, feature_count), d_values.reshape(-1, feature_count)], axis=1)
    return joined.astype(jnp.bfloat16)

def to_experts(blocked):
    block_count = blocked.shape[0]
    grouped = blocked.reshape(block_count, EXPERTS, CAP, blocked.shape[-1])
    return jnp.transpose(grouped, (1, 0, 2, 3)).reshape(EXPERTS, block_count * CAP, blocked.shape[-1])

def from_experts(rows_by_expert, block_count):
    grouped = rows_by_expert.reshape(EXPERTS, block_count, CAP, rows_by_expert.shape[-1])
    return jnp.transpose(grouped, (1, 0, 2, 3)).reshape(block_count, EXPERTS * CAP, rows_by_expert.shape[-1])

def tables(expert_ids, slot_ids):
    slot_index = jnp.where(slot_ids < CAP, expert_ids * CAP + slot_ids, -1)
    onehot = (slot_index[..., None] == jnp.arange(EXPERTS * CAP, dtype=jnp.int32)).astype(jnp.float32)
    chosen = (expert_ids[..., None] == jnp.arange(EXPERTS, dtype=jnp.int32)).astype(jnp.float32)
    return (onehot, chosen)

def layer_forward(inputs, params, expert_ids, slot_ids):
    gain_rows, shift_rows, weight_qkv, weight_out, weight_router, weight_up, weight_down = params
    block_count, block_rows = (expert_ids.shape[0], expert_ids.shape[1])
    normed_one, unit_one, inverse_one = norm_forward(inputs, gain_rows[0], shift_rows[0])
    norm_one = normed_one.astype(jnp.bfloat16)
    qkv_rows = jnp.dot(norm_one, weight_qkv, preferred_element_type=jnp.float32).astype(jnp.bfloat16)
    attended, log_totals = attend_forward(qkv_rows, IMAGES)
    middle = inputs + jnp.dot(attended, weight_out, preferred_element_type=jnp.float32)
    normed_two, unit_two, inverse_two = norm_forward(middle, gain_rows[1], shift_rows[1])
    norm_two = normed_two.astype(jnp.bfloat16)
    logits = jnp.dot(norm_two, weight_router, preferred_element_type=jnp.float32).reshape(block_count, block_rows, EXPERTS)
    onehot, chosen = tables(expert_ids, slot_ids)
    picked = lax.optimization_barrier(jnp.sum(logits[:, :, None, :] * chosen, axis=-1))
    leading = jax.nn.sigmoid(picked[..., 0] - picked[..., 1])
    gate_pair = jnp.stack([leading, 1.0 - leading], axis=-1)
    norm_blocks = norm_two.reshape(block_count, block_rows, -1).astype(jnp.float32)
    buffer = jnp.einsum('btjs,btd->bsd', onehot, norm_blocks).astype(jnp.bfloat16)
    inbound = to_experts(buffer)
    pre_act = jnp.einsum('erd,edf->erf', inbound.astype(jnp.float32), weight_up.astype(jnp.float32))
    hidden = jax.nn.gelu(pre_act, approximate=False).astype(jnp.bfloat16)
    results = jnp.einsum('erf,efd->erd', hidden.astype(jnp.float32), weight_down.astype(jnp.float32)).astype(jnp.bfloat16)
    back_rows = from_experts(results, block_count)
    selected = jnp.einsum('btjs,bsd->btjd', onehot, back_rows.astype(jnp.float32))
    out_rows = middle + lax.optimization_barrier(jnp.sum(gate_pair[..., None] * selected, axis=2)).reshape(middle.shape)
    saved = (unit_one, inverse_one, norm_one, qkv_rows, log_totals, attended, unit_two, inverse_two, norm_two, gate_pair, selected, inbound, pre_act, hidden)
    return (out_rows, saved)

def layer_backward(d_out, saved, params, expert_ids, slot_ids):
    gain_rows, shift_rows, weight_qkv, weight_out, weight_router, weight_up, weight_down = params
    unit_one, inverse_one, norm_one, qkv_rows, log_totals, attended, unit_two, inverse_two, norm_two, gate_pair, selected, inbound, pre_act, hidden = saved
    block_count, block_rows = (expert_ids.shape[0], expert_ids.shape[1])
    onehot, chosen = tables(expert_ids, slot_ids)
    d_blocks = d_out.reshape(block_count, block_rows, -1)
    d_gate = lax.optimization_barrier(jnp.sum(d_blocks[:, :, None, :] * selected, axis=-1))
    d_lead = (d_gate[..., 0] - d_gate[..., 1]) * gate_pair[..., 0] * gate_pair[..., 1]
    d_logits = (d_lead[..., None] * (chosen[:, :, 0, :] - chosen[:, :, 1, :])).astype(jnp.bfloat16).reshape(-1, EXPERTS)
    router_grad = jnp.einsum('td,te->de', norm_two.astype(jnp.float32), d_logits.astype(jnp.float32))
    weighted = gate_pair[..., None] * d_blocks[:, :, None, :]
    d_buffer = jnp.einsum('btjs,btjd->bsd', onehot, weighted, precision=lax.Precision.HIGHEST).astype(jnp.bfloat16)
    d_results = to_experts(d_buffer).astype(jnp.float32)
    down_grad = jnp.einsum('erf,erd->efd', hidden.astype(jnp.float32), d_results)
    d_hidden = jnp.einsum('erd,efd->erf', d_results, weight_down.astype(jnp.float32))
    d_pre = (d_hidden * gelu_slope(pre_act)).astype(jnp.bfloat16).astype(jnp.float32)
    up_grad = jnp.einsum('erd,erf->edf', inbound.astype(jnp.float32), d_pre)
    d_inbound = jnp.einsum('erf,edf->erd', d_pre, weight_up.astype(jnp.float32)).astype(jnp.bfloat16)
    d_back = from_experts(d_inbound, block_count).astype(jnp.float32)
    d_norm_two = jnp.einsum('btjs,bsd->btd', onehot, d_back).reshape(d_out.shape)
    d_norm_two = d_norm_two + jnp.dot(d_logits, weight_router.T, preferred_element_type=jnp.float32)
    d_middle_norm, gain_two, shift_two = norm_backward(d_norm_two, unit_two, inverse_two, gain_rows[1])
    d_middle = d_out + d_middle_norm
    d_middle_half = d_middle.astype(jnp.bfloat16)
    out_grad = jnp.einsum('td,te->de', attended.astype(jnp.float32), d_middle_half.astype(jnp.float32))
    d_attended = jnp.dot(d_middle_half, weight_out.T, preferred_element_type=jnp.float32).astype(jnp.bfloat16)
    d_qkv = attend_backward(qkv_rows, log_totals, d_attended, IMAGES)
    qkv_grad = jnp.einsum('td,te->de', norm_one.astype(jnp.float32), d_qkv.astype(jnp.float32))
    d_norm_one = jnp.dot(d_qkv, weight_qkv.T, preferred_element_type=jnp.float32)
    d_input_norm, gain_one, shift_one = norm_backward(d_norm_one, unit_one, inverse_one, gain_rows[0])
    d_input = d_middle + d_input_norm
    grads = (jnp.stack([gain_one, gain_two]), jnp.stack([shift_one, shift_two]), qkv_grad, out_grad, router_grad, up_grad, down_grad)
    return (d_input, grads)

def round_trip(values):
    return lax.optimization_barrier(values.astype(jnp.bfloat16)).astype(jnp.float32)

def reference(boundary_in, routes, capacity_slots, ln_gain, ln_bias, w_qkv, w_out, w_router, w_up, w_down):
    block_count = IMAGES // IMG_DEV
    block_rows = IMG_DEV * SEQ
    layer_params = [(ln_gain[layer_index].astype(jnp.float32), ln_bias[layer_index].astype(jnp.float32), w_qkv[layer_index], w_out[layer_index], w_router[layer_index], w_up[layer_index], w_down[layer_index]) for layer_index in range(LAYERS)]
    grad_totals = [None for layer_index in range(LAYERS)]
    input_grads = []
    layer_outputs = []
    for micro_index in range(MB):
        route_now = [routes[layer_index, micro_index].reshape(block_count, block_rows, 2) for layer_index in range(LAYERS)]
        slot_now = [capacity_slots[layer_index, micro_index].reshape(block_count, block_rows, 2) for layer_index in range(LAYERS)]
        stream = boundary_in[0, micro_index].reshape(-1, D)
        saved_list = []
        for layer_index in range(LAYERS):
            if layer_index > 0:
                stream = round_trip(stream)
            stream, saved = layer_forward(stream, layer_params[layer_index], route_now[layer_index], slot_now[layer_index])
            saved_list.append(saved)
        layer_outputs.append(stream)
        cotangent = boundary_in[1, micro_index].reshape(-1, D)
        for layer_index in reversed(range(LAYERS)):
            if layer_index < LAYERS - 1:
                cotangent = round_trip(cotangent)
            cotangent, grads = layer_backward(cotangent, saved_list[layer_index], layer_params[layer_index], route_now[layer_index], slot_now[layer_index])
            if grad_totals[layer_index] is None:
                grad_totals[layer_index] = grads
            else:
                grad_totals[layer_index] = jax.tree.map(jnp.add, grad_totals[layer_index], grads)
        input_grads.append(cotangent)
    boundary_out = jnp.stack([jnp.stack(input_grads), jnp.stack(layer_outputs)]).reshape(2, MB, IMAGES, SEQ, D)
    stacked = [jnp.stack([grad_totals[layer_index][part_index] for layer_index in range(LAYERS)]) for part_index in range(7)]
    return (boundary_out, stacked[0], stacked[1], stacked[2], stacked[3], stacked[4], stacked[5], stacked[6])
```

```python
import functools
import math

import jax
import jax.numpy as jnp
from jax import lax
from jax.experimental import pallas as pl
from jax.experimental.pallas import tpu as pltpu
from jax.sharding import PartitionSpec as P

HEADS = 12
HEAD_DIM = 64
EXP_DEV = 2
MB = 2


EPS = 1e-06
SQRT_HALF = 0.7071067811865476
INV_ROOT_TAU = 0.3989422804014327
MESH = pl.DeviceIdType.MESH


def round_up(value, unit):
    return (value + unit - 1) // unit * unit


def z_order(step, z, depth):
    if depth == 1:
        return z
    direction = 1 - 2 * (z // (depth // 2))
    return lax.rem(z + step * direction + depth, depth)


def f32_dot(a, b, dims):
    return lax.dot_general(a, b, (dims, ((), ())), preferred_element_type=jnp.float32)


def moe_kernel(backward, shape, *refs):
    depth, groups, cap_rows, token_rows, model_width, hidden_width = shape
    if backward:
        (
            rows_ref, slots_ref, up_ref, down_ref, gates_ref, hidden_ref, slope_ref, back_ref,
            out_ref, inbox, d_pre_ref,
            raw, sent_rows, sent_back, sent_home, home, back, d_gates, *sems,
        ) = refs
    else:
        (
            rows_ref, slots_ref, up_ref, down_ref,
            out_ref, inbox, hidden_ref, slope_ref, back, gates_ref,
            raw, sent_rows, sent_back, sent_home, home, *sems,
        ) = refs
    far_send, far_recv, go_send, go_recv, back_send, back_recv, home_send, home_recv = sems
    half = jnp.bfloat16
    section, z, column = (
        lax.axis_index("section"), lax.axis_index("dp"), lax.axis_index("expert")
    )
    slot_count = 2 * groups * cap_rows
    tail = token_rows - 16

    def z_peer(distance):
        return (section, lax.rem(z + distance, depth), column)

    def xy_peer(distance):
        return lax.rem(column + distance, groups)

    barrier = pltpu.get_barrier_semaphore()

    def greet_z(distance, carry):
        pl.semaphore_signal(barrier, inc=1, device_id=z_peer(distance), device_id_type=MESH)
        return carry

    def greet_xy(distance, carry):
        pl.semaphore_signal(
            barrier, inc=1, device_id=(section, z, xy_peer(distance)), device_id_type=MESH
        )
        return carry

    lax.fori_loop(1, depth, greet_z, 0)
    lax.fori_loop(1, groups, greet_xy, 0)
    pl.semaphore_wait(barrier, depth - 1 + groups - 1)

    def far_copy(direction, image):
        target = lax.rem(z + 2 * direction - 1 + depth, depth)
        source = raw.at[image]
        return pltpu.make_async_remote_copy(
            src_ref=source, dst_ref=raw.at[image],
            send_sem=far_send.at[direction, image], recv_sem=far_recv.at[image],
            device_id=(section, target, column), device_id_type=MESH,
        )

    def go_copy(image, source, target):
        return pltpu.make_async_remote_copy(
            src_ref=sent_rows.at[image, target], dst_ref=inbox.at[:, image, source],
            send_sem=go_send.at[image, target], recv_sem=go_recv.at[image, source],
            device_id=(section, z, target), device_id_type=MESH,
        )

    def back_copy(image, source, target):
        return pltpu.make_async_remote_copy(
            src_ref=sent_back.at[image, target], dst_ref=back.at[image, source],
            send_sem=back_send.at[image, target], recv_sem=back_recv.at[image, source],
            device_id=(section, z, target), device_id_type=MESH,
        )

    def home_copy(source, target):
        return pltpu.make_async_remote_copy(
            src_ref=sent_home.at[target], dst_ref=home.at[source],
            send_sem=home_send.at[target], recv_sem=home_recv.at[source],
            device_id=(section, target, column), device_id_type=MESH,
        )

    raw[z] = rows_ref[...]

    @pl.when(z < depth - 1)
    def _():
        far_copy(1, z).start()

    @pl.when(z > 0)
    def _():
        far_copy(0, z).start()

    def match(image):
        slots = slots_ref[image][:, :token_rows]
        index = lax.broadcasted_iota(jnp.int32, (slot_count, token_rows), 0)
        return index == slots[0:1], index == slots[1:2]

    def gate_table(image):
        first, second = match(image)
        gates = gates_ref[image]
        table = jnp.where(first, gates[0:1], 0.0) + jnp.where(second, gates[1:2], 0.0)
        return table.astype(half)

    def ones_table(image):
        first, second = match(image)
        return jnp.where(first | second, 1.0, 0.0).astype(half)

    def pass_on(step):
        low, high = z - step, z + step

        @pl.when(low >= 0)
        def _():
            far_copy(1, low).wait_recv()

            @pl.when(z < depth - 1)
            def _():
                far_copy(1, low).start()

        @pl.when(high < depth)
        def _():
            far_copy(0, high).wait_recv()

            @pl.when(z > 0)
            def _():
                far_copy(0, high).start()

    def dispatch(image):
        if not backward:
            gates_ref[image] = raw[image, tail:, :token_rows].astype(jnp.float32)[8:16]
        table = gate_table(image) if backward else ones_table(image)
        rows = raw[image]
        blocks = f32_dot(table, rows, ((1,), (0,))).astype(half)
        sent_rows[image] = blocks.reshape(groups, 2, cap_rows, model_width)

        def send(distance, carry):
            go_copy(image, column, xy_peer(distance)).start()
            return carry

        lax.fori_loop(1, groups, send, 0)
        inbox[:, image, column] = sent_rows[image, column]
        if backward:
            first, second = match(image)
            returned = back_ref[image].reshape(slot_count, model_width)
            ones = jnp.ones((8, model_width), half)
            row_index = lax.broadcasted_iota(jnp.int32, (8, token_rows), 0)
            packed = jnp.zeros((8, token_rows), jnp.float32)
            for choice, found in enumerate((first, second)):
                table = jnp.where(found, 1.0, 0.0).astype(half)
                selected = f32_dot(table, returned, ((0,), (0,)))
                product = (selected * rows.astype(jnp.float32)).astype(half)
                sums = f32_dot(ones, product, ((1,), (1,)))
                high = sums.astype(half).astype(jnp.float32)
                packed = jnp.where(row_index == 2 * choice, high, packed)
                packed = jnp.where(row_index == 2 * choice + 1, sums - high, packed)
            d_gates[image] = packed

    def experts(image):
        def arrive(distance, carry):
            go_copy(image, xy_peer(distance), column).wait_recv()
            return carry

        lax.fori_loop(1, groups, arrive, 0)
        for expert in range(2):
            rows = inbox[expert, image].reshape(groups * cap_rows, model_width)
            if backward:
                d_hidden = f32_dot(rows, down_ref[expert], ((1,), (1,)))
                d_pre = (d_hidden * slope_ref[expert, image].astype(jnp.float32)).astype(half)
                d_pre_ref[expert, image] = d_pre
                result = f32_dot(d_pre, up_ref[expert], ((1,), (1,)))
            else:
                pre = f32_dot(rows, up_ref[expert], ((1,), (0,)))
                share = 0.5 * (1.0 + lax.erf(pre * SQRT_HALF))
                slope = share + pre * jnp.exp(-0.5 * pre * pre) * INV_ROOT_TAU
                hidden = (pre * share).astype(half)
                hidden_ref[expert, image] = hidden
                slope_ref[expert, image] = slope.astype(half)
                result = f32_dot(hidden, down_ref[expert], ((1,), (0,)))
            sent_back[image, :, expert] = result.astype(half).reshape(
                groups, cap_rows, model_width
            )

        def send(distance, carry):
            back_copy(image, column, xy_peer(distance)).start()
            return carry

        lax.fori_loop(1, groups, send, 0)
        back[image, column] = sent_back[image, column]

    def combine(image):
        def arrive(distance, carry):
            back_copy(image, xy_peer(distance), column).wait_recv()
            return carry

        lax.fori_loop(1, groups, arrive, 0)
        table = ones_table(image) if backward else gate_table(image)
        total = f32_dot(table, back[image].reshape(slot_count, model_width), ((0,), (0,)))
        if backward:
            extra = jnp.concatenate(
                [jnp.zeros((8, token_rows), jnp.float32), d_gates[image]], axis=0
            )

        @pl.when(image == z)
        def _():
            out_ref[...] = total
            if backward:
                out_ref[tail:, :token_rows] = total[tail:, :token_rows] + extra

        @pl.when(image != z)
        def _():
            sent_home[image] = total.astype(half)
            if backward:
                sent_home[image, tail:, :token_rows] = (
                    total[tail:, :token_rows] + extra
                ).astype(half)
            home_copy(z, image).start()

    def stage(step, carry):
        @pl.when(jnp.logical_and(step >= 1, step < depth))
        def _():
            pass_on(step)

        @pl.when(step < depth)
        def _():
            dispatch(z_order(step, z, depth))

        @pl.when(jnp.logical_and(step >= 1, step < depth + 1))
        def _():
            experts(z_order(step - 1, z, depth))

        @pl.when(step >= 2)
        def _():
            combine(z_order(step - 2, z, depth))

        return carry

    lax.fori_loop(0, depth + 2, stage, 0)

    def finish_home(distance, carry):
        source = lax.rem(z + distance, depth)
        home_copy(source, z).wait_recv()
        out_ref[...] += home[source].astype(jnp.float32)
        return carry

    lax.fori_loop(1, depth, finish_home, 0)

    def drain_home(distance, carry):
        home_copy(z, lax.rem(z + distance, depth)).wait_send()
        return carry

    lax.fori_loop(1, depth, drain_home, 0)

    def drain_image(image, carry):
        @pl.when(jnp.logical_and(z < depth - 1, image <= z))
        def _():
            far_copy(1, image).wait_send()

        @pl.when(jnp.logical_and(z > 0, image >= z))
        def _():
            far_copy(0, image).wait_send()

        def drain(distance, inner):
            go_copy(image, column, xy_peer(distance)).wait_send()
            back_copy(image, column, xy_peer(distance)).wait_send()
            return inner

        lax.fori_loop(1, groups, drain, 0)
        return carry

    lax.fori_loop(0, depth, drain_image, 0)


def moe_call(backward, call_id, depth, groups, cap_rows, rows, slots, up, down, saved=()):
    token_rows, model_width = rows.shape
    hidden_width = up.shape[2]
    half = jnp.bfloat16
    shape = (depth, groups, cap_rows, token_rows, model_width, hidden_width)
    inbox = jax.ShapeDtypeStruct((2, depth, groups, cap_rows, model_width), half)
    hidden = jax.ShapeDtypeStruct((2, depth, groups * cap_rows, hidden_width), half)
    back = (depth, groups, 2, cap_rows, model_width)
    out = jax.ShapeDtypeStruct((token_rows, model_width), jnp.float32)
    if backward:
        out_shape = (out, inbox, hidden)
    else:
        gates = jax.ShapeDtypeStruct((depth, 8, token_rows), jnp.float32)
        out_shape = (out, inbox, hidden, hidden, jax.ShapeDtypeStruct(back, half), gates)
    scratch = [
        pltpu.VMEM((depth, token_rows, model_width), half),
        pltpu.VMEM((depth, groups, 2, cap_rows, model_width), half),
        pltpu.VMEM(back, half),
        pltpu.VMEM((depth, token_rows, model_width), half),
        pltpu.VMEM((depth, token_rows, model_width), half),
    ]
    if backward:
        scratch += [
            pltpu.VMEM(back, half),
            pltpu.VMEM((depth, 8, token_rows), jnp.float32),
        ]
    scratch += [
        pltpu.SemaphoreType.DMA((2, depth)),
        pltpu.SemaphoreType.DMA((depth,)),
        pltpu.SemaphoreType.DMA((depth, groups)),
        pltpu.SemaphoreType.DMA((depth, groups)),
        pltpu.SemaphoreType.DMA((depth, groups)),
        pltpu.SemaphoreType.DMA((depth, groups)),
        pltpu.SemaphoreType.DMA((depth,)),
        pltpu.SemaphoreType.DMA((depth,)),
    ]
    return pl.pallas_call(
        functools.partial(moe_kernel, backward, shape),
        out_shape=out_shape,
        in_specs=[pl.BlockSpec(memory_space=pltpu.VMEM)] * (4 + len(saved)),
        out_specs=[pl.BlockSpec(memory_space=pltpu.VMEM)] * len(out_shape),
        scratch_shapes=scratch,
        compiler_params=pltpu.CompilerParams(
            collective_id=call_id, has_side_effects=True, vmem_limit_bytes=50 * 2**20
        ),
        name="moe_backward" if backward else "moe_forward",
    )(rows, slots, up, down, *saved)


def norm_forward(values, gain_row, shift_row):
    centred = values - jnp.mean(values, axis=-1, keepdims=True)
    variance = jnp.mean(centred * centred, axis=-1, keepdims=True)
    inverse = lax.rsqrt(variance + EPS)
    unit_rows = centred * inverse
    return (unit_rows * gain_row + shift_row, unit_rows, inverse)


def norm_backward(d_normed, unit_rows, inverse, gain_row):
    d_gain = jnp.sum(d_normed * unit_rows, axis=0)
    d_shift = jnp.sum(d_normed, axis=0)
    scaled = d_normed * gain_row
    d_values = inverse * (
        scaled
        - jnp.mean(scaled, axis=-1, keepdims=True)
        - unit_rows * jnp.mean(scaled * unit_rows, axis=-1, keepdims=True)
    )
    return (d_values, d_gain, d_shift)


def gelu_slope(pre_act):
    return (
        0.5 * (1.0 + lax.erf(pre_act * SQRT_HALF))
        + pre_act * jnp.exp(-0.5 * pre_act * pre_act) * INV_ROOT_TAU
    )


def split_heads(qkv_rows, image_count):
    feature_count = qkv_rows.shape[1] // 3
    return [
        qkv_rows[:, part_index * feature_count : (part_index + 1) * feature_count].reshape(
            image_count, -1, HEADS, HEAD_DIM
        )
        for part_index in range(3)
    ]


def attend_forward(qkv_rows, image_count):
    queries, key_rows, value_rows = split_heads(qkv_rows, image_count)
    scale_factor = 1.0 / math.sqrt(HEAD_DIM)
    scores = (
        jnp.einsum("bqhd,bkhd->bhqk", queries, key_rows, preferred_element_type=jnp.float32)
        * scale_factor
    )
    log_totals = jnp.log(jnp.sum(jnp.exp(scores), axis=-1))
    probs_half = jnp.exp(scores - log_totals[..., None]).astype(jnp.bfloat16)
    attended = jnp.einsum(
        "bhqk,bkhd->bqhd", probs_half, value_rows, preferred_element_type=jnp.float32
    )
    return (attended.astype(jnp.bfloat16).reshape(-1, HEADS * HEAD_DIM), log_totals)


def attend_backward(qkv_rows, log_totals, d_attended, image_count):
    queries, key_rows, value_rows = split_heads(qkv_rows, image_count)
    scale_factor = 1.0 / math.sqrt(HEAD_DIM)
    scores = (
        jnp.einsum("bqhd,bkhd->bhqk", queries, key_rows, preferred_element_type=jnp.float32)
        * scale_factor
    )
    probs = jnp.exp(scores - log_totals[..., None])
    probs_half = probs.astype(jnp.bfloat16)
    d_heads = d_attended.reshape(image_count, -1, HEADS, HEAD_DIM)
    d_values = jnp.einsum(
        "bhqk,bqhd->bkhd", probs_half, d_heads, preferred_element_type=jnp.float32
    )
    d_probs = jnp.einsum("bqhd,bkhd->bhqk", d_heads, value_rows, preferred_element_type=jnp.float32)
    row_dot = jnp.sum(probs * d_probs, axis=-1, keepdims=True)
    d_scores = (probs * (d_probs - row_dot) * scale_factor).astype(jnp.bfloat16)
    d_queries = jnp.einsum(
        "bhqk,bkhd->bqhd", d_scores, key_rows, preferred_element_type=jnp.float32
    )
    d_keys = jnp.einsum("bhqk,bqhd->bkhd", d_scores, queries, preferred_element_type=jnp.float32)
    feature_count = HEADS * HEAD_DIM
    joined = jnp.concatenate(
        [
            d_queries.reshape(-1, feature_count),
            d_keys.reshape(-1, feature_count),
            d_values.reshape(-1, feature_count),
        ],
        axis=1,
    )
    return joined.astype(jnp.bfloat16)


def on_device(
    boundary_in, routes, capacity_slots, ln_gain, ln_bias, w_qkv, w_out, w_router, w_up, w_down
):
    section_index = lax.axis_index("section")
    is_first = section_index == 0
    depth = lax.axis_size("dp")
    groups = lax.axis_size("expert")
    expert_count = EXP_DEV * groups
    local_images = boundary_in.shape[2]
    token_rows = local_images * boundary_in.shape[3]
    model_width = boundary_in.shape[4]
    capacity = 26 * token_rows // (16 * expert_count)
    chips = ("dp", "expert")
    half = jnp.bfloat16

    def by_micro(values):
        return lax.all_to_all(values, "section", split_axis=0, concat_axis=0, tiled=True)

    edge_rows = by_micro(boundary_in[0].reshape(MB, token_rows, model_width))
    route_rows = by_micro(routes[0].reshape(MB, token_rows, 2))
    slot_rows = by_micro(capacity_slots[0].reshape(MB, token_rows, 2))

    norm_columns = jnp.concatenate([ln_gain, ln_bias], axis=1).transpose(0, 2, 1)
    used = 4 * model_width + expert_count + 4
    padding = -used % 128
    packed = jnp.concatenate([w_qkv, w_out, w_router, norm_columns], axis=2)
    packed = jnp.pad(packed, ((0, 0), (0, 0), (0, padding)))
    packed = lax.all_gather(packed, chips, axis=1, tiled=True)
    packed = lax.all_gather(packed, "section", axis=0, tiled=True)
    qkv_all = packed[:, :, : 3 * model_width]
    out_all = packed[:, :, 3 * model_width : 4 * model_width]
    router_all = packed[:, :, 4 * model_width : used - 4]
    norm_all = packed[:, :, used - 4 : used].transpose(0, 2, 1).astype(jnp.float32)
    gain_all = norm_all[:, 0:2]
    shift_all = norm_all[:, 2:4]
    up_all = lax.all_gather(w_up, "section", axis=0, tiled=True)
    down_all = lax.all_gather(w_down, "section", axis=0, tiled=True)

    cap_rows = round_up(capacity, 16)
    padded_rows = round_up(token_rows + 8, 16)
    slot_index = jnp.where(slot_rows < capacity, route_rows * cap_rows + slot_rows, -1)
    slot_index = jnp.pad(
        slot_index.transpose(0, 2, 1),
        ((0, 0), (0, 6), (0, padded_rows - token_rows)),
        constant_values=-1,
    )
    slot_index = lax.all_gather(slot_index, "dp", axis=1)
    chosen_all = (route_rows[..., None] == jnp.arange(expert_count, dtype=jnp.int32)).astype(
        jnp.float32
    )
    moe = functools.partial(moe_call, depth=depth, groups=groups, cap_rows=cap_rows)

    def layer_forward(layer, inputs):
        chosen = chosen_all[layer]
        normed_one, unit_one, inverse_one = norm_forward(
            inputs, gain_all[layer, 0], shift_all[layer, 0]
        )
        norm_one = normed_one.astype(half)
        qkv_rows = jnp.dot(norm_one, qkv_all[layer], preferred_element_type=jnp.float32).astype(half)
        attended, log_totals = attend_forward(qkv_rows, local_images)
        middle = inputs + jnp.dot(attended, out_all[layer], preferred_element_type=jnp.float32)
        normed_two, unit_two, inverse_two = norm_forward(
            middle, gain_all[layer, 1], shift_all[layer, 1]
        )
        norm_two = normed_two.astype(half)
        logits = jnp.dot(norm_two, router_all[layer], preferred_element_type=jnp.float32)
        picked = jnp.sum(logits[:, None, :] * chosen, axis=-1)
        leading = jax.nn.sigmoid(picked[:, 0] - picked[:, 1])
        gate_pair = jnp.stack([leading, 1.0 - leading], axis=-1)
        gate_rows = jnp.pad(gate_pair.T, ((0, 0), (0, model_width - token_rows)))
        sent = jnp.concatenate(
            [
                norm_two,
                jnp.zeros((padded_rows - 8 - token_rows, model_width), half),
                gate_rows.astype(half),
                jnp.zeros((6, model_width), half),
            ]
        )
        combined, *expert_saved = moe(
            False, 2 * layer, rows=sent, slots=slot_index[layer], up=up_all[layer],
            down=down_all[layer],
        )
        out_rows = middle + combined[:token_rows]
        saved = (
            inputs, norm_one, qkv_rows, log_totals, attended, middle, norm_two, gate_pair,
            expert_saved,
        )
        return (out_rows, saved)

    def layer_backward(layer, d_out, saved):
        (
            inputs, norm_one, qkv_rows, log_totals, attended, middle, norm_two, gate_pair,
            expert_saved,
        ) = saved
        chosen = chosen_all[layer]
        all_rows, hidden, slope, back_rows, gates = expert_saved
        sent = jnp.pad(d_out.astype(half), ((0, padded_rows - token_rows), (0, 0)))
        combined, grads_in, d_pre = moe(
            True, 2 * layer + 1, rows=sent, slots=slot_index[layer], up=up_all[layer],
            down=down_all[layer], saved=(gates, hidden, slope, back_rows),
        )
        d_gate_rows = combined[padded_rows - 8 :, :token_rows]
        d_gate = jnp.stack([d_gate_rows[0] + d_gate_rows[1], d_gate_rows[2] + d_gate_rows[3]], axis=1)
        d_lead = (d_gate[:, 0] - d_gate[:, 1]) * gate_pair[:, 0] * gate_pair[:, 1]
        d_logits = (d_lead[:, None] * (chosen[:, 0] - chosen[:, 1])).astype(half)
        expert_rows = depth * groups * cap_rows
        up_grad = jnp.einsum(
            "erd,erf->edf", all_rows.reshape(EXP_DEV, expert_rows, model_width),
            d_pre.reshape(EXP_DEV, expert_rows, -1), preferred_element_type=jnp.float32,
        )
        down_grad = jnp.einsum(
            "erf,erd->efd", hidden.reshape(EXP_DEV, expert_rows, -1),
            grads_in.reshape(EXP_DEV, expert_rows, model_width), preferred_element_type=jnp.float32,
        )
        owner_pairs = [(1 - layer, layer)]
        up_sent = lax.ppermute(up_grad.astype(half), "section", owner_pairs)
        down_sent = lax.ppermute(down_grad.astype(half), "section", owner_pairs)
        d_norm_two = combined[:token_rows] + jnp.einsum(
            "te,de->td", d_logits, router_all[layer], preferred_element_type=jnp.float32
        )
        normed_two, unit_two, inverse_two = norm_forward(
            middle, gain_all[layer, 1], shift_all[layer, 1]
        )
        d_middle_norm, gain_two, shift_two = norm_backward(
            d_norm_two, unit_two, inverse_two, gain_all[layer, 1]
        )
        d_middle = d_out + d_middle_norm
        d_middle_half = d_middle.astype(half)
        d_attended = jnp.einsum(
            "te,de->td", d_middle_half, out_all[layer], preferred_element_type=jnp.float32
        ).astype(half)
        d_qkv = attend_backward(qkv_rows, log_totals, d_attended, local_images)
        d_norm_one = jnp.einsum(
            "te,de->td", d_qkv, qkv_all[layer], preferred_element_type=jnp.float32
        )
        normed_one, unit_one, inverse_one = norm_forward(
            inputs, gain_all[layer, 0], shift_all[layer, 0]
        )
        d_input_norm, gain_one, shift_one = norm_backward(
            d_norm_one, unit_one, inverse_one, gain_all[layer, 0]
        )
        d_input = d_middle + d_input_norm
        operands = [
            lax.ppermute(item, "section", owner_pairs)
            for item in (norm_one, d_qkv, attended, d_middle_half)
        ]
        own = (norm_one, d_qkv, attended, d_middle_half)
        small = jnp.concatenate(
            [
                jnp.einsum("td,te->ed", norm_two, d_logits, preferred_element_type=jnp.float32),
                jnp.stack([gain_one, gain_two, shift_one, shift_two]),
            ]
        )
        small_sent = lax.ppermute(small, "section", owner_pairs)
        small = small + small_sent
        return (d_input, own, operands, small, (up_grad, up_sent), (down_grad, down_sent))

    stream = edge_rows[0]
    saved_list = []
    for layer in range(2):
        if layer > 0:
            stream = stream.astype(half).astype(jnp.float32)
        stream, saved = layer_forward(layer, stream)
        saved_list.append(saved)
    cotangent = edge_rows[1]
    parts = [None, None]
    for layer in (1, 0):
        if layer < 1:
            cotangent = cotangent.astype(half).astype(jnp.float32)
        cotangent, *parts[layer] = layer_backward(layer, cotangent, saved_list[layer])

    def mine(first, second):
        return jnp.where(is_first, first, second)

    own = [mine(a, b) for a, b in zip(parts[0][0], parts[1][0])]
    other = [mine(a, b) for a, b in zip(parts[0][1], parts[1][1])]
    pairs = [jnp.stack([a, b]) for a, b in zip(own, other)]
    qkv_grad = jnp.einsum("ktd,kte->de", pairs[0], pairs[1], preferred_element_type=jnp.float32)
    out_grad = jnp.einsum("ktd,kte->de", pairs[2], pairs[3], preferred_element_type=jnp.float32)
    small_mine = mine(parts[0][2], parts[1][2])

    packed_grad = jnp.concatenate(
        [qkv_grad, out_grad, small_mine.T, jnp.zeros((model_width, padding), jnp.float32)], axis=1
    ).astype(half)
    blocks = packed_grad.reshape(depth, groups, -1, packed_grad.shape[1]).transpose(1, 0, 2, 3)
    blocks = lax.all_to_all(blocks, "expert", split_axis=0, concat_axis=0, tiled=True)
    blocks = jnp.sum(blocks.astype(jnp.float32), axis=0).astype(half)
    blocks = lax.all_to_all(blocks, "dp", split_axis=0, concat_axis=0, tiled=True)
    grad_shard = jnp.sum(blocks.astype(jnp.float32), axis=0)
    norm_shard = grad_shard[:, used - 4 : used].T

    def expert_grad(index):
        first = parts[0][index][0] + parts[0][index][1].astype(jnp.float32)
        second = parts[1][index][0] + parts[1][index][1].astype(jnp.float32)
        return mine(first, second)[None]

    up_shard = expert_grad(3)
    down_shard = expert_grad(4)
    out_sent = lax.ppermute(stream, "section", [(0, 1)])
    grad_sent = lax.ppermute(cotangent, "section", [(1, 0)])
    boundary_rows = mine(jnp.stack([cotangent, grad_sent]), jnp.stack([out_sent, stream]))
    boundary_out = boundary_rows.reshape(1, MB, local_images, boundary_in.shape[3], model_width)
    return (
        boundary_out,
        norm_shard[None, 0:2],
        norm_shard[None, 2:4],
        grad_shard[None, :, : 3 * model_width],
        grad_shard[None, :, 3 * model_width : 4 * model_width],
        grad_shard[None, :, 4 * model_width : used - 4],
        up_shard,
        down_shard,
    )


def solution(mesh):
    in_specs = (
        P("section", None, ("dp", "expert"), None, None),
        P("section", None, ("dp", "expert"), None, None),
        P("section", None, ("dp", "expert"), None, None),
        P("section", None, ("dp", "expert")),
        P("section", None, ("dp", "expert")),
        P("section", ("dp", "expert"), None),
        P("section", ("dp", "expert"), None),
        P("section", ("dp", "expert"), None),
        P("section", "expert", None, "dp"),
        P("section", "expert", "dp", None),
    )
    out_specs = (
        P("section", None, ("dp", "expert"), None, None),
        P("section", None, ("dp", "expert")),
        P("section", None, ("dp", "expert")),
        P("section", ("dp", "expert"), None),
        P("section", ("dp", "expert"), None),
        P("section", ("dp", "expert"), None),
        P("section", "expert", None, "dp"),
        P("section", "expert", "dp", None),
    )
    return jax.shard_map(
        on_device, mesh=mesh, in_specs=in_specs, out_specs=out_specs, check_vma=False
    )
```

```python
import functools
import math

import jax
import jax.numpy as jnp
from jax import lax
from jax.experimental import pallas as pl
from jax.experimental.pallas import tpu as pltpu
from jax.sharding import PartitionSpec as P

HEADS = 12
HEAD_DIM = 64
EXP_DEV = 2
MB = 2


EPS = 1e-06
SQRT_HALF = 0.7071067811865476
INV_ROOT_TAU = 0.3989422804014327
MESH = pl.DeviceIdType.MESH


def round_up(value, unit):
    return (value + unit - 1) // unit * unit


def z_order(step, z, depth):
    if depth == 1:
        return z
    direction = 1 - 2 * (z // (depth // 2))
    return lax.rem(z + step * direction + depth, depth)


def f32_dot(a, b, dims):
    return lax.dot_general(a, b, (dims, ((), ())), preferred_element_type=jnp.float32)


def moe_kernel(backward, shape, *refs):
    depth, groups, cap_rows, token_rows, model_width, hidden_width = shape
    if backward:
        (
            rows_ref, slots_ref, up_ref, down_ref, gates_ref, hidden_ref, slope_ref, back_ref,
            kept_ref, out_ref, up_grad_ref, down_grad_ref, inbox, d_pre_ref,
            raw, sent_rows, sent_back, sent_home, home, back, d_gates, *sems,
        ) = refs
    else:
        (
            rows_ref, slots_ref, up_ref, down_ref,
            out_ref, inbox, hidden_ref, slope_ref, back, gates_ref,
            raw, sent_rows, sent_back, sent_home, home, *sems,
        ) = refs
    far_send, far_recv, go_send, go_recv, back_send, back_recv, home_send, home_recv = sems
    half = jnp.bfloat16
    section, z, column = (
        lax.axis_index("section"), lax.axis_index("dp"), lax.axis_index("expert")
    )
    slot_count = 2 * groups * cap_rows
    tail = token_rows - 16

    def z_peer(distance):
        return (section, lax.rem(z + distance, depth), column)

    def xy_peer(distance):
        return lax.rem(column + distance, groups)

    barrier = pltpu.get_barrier_semaphore()

    def greet_z(distance, carry):
        pl.semaphore_signal(barrier, inc=1, device_id=z_peer(distance), device_id_type=MESH)
        return carry

    def greet_xy(distance, carry):
        pl.semaphore_signal(
            barrier, inc=1, device_id=(section, z, xy_peer(distance)), device_id_type=MESH
        )
        return carry

    lax.fori_loop(1, depth, greet_z, 0)
    lax.fori_loop(1, groups, greet_xy, 0)
    pl.semaphore_wait(barrier, depth - 1 + groups - 1)

    def far_copy(direction, image):
        target = lax.rem(z + 2 * direction - 1 + depth, depth)
        source = raw.at[image]
        return pltpu.make_async_remote_copy(
            src_ref=source, dst_ref=raw.at[image],
            send_sem=far_send.at[direction, image], recv_sem=far_recv.at[image],
            device_id=(section, target, column), device_id_type=MESH,
        )

    def go_copy(image, source, target):
        return pltpu.make_async_remote_copy(
            src_ref=sent_rows.at[image, target], dst_ref=inbox.at[:, image, source],
            send_sem=go_send.at[image, target], recv_sem=go_recv.at[image, source],
            device_id=(section, z, target), device_id_type=MESH,
        )

    def back_copy(image, source, target):
        return pltpu.make_async_remote_copy(
            src_ref=sent_back.at[image, target], dst_ref=back.at[image, source],
            send_sem=back_send.at[image, target], recv_sem=back_recv.at[image, source],
            device_id=(section, z, target), device_id_type=MESH,
        )

    def home_copy(source, target):
        return pltpu.make_async_remote_copy(
            src_ref=sent_home.at[target], dst_ref=home.at[source],
            send_sem=home_send.at[target], recv_sem=home_recv.at[source],
            device_id=(section, target, column), device_id_type=MESH,
        )

    raw[z] = rows_ref[...]

    @pl.when(z < depth - 1)
    def _():
        far_copy(1, z).start()

    @pl.when(z > 0)
    def _():
        far_copy(0, z).start()

    def match(image):
        slots = slots_ref[image][:, :token_rows]
        index = lax.broadcasted_iota(jnp.int32, (slot_count, token_rows), 0)
        return index == slots[0:1], index == slots[1:2]

    def gate_table(image):
        first, second = match(image)
        gates = gates_ref[image]
        table = jnp.where(first, gates[0:1], 0.0) + jnp.where(second, gates[1:2], 0.0)
        return table.astype(half)

    def ones_table(image):
        first, second = match(image)
        return jnp.where(first | second, 1.0, 0.0).astype(half)

    def pass_on(step):
        low, high = z - step, z + step

        @pl.when(low >= 0)
        def _():
            far_copy(1, low).wait_recv()

            @pl.when(z < depth - 1)
            def _():
                far_copy(1, low).start()

        @pl.when(high < depth)
        def _():
            far_copy(0, high).wait_recv()

            @pl.when(z > 0)
            def _():
                far_copy(0, high).start()

    def dispatch(image):
        if not backward:
            gates_ref[image] = raw[image, tail:, :token_rows].astype(jnp.float32)[8:16]
        table = gate_table(image) if backward else ones_table(image)
        rows = raw[image]
        blocks = f32_dot(table, rows, ((1,), (0,))).astype(half)
        sent_rows[image] = blocks.reshape(groups, 2, cap_rows, model_width)

        def send(distance, carry):
            go_copy(image, column, xy_peer(distance)).start()
            return carry

        lax.fori_loop(1, groups, send, 0)
        inbox[:, image, column] = sent_rows[image, column]
        if backward:
            first, second = match(image)
            returned = back_ref[image].reshape(slot_count, model_width)
            ones = jnp.ones((8, model_width), half)
            row_index = lax.broadcasted_iota(jnp.int32, (8, token_rows), 0)
            packed = jnp.zeros((8, token_rows), jnp.float32)
            for choice, found in enumerate((first, second)):
                table = jnp.where(found, 1.0, 0.0).astype(half)
                selected = f32_dot(table, returned, ((0,), (0,)))
                product = (selected * rows.astype(jnp.float32)).astype(half)
                sums = f32_dot(ones, product, ((1,), (1,)))
                high = sums.astype(half).astype(jnp.float32)
                packed = jnp.where(row_index == 2 * choice, high, packed)
                packed = jnp.where(row_index == 2 * choice + 1, sums - high, packed)
            d_gates[image] = packed

    def experts(image):
        def arrive(distance, carry):
            go_copy(image, xy_peer(distance), column).wait_recv()
            return carry

        lax.fori_loop(1, groups, arrive, 0)
        for expert in range(2):
            rows = inbox[expert, image].reshape(groups * cap_rows, model_width)
            if backward:
                d_hidden = f32_dot(rows, down_ref[expert], ((1,), (1,)))
                d_pre = (d_hidden * slope_ref[expert, image].astype(jnp.float32)).astype(half)
                d_pre_ref[expert, image] = d_pre
                result = f32_dot(d_pre, up_ref[expert], ((1,), (1,)))
            else:
                pre = f32_dot(rows, up_ref[expert], ((1,), (0,)))
                share = 0.5 * (1.0 + lax.erf(pre * SQRT_HALF))
                slope = share + pre * jnp.exp(-0.5 * pre * pre) * INV_ROOT_TAU
                hidden = (pre * share).astype(half)
                hidden_ref[expert, image] = hidden
                slope_ref[expert, image] = slope.astype(half)
                result = f32_dot(hidden, down_ref[expert], ((1,), (0,)))
            sent_back[image, :, expert] = result.astype(half).reshape(
                groups, cap_rows, model_width
            )

        def send(distance, carry):
            back_copy(image, column, xy_peer(distance)).start()
            return carry

        lax.fori_loop(1, groups, send, 0)
        back[image, column] = sent_back[image, column]

    def combine(image):
        def arrive(distance, carry):
            back_copy(image, xy_peer(distance), column).wait_recv()
            return carry

        lax.fori_loop(1, groups, arrive, 0)
        table = ones_table(image) if backward else gate_table(image)
        total = f32_dot(table, back[image].reshape(slot_count, model_width), ((0,), (0,)))
        if backward:
            extra = jnp.concatenate(
                [jnp.zeros((8, token_rows), jnp.float32), d_gates[image]], axis=0
            )

        @pl.when(image == z)
        def _():
            out_ref[...] = total
            if backward:
                out_ref[tail:, :token_rows] = total[tail:, :token_rows] + extra

        @pl.when(image != z)
        def _():
            sent_home[image] = total.astype(half)
            if backward:
                sent_home[image, tail:, :token_rows] = (
                    total[tail:, :token_rows] + extra
                ).astype(half)
            home_copy(z, image).start()

    def stage(step, carry):
        @pl.when(jnp.logical_and(step >= 1, step < depth))
        def _():
            pass_on(step)

        @pl.when(step < depth)
        def _():
            dispatch(z_order(step, z, depth))

        @pl.when(jnp.logical_and(step >= 1, step < depth + 1))
        def _():
            experts(z_order(step - 1, z, depth))

        @pl.when(step >= 2)
        def _():
            combine(z_order(step - 2, z, depth))

        return carry

    lax.fori_loop(0, depth + 2, stage, 0)

    if backward:

        def expert_gradients(expert, carry):
            kept = kept_ref[expert].reshape(depth * groups * cap_rows, model_width)
            d_pre = d_pre_ref[expert].reshape(depth * groups * cap_rows, hidden_width)
            up_grad_ref[expert] = f32_dot(kept, d_pre, ((0,), (0,))).astype(half)
            hidden = hidden_ref[expert].reshape(depth * groups * cap_rows, hidden_width)
            grads = inbox[expert].reshape(depth * groups * cap_rows, model_width)
            down_grad_ref[expert] = f32_dot(hidden, grads, ((0,), (0,))).astype(half)
            return carry

        lax.fori_loop(0, 2, expert_gradients, 0)

    def finish_home(distance, carry):
        source = lax.rem(z + distance, depth)
        home_copy(source, z).wait_recv()
        out_ref[...] += home[source].astype(jnp.float32)
        return carry

    lax.fori_loop(1, depth, finish_home, 0)

    def drain_home(distance, carry):
        home_copy(z, lax.rem(z + distance, depth)).wait_send()
        return carry

    lax.fori_loop(1, depth, drain_home, 0)

    def drain_image(image, carry):
        @pl.when(jnp.logical_and(z < depth - 1, image <= z))
        def _():
            far_copy(1, image).wait_send()

        @pl.when(jnp.logical_and(z > 0, image >= z))
        def _():
            far_copy(0, image).wait_send()

        def drain(distance, inner):
            go_copy(image, column, xy_peer(distance)).wait_send()
            back_copy(image, column, xy_peer(distance)).wait_send()
            return inner

        lax.fori_loop(1, groups, drain, 0)
        return carry

    lax.fori_loop(0, depth, drain_image, 0)


def moe_call(backward, call_id, depth, groups, cap_rows, rows, slots, up, down, saved=()):
    token_rows, model_width = rows.shape
    hidden_width = up.shape[2]
    half = jnp.bfloat16
    shape = (depth, groups, cap_rows, token_rows, model_width, hidden_width)
    inbox = jax.ShapeDtypeStruct((2, depth, groups, cap_rows, model_width), half)
    hidden = jax.ShapeDtypeStruct((2, depth, groups * cap_rows, hidden_width), half)
    back = (depth, groups, 2, cap_rows, model_width)
    out = jax.ShapeDtypeStruct((token_rows, model_width), jnp.float32)
    if backward:
        out_shape = (
            out, jax.ShapeDtypeStruct(up.shape, half), jax.ShapeDtypeStruct(down.shape, half)
        )
    else:
        gates = jax.ShapeDtypeStruct((depth, 8, token_rows), jnp.float32)
        out_shape = (out, inbox, hidden, hidden, jax.ShapeDtypeStruct(back, half), gates)
    scratch = [
        pltpu.VMEM((depth, token_rows, model_width), half),
        pltpu.VMEM((depth, groups, 2, cap_rows, model_width), half),
        pltpu.VMEM(back, half),
        pltpu.VMEM((depth, token_rows, model_width), half),
        pltpu.VMEM((depth, token_rows, model_width), half),
    ]
    if backward:
        scratch = [pltpu.VMEM(inbox.shape, half), pltpu.VMEM(hidden.shape, half)] + scratch
        scratch += [
            pltpu.VMEM(back, half),
            pltpu.VMEM((depth, 8, token_rows), jnp.float32),
        ]
    scratch += [
        pltpu.SemaphoreType.DMA((2, depth)),
        pltpu.SemaphoreType.DMA((depth,)),
        pltpu.SemaphoreType.DMA((depth, groups)),
        pltpu.SemaphoreType.DMA((depth, groups)),
        pltpu.SemaphoreType.DMA((depth, groups)),
        pltpu.SemaphoreType.DMA((depth, groups)),
        pltpu.SemaphoreType.DMA((depth,)),
        pltpu.SemaphoreType.DMA((depth,)),
    ]
    return pl.pallas_call(
        functools.partial(moe_kernel, backward, shape),
        out_shape=out_shape,
        in_specs=[pl.BlockSpec(memory_space=pltpu.VMEM)] * (4 + len(saved)),
        out_specs=[pl.BlockSpec(memory_space=pltpu.VMEM)] * len(out_shape),
        scratch_shapes=scratch,
        compiler_params=pltpu.CompilerParams(
            collective_id=call_id, has_side_effects=True, vmem_limit_bytes=50 * 2**20
        ),
        name="moe_backward" if backward else "moe_forward",
    )(rows, slots, up, down, *saved)

def start_kernel(shape, *refs):
    depth, groups, half_width = shape
    (
        packed_ref, up_ref, down_ref, edge_ref, table_ref,
        dense_ref, later_ref, up_first, up_second, down_first, down_second,
        rows_ref, cotangent_ref, table_first, table_second,
        shard_send, shard_recv, core_send, core_recv, table_send, table_recv, own_sem,
    ) = refs
    section, z, column = (
        lax.axis_index("section"), lax.axis_index("dp"), lax.axis_index("expert")
    )
    other = (1 - section, z, column)
    is_first = section == 0

    def z_peer(distance):
        return lax.rem(z + distance, depth)

    def xy_peer(distance):
        return lax.rem(column + distance, groups)

    barrier = pltpu.get_barrier_semaphore()

    def greet_z(distance, carry):
        pl.semaphore_signal(
            barrier, inc=1, device_id=(section, z_peer(distance), column), device_id_type=MESH
        )
        return carry

    def greet_xy(distance, carry):
        pl.semaphore_signal(
            barrier, inc=1, device_id=(section, z, xy_peer(distance)), device_id_type=MESH
        )
        return carry

    pl.semaphore_signal(barrier, inc=1, device_id=other, device_id_type=MESH)
    lax.fori_loop(1, depth, greet_z, 0)
    lax.fori_loop(1, groups, greet_xy, 0)
    pl.semaphore_wait(barrier, depth + groups - 1)

    def remote(source, target, send, recv, device):
        return pltpu.make_async_remote_copy(
            src_ref=source, dst_ref=target, send_sem=send, recv_sem=recv,
            device_id=device, device_id_type=MESH,
        )

    def shard_copy(kind, source_ref, plane, lane, device):
        return remote(
            source_ref, dense_ref.at[plane, lane], shard_send.at[kind, plane, lane],
            shard_recv.at[plane, lane], device,
        )

    def z_copy(direction, plane):
        device = (section, lax.rem(z + 2 * direction - 1 + depth, depth), column)
        return shard_copy(direction, dense_ref.at[plane, column], plane, column, device)

    def core_copy(plane, lane):
        return shard_copy(2, dense_ref.at[plane, lane], plane, lane, other)

    def xy_copy(plane, source, target):
        return remote(
            dense_ref.at[plane, source], dense_ref.at[plane, source],
            shard_send.at[3 + target, plane, source], shard_recv.at[plane, source],
            (section, z, target),
        )

    def swap(index, source, target):
        return remote(source, target, core_send.at[index], core_recv.at[index], other)

    def local(index, source, target):
        return pltpu.make_async_copy(source, target, own_sem.at[index])

    def spread(plane):
        core_copy(plane, column).start()

        def send(distance, carry):
            xy_copy(plane, column, xy_peer(distance)).start()
            return carry

        lax.fori_loop(1, groups, send, 0)

    own_shard = local(0, packed_ref, dense_ref.at[z, column])
    left, right = pl.ds(0, half_width), pl.ds(half_width, half_width)

    def first_copies():
        remote_ones = [
            swap(0, edge_ref.at[1], rows_ref),
            swap(1, table_ref.at[1], table_first.at[z]),
            swap(2, up_ref, up_first),
            swap(3, down_ref, down_first),
        ]
        local_ones = [
            local(1, edge_ref.at[0], rows_ref),
            local(2, table_ref.at[0], table_first.at[z]),
            local(3, up_ref, up_first),
            local(4, down_ref, down_first),
        ]
        return remote_ones, local_ones

    def second_copies():
        remote_ones = [
            swap(0, edge_ref.at[0], cotangent_ref),
            swap(1, table_ref.at[0], table_second.at[z]),
            swap(2, up_ref, up_second),
            swap(3, down_ref, down_second),
            swap(4, packed_ref.at[:, left], later_ref),
        ]
        local_ones = [
            local(1, edge_ref.at[1], cotangent_ref),
            local(2, table_ref.at[1], table_second.at[z]),
            local(3, up_ref, up_second),
            local(4, down_ref, down_second),
            local(5, packed_ref.at[:, right], later_ref),
        ]
        return remote_ones, local_ones

    @pl.when(is_first)
    def _():
        own_shard.start()
        remote_ones, local_ones = first_copies()
        own_shard.wait()

        @pl.when(z < depth - 1)
        def _():
            z_copy(1, z).start()

        @pl.when(z > 0)
        def _():
            z_copy(0, z).start()

        spread(z)
        for copy in remote_ones[:2] + local_ones + remote_ones[2:]:
            copy.start()

        def step(distance, carry):
            low, high = z - distance, z + distance

            @pl.when(low >= 0)
            def _():
                z_copy(1, low).wait_recv()

                @pl.when(z < depth - 1)
                def _():
                    z_copy(1, low).start()

                spread(low)

            @pl.when(high < depth)
            def _():
                z_copy(0, high).wait_recv()

                @pl.when(z > 0)
                def _():
                    z_copy(0, high).start()

                spread(high)

            return carry

        lax.fori_loop(1, depth, step, 0)

    @pl.when(jnp.logical_not(is_first))
    def _():
        remote_ones, local_ones = second_copies()
        for copy in remote_ones[:2] + remote_ones[4:] + local_ones + remote_ones[2:4]:
            copy.start()

    first_remote, first_local = first_copies()
    second_remote, second_local = second_copies()

    def table_copies(source, target):
        pairs = []
        for layer, table in enumerate((table_first, table_second)):
            pairs.append(
                remote(
                    table.at[source], table.at[source], table_send.at[layer, target],
                    table_recv.at[layer, source], (section, target, column),
                )
            )
        return pairs

    @pl.when(is_first)
    def _():
        first_local[1].wait()
        second_remote[1].wait_recv()

    @pl.when(jnp.logical_not(is_first))
    def _():
        second_local[1].wait()
        first_remote[1].wait_recv()

    def send_tables(distance, carry):
        for copy in table_copies(z, z_peer(distance)):
            copy.start()
        return carry

    lax.fori_loop(1, depth, send_tables, 0)

    @pl.when(is_first)
    def _():
        def forward(step, carry):
            plane = z_order(step, z, depth)

            def arrive(distance, inner):
                lane = xy_peer(distance)
                xy_copy(plane, lane, column).wait_recv()
                core_copy(plane, lane).start()
                return inner

            return lax.fori_loop(1, groups, arrive, carry)

        lax.fori_loop(0, depth, forward, 0)
        for copy in second_remote:
            copy.wait_recv() if copy is not second_remote[1] else None
        for copy in first_remote:
            copy.wait_send()
        for copy in first_local[:1] + first_local[2:]:
            copy.wait()

        def drain(plane, carry):
            @pl.when(jnp.logical_and(z < depth - 1, plane <= z))
            def _():
                z_copy(1, plane).wait_send()

            @pl.when(jnp.logical_and(z > 0, plane >= z))
            def _():
                z_copy(0, plane).wait_send()

            def drain_core(lane, inner):
                core_copy(plane, lane).wait_send()
                return inner

            def drain_xy(distance, inner):
                xy_copy(plane, column, xy_peer(distance)).wait_send()
                return inner

            lax.fori_loop(0, groups, drain_core, 0)
            return lax.fori_loop(1, groups, drain_xy, carry)

        lax.fori_loop(0, depth, drain, 0)

    @pl.when(jnp.logical_not(is_first))
    def _():
        def arrive(plane, carry):
            def inner_arrive(lane, inner):
                core_copy(plane, lane).wait_recv()
                return inner

            return lax.fori_loop(0, groups, inner_arrive, carry)

        lax.fori_loop(0, depth, arrive, 0)
        for index in (0, 2, 3):
            first_remote[index].wait_recv()
        for copy in second_remote:
            copy.wait_send()
        for copy in second_local[:1] + second_local[2:]:
            copy.wait()

    def finish_tables(distance, carry):
        for copy in table_copies(z_peer(distance), z):
            copy.wait_recv()
        for copy in table_copies(z, z_peer(distance)):
            copy.wait_send()
        return carry

    lax.fori_loop(1, depth, finish_tables, 0)


def start_call(call_id, depth, groups, packed, up, down, edge, table):
    rows, width = packed.shape
    half = jnp.bfloat16
    out_shape = (
        jax.ShapeDtypeStruct((depth, groups, rows, width), half),
        jax.ShapeDtypeStruct((rows, width // 2), half),
        jax.ShapeDtypeStruct(up.shape, half),
        jax.ShapeDtypeStruct(up.shape, half),
        jax.ShapeDtypeStruct(down.shape, half),
        jax.ShapeDtypeStruct(down.shape, half),
        jax.ShapeDtypeStruct(edge.shape[1:], jnp.float32),
        jax.ShapeDtypeStruct(edge.shape[1:], jnp.float32),
        jax.ShapeDtypeStruct((depth,) + table.shape[1:], jnp.int32),
        jax.ShapeDtypeStruct((depth,) + table.shape[1:], jnp.int32),
    )
    return pl.pallas_call(
        functools.partial(start_kernel, (depth, groups, width // 2)),
        out_shape=out_shape,
        in_specs=[pl.BlockSpec(memory_space=pltpu.VMEM)] * 5,
        out_specs=[pl.BlockSpec(memory_space=pl.ANY)] * len(out_shape),
        scratch_shapes=[
            pltpu.SemaphoreType.DMA((3 + groups, depth, groups)),
            pltpu.SemaphoreType.DMA((depth, groups)),
            pltpu.SemaphoreType.DMA((5,)),
            pltpu.SemaphoreType.DMA((5,)),
            pltpu.SemaphoreType.DMA((2, depth)),
            pltpu.SemaphoreType.DMA((2, depth)),
            pltpu.SemaphoreType.DMA((6,)),
        ],
        compiler_params=pltpu.CompilerParams(
            collective_id=call_id, has_side_effects=True, vmem_limit_bytes=40 * 2**20
        ),
        name="start_exchange",
    )(packed, up, down, edge, table)

def finish_kernel(shape, *refs):
    depth, groups, token_rows, padded_rows, model_width = shape
    first_refs, second_refs, rest = refs[0:5], refs[5:10], refs[10:]
    (
        up_first, down_first, up_second, down_second, rows_first, rows_second,
        shard_ref, up_ref, down_ref, rows_ref,
        pair, away, small_pair, table, inbox, sent_home, home,
        core_send, core_recv, go_send, go_recv, home_send, home_recv,
    ) = rest
    half = jnp.bfloat16
    section, z, column = (
        lax.axis_index("section"), lax.axis_index("dp"), lax.axis_index("expert")
    )
    other = (1 - section, z, column)
    is_first = section == 0
    shard_rows = table.shape[1]

    def z_peer(distance):
        return lax.rem(z + distance, depth)

    def xy_peer(distance):
        return lax.rem(column + distance, groups)

    barrier = pltpu.get_barrier_semaphore()

    def greet_z(distance, carry):
        pl.semaphore_signal(
            barrier, inc=1, device_id=(section, z_peer(distance), column), device_id_type=MESH
        )
        return carry

    def greet_xy(distance, carry):
        pl.semaphore_signal(
            barrier, inc=1, device_id=(section, z, xy_peer(distance)), device_id_type=MESH
        )
        return carry

    pl.semaphore_signal(barrier, inc=1, device_id=other, device_id_type=MESH)
    lax.fori_loop(1, depth, greet_z, 0)
    lax.fori_loop(1, groups, greet_xy, 0)
    pl.semaphore_wait(barrier, depth + groups - 1)

    def swap(index, source, target):
        return pltpu.make_async_remote_copy(
            src_ref=source, dst_ref=target, send_sem=core_send.at[index],
            recv_sem=core_recv.at[index], device_id=other, device_id_type=MESH,
        )

    def pack(target, operands):
        target[padded_rows - 16 :, :] = jnp.zeros((16, target.shape[1]), half)
        offset = 0
        for operand in operands:
            width = operand.shape[1]
            target[:token_rows, offset : offset + width] = operand[...]
            offset += width

    def side_copies(first):
        if first:
            sources = (second_refs[4], up_second, down_second, rows_second)
        else:
            sources = (first_refs[4], up_first, down_first, rows_first)
        targets = (small_pair.at[1], up_ref, down_ref, rows_ref)
        return [
            swap(1 + index, source, target)
            for index, (source, target) in enumerate(zip(sources, targets))
        ]

    operand_copy = swap(0, away, pair.at[1])
    for first in (True, False):

        @pl.when(is_first if first else jnp.logical_not(is_first))
        def _():
            mine, others = (first_refs, second_refs) if first else (second_refs, first_refs)
            pack(away, others[:4])
            operand_copy.start()
            for copy in side_copies(first):
                copy.start()
            pack(pair.at[0], mine[:4])
            small_pair[0] = mine[4][...]

    operand_copy.wait_recv()
    rows = 2 * padded_rows

    def product(left, right, target):
        a = pair[:, :, left : left + model_width].reshape(rows, model_width)
        b = pair[:, :, right : right + model_width].reshape(rows, model_width)
        value = f32_dot(a, b, ((0,), (0,))).astype(half)
        table[:, :, target : target + model_width] = value.reshape(
            depth * groups, shard_rows, model_width
        )

    for index in range(3):
        product(0, (1 + index) * model_width, index * model_width)
    product(4 * model_width, 5 * model_width, 3 * model_width)
    for copy in side_copies(True)[:1]:
        copy.wait_recv()
    small = (small_pair[0] + small_pair[1]).astype(half)
    table[:, :, 4 * model_width :] = small.reshape(depth * groups, shard_rows, small.shape[1])

    def go_copy(plane, source, target):
        return pltpu.make_async_remote_copy(
            src_ref=table.at[plane * groups + target], dst_ref=inbox.at[plane, source],
            send_sem=go_send.at[plane, target], recv_sem=go_recv.at[plane, source],
            device_id=(section, z, target), device_id_type=MESH,
        )

    def home_copy(source, target):
        return pltpu.make_async_remote_copy(
            src_ref=sent_home.at[target], dst_ref=home.at[source],
            send_sem=home_send.at[target], recv_sem=home_recv.at[source],
            device_id=(section, target, column), device_id_type=MESH,
        )

    def send_plane(step, carry):
        plane = z_peer(step)

        def send(distance, inner):
            go_copy(plane, column, xy_peer(distance)).start()
            return inner

        return lax.fori_loop(1, groups, send, carry)

    lax.fori_loop(1, depth + 1, send_plane, 0)

    def sum_plane(step, carry):
        plane = z_peer(step)

        def arrive(distance, total):
            lane = xy_peer(distance)
            go_copy(plane, lane, column).wait_recv()
            return total + inbox[plane, lane].astype(jnp.float32)

        own = table[plane * groups + column].astype(jnp.float32)
        total = lax.fori_loop(1, groups, arrive, own)

        @pl.when(plane == z)
        def _():
            shard_ref[...] = total

        @pl.when(plane != z)
        def _():
            sent_home[plane] = total.astype(half)
            home_copy(z, plane).start()

        return carry

    lax.fori_loop(1, depth + 1, sum_plane, 0)

    def finish_home(distance, carry):
        source = z_peer(distance)
        home_copy(source, z).wait_recv()
        shard_ref[...] += home[source].astype(jnp.float32)
        home_copy(z, source).wait_send()
        return carry

    lax.fori_loop(1, depth, finish_home, 0)

    def drain_plane(plane, carry):
        def drain(distance, inner):
            go_copy(plane, column, xy_peer(distance)).wait_send()
            return inner

        return lax.fori_loop(1, groups, drain, carry)

    lax.fori_loop(0, depth, drain_plane, 0)
    operand_copy.wait_send()
    for index, copy in enumerate(side_copies(True)):
        copy.wait_send()
        if index > 0:
            copy.wait_recv()


def finish_call(call_id, depth, groups, first, second, up_first, down_first, up_second, down_second,
                rows_first, rows_second):
    token_rows, model_width = first[0].shape
    padded_rows = round_up(token_rows, 16)
    small_width = first[4].shape[1]
    width = 4 * model_width + small_width
    shard_rows = model_width // (depth * groups)
    half = jnp.bfloat16
    out_shape = (
        jax.ShapeDtypeStruct((shard_rows, width), jnp.float32),
        jax.ShapeDtypeStruct(up_first.shape, half),
        jax.ShapeDtypeStruct(down_first.shape, half),
        jax.ShapeDtypeStruct(rows_first.shape, jnp.float32),
    )
    home = pltpu.VMEM((depth, shard_rows, width), half)
    return pl.pallas_call(
        functools.partial(
            finish_kernel, (depth, groups, token_rows, padded_rows, model_width)
        ),
        out_shape=out_shape,
        in_specs=[pl.BlockSpec(memory_space=pltpu.VMEM)] * 16,
        out_specs=[pl.BlockSpec(memory_space=pltpu.VMEM)] + [pl.BlockSpec(memory_space=pl.ANY)] * 3,
        scratch_shapes=[
            pltpu.VMEM((2, padded_rows, 6 * model_width), half),
            pltpu.VMEM((padded_rows, 6 * model_width), half),
            pltpu.VMEM((2, model_width, small_width), jnp.float32),
            pltpu.VMEM((depth * groups, shard_rows, width), half),
            pltpu.VMEM((depth, groups, shard_rows, width), half),
            home,
            home,
            pltpu.SemaphoreType.DMA((5,)),
            pltpu.SemaphoreType.DMA((5,)),
            pltpu.SemaphoreType.DMA((depth, groups)),
            pltpu.SemaphoreType.DMA((depth, groups)),
            pltpu.SemaphoreType.DMA((depth,)),
            pltpu.SemaphoreType.DMA((depth,)),
        ],
        compiler_params=pltpu.CompilerParams(
            collective_id=call_id, has_side_effects=True, vmem_limit_bytes=50 * 2**20
        ),
        name="finish_exchange",
    )(*first, *second, up_first, down_first, up_second, down_second, rows_first, rows_second)


def norm_forward(values, gain_row, shift_row):
    centred = values - jnp.mean(values, axis=-1, keepdims=True)
    variance = jnp.mean(centred * centred, axis=-1, keepdims=True)
    inverse = lax.rsqrt(variance + EPS)
    unit_rows = centred * inverse
    return (unit_rows * gain_row + shift_row, unit_rows, inverse)


def norm_backward(d_normed, unit_rows, inverse, gain_row):
    d_gain = jnp.sum(d_normed * unit_rows, axis=0)
    d_shift = jnp.sum(d_normed, axis=0)
    scaled = d_normed * gain_row
    d_values = inverse * (
        scaled
        - jnp.mean(scaled, axis=-1, keepdims=True)
        - unit_rows * jnp.mean(scaled * unit_rows, axis=-1, keepdims=True)
    )
    return (d_values, d_gain, d_shift)


def gelu_slope(pre_act):
    return (
        0.5 * (1.0 + lax.erf(pre_act * SQRT_HALF))
        + pre_act * jnp.exp(-0.5 * pre_act * pre_act) * INV_ROOT_TAU
    )


def split_heads(qkv_rows, image_count):
    feature_count = qkv_rows.shape[1] // 3
    return [
        qkv_rows[:, part_index * feature_count : (part_index + 1) * feature_count].reshape(
            image_count, -1, HEADS, HEAD_DIM
        )
        for part_index in range(3)
    ]


def attend_forward(qkv_rows, image_count):
    queries, key_rows, value_rows = split_heads(qkv_rows, image_count)
    scale_factor = 1.0 / math.sqrt(HEAD_DIM)
    scores = (
        jnp.einsum("bqhd,bkhd->bhqk", queries, key_rows, preferred_element_type=jnp.float32)
        * scale_factor
    )
    log_totals = jnp.log(jnp.sum(jnp.exp(scores), axis=-1))
    probs_half = jnp.exp(scores - log_totals[..., None]).astype(jnp.bfloat16)
    attended = jnp.einsum(
        "bhqk,bkhd->bqhd", probs_half, value_rows, preferred_element_type=jnp.float32
    )
    return (attended.astype(jnp.bfloat16).reshape(-1, HEADS * HEAD_DIM), log_totals)


def attend_backward(qkv_rows, log_totals, d_attended, image_count):
    queries, key_rows, value_rows = split_heads(qkv_rows, image_count)
    scale_factor = 1.0 / math.sqrt(HEAD_DIM)
    scores = (
        jnp.einsum("bqhd,bkhd->bhqk", queries, key_rows, preferred_element_type=jnp.float32)
        * scale_factor
    )
    probs = jnp.exp(scores - log_totals[..., None])
    probs_half = probs.astype(jnp.bfloat16)
    d_heads = d_attended.reshape(image_count, -1, HEADS, HEAD_DIM)
    d_values = jnp.einsum(
        "bhqk,bqhd->bkhd", probs_half, d_heads, preferred_element_type=jnp.float32
    )
    d_probs = jnp.einsum("bqhd,bkhd->bhqk", d_heads, value_rows, preferred_element_type=jnp.float32)
    row_dot = jnp.sum(probs * d_probs, axis=-1, keepdims=True)
    d_scores = (probs * (d_probs - row_dot) * scale_factor).astype(jnp.bfloat16)
    d_queries = jnp.einsum(
        "bhqk,bkhd->bqhd", d_scores, key_rows, preferred_element_type=jnp.float32
    )
    d_keys = jnp.einsum("bhqk,bqhd->bkhd", d_scores, queries, preferred_element_type=jnp.float32)
    feature_count = HEADS * HEAD_DIM
    joined = jnp.concatenate(
        [
            d_queries.reshape(-1, feature_count),
            d_keys.reshape(-1, feature_count),
            d_values.reshape(-1, feature_count),
        ],
        axis=1,
    )
    return joined.astype(jnp.bfloat16)


def on_device(
    boundary_in, routes, capacity_slots, ln_gain, ln_bias, w_qkv, w_out, w_router, w_up, w_down
):
    section_index = lax.axis_index("section")
    is_first = section_index == 0
    depth = lax.axis_size("dp")
    groups = lax.axis_size("expert")
    expert_count = EXP_DEV * groups
    local_images = boundary_in.shape[2]
    token_rows = local_images * boundary_in.shape[3]
    model_width = boundary_in.shape[4]
    capacity = 26 * token_rows // (16 * expert_count)
    cap_rows = round_up(capacity, 16)
    padded_rows = round_up(token_rows + 8, 16)
    chips = ("dp", "expert")
    half = jnp.bfloat16
    swapped = [(0, 1), (1, 0)]

    edge = boundary_in[0].reshape(MB, token_rows, model_width)
    route_rows = routes[0].reshape(MB, token_rows, 2)
    slot_rows = capacity_slots[0].reshape(MB, token_rows, 2)
    slot_index = jnp.where(slot_rows < capacity, route_rows * cap_rows + slot_rows, -1)
    table = jnp.concatenate([slot_index, route_rows], axis=2).transpose(0, 2, 1)
    table = jnp.pad(
        table, ((0, 0), (0, 4), (0, padded_rows - token_rows)), constant_values=-1
    )

    norm_columns = jnp.concatenate([ln_gain, ln_bias], axis=1).transpose(0, 2, 1)
    used = 4 * model_width + expert_count + 4
    padding = -used % 256
    packed = jnp.concatenate([w_qkv, w_out, w_router, norm_columns], axis=2)
    packed = jnp.pad(packed, ((0, 0), (0, 0), (0, padding)))
    (
        dense_first, later_half, up_first, up_second, down_first, down_second,
        stream, cotangent, table_first, table_second,
    ) = start_call(8, depth, groups, packed[0], w_up[0], w_down[0], edge, table)
    dense_first = dense_first.reshape(model_width, used + padding)
    later_half = lax.all_gather(later_half, chips, axis=0, tiled=True)
    qkv_all, out_all, router_all, norm_all = [], [], [], []

    def add_dense(item):
        qkv_all.append(item[:, : 3 * model_width])
        out_all.append(item[:, 3 * model_width : 4 * model_width])
        router_all.append(item[:, 4 * model_width : used - 4])
        norm_all.append(item[:, used - 4 : used].T.astype(jnp.float32))

    add_dense(dense_first)
    up_all = (up_first, up_second)
    down_all = (down_first, down_second)
    slot_tables = (table_first, table_second)
    z_index = lax.axis_index("dp")
    chosen_all = [
        (
            lax.dynamic_index_in_dim(item, z_index, 0, False)[2:4, :token_rows].T[..., None]
            == jnp.arange(expert_count, dtype=jnp.int32)
        ).astype(jnp.float32)
        for item in slot_tables
    ]
    moe = functools.partial(moe_call, depth=depth, groups=groups, cap_rows=cap_rows)

    def layer_forward(layer, inputs):
        chosen = chosen_all[layer]
        normed_one, unit_one, inverse_one = norm_forward(
            inputs, norm_all[layer][0], norm_all[layer][2]
        )
        norm_one = normed_one.astype(half)
        qkv_rows = jnp.dot(norm_one, qkv_all[layer], preferred_element_type=jnp.float32).astype(half)
        attended, log_totals = attend_forward(qkv_rows, local_images)
        middle = inputs + jnp.dot(attended, out_all[layer], preferred_element_type=jnp.float32)
        normed_two, unit_two, inverse_two = norm_forward(
            middle, norm_all[layer][1], norm_all[layer][3]
        )
        norm_two = normed_two.astype(half)
        logits = jnp.dot(norm_two, router_all[layer], preferred_element_type=jnp.float32)
        picked = jnp.sum(logits[:, None, :] * chosen, axis=-1)
        leading = jax.nn.sigmoid(picked[:, 0] - picked[:, 1])
        gate_pair = jnp.stack([leading, 1.0 - leading], axis=-1)
        gate_rows = jnp.pad(gate_pair.T, ((0, 0), (0, model_width - token_rows)))
        sent = jnp.concatenate(
            [
                norm_two,
                jnp.zeros((padded_rows - 8 - token_rows, model_width), half),
                gate_rows.astype(half),
                jnp.zeros((6, model_width), half),
            ]
        )
        combined, *expert_saved = moe(
            False, 2 * layer, rows=sent, slots=slot_tables[layer], up=up_all[layer],
            down=down_all[layer],
        )
        out_rows = middle + combined[:token_rows]
        saved = (
            inputs, norm_one, qkv_rows, log_totals, attended, middle, norm_two, gate_pair,
            expert_saved,
        )
        return (out_rows, saved)

    def layer_backward(layer, d_out, saved):
        (
            inputs, norm_one, qkv_rows, log_totals, attended, middle, norm_two, gate_pair,
            expert_saved,
        ) = saved
        chosen = chosen_all[layer]
        all_rows, hidden, slope, back_rows, gates = expert_saved
        sent = jnp.pad(d_out.astype(half), ((0, padded_rows - token_rows), (0, 0)))
        combined, up_grad, down_grad = moe(
            True, 2 * layer + 1, rows=sent, slots=slot_tables[layer], up=up_all[layer],
            down=down_all[layer], saved=(gates, hidden, slope, back_rows, all_rows),
        )
        d_gate_rows = combined[padded_rows - 8 :, :token_rows]
        d_gate = jnp.stack([d_gate_rows[0] + d_gate_rows[1], d_gate_rows[2] + d_gate_rows[3]], axis=1)
        d_lead = (d_gate[:, 0] - d_gate[:, 1]) * gate_pair[:, 0] * gate_pair[:, 1]
        d_logits = (d_lead[:, None] * (chosen[:, 0] - chosen[:, 1])).astype(half)
        d_norm_two = combined[:token_rows] + jnp.einsum(
            "te,de->td", d_logits, router_all[layer], preferred_element_type=jnp.float32
        )
        normed_two, unit_two, inverse_two = norm_forward(
            middle, norm_all[layer][1], norm_all[layer][3]
        )
        d_middle_norm, gain_two, shift_two = norm_backward(
            d_norm_two, unit_two, inverse_two, norm_all[layer][1]
        )
        d_middle = d_out + d_middle_norm
        d_middle_half = d_middle.astype(half)
        d_attended = jnp.einsum(
            "te,de->td", d_middle_half, out_all[layer], preferred_element_type=jnp.float32
        ).astype(half)
        d_qkv = attend_backward(qkv_rows, log_totals, d_attended, local_images)
        d_norm_one = jnp.einsum(
            "te,de->td", d_qkv, qkv_all[layer], preferred_element_type=jnp.float32
        )
        normed_one, unit_one, inverse_one = norm_forward(
            inputs, norm_all[layer][0], norm_all[layer][2]
        )
        d_input_norm, gain_one, shift_one = norm_backward(
            d_norm_one, unit_one, inverse_one, norm_all[layer][0]
        )
        d_input = d_middle + d_input_norm
        small = jnp.concatenate(
            [
                jnp.einsum("td,te->de", norm_two, d_logits, preferred_element_type=jnp.float32),
                jnp.stack([gain_one, gain_two, shift_one, shift_two], axis=1),
            ],
            axis=1,
        )
        return (d_input, (norm_one, d_qkv, attended, d_middle_half, small), (up_grad, down_grad))

    qkv_part, out_part = 3 * model_width // 2, model_width // 2
    small_width = round_up(expert_count + 4, 128)

    def dense_gradients(norm_one, d_qkv, attended, d_middle_half, small):
        own = jnp.concatenate([norm_one, d_qkv, attended, d_middle_half], axis=1)
        pair = jnp.concatenate([own, lax.ppermute(own, "section", swapped)], axis=0)
        d_qkv_part = lax.dynamic_slice_in_dim(
            pair, model_width + section_index * qkv_part, qkv_part, axis=1
        )
        d_out_part = lax.dynamic_slice_in_dim(
            pair, 5 * model_width + section_index * out_part, out_part, axis=1
        )
        qkv_grad = jnp.einsum(
            "td,te->de", pair[:, :model_width], d_qkv_part, preferred_element_type=jnp.float32
        )
        out_grad = jnp.einsum(
            "td,te->de", pair[:, 4 * model_width : 5 * model_width], d_out_part,
            preferred_element_type=jnp.float32,
        )
        small = jnp.pad(small, ((0, 0), (0, small_width - expert_count - 4)))
        packed_grad = jnp.concatenate(
            [qkv_grad.astype(half), out_grad.astype(half), small.astype(half)], axis=1
        )
        blocks = packed_grad.reshape(depth, groups, -1, packed_grad.shape[1]).transpose(1, 0, 2, 3)
        blocks = lax.all_to_all(blocks, "expert", split_axis=0, concat_axis=0, tiled=True)
        blocks = jnp.sum(blocks.astype(jnp.float32), axis=0).astype(half)
        blocks = lax.all_to_all(blocks, "dp", split_axis=0, concat_axis=0, tiled=True)
        return jnp.sum(blocks.astype(jnp.float32), axis=0)

    saved_list = []
    for layer in range(2):
        if layer > 0:
            stream, later_half = lax.optimization_barrier((stream.astype(half), later_half))
            stream = stream.astype(jnp.float32)
            add_dense(lax.all_gather(later_half, "section", axis=1, tiled=True))
        stream, saved = layer_forward(layer, stream)
        saved_list.append(saved)
    dense_operands = [None, None]
    expert_grads = [None, None]
    for layer in (1, 0):
        if layer < 1:
            cotangent = cotangent.astype(half).astype(jnp.float32)
        cotangent, operands, expert_grads[layer] = layer_backward(
            layer, cotangent, saved_list[layer]
        )
        dense_operands[layer] = operands

    def mine(first, second):
        return jnp.where(is_first, first, second)

    def both(first, second):
        own, away = mine(first, second), mine(second, first)
        return own, lax.ppermute(away, "section", swapped)

    if model_width % (16 * depth * groups) == 0:
        operands = [
            item[:4] + (jnp.pad(item[4], ((0, 0), (0, small_width - expert_count - 4))),)
            for item in dense_operands
        ]
        shard, other_up, other_down, other_rows = finish_call(
            9, depth, groups, operands[0], operands[1], *expert_grads[0], *expert_grads[1],
            cotangent, stream,
        )
        own_up = mine(expert_grads[0][0], expert_grads[1][0])
        own_down = mine(expert_grads[0][1], expert_grads[1][1])
        own_rows = mine(cotangent, stream)
        qkv_shard = shard[:, : 3 * model_width]
        out_shard = shard[:, 3 * model_width : 4 * model_width]
        small_shard = shard[:, 4 * model_width :]
    else:
        shards = [dense_gradients(*item) for item in dense_operands]
        own_shard, other_shard = both(shards[0], shards[1])
        low, high = mine(own_shard, other_shard), mine(other_shard, own_shard)
        qkv_shard = jnp.concatenate([low[:, :qkv_part], high[:, :qkv_part]], axis=1)
        out_shard = jnp.concatenate(
            [low[:, qkv_part : qkv_part + out_part], high[:, qkv_part : qkv_part + out_part]], axis=1
        )
        small_shard = (low + high)[:, qkv_part + out_part :]
        own_up, other_up = both(expert_grads[0][0], expert_grads[1][0])
        own_down, other_down = both(expert_grads[0][1], expert_grads[1][1])
        own_rows, other_rows = both(cotangent, stream)
    norm_shard = small_shard[:, expert_count : expert_count + 4].T

    def expert_grad(own, other):
        return (own.astype(jnp.float32) + other.astype(jnp.float32))[None]

    boundary_rows = jnp.stack([mine(own_rows, other_rows), mine(other_rows, own_rows)])
    boundary_out = boundary_rows.reshape(1, MB, local_images, boundary_in.shape[3], model_width)
    return (
        boundary_out,
        norm_shard[None, 0:2],
        norm_shard[None, 2:4],
        qkv_shard[None],
        out_shard[None],
        small_shard[None, :, :expert_count],
        expert_grad(own_up, other_up),
        expert_grad(own_down, other_down),
    )


def solution(mesh):
    in_specs = (
        P("section", None, ("dp", "expert"), None, None),
        P("section", None, ("dp", "expert"), None, None),
        P("section", None, ("dp", "expert"), None, None),
        P("section", None, ("dp", "expert")),
        P("section", None, ("dp", "expert")),
        P("section", ("dp", "expert"), None),
        P("section", ("dp", "expert"), None),
        P("section", ("dp", "expert"), None),
        P("section", "expert", None, "dp"),
        P("section", "expert", "dp", None),
    )
    out_specs = (
        P("section", None, ("dp", "expert"), None, None),
        P("section", None, ("dp", "expert")),
        P("section", None, ("dp", "expert")),
        P("section", ("dp", "expert"), None),
        P("section", ("dp", "expert"), None),
        P("section", ("dp", "expert"), None),
        P("section", "expert", None, "dp"),
        P("section", "expert", "dp", None),
    )
    return jax.shard_map(
        on_device, mesh=mesh, in_specs=in_specs, out_specs=out_specs, check_vma=False
    )
```

```python
import functools
import math

import jax
import jax.numpy as jnp
from jax import lax
from jax.experimental import pallas as pl
from jax.experimental.pallas import tpu as pltpu
from jax.sharding import PartitionSpec as P

HEADS = 12
HEAD_DIM = 64
EXP_DEV = 2
MB = 2


EPS = 1e-06
SQRT_HALF = 0.7071067811865476
INV_ROOT_TAU = 0.3989422804014327
MESH = pl.DeviceIdType.MESH


def round_up(value, unit):
    return (value + unit - 1) // unit * unit


def z_order(step, z, depth):
    if depth == 1:
        return z
    direction = 1 - 2 * (z // (depth // 2))
    return lax.rem(z + step * direction + depth, depth)


def f32_dot(a, b, dims):
    return lax.dot_general(a, b, (dims, ((), ())), preferred_element_type=jnp.float32)


def moe_kernel(backward, shape, *refs):
    depth, groups, cap_rows, token_rows, model_width, hidden_width = shape
    if backward:
        (
            rows_ref, slots_ref, up_ref, down_ref, gates_ref, hidden_ref, slope_ref, back_ref,
            kept_ref, out_ref, up_grad_ref, down_grad_ref, inbox, d_pre_ref, taken_ref,
            raw, sent_rows, sent_back, sent_home, home, back, d_gates, *sems,
        ) = refs
    else:
        (
            rows_ref, slots_ref, up_ref, down_ref,
            out_ref, taken_ref, hidden_ref, slope_ref, back, gates_ref,
            inbox, raw, sent_rows, sent_back, sent_home, home, *sems,
        ) = refs
    far_send, far_recv, go_send, go_recv, back_send, back_recv, home_send, home_recv = sems
    half = jnp.bfloat16
    section, z, column = (
        lax.axis_index("section"), lax.axis_index("dp"), lax.axis_index("expert")
    )
    slot_count = 2 * groups * cap_rows
    tail = token_rows - 16

    def z_peer(distance):
        return (section, lax.rem(z + distance, depth), column)

    def xy_peer(distance):
        return lax.rem(column + distance, groups)

    barrier = pltpu.get_barrier_semaphore()

    def greet_z(distance, carry):
        pl.semaphore_signal(barrier, inc=1, device_id=z_peer(distance), device_id_type=MESH)
        return carry

    def greet_xy(distance, carry):
        pl.semaphore_signal(
            barrier, inc=1, device_id=(section, z, xy_peer(distance)), device_id_type=MESH
        )
        return carry

    lax.fori_loop(1, depth, greet_z, 0)
    lax.fori_loop(1, groups, greet_xy, 0)
    pl.semaphore_wait(barrier, depth - 1 + groups - 1)

    def far_copy(direction, image):
        target = lax.rem(z + 2 * direction - 1 + depth, depth)
        source = raw.at[image]
        return pltpu.make_async_remote_copy(
            src_ref=source, dst_ref=raw.at[image],
            send_sem=far_send.at[direction, image], recv_sem=far_recv.at[image],
            device_id=(section, target, column), device_id_type=MESH,
        )

    def go_copy(image, source, target):
        return pltpu.make_async_remote_copy(
            src_ref=sent_rows.at[image, target], dst_ref=inbox.at[image, source],
            send_sem=go_send.at[image, target], recv_sem=go_recv.at[image, source],
            device_id=(section, z, target), device_id_type=MESH,
        )

    def back_copy(image, source, target):
        return pltpu.make_async_remote_copy(
            src_ref=sent_back.at[image, target], dst_ref=back.at[image, source],
            send_sem=back_send.at[image, target], recv_sem=back_recv.at[image, source],
            device_id=(section, z, target), device_id_type=MESH,
        )

    def home_copy(source, target):
        return pltpu.make_async_remote_copy(
            src_ref=sent_home.at[target], dst_ref=home.at[source],
            send_sem=home_send.at[target], recv_sem=home_recv.at[source],
            device_id=(section, target, column), device_id_type=MESH,
        )

    raw[z] = rows_ref[...]

    @pl.when(z < depth - 1)
    def _():
        far_copy(1, z).start()

    @pl.when(z > 0)
    def _():
        far_copy(0, z).start()

    def match(image):
        slots = slots_ref[image][:, :token_rows]
        index = lax.broadcasted_iota(jnp.int32, (slot_count, token_rows), 0)
        return index == slots[0:1], index == slots[1:2]

    def gate_table(image):
        first, second = match(image)
        gates = gates_ref[image]
        table = jnp.where(first, gates[0:1], 0.0) + jnp.where(second, gates[1:2], 0.0)
        return table.astype(half)

    def ones_table(image):
        first, second = match(image)
        return jnp.where(first | second, 1.0, 0.0).astype(half)

    def pass_on(step):
        low, high = z - step, z + step

        @pl.when(low >= 0)
        def _():
            far_copy(1, low).wait_recv()

            @pl.when(z < depth - 1)
            def _():
                far_copy(1, low).start()

        @pl.when(high < depth)
        def _():
            far_copy(0, high).wait_recv()

            @pl.when(z > 0)
            def _():
                far_copy(0, high).start()

    def dispatch(image):
        if not backward:
            gates_ref[image] = raw[image, tail:, :token_rows].astype(jnp.float32)[8:16]
        table = gate_table(image) if backward else ones_table(image)
        rows = raw[image]
        blocks = f32_dot(table, rows, ((1,), (0,))).astype(half)
        sent_rows[image] = blocks.reshape(groups, 2 * cap_rows, model_width)

        def send(distance, carry):
            go_copy(image, column, xy_peer(distance)).start()
            return carry

        lax.fori_loop(1, groups, send, 0)
        inbox[image, column] = sent_rows[image, column]
        if backward:
            first, second = match(image)
            returned = back_ref[image].reshape(slot_count, model_width)
            ones = jnp.ones((8, model_width), half)
            row_index = lax.broadcasted_iota(jnp.int32, (8, token_rows), 0)
            packed = jnp.zeros((8, token_rows), jnp.float32)
            for choice, found in enumerate((first, second)):
                table = jnp.where(found, 1.0, 0.0).astype(half)
                selected = f32_dot(table, returned, ((0,), (0,)))
                product = (selected * rows.astype(jnp.float32)).astype(half)
                sums = f32_dot(ones, product, ((1,), (1,)))
                high = sums.astype(half).astype(jnp.float32)
                packed = jnp.where(row_index == 2 * choice, high, packed)
                packed = jnp.where(row_index == 2 * choice + 1, sums - high, packed)
            d_gates[image] = packed

    def experts(image):
        def arrive(distance, carry):
            go_copy(image, xy_peer(distance), column).wait_recv()
            return carry

        lax.fori_loop(1, groups, arrive, 0)
        block = inbox[image].astype(jnp.float32)
        results = []
        for expert in range(2):
            rows = block[:, expert * cap_rows : (expert + 1) * cap_rows]
            rows = rows.reshape(groups * cap_rows, model_width).astype(half)
            taken_ref[expert, image] = rows
            if backward:
                d_hidden = f32_dot(rows, down_ref[expert], ((1,), (1,)))
                d_pre = (d_hidden * slope_ref[expert, image].astype(jnp.float32)).astype(half)
                d_pre_ref[expert, image] = d_pre
                result = f32_dot(d_pre, up_ref[expert], ((1,), (1,)))
            else:
                pre = f32_dot(rows, up_ref[expert], ((1,), (0,)))
                share = 0.5 * (1.0 + lax.erf(pre * SQRT_HALF))
                slope = share + pre * jnp.exp(-0.5 * pre * pre) * INV_ROOT_TAU
                hidden = (pre * share).astype(half)
                hidden_ref[expert, image] = hidden
                slope_ref[expert, image] = slope.astype(half)
                result = f32_dot(hidden, down_ref[expert], ((1,), (0,)))
            results.append(result.reshape(groups, cap_rows, model_width))
        sent_back[image] = jnp.concatenate(results, axis=1).astype(half)

        def send(distance, carry):
            back_copy(image, column, xy_peer(distance)).start()
            return carry

        lax.fori_loop(1, groups, send, 0)
        back[image, column] = sent_back[image, column]

    def combine(image):
        def arrive(distance, carry):
            back_copy(image, xy_peer(distance), column).wait_recv()
            return carry

        lax.fori_loop(1, groups, arrive, 0)
        table = ones_table(image) if backward else gate_table(image)
        total = f32_dot(table, back[image].reshape(slot_count, model_width), ((0,), (0,)))
        if backward:
            extra = jnp.concatenate(
                [jnp.zeros((8, token_rows), jnp.float32), d_gates[image]], axis=0
            )

        @pl.when(image == z)
        def _():
            out_ref[...] = total
            if backward:
                out_ref[tail:, :token_rows] = total[tail:, :token_rows] + extra

        @pl.when(image != z)
        def _():
            sent_home[image] = total.astype(half)
            if backward:
                sent_home[image, tail:, :token_rows] = (
                    total[tail:, :token_rows] + extra
                ).astype(half)
            home_copy(z, image).start()

    def stage(step, carry):
        @pl.when(jnp.logical_and(step >= 1, step < depth))
        def _():
            pass_on(step)

        @pl.when(step < depth)
        def _():
            dispatch(z_order(step, z, depth))

        @pl.when(jnp.logical_and(step >= 1, step < depth + 1))
        def _():
            experts(z_order(step - 1, z, depth))

        @pl.when(step >= 2)
        def _():
            combine(z_order(step - 2, z, depth))

        return carry

    lax.fori_loop(0, depth + 2, stage, 0)

    if backward:

        def expert_gradients(expert, carry):
            kept = kept_ref[expert].reshape(depth * groups * cap_rows, model_width)
            d_pre = d_pre_ref[expert].reshape(depth * groups * cap_rows, hidden_width)
            up_grad_ref[expert] = f32_dot(kept, d_pre, ((0,), (0,))).astype(half)
            hidden = hidden_ref[expert].reshape(depth * groups * cap_rows, hidden_width)
            grads = taken_ref[expert].reshape(depth * groups * cap_rows, model_width)
            down_grad_ref[expert] = f32_dot(hidden, grads, ((0,), (0,))).astype(half)
            return carry

        lax.fori_loop(0, 2, expert_gradients, 0)

    def finish_home(distance, carry):
        source = lax.rem(z + distance, depth)
        home_copy(source, z).wait_recv()
        out_ref[...] += home[source].astype(jnp.float32)
        return carry

    lax.fori_loop(1, depth, finish_home, 0)

    def drain_home(distance, carry):
        home_copy(z, lax.rem(z + distance, depth)).wait_send()
        return carry

    lax.fori_loop(1, depth, drain_home, 0)

    def drain_image(image, carry):
        @pl.when(jnp.logical_and(z < depth - 1, image <= z))
        def _():
            far_copy(1, image).wait_send()

        @pl.when(jnp.logical_and(z > 0, image >= z))
        def _():
            far_copy(0, image).wait_send()

        def drain(distance, inner):
            go_copy(image, column, xy_peer(distance)).wait_send()
            back_copy(image, column, xy_peer(distance)).wait_send()
            return inner

        lax.fori_loop(1, groups, drain, 0)
        return carry

    lax.fori_loop(0, depth, drain_image, 0)


def moe_call(backward, call_id, depth, groups, cap_rows, rows, slots, up, down, saved=()):
    token_rows, model_width = rows.shape
    hidden_width = up.shape[2]
    half = jnp.bfloat16
    shape = (depth, groups, cap_rows, token_rows, model_width, hidden_width)
    taken = jax.ShapeDtypeStruct((2, depth, groups * cap_rows, model_width), half)
    hidden = jax.ShapeDtypeStruct((2, depth, groups * cap_rows, hidden_width), half)
    back = (depth, groups, 2 * cap_rows, model_width)
    out = jax.ShapeDtypeStruct((token_rows, model_width), jnp.float32)
    if backward:
        out_shape = (
            out, jax.ShapeDtypeStruct(up.shape, half), jax.ShapeDtypeStruct(down.shape, half)
        )
    else:
        gates = jax.ShapeDtypeStruct((depth, 8, token_rows), jnp.float32)
        out_shape = (out, taken, hidden, hidden, jax.ShapeDtypeStruct(back, half), gates)
    scratch = [
        pltpu.VMEM((depth, token_rows, model_width), half),
        pltpu.VMEM(back, half),
        pltpu.VMEM(back, half),
        pltpu.VMEM((depth, token_rows, model_width), half),
        pltpu.VMEM((depth, token_rows, model_width), half),
    ]
    if backward:
        scratch = [pltpu.VMEM(hidden.shape, half), pltpu.VMEM(taken.shape, half)] + scratch
        scratch += [
            pltpu.VMEM(back, half),
            pltpu.VMEM((depth, 8, token_rows), jnp.float32),
        ]
    scratch = [pltpu.VMEM(back, half)] + scratch
    scratch += [
        pltpu.SemaphoreType.DMA((2, depth)),
        pltpu.SemaphoreType.DMA((depth,)),
        pltpu.SemaphoreType.DMA((depth, groups)),
        pltpu.SemaphoreType.DMA((depth, groups)),
        pltpu.SemaphoreType.DMA((depth, groups)),
        pltpu.SemaphoreType.DMA((depth, groups)),
        pltpu.SemaphoreType.DMA((depth,)),
        pltpu.SemaphoreType.DMA((depth,)),
    ]
    return pl.pallas_call(
        functools.partial(moe_kernel, backward, shape),
        out_shape=out_shape,
        in_specs=[pl.BlockSpec(memory_space=pltpu.VMEM)] * (4 + len(saved)),
        out_specs=[pl.BlockSpec(memory_space=pltpu.VMEM)] * len(out_shape),
        scratch_shapes=scratch,
        compiler_params=pltpu.CompilerParams(
            collective_id=call_id, has_side_effects=True, vmem_limit_bytes=50 * 2**20
        ),
        name="moe_backward" if backward else "moe_forward",
    )(rows, slots, up, down, *saved)

def start_kernel(shape, *refs):
    depth, groups, half_width = shape
    (
        packed_ref, up_ref, down_ref, edge_ref, table_ref,
        dense_ref, later_ref, up_first, up_second, down_first, down_second,
        rows_ref, cotangent_ref, table_first, table_second,
        shard_send, shard_recv, core_send, core_recv, table_send, table_recv, own_sem,
    ) = refs
    section, z, column = (
        lax.axis_index("section"), lax.axis_index("dp"), lax.axis_index("expert")
    )
    other = (1 - section, z, column)
    is_first = section == 0

    def z_peer(distance):
        return lax.rem(z + distance, depth)

    def xy_peer(distance):
        return lax.rem(column + distance, groups)

    barrier = pltpu.get_barrier_semaphore()

    def greet_z(distance, carry):
        pl.semaphore_signal(
            barrier, inc=1, device_id=(section, z_peer(distance), column), device_id_type=MESH
        )
        return carry

    def greet_xy(distance, carry):
        pl.semaphore_signal(
            barrier, inc=1, device_id=(section, z, xy_peer(distance)), device_id_type=MESH
        )
        return carry

    pl.semaphore_signal(barrier, inc=1, device_id=other, device_id_type=MESH)
    lax.fori_loop(1, depth, greet_z, 0)
    lax.fori_loop(1, groups, greet_xy, 0)
    pl.semaphore_wait(barrier, depth + groups - 1)

    def remote(source, target, send, recv, device):
        return pltpu.make_async_remote_copy(
            src_ref=source, dst_ref=target, send_sem=send, recv_sem=recv,
            device_id=device, device_id_type=MESH,
        )

    def shard_copy(kind, source_ref, plane, lane, device):
        return remote(
            source_ref, dense_ref.at[plane, lane], shard_send.at[kind, plane, lane],
            shard_recv.at[plane, lane], device,
        )

    def z_copy(direction, plane):
        device = (section, lax.rem(z + 2 * direction - 1 + depth, depth), column)
        return shard_copy(direction, dense_ref.at[plane, column], plane, column, device)

    def core_copy(plane, lane):
        return shard_copy(2, dense_ref.at[plane, lane], plane, lane, other)

    def xy_copy(plane, source, target):
        return remote(
            dense_ref.at[plane, source], dense_ref.at[plane, source],
            shard_send.at[3 + target, plane, source], shard_recv.at[plane, source],
            (section, z, target),
        )

    def swap(index, source, target):
        return remote(source, target, core_send.at[index], core_recv.at[index], other)

    def local(index, source, target):
        return pltpu.make_async_copy(source, target, own_sem.at[index])

    def spread(plane):
        core_copy(plane, column).start()

        def send(distance, carry):
            xy_copy(plane, column, xy_peer(distance)).start()
            return carry

        lax.fori_loop(1, groups, send, 0)

    own_shard = local(0, packed_ref, dense_ref.at[z, column])
    left, right = pl.ds(0, half_width), pl.ds(half_width, half_width)

    def first_copies():
        remote_ones = [
            swap(0, edge_ref.at[1], rows_ref),
            swap(1, table_ref.at[1], table_first.at[z]),
            swap(2, up_ref, up_first),
            swap(3, down_ref, down_first),
        ]
        local_ones = [
            local(1, edge_ref.at[0], rows_ref),
            local(2, table_ref.at[0], table_first.at[z]),
            local(3, up_ref, up_first),
            local(4, down_ref, down_first),
        ]
        return remote_ones, local_ones

    def second_copies():
        remote_ones = [
            swap(0, edge_ref.at[0], cotangent_ref),
            swap(1, table_ref.at[0], table_second.at[z]),
            swap(2, up_ref, up_second),
            swap(3, down_ref, down_second),
            swap(4, packed_ref.at[:, left], later_ref),
        ]
        local_ones = [
            local(1, edge_ref.at[1], cotangent_ref),
            local(2, table_ref.at[1], table_second.at[z]),
            local(3, up_ref, up_second),
            local(4, down_ref, down_second),
            local(5, packed_ref.at[:, right], later_ref),
        ]
        return remote_ones, local_ones

    @pl.when(is_first)
    def _():
        own_shard.start()
        remote_ones, local_ones = first_copies()
        own_shard.wait()

        @pl.when(z < depth - 1)
        def _():
            z_copy(1, z).start()

        @pl.when(z > 0)
        def _():
            z_copy(0, z).start()

        spread(z)
        for copy in remote_ones[:2] + local_ones + remote_ones[2:]:
            copy.start()

        def step(distance, carry):
            low, high = z - distance, z + distance

            @pl.when(low >= 0)
            def _():
                z_copy(1, low).wait_recv()

                @pl.when(z < depth - 1)
                def _():
                    z_copy(1, low).start()

                spread(low)

            @pl.when(high < depth)
            def _():
                z_copy(0, high).wait_recv()

                @pl.when(z > 0)
                def _():
                    z_copy(0, high).start()

                spread(high)

            return carry

        lax.fori_loop(1, depth, step, 0)

    @pl.when(jnp.logical_not(is_first))
    def _():
        remote_ones, local_ones = second_copies()
        for copy in remote_ones[:2] + remote_ones[4:] + local_ones + remote_ones[2:4]:
            copy.start()

    first_remote, first_local = first_copies()
    second_remote, second_local = second_copies()

    def table_copies(source, target):
        pairs = []
        for layer, table in enumerate((table_first, table_second)):
            pairs.append(
                remote(
                    table.at[source], table.at[source], table_send.at[layer, target],
                    table_recv.at[layer, source], (section, target, column),
                )
            )
        return pairs

    @pl.when(is_first)
    def _():
        first_local[1].wait()
        second_remote[1].wait_recv()

    @pl.when(jnp.logical_not(is_first))
    def _():
        second_local[1].wait()
        first_remote[1].wait_recv()

    def send_tables(distance, carry):
        for copy in table_copies(z, z_peer(distance)):
            copy.start()
        return carry

    lax.fori_loop(1, depth, send_tables, 0)

    @pl.when(is_first)
    def _():
        def forward(step, carry):
            plane = z_order(step, z, depth)

            def arrive(distance, inner):
                lane = xy_peer(distance)
                xy_copy(plane, lane, column).wait_recv()
                core_copy(plane, lane).start()
                return inner

            return lax.fori_loop(1, groups, arrive, carry)

        lax.fori_loop(0, depth, forward, 0)
        for copy in second_remote:
            copy.wait_recv() if copy is not second_remote[1] else None
        for copy in first_remote:
            copy.wait_send()
        for copy in first_local[:1] + first_local[2:]:
            copy.wait()

        def drain(plane, carry):
            @pl.when(jnp.logical_and(z < depth - 1, plane <= z))
            def _():
                z_copy(1, plane).wait_send()

            @pl.when(jnp.logical_and(z > 0, plane >= z))
            def _():
                z_copy(0, plane).wait_send()

            def drain_core(lane, inner):
                core_copy(plane, lane).wait_send()
                return inner

            def drain_xy(distance, inner):
                xy_copy(plane, column, xy_peer(distance)).wait_send()
                return inner

            lax.fori_loop(0, groups, drain_core, 0)
            return lax.fori_loop(1, groups, drain_xy, carry)

        lax.fori_loop(0, depth, drain, 0)

    @pl.when(jnp.logical_not(is_first))
    def _():
        def arrive(plane, carry):
            def inner_arrive(lane, inner):
                core_copy(plane, lane).wait_recv()
                return inner

            return lax.fori_loop(0, groups, inner_arrive, carry)

        lax.fori_loop(0, depth, arrive, 0)
        for index in (0, 2, 3):
            first_remote[index].wait_recv()
        for copy in second_remote:
            copy.wait_send()
        for copy in second_local[:1] + second_local[2:]:
            copy.wait()

    def finish_tables(distance, carry):
        for copy in table_copies(z_peer(distance), z):
            copy.wait_recv()
        for copy in table_copies(z, z_peer(distance)):
            copy.wait_send()
        return carry

    lax.fori_loop(1, depth, finish_tables, 0)


def start_call(call_id, depth, groups, packed, up, down, edge, table):
    rows, width = packed.shape
    half = jnp.bfloat16
    out_shape = (
        jax.ShapeDtypeStruct((depth, groups, rows, width), half),
        jax.ShapeDtypeStruct((rows, width // 2), half),
        jax.ShapeDtypeStruct(up.shape, half),
        jax.ShapeDtypeStruct(up.shape, half),
        jax.ShapeDtypeStruct(down.shape, half),
        jax.ShapeDtypeStruct(down.shape, half),
        jax.ShapeDtypeStruct(edge.shape[1:], jnp.float32),
        jax.ShapeDtypeStruct(edge.shape[1:], jnp.float32),
        jax.ShapeDtypeStruct((depth,) + table.shape[1:], jnp.int32),
        jax.ShapeDtypeStruct((depth,) + table.shape[1:], jnp.int32),
    )
    return pl.pallas_call(
        functools.partial(start_kernel, (depth, groups, width // 2)),
        out_shape=out_shape,
        in_specs=[pl.BlockSpec(memory_space=pltpu.VMEM)] * 5,
        out_specs=[pl.BlockSpec(memory_space=pl.ANY)] * len(out_shape),
        scratch_shapes=[
            pltpu.SemaphoreType.DMA((3 + groups, depth, groups)),
            pltpu.SemaphoreType.DMA((depth, groups)),
            pltpu.SemaphoreType.DMA((5,)),
            pltpu.SemaphoreType.DMA((5,)),
            pltpu.SemaphoreType.DMA((2, depth)),
            pltpu.SemaphoreType.DMA((2, depth)),
            pltpu.SemaphoreType.DMA((6,)),
        ],
        compiler_params=pltpu.CompilerParams(
            collective_id=call_id, has_side_effects=True, vmem_limit_bytes=40 * 2**20
        ),
        name="start_exchange",
    )(packed, up, down, edge, table)

def finish_kernel(shape, *refs):
    depth, groups, token_rows, padded_rows, model_width = shape
    first_refs, second_refs, rest = refs[0:5], refs[5:10], refs[10:]
    (
        up_first, down_first, up_second, down_second, rows_first, rows_second,
        shard_ref, up_ref, down_ref, rows_ref,
        pair, away, small_pair, table, inbox, sent_home, home,
        core_send, core_recv, go_send, go_recv, home_send, home_recv,
    ) = rest
    half = jnp.bfloat16
    section, z, column = (
        lax.axis_index("section"), lax.axis_index("dp"), lax.axis_index("expert")
    )
    other = (1 - section, z, column)
    is_first = section == 0
    shard_rows = table.shape[1]

    def z_peer(distance):
        return lax.rem(z + distance, depth)

    def xy_peer(distance):
        return lax.rem(column + distance, groups)

    barrier = pltpu.get_barrier_semaphore()

    def greet_z(distance, carry):
        pl.semaphore_signal(
            barrier, inc=1, device_id=(section, z_peer(distance), column), device_id_type=MESH
        )
        return carry

    def greet_xy(distance, carry):
        pl.semaphore_signal(
            barrier, inc=1, device_id=(section, z, xy_peer(distance)), device_id_type=MESH
        )
        return carry

    pl.semaphore_signal(barrier, inc=1, device_id=other, device_id_type=MESH)
    lax.fori_loop(1, depth, greet_z, 0)
    lax.fori_loop(1, groups, greet_xy, 0)
    pl.semaphore_wait(barrier, depth + groups - 1)

    def swap(index, source, target):
        return pltpu.make_async_remote_copy(
            src_ref=source, dst_ref=target, send_sem=core_send.at[index],
            recv_sem=core_recv.at[index], device_id=other, device_id_type=MESH,
        )

    def pack(target, operands):
        target[padded_rows - 16 :, :] = jnp.zeros((16, target.shape[1]), half)
        offset = 0
        for operand in operands:
            width = operand.shape[1]
            target[:token_rows, offset : offset + width] = operand[...]
            offset += width

    def side_copies(first):
        if first:
            sources = (second_refs[4], up_second, down_second, rows_second)
        else:
            sources = (first_refs[4], up_first, down_first, rows_first)
        targets = (small_pair.at[1], up_ref, down_ref, rows_ref)
        return [
            swap(1 + index, source, target)
            for index, (source, target) in enumerate(zip(sources, targets))
        ]

    operand_copy = swap(0, away, pair.at[1])
    for first in (True, False):

        @pl.when(is_first if first else jnp.logical_not(is_first))
        def _():
            mine, others = (first_refs, second_refs) if first else (second_refs, first_refs)
            pack(away, others[:4])
            operand_copy.start()
            for copy in side_copies(first):
                copy.start()
            pack(pair.at[0], mine[:4])
            small_pair[0] = mine[4][...]

    operand_copy.wait_recv()
    rows = 2 * padded_rows

    def product(left, right, target):
        a = pair[:, :, left : left + model_width].reshape(rows, model_width)
        b = pair[:, :, right : right + model_width].reshape(rows, model_width)
        value = f32_dot(a, b, ((0,), (0,))).astype(half)
        table[:, :, target : target + model_width] = value.reshape(
            depth * groups, shard_rows, model_width
        )

    for index in range(3):
        product(0, (1 + index) * model_width, index * model_width)
    product(4 * model_width, 5 * model_width, 3 * model_width)
    for copy in side_copies(True)[:1]:
        copy.wait_recv()
    small = (small_pair[0] + small_pair[1]).astype(half)
    table[:, :, 4 * model_width :] = small.reshape(depth * groups, shard_rows, small.shape[1])

    def go_copy(plane, source, target):
        return pltpu.make_async_remote_copy(
            src_ref=table.at[plane * groups + target], dst_ref=inbox.at[plane, source],
            send_sem=go_send.at[plane, target], recv_sem=go_recv.at[plane, source],
            device_id=(section, z, target), device_id_type=MESH,
        )

    def home_copy(source, target):
        return pltpu.make_async_remote_copy(
            src_ref=sent_home.at[target], dst_ref=home.at[source],
            send_sem=home_send.at[target], recv_sem=home_recv.at[source],
            device_id=(section, target, column), device_id_type=MESH,
        )

    def send_plane(step, carry):
        plane = z_peer(step)

        def send(distance, inner):
            go_copy(plane, column, xy_peer(distance)).start()
            return inner

        return lax.fori_loop(1, groups, send, carry)

    lax.fori_loop(1, depth + 1, send_plane, 0)

    def sum_plane(step, carry):
        plane = z_peer(step)

        def arrive(distance, total):
            lane = xy_peer(distance)
            go_copy(plane, lane, column).wait_recv()
            return total + inbox[plane, lane].astype(jnp.float32)

        own = table[plane * groups + column].astype(jnp.float32)
        total = lax.fori_loop(1, groups, arrive, own)

        @pl.when(plane == z)
        def _():
            shard_ref[...] = total

        @pl.when(plane != z)
        def _():
            sent_home[plane] = total.astype(half)
            home_copy(z, plane).start()

        return carry

    lax.fori_loop(1, depth + 1, sum_plane, 0)

    def finish_home(distance, carry):
        source = z_peer(distance)
        home_copy(source, z).wait_recv()
        shard_ref[...] += home[source].astype(jnp.float32)
        home_copy(z, source).wait_send()
        return carry

    lax.fori_loop(1, depth, finish_home, 0)

    def drain_plane(plane, carry):
        def drain(distance, inner):
            go_copy(plane, column, xy_peer(distance)).wait_send()
            return inner

        return lax.fori_loop(1, groups, drain, carry)

    lax.fori_loop(0, depth, drain_plane, 0)
    operand_copy.wait_send()
    for index, copy in enumerate(side_copies(True)):
        copy.wait_send()
        if index > 0:
            copy.wait_recv()


def finish_call(call_id, depth, groups, first, second, up_first, down_first, up_second, down_second,
                rows_first, rows_second):
    token_rows, model_width = first[0].shape
    padded_rows = round_up(token_rows, 16)
    small_width = first[4].shape[1]
    width = 4 * model_width + small_width
    shard_rows = model_width // (depth * groups)
    half = jnp.bfloat16
    out_shape = (
        jax.ShapeDtypeStruct((shard_rows, width), jnp.float32),
        jax.ShapeDtypeStruct(up_first.shape, half),
        jax.ShapeDtypeStruct(down_first.shape, half),
        jax.ShapeDtypeStruct(rows_first.shape, jnp.float32),
    )
    home = pltpu.VMEM((depth, shard_rows, width), half)
    return pl.pallas_call(
        functools.partial(
            finish_kernel, (depth, groups, token_rows, padded_rows, model_width)
        ),
        out_shape=out_shape,
        in_specs=[pl.BlockSpec(memory_space=pltpu.VMEM)] * 16,
        out_specs=[pl.BlockSpec(memory_space=pltpu.VMEM)] + [pl.BlockSpec(memory_space=pl.ANY)] * 3,
        scratch_shapes=[
            pltpu.VMEM((2, padded_rows, 6 * model_width), half),
            pltpu.VMEM((padded_rows, 6 * model_width), half),
            pltpu.VMEM((2, model_width, small_width), jnp.float32),
            pltpu.VMEM((depth * groups, shard_rows, width), half),
            pltpu.VMEM((depth, groups, shard_rows, width), half),
            home,
            home,
            pltpu.SemaphoreType.DMA((5,)),
            pltpu.SemaphoreType.DMA((5,)),
            pltpu.SemaphoreType.DMA((depth, groups)),
            pltpu.SemaphoreType.DMA((depth, groups)),
            pltpu.SemaphoreType.DMA((depth,)),
            pltpu.SemaphoreType.DMA((depth,)),
        ],
        compiler_params=pltpu.CompilerParams(
            collective_id=call_id, has_side_effects=True, vmem_limit_bytes=50 * 2**20
        ),
        name="finish_exchange",
    )(*first, *second, up_first, down_first, up_second, down_second, rows_first, rows_second)

def head_mask(head):
    lanes = lax.broadcasted_iota(jnp.int32, (1, 2 * HEAD_DIM), 1)
    return jnp.where(lanes // HEAD_DIM == head, 1.0, 0.0).astype(jnp.bfloat16)


def attend_kernel(width, qkv_ref, out_ref):
    scale_factor = 1.0 / math.sqrt(HEAD_DIM)
    pair_width = 2 * HEAD_DIM

    def pair(index, carry):
        def columns(part):
            start = pl.multiple_of(part * width + index * pair_width, pair_width)
            return qkv_ref[:, pl.ds(start, pair_width)]

        queries, keys, values = columns(0), columns(1), columns(2)
        total = jnp.zeros(queries.shape, jnp.float32)
        for head in range(2):
            mask = head_mask(head)
            scores = f32_dot(queries * mask, keys, ((1,), (1,))) * scale_factor
            log_totals = jnp.log(jnp.sum(jnp.exp(scores), axis=1, keepdims=True))
            probs = jnp.exp(scores - log_totals).astype(jnp.bfloat16)
            total = total + f32_dot(probs, values * mask, ((1,), (0,)))
        start = pl.multiple_of(index * pair_width, pair_width)
        out_ref[:, pl.ds(start, pair_width)] = total.astype(jnp.bfloat16)
        return carry

    lax.fori_loop(0, width // pair_width, pair, 0)


def attend_backward_kernel(width, qkv_ref, d_out_ref, d_qkv_ref):
    scale_factor = 1.0 / math.sqrt(HEAD_DIM)
    pair_width = 2 * HEAD_DIM
    half = jnp.bfloat16

    def pair(index, carry):
        def place(part):
            return pl.ds(pl.multiple_of(part * width + index * pair_width, pair_width), pair_width)

        queries, keys, values = (qkv_ref[:, place(part)] for part in range(3))
        d_out = d_out_ref[:, place(0)]
        d_queries = jnp.zeros(queries.shape, jnp.float32)
        d_keys, d_values = d_queries, d_queries
        for head in range(2):
            mask = head_mask(head)
            own_queries, own_d_out = queries * mask, d_out * mask
            scores = f32_dot(keys, own_queries, ((1,), (1,))) * scale_factor
            log_totals = jnp.log(jnp.sum(jnp.exp(scores), axis=0, keepdims=True))
            probs = jnp.exp(scores - log_totals)
            d_probs = f32_dot(values, own_d_out, ((1,), (1,)))
            row_dot = jnp.sum(probs * d_probs, axis=0, keepdims=True)
            d_scores = (probs * (d_probs - row_dot) * scale_factor).astype(half)
            d_values = d_values + f32_dot(probs.astype(half), own_d_out, ((1,), (0,)))
            d_keys = d_keys + f32_dot(d_scores, own_queries, ((1,), (0,)))
            d_queries = d_queries + f32_dot(d_scores, keys * mask, ((0,), (0,)))
        for part, value in enumerate((d_queries, d_keys, d_values)):
            d_qkv_ref[:, place(part)] = value.astype(half)
        return carry

    lax.fori_loop(0, width // pair_width, pair, 0)


def attend_call(qkv_rows, d_attended=None):
    rows, width = qkv_rows.shape
    width = width // 3
    operands = (qkv_rows,) if d_attended is None else (qkv_rows, d_attended)
    kernel = attend_kernel if d_attended is None else attend_backward_kernel
    out_width = width if d_attended is None else 3 * width
    return pl.pallas_call(
        functools.partial(kernel, width),
        out_shape=jax.ShapeDtypeStruct((rows, out_width), jnp.bfloat16),
        in_specs=[pl.BlockSpec(memory_space=pltpu.VMEM)] * len(operands),
        out_specs=pl.BlockSpec(memory_space=pltpu.VMEM),
        compiler_params=pltpu.CompilerParams(vmem_limit_bytes=24 * 2**20),
        name="attend" if d_attended is None else "attend_backward",
    )(*operands)


def norm_forward(values, gain_row, shift_row):
    centred = values - jnp.mean(values, axis=-1, keepdims=True)
    variance = jnp.mean(centred * centred, axis=-1, keepdims=True)
    inverse = lax.rsqrt(variance + EPS)
    unit_rows = centred * inverse
    return (unit_rows * gain_row + shift_row, unit_rows, inverse)


def norm_backward(d_normed, unit_rows, inverse, gain_row):
    d_gain = jnp.sum(d_normed * unit_rows, axis=0)
    d_shift = jnp.sum(d_normed, axis=0)
    scaled = d_normed * gain_row
    d_values = inverse * (
        scaled
        - jnp.mean(scaled, axis=-1, keepdims=True)
        - unit_rows * jnp.mean(scaled * unit_rows, axis=-1, keepdims=True)
    )
    return (d_values, d_gain, d_shift)


def gelu_slope(pre_act):
    return (
        0.5 * (1.0 + lax.erf(pre_act * SQRT_HALF))
        + pre_act * jnp.exp(-0.5 * pre_act * pre_act) * INV_ROOT_TAU
    )


def split_heads(qkv_rows, image_count):
    feature_count = qkv_rows.shape[1] // 3
    return [
        qkv_rows[:, part_index * feature_count : (part_index + 1) * feature_count].reshape(
            image_count, -1, HEADS, HEAD_DIM
        )
        for part_index in range(3)
    ]


def attend_forward(qkv_rows, image_count):
    queries, key_rows, value_rows = split_heads(qkv_rows, image_count)
    scale_factor = 1.0 / math.sqrt(HEAD_DIM)
    scores = (
        jnp.einsum("bqhd,bkhd->bhqk", queries, key_rows, preferred_element_type=jnp.float32)
        * scale_factor
    )
    log_totals = jnp.log(jnp.sum(jnp.exp(scores), axis=-1))
    probs_half = jnp.exp(scores - log_totals[..., None]).astype(jnp.bfloat16)
    attended = jnp.einsum(
        "bhqk,bkhd->bqhd", probs_half, value_rows, preferred_element_type=jnp.float32
    )
    return (attended.astype(jnp.bfloat16).reshape(-1, HEADS * HEAD_DIM), log_totals)


def attend_backward(qkv_rows, log_totals, d_attended, image_count):
    queries, key_rows, value_rows = split_heads(qkv_rows, image_count)
    scale_factor = 1.0 / math.sqrt(HEAD_DIM)
    scores = (
        jnp.einsum("bqhd,bkhd->bhqk", queries, key_rows, preferred_element_type=jnp.float32)
        * scale_factor
    )
    probs = jnp.exp(scores - log_totals[..., None])
    probs_half = probs.astype(jnp.bfloat16)
    d_heads = d_attended.reshape(image_count, -1, HEADS, HEAD_DIM)
    d_values = jnp.einsum(
        "bhqk,bqhd->bkhd", probs_half, d_heads, preferred_element_type=jnp.float32
    )
    d_probs = jnp.einsum("bqhd,bkhd->bhqk", d_heads, value_rows, preferred_element_type=jnp.float32)
    row_dot = jnp.sum(probs * d_probs, axis=-1, keepdims=True)
    d_scores = (probs * (d_probs - row_dot) * scale_factor).astype(jnp.bfloat16)
    d_queries = jnp.einsum(
        "bhqk,bkhd->bqhd", d_scores, key_rows, preferred_element_type=jnp.float32
    )
    d_keys = jnp.einsum("bhqk,bqhd->bkhd", d_scores, queries, preferred_element_type=jnp.float32)
    feature_count = HEADS * HEAD_DIM
    joined = jnp.concatenate(
        [
            d_queries.reshape(-1, feature_count),
            d_keys.reshape(-1, feature_count),
            d_values.reshape(-1, feature_count),
        ],
        axis=1,
    )
    return joined.astype(jnp.bfloat16)


def on_device(
    boundary_in, routes, capacity_slots, ln_gain, ln_bias, w_qkv, w_out, w_router, w_up, w_down
):
    section_index = lax.axis_index("section")
    is_first = section_index == 0
    depth = lax.axis_size("dp")
    groups = lax.axis_size("expert")
    expert_count = EXP_DEV * groups
    local_images = boundary_in.shape[2]
    token_rows = local_images * boundary_in.shape[3]
    model_width = boundary_in.shape[4]
    capacity = 26 * token_rows // (16 * expert_count)
    cap_rows = round_up(capacity, 8)
    padded_rows = round_up(token_rows + 8, 16)
    chips = ("dp", "expert")
    half = jnp.bfloat16
    swapped = [(0, 1), (1, 0)]

    edge = boundary_in[0].reshape(MB, token_rows, model_width)
    route_rows = routes[0].reshape(MB, token_rows, 2)
    slot_rows = capacity_slots[0].reshape(MB, token_rows, 2)
    slot_index = jnp.where(slot_rows < capacity, route_rows * cap_rows + slot_rows, -1)
    table = jnp.concatenate([slot_index, route_rows], axis=2).transpose(0, 2, 1)
    table = jnp.pad(
        table, ((0, 0), (0, 4), (0, padded_rows - token_rows)), constant_values=-1
    )

    norm_columns = jnp.concatenate([ln_gain, ln_bias], axis=1).transpose(0, 2, 1)
    used = 4 * model_width + expert_count + 4
    padding = -used % 256
    packed = jnp.concatenate([w_qkv, w_out, w_router, norm_columns], axis=2)
    packed = jnp.pad(packed, ((0, 0), (0, 0), (0, padding)))
    (
        dense_first, later_half, up_first, up_second, down_first, down_second,
        stream, cotangent, table_first, table_second,
    ) = start_call(8, depth, groups, packed[0], w_up[0], w_down[0], edge, table)
    dense_first = dense_first.reshape(model_width, used + padding)
    later_half = lax.all_gather(later_half, chips, axis=0, tiled=True)
    qkv_all, out_all, router_all, norm_all = [], [], [], []

    def add_dense(item):
        qkv_all.append(item[:, : 3 * model_width])
        out_all.append(item[:, 3 * model_width : 4 * model_width])
        router_all.append(item[:, 4 * model_width : used - 4])
        norm_all.append(item[:, used - 4 : used].T.astype(jnp.float32))

    add_dense(dense_first)
    up_all = (up_first, up_second)
    down_all = (down_first, down_second)
    slot_tables = (table_first, table_second)
    z_index = lax.axis_index("dp")
    chosen_all = [
        (
            lax.dynamic_index_in_dim(item, z_index, 0, False)[2:4, :token_rows].T[..., None]
            == jnp.arange(expert_count, dtype=jnp.int32)
        ).astype(jnp.float32)
        for item in slot_tables
    ]
    moe = functools.partial(moe_call, depth=depth, groups=groups, cap_rows=cap_rows)

    def layer_forward(layer, inputs):
        chosen = chosen_all[layer]
        normed_one, unit_one, inverse_one = norm_forward(
            inputs, norm_all[layer][0], norm_all[layer][2]
        )
        norm_one = normed_one.astype(half)
        qkv_rows = jnp.dot(norm_one, qkv_all[layer], preferred_element_type=jnp.float32).astype(half)
        if local_images == 1:
            attended, log_totals = attend_call(qkv_rows), None
        else:
            attended, log_totals = attend_forward(qkv_rows, local_images)
        middle = inputs + jnp.dot(attended, out_all[layer], preferred_element_type=jnp.float32)
        normed_two, unit_two, inverse_two = norm_forward(
            middle, norm_all[layer][1], norm_all[layer][3]
        )
        norm_two = normed_two.astype(half)
        logits = jnp.dot(norm_two, router_all[layer], preferred_element_type=jnp.float32)
        picked = jnp.sum(logits[:, None, :] * chosen, axis=-1)
        leading = jax.nn.sigmoid(picked[:, 0] - picked[:, 1])
        gate_pair = jnp.stack([leading, 1.0 - leading], axis=-1)
        gate_rows = jnp.pad(gate_pair.T, ((0, 0), (0, model_width - token_rows)))
        sent = jnp.concatenate(
            [
                norm_two,
                jnp.zeros((padded_rows - 8 - token_rows, model_width), half),
                gate_rows.astype(half),
                jnp.zeros((6, model_width), half),
            ]
        )
        combined, *expert_saved = moe(
            False, 2 * layer, rows=sent, slots=slot_tables[layer], up=up_all[layer],
            down=down_all[layer],
        )
        out_rows = middle + combined[:token_rows]
        saved = (
            inputs, norm_one, qkv_rows, log_totals, attended, middle, norm_two, gate_pair,
            expert_saved,
        )
        return (out_rows, saved)

    def layer_backward(layer, d_out, saved):
        (
            inputs, norm_one, qkv_rows, log_totals, attended, middle, norm_two, gate_pair,
            expert_saved,
        ) = saved
        chosen = chosen_all[layer]
        all_rows, hidden, slope, back_rows, gates = expert_saved
        sent = jnp.pad(d_out.astype(half), ((0, padded_rows - token_rows), (0, 0)))
        combined, up_grad, down_grad = moe(
            True, 2 * layer + 1, rows=sent, slots=slot_tables[layer], up=up_all[layer],
            down=down_all[layer], saved=(gates, hidden, slope, back_rows, all_rows),
        )
        d_gate_rows = combined[padded_rows - 8 :, :token_rows]
        d_gate = jnp.stack([d_gate_rows[0] + d_gate_rows[1], d_gate_rows[2] + d_gate_rows[3]], axis=1)
        d_lead = (d_gate[:, 0] - d_gate[:, 1]) * gate_pair[:, 0] * gate_pair[:, 1]
        d_logits = (d_lead[:, None] * (chosen[:, 0] - chosen[:, 1])).astype(half)
        d_norm_two = combined[:token_rows] + jnp.einsum(
            "te,de->td", d_logits, router_all[layer], preferred_element_type=jnp.float32
        )
        normed_two, unit_two, inverse_two = norm_forward(
            middle, norm_all[layer][1], norm_all[layer][3]
        )
        d_middle_norm, gain_two, shift_two = norm_backward(
            d_norm_two, unit_two, inverse_two, norm_all[layer][1]
        )
        d_middle = d_out + d_middle_norm
        d_middle_half = d_middle.astype(half)
        d_attended = jnp.einsum(
            "te,de->td", d_middle_half, out_all[layer], preferred_element_type=jnp.float32
        ).astype(half)
        if local_images == 1:
            d_qkv = attend_call(qkv_rows, d_attended)
        else:
            d_qkv = attend_backward(qkv_rows, log_totals, d_attended, local_images)
        d_norm_one = jnp.einsum(
            "te,de->td", d_qkv, qkv_all[layer], preferred_element_type=jnp.float32
        )
        normed_one, unit_one, inverse_one = norm_forward(
            inputs, norm_all[layer][0], norm_all[layer][2]
        )
        d_input_norm, gain_one, shift_one = norm_backward(
            d_norm_one, unit_one, inverse_one, norm_all[layer][0]
        )
        d_input = d_middle + d_input_norm
        small = jnp.concatenate(
            [
                jnp.einsum("td,te->de", norm_two, d_logits, preferred_element_type=jnp.float32),
                jnp.stack([gain_one, gain_two, shift_one, shift_two], axis=1),
            ],
            axis=1,
        )
        return (d_input, (norm_one, d_qkv, attended, d_middle_half, small), (up_grad, down_grad))

    qkv_part, out_part = 3 * model_width // 2, model_width // 2
    small_width = round_up(expert_count + 4, 128)

    def dense_gradients(norm_one, d_qkv, attended, d_middle_half, small):
        own = jnp.concatenate([norm_one, d_qkv, attended, d_middle_half], axis=1)
        pair = jnp.concatenate([own, lax.ppermute(own, "section", swapped)], axis=0)
        d_qkv_part = lax.dynamic_slice_in_dim(
            pair, model_width + section_index * qkv_part, qkv_part, axis=1
        )
        d_out_part = lax.dynamic_slice_in_dim(
            pair, 5 * model_width + section_index * out_part, out_part, axis=1
        )
        qkv_grad = jnp.einsum(
            "td,te->de", pair[:, :model_width], d_qkv_part, preferred_element_type=jnp.float32
        )
        out_grad = jnp.einsum(
            "td,te->de", pair[:, 4 * model_width : 5 * model_width], d_out_part,
            preferred_element_type=jnp.float32,
        )
        small = jnp.pad(small, ((0, 0), (0, small_width - expert_count - 4)))
        packed_grad = jnp.concatenate(
            [qkv_grad.astype(half), out_grad.astype(half), small.astype(half)], axis=1
        )
        blocks = packed_grad.reshape(depth, groups, -1, packed_grad.shape[1]).transpose(1, 0, 2, 3)
        blocks = lax.all_to_all(blocks, "expert", split_axis=0, concat_axis=0, tiled=True)
        blocks = jnp.sum(blocks.astype(jnp.float32), axis=0).astype(half)
        blocks = lax.all_to_all(blocks, "dp", split_axis=0, concat_axis=0, tiled=True)
        return jnp.sum(blocks.astype(jnp.float32), axis=0)

    saved_list = []
    for layer in range(2):
        if layer > 0:
            stream, later_half = lax.optimization_barrier((stream.astype(half), later_half))
            stream = stream.astype(jnp.float32)
            add_dense(lax.all_gather(later_half, "section", axis=1, tiled=True))
        stream, saved = layer_forward(layer, stream)
        saved_list.append(saved)
    dense_operands = [None, None]
    expert_grads = [None, None]
    for layer in (1, 0):
        if layer < 1:
            cotangent = cotangent.astype(half).astype(jnp.float32)
        cotangent, operands, expert_grads[layer] = layer_backward(
            layer, cotangent, saved_list[layer]
        )
        dense_operands[layer] = operands

    def mine(first, second):
        return jnp.where(is_first, first, second)

    def both(first, second):
        own, away = mine(first, second), mine(second, first)
        return own, lax.ppermute(away, "section", swapped)

    if model_width % (16 * depth * groups) == 0:
        operands = [
            item[:4] + (jnp.pad(item[4], ((0, 0), (0, small_width - expert_count - 4))),)
            for item in dense_operands
        ]
        shard, other_up, other_down, other_rows = finish_call(
            9, depth, groups, operands[0], operands[1], *expert_grads[0], *expert_grads[1],
            cotangent, stream,
        )
        own_up = mine(expert_grads[0][0], expert_grads[1][0])
        own_down = mine(expert_grads[0][1], expert_grads[1][1])
        own_rows = mine(cotangent, stream)
        qkv_shard = shard[:, : 3 * model_width]
        out_shard = shard[:, 3 * model_width : 4 * model_width]
        small_shard = shard[:, 4 * model_width :]
    else:
        shards = [dense_gradients(*item) for item in dense_operands]
        own_shard, other_shard = both(shards[0], shards[1])
        low, high = mine(own_shard, other_shard), mine(other_shard, own_shard)
        qkv_shard = jnp.concatenate([low[:, :qkv_part], high[:, :qkv_part]], axis=1)
        out_shard = jnp.concatenate(
            [low[:, qkv_part : qkv_part + out_part], high[:, qkv_part : qkv_part + out_part]], axis=1
        )
        small_shard = (low + high)[:, qkv_part + out_part :]
        own_up, other_up = both(expert_grads[0][0], expert_grads[1][0])
        own_down, other_down = both(expert_grads[0][1], expert_grads[1][1])
        own_rows, other_rows = both(cotangent, stream)
    norm_shard = small_shard[:, expert_count : expert_count + 4].T

    def expert_grad(own, other):
        return (own.astype(jnp.float32) + other.astype(jnp.float32))[None]

    boundary_rows = jnp.stack([mine(own_rows, other_rows), mine(other_rows, own_rows)])
    boundary_out = boundary_rows.reshape(1, MB, local_images, boundary_in.shape[3], model_width)
    return (
        boundary_out,
        norm_shard[None, 0:2],
        norm_shard[None, 2:4],
        qkv_shard[None],
        out_shard[None],
        small_shard[None, :, :expert_count],
        expert_grad(own_up, other_up),
        expert_grad(own_down, other_down),
    )


def solution(mesh):
    in_specs = (
        P("section", None, ("dp", "expert"), None, None),
        P("section", None, ("dp", "expert"), None, None),
        P("section", None, ("dp", "expert"), None, None),
        P("section", None, ("dp", "expert")),
        P("section", None, ("dp", "expert")),
        P("section", ("dp", "expert"), None),
        P("section", ("dp", "expert"), None),
        P("section", ("dp", "expert"), None),
        P("section", "expert", None, "dp"),
        P("section", "expert", "dp", None),
    )
    out_specs = (
        P("section", None, ("dp", "expert"), None, None),
        P("section", None, ("dp", "expert")),
        P("section", None, ("dp", "expert")),
        P("section", ("dp", "expert"), None),
        P("section", ("dp", "expert"), None),
        P("section", ("dp", "expert"), None),
        P("section", "expert", None, "dp"),
        P("section", "expert", "dp", None),
    )
    return jax.shard_map(
        on_device, mesh=mesh, in_specs=in_specs, out_specs=out_specs, check_vma=False
    )
```

```python
import functools
import math

import jax
import jax.numpy as jnp
from jax import lax
from jax.experimental import pallas as pl
from jax.experimental.pallas import tpu as pltpu
from jax.sharding import PartitionSpec as P

HEADS = 12
HEAD_DIM = 64
EXP_DEV = 2
MB = 2


EPS = 1e-06
SQRT_HALF = 0.7071067811865476
INV_ROOT_TAU = 0.3989422804014327
MESH = pl.DeviceIdType.MESH


def round_up(value, unit):
    return (value + unit - 1) // unit * unit


def z_order(step, z, depth):
    if depth == 1:
        return z
    direction = 1 - 2 * (z // (depth // 2))
    return lax.rem(z + step * direction + depth, depth)


def f32_dot(a, b, dims):
    return lax.dot_general(a, b, (dims, ((), ())), preferred_element_type=jnp.float32)


def moe_kernel(backward, shape, *refs):
    depth, groups, cap_rows, token_rows, model_width, hidden_width = shape
    if backward:
        (
            rows_ref, slots_ref, up_ref, down_ref, gates_ref, hidden_ref, slope_ref, back_ref,
            kept_ref, out_ref, up_grad_ref, down_grad_ref, inbox, d_pre_ref, taken_ref,
            raw, sent_rows, sent_back, sent_home, home, back, d_gates, *sems,
        ) = refs
    else:
        (
            rows_ref, slots_ref, up_ref, down_ref,
            out_ref, taken_ref, hidden_ref, slope_ref, back, gates_ref,
            inbox, raw, sent_rows, sent_back, sent_home, home, *sems,
        ) = refs
    far_send, far_recv, go_send, go_recv, back_send, back_recv, home_send, home_recv = sems
    half = jnp.bfloat16
    section, z, column = (
        lax.axis_index("section"), lax.axis_index("dp"), lax.axis_index("expert")
    )
    slot_count = 2 * groups * cap_rows
    tail = token_rows - 16

    def z_peer(distance):
        return (section, lax.rem(z + distance, depth), column)

    def xy_peer(distance):
        return lax.rem(column + distance, groups)

    barrier = pltpu.get_barrier_semaphore()

    def greet_z(distance, carry):
        pl.semaphore_signal(barrier, inc=1, device_id=z_peer(distance), device_id_type=MESH)
        return carry

    def greet_xy(distance, carry):
        pl.semaphore_signal(
            barrier, inc=1, device_id=(section, z, xy_peer(distance)), device_id_type=MESH
        )
        return carry

    lax.fori_loop(1, depth, greet_z, 0)
    lax.fori_loop(1, groups, greet_xy, 0)
    pl.semaphore_wait(barrier, depth - 1 + groups - 1)

    def far_copy(direction, image):
        target = lax.rem(z + 2 * direction - 1 + depth, depth)
        source = raw.at[image]
        return pltpu.make_async_remote_copy(
            src_ref=source, dst_ref=raw.at[image],
            send_sem=far_send.at[direction, image], recv_sem=far_recv.at[image],
            device_id=(section, target, column), device_id_type=MESH,
        )

    def go_copy(image, source, target):
        return pltpu.make_async_remote_copy(
            src_ref=sent_rows.at[image, target], dst_ref=inbox.at[image, source],
            send_sem=go_send.at[image, target], recv_sem=go_recv.at[image, source],
            device_id=(section, z, target), device_id_type=MESH,
        )

    def back_copy(image, source, target):
        return pltpu.make_async_remote_copy(
            src_ref=sent_back.at[image, target], dst_ref=back.at[image, source],
            send_sem=back_send.at[image, target], recv_sem=back_recv.at[image, source],
            device_id=(section, z, target), device_id_type=MESH,
        )

    def home_copy(source, target):
        return pltpu.make_async_remote_copy(
            src_ref=sent_home.at[target], dst_ref=home.at[source],
            send_sem=home_send.at[target], recv_sem=home_recv.at[source],
            device_id=(section, target, column), device_id_type=MESH,
        )

    raw[z] = rows_ref[...]

    @pl.when(z < depth - 1)
    def _():
        far_copy(1, z).start()

    @pl.when(z > 0)
    def _():
        far_copy(0, z).start()

    def match(image):
        slots = slots_ref[image][:, :token_rows]
        index = lax.broadcasted_iota(jnp.int32, (slot_count, token_rows), 0)
        return index == slots[0:1], index == slots[1:2]

    def gate_table(image):
        first, second = match(image)
        gates = gates_ref[image]
        table = jnp.where(first, gates[0:1], 0.0) + jnp.where(second, gates[1:2], 0.0)
        return table.astype(half)

    def ones_table(image):
        first, second = match(image)
        return jnp.where(first | second, 1.0, 0.0).astype(half)

    def pass_on(step):
        low, high = z - step, z + step

        @pl.when(low >= 0)
        def _():
            far_copy(1, low).wait_recv()

            @pl.when(z < depth - 1)
            def _():
                far_copy(1, low).start()

        @pl.when(high < depth)
        def _():
            far_copy(0, high).wait_recv()

            @pl.when(z > 0)
            def _():
                far_copy(0, high).start()

    def dispatch(image):
        if not backward:
            gates_ref[image] = raw[image, tail:, :token_rows].astype(jnp.float32)[8:16]
        table = gate_table(image) if backward else ones_table(image)
        rows = raw[image]
        blocks = f32_dot(table, rows, ((1,), (0,))).astype(half)
        sent_rows[image] = blocks.reshape(groups, 2 * cap_rows, model_width)

        def send(distance, carry):
            go_copy(image, column, xy_peer(distance)).start()
            return carry

        lax.fori_loop(1, groups, send, 0)
        inbox[image, column] = sent_rows[image, column]
        if backward:
            first, second = match(image)
            returned = back_ref[image].reshape(slot_count, model_width)
            ones = jnp.ones((8, model_width), half)
            row_index = lax.broadcasted_iota(jnp.int32, (8, token_rows), 0)
            packed = jnp.zeros((8, token_rows), jnp.float32)
            for choice, found in enumerate((first, second)):
                table = jnp.where(found, 1.0, 0.0).astype(half)
                selected = f32_dot(table, returned, ((0,), (0,)))
                product = (selected * rows.astype(jnp.float32)).astype(half)
                sums = f32_dot(ones, product, ((1,), (1,)))
                high = sums.astype(half).astype(jnp.float32)
                packed = jnp.where(row_index == 2 * choice, high, packed)
                packed = jnp.where(row_index == 2 * choice + 1, sums - high, packed)
            d_gates[image] = packed

    def experts(image):
        def arrive(distance, carry):
            go_copy(image, xy_peer(distance), column).wait_recv()
            return carry

        lax.fori_loop(1, groups, arrive, 0)
        block = inbox[image].astype(jnp.float32)
        results = []
        for expert in range(2):
            rows = block[:, expert * cap_rows : (expert + 1) * cap_rows]
            rows = rows.reshape(groups * cap_rows, model_width).astype(half)
            taken_ref[expert, image] = rows
            if backward:
                d_hidden = f32_dot(rows, down_ref[expert], ((1,), (1,)))
                d_pre = (d_hidden * slope_ref[expert, image].astype(jnp.float32)).astype(half)
                d_pre_ref[expert, image] = d_pre
                result = f32_dot(d_pre, up_ref[expert], ((1,), (1,)))
            else:
                pre = f32_dot(rows, up_ref[expert], ((1,), (0,)))
                share = 0.5 * (1.0 + lax.erf(pre * SQRT_HALF))
                slope = share + pre * jnp.exp(-0.5 * pre * pre) * INV_ROOT_TAU
                hidden = (pre * share).astype(half)
                hidden_ref[expert, image] = hidden
                slope_ref[expert, image] = slope.astype(half)
                result = f32_dot(hidden, down_ref[expert], ((1,), (0,)))
            results.append(result.reshape(groups, cap_rows, model_width))
        sent_back[image] = jnp.concatenate(results, axis=1).astype(half)

        def send(distance, carry):
            back_copy(image, column, xy_peer(distance)).start()
            return carry

        lax.fori_loop(1, groups, send, 0)
        back[image, column] = sent_back[image, column]

    def combine(image):
        def arrive(distance, carry):
            back_copy(image, xy_peer(distance), column).wait_recv()
            return carry

        lax.fori_loop(1, groups, arrive, 0)
        table = ones_table(image) if backward else gate_table(image)
        total = f32_dot(table, back[image].reshape(slot_count, model_width), ((0,), (0,)))
        if backward:
            extra = jnp.concatenate(
                [jnp.zeros((8, token_rows), jnp.float32), d_gates[image]], axis=0
            )

        @pl.when(image == z)
        def _():
            out_ref[...] = total
            if backward:
                out_ref[tail:, :token_rows] = total[tail:, :token_rows] + extra

        @pl.when(image != z)
        def _():
            sent_home[image] = total.astype(half)
            if backward:
                sent_home[image, tail:, :token_rows] = (
                    total[tail:, :token_rows] + extra
                ).astype(half)
            home_copy(z, image).start()

    def stage(step, carry):
        @pl.when(jnp.logical_and(step >= 1, step < depth))
        def _():
            pass_on(step)

        @pl.when(step < depth)
        def _():
            dispatch(z_order(step, z, depth))

        @pl.when(jnp.logical_and(step >= 2, step < depth + 2))
        def _():
            experts(z_order(lax.rem(step - 1, depth), z, depth))

        @pl.when(step >= 3)
        def _():
            combine(z_order(lax.rem(step - 2, depth), z, depth))

        return carry

    lax.fori_loop(0, depth + 3, stage, 0)

    if backward:

        def expert_gradients(expert, carry):
            kept = kept_ref[expert].reshape(depth * groups * cap_rows, model_width)
            d_pre = d_pre_ref[expert].reshape(depth * groups * cap_rows, hidden_width)
            up_grad_ref[expert] = f32_dot(kept, d_pre, ((0,), (0,))).astype(half)
            hidden = hidden_ref[expert].reshape(depth * groups * cap_rows, hidden_width)
            grads = taken_ref[expert].reshape(depth * groups * cap_rows, model_width)
            down_grad_ref[expert] = f32_dot(hidden, grads, ((0,), (0,))).astype(half)
            return carry

        lax.fori_loop(0, 2, expert_gradients, 0)

    def finish_home(distance, carry):
        source = lax.rem(z + distance, depth)
        home_copy(source, z).wait_recv()
        out_ref[...] += home[source].astype(jnp.float32)
        return carry

    lax.fori_loop(1, depth, finish_home, 0)

    def drain_home(distance, carry):
        home_copy(z, lax.rem(z + distance, depth)).wait_send()
        return carry

    lax.fori_loop(1, depth, drain_home, 0)

    def drain_image(image, carry):
        @pl.when(jnp.logical_and(z < depth - 1, image <= z))
        def _():
            far_copy(1, image).wait_send()

        @pl.when(jnp.logical_and(z > 0, image >= z))
        def _():
            far_copy(0, image).wait_send()

        def drain(distance, inner):
            go_copy(image, column, xy_peer(distance)).wait_send()
            back_copy(image, column, xy_peer(distance)).wait_send()
            return inner

        lax.fori_loop(1, groups, drain, 0)
        return carry

    lax.fori_loop(0, depth, drain_image, 0)


def moe_call(backward, call_id, depth, groups, cap_rows, rows, slots, up, down, saved=()):
    token_rows, model_width = rows.shape
    hidden_width = up.shape[2]
    half = jnp.bfloat16
    shape = (depth, groups, cap_rows, token_rows, model_width, hidden_width)
    taken = jax.ShapeDtypeStruct((2, depth, groups * cap_rows, model_width), half)
    hidden = jax.ShapeDtypeStruct((2, depth, groups * cap_rows, hidden_width), half)
    back = (depth, groups, 2 * cap_rows, model_width)
    out = jax.ShapeDtypeStruct((token_rows, model_width), jnp.float32)
    if backward:
        out_shape = (
            out, jax.ShapeDtypeStruct(up.shape, half), jax.ShapeDtypeStruct(down.shape, half)
        )
    else:
        gates = jax.ShapeDtypeStruct((depth, 8, token_rows), jnp.float32)
        out_shape = (out, taken, hidden, hidden, jax.ShapeDtypeStruct(back, half), gates)
    scratch = [
        pltpu.VMEM((depth, token_rows, model_width), half),
        pltpu.VMEM(back, half),
        pltpu.VMEM(back, half),
        pltpu.VMEM((depth, token_rows, model_width), half),
        pltpu.VMEM((depth, token_rows, model_width), half),
    ]
    if backward:
        scratch = [pltpu.VMEM(hidden.shape, half), pltpu.VMEM(taken.shape, half)] + scratch
        scratch += [
            pltpu.VMEM(back, half),
            pltpu.VMEM((depth, 8, token_rows), jnp.float32),
        ]
    scratch = [pltpu.VMEM(back, half)] + scratch
    scratch += [
        pltpu.SemaphoreType.DMA((2, depth)),
        pltpu.SemaphoreType.DMA((depth,)),
        pltpu.SemaphoreType.DMA((depth, groups)),
        pltpu.SemaphoreType.DMA((depth, groups)),
        pltpu.SemaphoreType.DMA((depth, groups)),
        pltpu.SemaphoreType.DMA((depth, groups)),
        pltpu.SemaphoreType.DMA((depth,)),
        pltpu.SemaphoreType.DMA((depth,)),
    ]
    return pl.pallas_call(
        functools.partial(moe_kernel, backward, shape),
        out_shape=out_shape,
        in_specs=[pl.BlockSpec(memory_space=pltpu.VMEM)] * (4 + len(saved)),
        out_specs=[pl.BlockSpec(memory_space=pltpu.VMEM)] * len(out_shape),
        scratch_shapes=scratch,
        compiler_params=pltpu.CompilerParams(
            collective_id=call_id, has_side_effects=True, vmem_limit_bytes=50 * 2**20
        ),
        name="moe_backward" if backward else "moe_forward",
    )(rows, slots, up, down, *saved)

def start_kernel(shape, *refs):
    depth, groups = shape
    (
        packed_ref, up_ref, down_ref, edge_ref, table_ref,
        dense_ref, up_first, up_second, down_first, down_second,
        rows_ref, cotangent_ref, table_first, table_second,
        shard_send, shard_recv, core_send, core_recv, table_send, table_recv, own_sem,
    ) = refs
    section, z, column = (
        lax.axis_index("section"), lax.axis_index("dp"), lax.axis_index("expert")
    )
    other = (1 - section, z, column)
    is_first = section == 0

    def z_peer(distance):
        return lax.rem(z + distance, depth)

    def xy_peer(distance):
        return lax.rem(column + distance, groups)

    barrier = pltpu.get_barrier_semaphore()

    def greet_z(distance, carry):
        pl.semaphore_signal(
            barrier, inc=1, device_id=(section, z_peer(distance), column), device_id_type=MESH
        )
        return carry

    def greet_xy(distance, carry):
        pl.semaphore_signal(
            barrier, inc=1, device_id=(section, z, xy_peer(distance)), device_id_type=MESH
        )
        return carry

    pl.semaphore_signal(barrier, inc=1, device_id=other, device_id_type=MESH)
    lax.fori_loop(1, depth, greet_z, 0)
    lax.fori_loop(1, groups, greet_xy, 0)
    pl.semaphore_wait(barrier, depth + groups - 1)

    def remote(source, target, send, recv, device):
        return pltpu.make_async_remote_copy(
            src_ref=source, dst_ref=target, send_sem=send, recv_sem=recv,
            device_id=device, device_id_type=MESH,
        )

    def shard_copy(kind, layer, plane, lane, device):
        return remote(
            dense_ref.at[layer, plane, lane], dense_ref.at[layer, plane, lane],
            shard_send.at[kind, plane, lane],
            shard_recv.at[0, plane, lane],
            device,
        )

    def z_copy(direction, plane):
        device = (section, lax.rem(z + 2 * direction - 1 + depth, depth), column)
        return shard_copy(direction, section, plane, column, device)

    def core_copy(layer, plane, lane):
        return remote(
            dense_ref.at[layer, plane, lane], dense_ref.at[layer, plane, lane],
            shard_send.at[2, plane, lane], shard_recv.at[1, plane, lane], other,
        )

    def xy_copy(plane, source, target):
        return shard_copy(3 + target, section, plane, source, (section, z, target))

    def pass_copy(plane, source, target):
        return shard_copy(3 + groups, section, plane, source, (section, z, target))

    def swap(index, source, target):
        return remote(source, target, core_send.at[index], core_recv.at[index], other)

    def local(index, source, target):
        return pltpu.make_async_copy(source, target, own_sem.at[index])

    square = groups == 4
    beside = column + 1 - 2 * lax.rem(column, 2)
    above = lax.rem(column + 2, groups)
    across = groups - 1 - column
    direct = 3 if square else groups

    def near(distance):
        if square:
            return beside + (distance - 1) * (above - beside)
        return xy_peer(distance)

    def spread(plane):
        core_copy(section, plane, column).start()

        def send(distance, carry):
            xy_copy(plane, column, near(distance)).start()
            return carry

        lax.fori_loop(1, direct, send, 0)

    def take(plane):
        def arrive(distance, carry):
            lane = near(distance)
            xy_copy(plane, lane, column).wait_recv()
            core_copy(section, plane, lane).start()
            if square:

                @pl.when(lax.rem(plane, 2) == distance - 1)
                def _():
                    pass_copy(plane, lane, near(3 - distance)).start()

            return carry

        lax.fori_loop(1, direct, arrive, 0)

    own_shard = local(0, packed_ref, dense_ref.at[section, z, column])

    def first_copies():
        remote_ones = [
            swap(0, edge_ref.at[1], rows_ref),
            swap(1, table_ref.at[1], table_first.at[z]),
            swap(2, up_ref, up_first),
            swap(3, down_ref, down_first),
        ]
        local_ones = [
            local(1, edge_ref.at[0], rows_ref),
            local(2, table_ref.at[0], table_first.at[z]),
            local(3, up_ref, up_first),
            local(4, down_ref, down_first),
        ]
        return remote_ones, local_ones

    def second_copies():
        remote_ones = [
            swap(0, edge_ref.at[0], cotangent_ref),
            swap(1, table_ref.at[0], table_second.at[z]),
            swap(2, up_ref, up_second),
            swap(3, down_ref, down_second),
        ]
        local_ones = [
            local(1, edge_ref.at[1], cotangent_ref),
            local(2, table_ref.at[1], table_second.at[z]),
            local(3, up_ref, up_second),
            local(4, down_ref, down_second),
        ]
        return remote_ones, local_ones

    own_shard.start()
    own_shard.wait()

    @pl.when(z < depth - 1)
    def _():
        z_copy(1, z).start()

    @pl.when(z > 0)
    def _():
        z_copy(0, z).start()

    spread(z)

    @pl.when(is_first)
    def _():
        remote_ones, local_ones = first_copies()
        for copy in remote_ones[:2] + local_ones + remote_ones[2:]:
            copy.start()

    @pl.when(jnp.logical_not(is_first))
    def _():
        remote_ones, local_ones = second_copies()
        for copy in remote_ones[:2] + local_ones + remote_ones[2:]:
            copy.start()

    def step(distance, carry):
        low, high = z - distance, z + distance

        @pl.when(low >= 0)
        def _():
            z_copy(1, low).wait_recv()

            @pl.when(z < depth - 1)
            def _():
                z_copy(1, low).start()

            spread(low)

        @pl.when(high < depth)
        def _():
            z_copy(0, high).wait_recv()

            @pl.when(z > 0)
            def _():
                z_copy(0, high).start()

            spread(high)

        take(z_order(distance - 1, z, depth))
        return carry

    lax.fori_loop(1, depth, step, 0)
    take(z_order(depth - 1, z, depth))

    first_remote, first_local = first_copies()
    second_remote, second_local = second_copies()

    def table_copies(source, target):
        pairs = []
        for layer, table in enumerate((table_first, table_second)):
            pairs.append(
                remote(
                    table.at[source], table.at[source], table_send.at[layer, target],
                    table_recv.at[layer, source], (section, target, column),
                )
            )
        return pairs

    @pl.when(is_first)
    def _():
        first_local[1].wait()
        second_remote[1].wait_recv()

    @pl.when(jnp.logical_not(is_first))
    def _():
        second_local[1].wait()
        first_remote[1].wait_recv()

    def send_tables(distance, carry):
        for copy in table_copies(z, z_peer(distance)):
            copy.start()
        return carry

    lax.fori_loop(1, depth, send_tables, 0)

    if square:

        def last_arrival(index, carry):
            plane = z_order(index, z, depth)
            pass_copy(plane, across, column).wait_recv()
            core_copy(section, plane, across).start()
            return carry

        lax.fori_loop(0, depth, last_arrival, 0)

    def drain(plane, carry):
        @pl.when(jnp.logical_and(z < depth - 1, plane <= z))
        def _():
            z_copy(1, plane).wait_send()

        @pl.when(jnp.logical_and(z > 0, plane >= z))
        def _():
            z_copy(0, plane).wait_send()

        def drain_core(lane, inner):
            core_copy(1 - section, plane, lane).wait_recv()
            core_copy(section, plane, lane).wait_send()
            return inner

        def drain_xy(distance, inner):
            xy_copy(plane, column, near(distance)).wait_send()
            if square:

                @pl.when(lax.rem(plane, 2) == distance - 1)
                def _():
                    pass_copy(plane, near(distance), near(3 - distance)).wait_send()

            return inner

        lax.fori_loop(0, groups, drain_core, 0)
        return lax.fori_loop(1, direct, drain_xy, carry)

    lax.fori_loop(0, depth, drain, 0)

    @pl.when(is_first)
    def _():
        for index in (0, 2, 3):
            second_remote[index].wait_recv()
        for copy in first_remote:
            copy.wait_send()
        for copy in first_local[:1] + first_local[2:]:
            copy.wait()

    @pl.when(jnp.logical_not(is_first))
    def _():
        for index in (0, 2, 3):
            first_remote[index].wait_recv()
        for copy in second_remote:
            copy.wait_send()
        for copy in second_local[:1] + second_local[2:]:
            copy.wait()

    def finish_tables(distance, carry):
        for copy in table_copies(z_peer(distance), z):
            copy.wait_recv()
        for copy in table_copies(z, z_peer(distance)):
            copy.wait_send()
        return carry

    lax.fori_loop(1, depth, finish_tables, 0)


def start_call(call_id, depth, groups, packed, up, down, edge, table):
    rows, width = packed.shape
    half = jnp.bfloat16
    out_shape = (
        jax.ShapeDtypeStruct((2, depth, groups, rows, width), half),
        jax.ShapeDtypeStruct(up.shape, half),
        jax.ShapeDtypeStruct(up.shape, half),
        jax.ShapeDtypeStruct(down.shape, half),
        jax.ShapeDtypeStruct(down.shape, half),
        jax.ShapeDtypeStruct(edge.shape[1:], jnp.float32),
        jax.ShapeDtypeStruct(edge.shape[1:], jnp.float32),
        jax.ShapeDtypeStruct((depth,) + table.shape[1:], jnp.int32),
        jax.ShapeDtypeStruct((depth,) + table.shape[1:], jnp.int32),
    )
    return pl.pallas_call(
        functools.partial(start_kernel, (depth, groups)),
        out_shape=out_shape,
        in_specs=[pl.BlockSpec(memory_space=pltpu.VMEM)] * 5,
        out_specs=[pl.BlockSpec(memory_space=pl.ANY)] * len(out_shape),
        scratch_shapes=[
            pltpu.SemaphoreType.DMA((4 + groups, depth, groups)),
            pltpu.SemaphoreType.DMA((2, depth, groups)),
            pltpu.SemaphoreType.DMA((4,)),
            pltpu.SemaphoreType.DMA((4,)),
            pltpu.SemaphoreType.DMA((2, depth)),
            pltpu.SemaphoreType.DMA((2, depth)),
            pltpu.SemaphoreType.DMA((5,)),
        ],
        compiler_params=pltpu.CompilerParams(
            collective_id=call_id, has_side_effects=True, vmem_limit_bytes=40 * 2**20
        ),
        name="start_exchange",
    )(packed, up, down, edge, table)

def finish_kernel(shape, *refs):
    depth, groups, token_rows, padded_rows, model_width = shape
    first_refs, second_refs, rest = refs[0:5], refs[5:10], refs[10:]
    (
        up_first, down_first, up_second, down_second, rows_first, rows_second,
        shard_ref, up_ref, down_ref, rows_ref,
        pair, away, small_pair, table, inbox, sent_home, home,
        core_send, core_recv, go_send, go_recv, home_send, home_recv,
    ) = rest
    half = jnp.bfloat16
    section, z, column = (
        lax.axis_index("section"), lax.axis_index("dp"), lax.axis_index("expert")
    )
    other = (1 - section, z, column)
    is_first = section == 0
    shard_rows = table.shape[1]

    def z_peer(distance):
        return lax.rem(z + distance, depth)

    def xy_peer(distance):
        return lax.rem(column + distance, groups)

    barrier = pltpu.get_barrier_semaphore()

    def greet_z(distance, carry):
        pl.semaphore_signal(
            barrier, inc=1, device_id=(section, z_peer(distance), column), device_id_type=MESH
        )
        return carry

    def greet_xy(distance, carry):
        pl.semaphore_signal(
            barrier, inc=1, device_id=(section, z, xy_peer(distance)), device_id_type=MESH
        )
        return carry

    pl.semaphore_signal(barrier, inc=1, device_id=other, device_id_type=MESH)
    lax.fori_loop(1, depth, greet_z, 0)
    lax.fori_loop(1, groups, greet_xy, 0)
    pl.semaphore_wait(barrier, depth + groups - 1)

    def swap(index, source, target):
        return pltpu.make_async_remote_copy(
            src_ref=source, dst_ref=target, send_sem=core_send.at[index],
            recv_sem=core_recv.at[index], device_id=other, device_id_type=MESH,
        )

    def pack(target, operands):
        target[padded_rows - 16 :, :] = jnp.zeros((16, target.shape[1]), half)
        offset = 0
        for operand in operands:
            width = operand.shape[1]
            target[:token_rows, offset : offset + width] = operand[...]
            offset += width

    def side_copies(first):
        if first:
            sources = (second_refs[4], up_second, down_second, rows_second)
        else:
            sources = (first_refs[4], up_first, down_first, rows_first)
        targets = (small_pair.at[1], up_ref, down_ref, rows_ref)
        return [
            swap(1 + index, source, target)
            for index, (source, target) in enumerate(zip(sources, targets))
        ]

    operand_copy = swap(0, away, pair.at[1])
    for first in (True, False):

        @pl.when(is_first if first else jnp.logical_not(is_first))
        def _():
            mine, others = (first_refs, second_refs) if first else (second_refs, first_refs)
            pack(away, others[:4])
            operand_copy.start()
            for copy in side_copies(first):
                copy.start()
            pack(pair.at[0], mine[:4])
            small_pair[0] = mine[4][...]

    operand_copy.wait_recv()
    rows = 2 * padded_rows

    def product(left, right, target):
        a = pair[:, :, left : left + model_width].reshape(rows, model_width)
        b = pair[:, :, right : right + model_width].reshape(rows, model_width)
        value = f32_dot(a, b, ((0,), (0,))).astype(half)
        table[:, :, target : target + model_width] = value.reshape(
            depth * groups, shard_rows, model_width
        )

    for index in range(3):
        product(0, (1 + index) * model_width, index * model_width)
    product(4 * model_width, 5 * model_width, 3 * model_width)
    for copy in side_copies(True)[:1]:
        copy.wait_recv()
    small = (small_pair[0] + small_pair[1]).astype(half)
    table[:, :, 4 * model_width :] = small.reshape(depth * groups, shard_rows, small.shape[1])

    def go_copy(plane, source, target):
        return pltpu.make_async_remote_copy(
            src_ref=table.at[plane * groups + target], dst_ref=inbox.at[plane, source],
            send_sem=go_send.at[plane, target], recv_sem=go_recv.at[plane, source],
            device_id=(section, z, target), device_id_type=MESH,
        )

    def home_copy(source, target):
        return pltpu.make_async_remote_copy(
            src_ref=sent_home.at[target], dst_ref=home.at[source],
            send_sem=home_send.at[target], recv_sem=home_recv.at[source],
            device_id=(section, target, column), device_id_type=MESH,
        )

    def send_plane(step, carry):
        plane = z_peer(step)

        def send(distance, inner):
            go_copy(plane, column, xy_peer(distance)).start()
            return inner

        return lax.fori_loop(1, groups, send, carry)

    lax.fori_loop(1, depth + 1, send_plane, 0)

    def sum_plane(step, carry):
        plane = z_peer(step)

        def arrive(distance, total):
            lane = xy_peer(distance)
            go_copy(plane, lane, column).wait_recv()
            return total + inbox[plane, lane].astype(jnp.float32)

        own = table[plane * groups + column].astype(jnp.float32)
        total = lax.fori_loop(1, groups, arrive, own)

        @pl.when(plane == z)
        def _():
            shard_ref[...] = total

        @pl.when(plane != z)
        def _():
            sent_home[plane] = total.astype(half)
            home_copy(z, plane).start()

        return carry

    lax.fori_loop(1, depth + 1, sum_plane, 0)

    def finish_home(distance, carry):
        source = z_peer(distance)
        home_copy(source, z).wait_recv()
        shard_ref[...] += home[source].astype(jnp.float32)
        home_copy(z, source).wait_send()
        return carry

    lax.fori_loop(1, depth, finish_home, 0)

    def drain_plane(plane, carry):
        def drain(distance, inner):
            go_copy(plane, column, xy_peer(distance)).wait_send()
            return inner

        return lax.fori_loop(1, groups, drain, carry)

    lax.fori_loop(0, depth, drain_plane, 0)
    operand_copy.wait_send()
    for index, copy in enumerate(side_copies(True)):
        copy.wait_send()
        if index > 0:
            copy.wait_recv()


def finish_call(call_id, depth, groups, first, second, up_first, down_first, up_second, down_second,
                rows_first, rows_second):
    token_rows, model_width = first[0].shape
    padded_rows = round_up(token_rows, 16)
    small_width = first[4].shape[1]
    width = 4 * model_width + small_width
    shard_rows = model_width // (depth * groups)
    half = jnp.bfloat16
    out_shape = (
        jax.ShapeDtypeStruct((shard_rows, width), jnp.float32),
        jax.ShapeDtypeStruct(up_first.shape, half),
        jax.ShapeDtypeStruct(down_first.shape, half),
        jax.ShapeDtypeStruct(rows_first.shape, jnp.float32),
    )
    home = pltpu.VMEM((depth, shard_rows, width), half)
    return pl.pallas_call(
        functools.partial(
            finish_kernel, (depth, groups, token_rows, padded_rows, model_width)
        ),
        out_shape=out_shape,
        in_specs=[pl.BlockSpec(memory_space=pltpu.VMEM)] * 16,
        out_specs=[pl.BlockSpec(memory_space=pltpu.VMEM)] + [pl.BlockSpec(memory_space=pl.ANY)] * 3,
        scratch_shapes=[
            pltpu.VMEM((2, padded_rows, 6 * model_width), half),
            pltpu.VMEM((padded_rows, 6 * model_width), half),
            pltpu.VMEM((2, model_width, small_width), jnp.float32),
            pltpu.VMEM((depth * groups, shard_rows, width), half),
            pltpu.VMEM((depth, groups, shard_rows, width), half),
            home,
            home,
            pltpu.SemaphoreType.DMA((5,)),
            pltpu.SemaphoreType.DMA((5,)),
            pltpu.SemaphoreType.DMA((depth, groups)),
            pltpu.SemaphoreType.DMA((depth, groups)),
            pltpu.SemaphoreType.DMA((depth,)),
            pltpu.SemaphoreType.DMA((depth,)),
        ],
        compiler_params=pltpu.CompilerParams(
            collective_id=call_id, has_side_effects=True, vmem_limit_bytes=50 * 2**20
        ),
        name="finish_exchange",
    )(*first, *second, up_first, down_first, up_second, down_second, rows_first, rows_second)

def head_mask(head):
    lanes = lax.broadcasted_iota(jnp.int32, (1, 2 * HEAD_DIM), 1)
    return jnp.where(lanes // HEAD_DIM == head, 1.0, 0.0).astype(jnp.bfloat16)


def attend_kernel(width, qkv_ref, out_ref):
    scale_factor = 1.0 / math.sqrt(HEAD_DIM)
    pair_width = 2 * HEAD_DIM

    def pair(index, carry):
        def columns(part):
            start = pl.multiple_of(part * width + index * pair_width, pair_width)
            return qkv_ref[:, pl.ds(start, pair_width)]

        queries, keys, values = columns(0), columns(1), columns(2)
        total = jnp.zeros(queries.shape, jnp.float32)
        for head in range(2):
            mask = head_mask(head)
            scores = f32_dot(queries * mask, keys, ((1,), (1,))) * scale_factor
            log_totals = jnp.log(jnp.sum(jnp.exp(scores), axis=1, keepdims=True))
            probs = jnp.exp(scores - log_totals).astype(jnp.bfloat16)
            total = total + f32_dot(probs, values * mask, ((1,), (0,)))
        start = pl.multiple_of(index * pair_width, pair_width)
        out_ref[:, pl.ds(start, pair_width)] = total.astype(jnp.bfloat16)
        return carry

    lax.fori_loop(0, width // pair_width, pair, 0)


def attend_backward_kernel(width, qkv_ref, d_out_ref, d_qkv_ref):
    scale_factor = 1.0 / math.sqrt(HEAD_DIM)
    pair_width = 2 * HEAD_DIM
    half = jnp.bfloat16

    def pair(index, carry):
        def place(part):
            return pl.ds(pl.multiple_of(part * width + index * pair_width, pair_width), pair_width)

        queries, keys, values = (qkv_ref[:, place(part)] for part in range(3))
        d_out = d_out_ref[:, place(0)]
        d_queries = jnp.zeros(queries.shape, jnp.float32)
        d_keys, d_values = d_queries, d_queries
        for head in range(2):
            mask = head_mask(head)
            own_queries, own_d_out = queries * mask, d_out * mask
            scores = f32_dot(keys, own_queries, ((1,), (1,))) * scale_factor
            log_totals = jnp.log(jnp.sum(jnp.exp(scores), axis=0, keepdims=True))
            probs = jnp.exp(scores - log_totals)
            d_probs = f32_dot(values, own_d_out, ((1,), (1,)))
            row_dot = jnp.sum(probs * d_probs, axis=0, keepdims=True)
            d_scores = (probs * (d_probs - row_dot) * scale_factor).astype(half)
            d_values = d_values + f32_dot(probs.astype(half), own_d_out, ((1,), (0,)))
            d_keys = d_keys + f32_dot(d_scores, own_queries, ((1,), (0,)))
            d_queries = d_queries + f32_dot(d_scores, keys * mask, ((0,), (0,)))
        for part, value in enumerate((d_queries, d_keys, d_values)):
            d_qkv_ref[:, place(part)] = value.astype(half)
        return carry

    lax.fori_loop(0, width // pair_width, pair, 0)


def attend_call(qkv_rows, d_attended=None):
    rows, width = qkv_rows.shape
    width = width // 3
    operands = (qkv_rows,) if d_attended is None else (qkv_rows, d_attended)
    kernel = attend_kernel if d_attended is None else attend_backward_kernel
    out_width = width if d_attended is None else 3 * width
    return pl.pallas_call(
        functools.partial(kernel, width),
        out_shape=jax.ShapeDtypeStruct((rows, out_width), jnp.bfloat16),
        in_specs=[pl.BlockSpec(memory_space=pltpu.VMEM)] * len(operands),
        out_specs=pl.BlockSpec(memory_space=pltpu.VMEM),
        compiler_params=pltpu.CompilerParams(vmem_limit_bytes=24 * 2**20),
        name="attend" if d_attended is None else "attend_backward",
    )(*operands)


def norm_forward(values, gain_row, shift_row):
    centred = values - jnp.mean(values, axis=-1, keepdims=True)
    variance = jnp.mean(centred * centred, axis=-1, keepdims=True)
    inverse = lax.rsqrt(variance + EPS)
    unit_rows = centred * inverse
    return (unit_rows * gain_row + shift_row, unit_rows, inverse)


def norm_backward(d_normed, unit_rows, inverse, gain_row):
    d_gain = jnp.sum(d_normed * unit_rows, axis=0)
    d_shift = jnp.sum(d_normed, axis=0)
    scaled = d_normed * gain_row
    d_values = inverse * (
        scaled
        - jnp.mean(scaled, axis=-1, keepdims=True)
        - unit_rows * jnp.mean(scaled * unit_rows, axis=-1, keepdims=True)
    )
    return (d_values, d_gain, d_shift)


def gelu_slope(pre_act):
    return (
        0.5 * (1.0 + lax.erf(pre_act * SQRT_HALF))
        + pre_act * jnp.exp(-0.5 * pre_act * pre_act) * INV_ROOT_TAU
    )


def split_heads(qkv_rows, image_count):
    feature_count = qkv_rows.shape[1] // 3
    return [
        qkv_rows[:, part_index * feature_count : (part_index + 1) * feature_count].reshape(
            image_count, -1, HEADS, HEAD_DIM
        )
        for part_index in range(3)
    ]


def attend_forward(qkv_rows, image_count):
    queries, key_rows, value_rows = split_heads(qkv_rows, image_count)
    scale_factor = 1.0 / math.sqrt(HEAD_DIM)
    scores = (
        jnp.einsum("bqhd,bkhd->bhqk", queries, key_rows, preferred_element_type=jnp.float32)
        * scale_factor
    )
    log_totals = jnp.log(jnp.sum(jnp.exp(scores), axis=-1))
    probs_half = jnp.exp(scores - log_totals[..., None]).astype(jnp.bfloat16)
    attended = jnp.einsum(
        "bhqk,bkhd->bqhd", probs_half, value_rows, preferred_element_type=jnp.float32
    )
    return (attended.astype(jnp.bfloat16).reshape(-1, HEADS * HEAD_DIM), log_totals)


def attend_backward(qkv_rows, log_totals, d_attended, image_count):
    queries, key_rows, value_rows = split_heads(qkv_rows, image_count)
    scale_factor = 1.0 / math.sqrt(HEAD_DIM)
    scores = (
        jnp.einsum("bqhd,bkhd->bhqk", queries, key_rows, preferred_element_type=jnp.float32)
        * scale_factor
    )
    probs = jnp.exp(scores - log_totals[..., None])
    probs_half = probs.astype(jnp.bfloat16)
    d_heads = d_attended.reshape(image_count, -1, HEADS, HEAD_DIM)
    d_values = jnp.einsum(
        "bhqk,bqhd->bkhd", probs_half, d_heads, preferred_element_type=jnp.float32
    )
    d_probs = jnp.einsum("bqhd,bkhd->bhqk", d_heads, value_rows, preferred_element_type=jnp.float32)
    row_dot = jnp.sum(probs * d_probs, axis=-1, keepdims=True)
    d_scores = (probs * (d_probs - row_dot) * scale_factor).astype(jnp.bfloat16)
    d_queries = jnp.einsum(
        "bhqk,bkhd->bqhd", d_scores, key_rows, preferred_element_type=jnp.float32
    )
    d_keys = jnp.einsum("bhqk,bqhd->bkhd", d_scores, queries, preferred_element_type=jnp.float32)
    feature_count = HEADS * HEAD_DIM
    joined = jnp.concatenate(
        [
            d_queries.reshape(-1, feature_count),
            d_keys.reshape(-1, feature_count),
            d_values.reshape(-1, feature_count),
        ],
        axis=1,
    )
    return joined.astype(jnp.bfloat16)


def on_device(
    boundary_in, routes, capacity_slots, ln_gain, ln_bias, w_qkv, w_out, w_router, w_up, w_down
):
    section_index = lax.axis_index("section")
    is_first = section_index == 0
    depth = lax.axis_size("dp")
    groups = lax.axis_size("expert")
    expert_count = EXP_DEV * groups
    local_images = boundary_in.shape[2]
    token_rows = local_images * boundary_in.shape[3]
    model_width = boundary_in.shape[4]
    capacity = 26 * token_rows // (16 * expert_count)
    cap_rows = round_up(capacity, 8)
    padded_rows = round_up(token_rows + 8, 16)
    half = jnp.bfloat16
    swapped = [(0, 1), (1, 0)]

    edge = boundary_in[0].reshape(MB, token_rows, model_width)
    route_rows = routes[0].reshape(MB, token_rows, 2)
    slot_rows = capacity_slots[0].reshape(MB, token_rows, 2)
    slot_index = jnp.where(slot_rows < capacity, route_rows * cap_rows + slot_rows, -1)
    table = jnp.concatenate([slot_index, route_rows], axis=2).transpose(0, 2, 1)
    table = jnp.pad(
        table, ((0, 0), (0, 4), (0, padded_rows - token_rows)), constant_values=-1
    )

    norm_columns = jnp.concatenate([ln_gain, ln_bias], axis=1).transpose(0, 2, 1)
    used = 4 * model_width + expert_count + 4
    padding = -used % 128
    packed = jnp.concatenate([w_qkv, w_out, w_router, norm_columns], axis=2)
    packed = jnp.pad(packed, ((0, 0), (0, 0), (0, padding)))
    (
        dense, up_first, up_second, down_first, down_second,
        stream, cotangent, table_first, table_second,
    ) = start_call(8, depth, groups, packed[0], w_up[0], w_down[0], edge, table)
    dense = dense.reshape(2, model_width, used + padding)
    qkv_all, out_all, router_all, norm_all = [], [], [], []

    def add_dense(item):
        qkv_all.append(item[:, : 3 * model_width])
        out_all.append(item[:, 3 * model_width : 4 * model_width])
        router_all.append(item[:, 4 * model_width : used - 4])
        norm_all.append(item[:, used - 4 : used].T.astype(jnp.float32))

    add_dense(dense[0])
    add_dense(dense[1])
    up_all = (up_first, up_second)
    down_all = (down_first, down_second)
    slot_tables = (table_first, table_second)
    z_index = lax.axis_index("dp")
    chosen_all = [
        (
            lax.dynamic_index_in_dim(item, z_index, 0, False)[2:4, :token_rows].T[..., None]
            == jnp.arange(expert_count, dtype=jnp.int32)
        ).astype(jnp.float32)
        for item in slot_tables
    ]
    moe = functools.partial(moe_call, depth=depth, groups=groups, cap_rows=cap_rows)

    def layer_forward(layer, inputs):
        chosen = chosen_all[layer]
        normed_one, unit_one, inverse_one = norm_forward(
            inputs, norm_all[layer][0], norm_all[layer][2]
        )
        norm_one = normed_one.astype(half)
        qkv_rows = jnp.dot(norm_one, qkv_all[layer], preferred_element_type=jnp.float32).astype(half)
        if local_images == 1:
            attended, log_totals = attend_call(qkv_rows), None
        else:
            attended, log_totals = attend_forward(qkv_rows, local_images)
        middle = inputs + jnp.dot(attended, out_all[layer], preferred_element_type=jnp.float32)
        normed_two, unit_two, inverse_two = norm_forward(
            middle, norm_all[layer][1], norm_all[layer][3]
        )
        norm_two = normed_two.astype(half)
        logits = jnp.dot(norm_two, router_all[layer], preferred_element_type=jnp.float32)
        picked = jnp.sum(logits[:, None, :] * chosen, axis=-1)
        leading = jax.nn.sigmoid(picked[:, 0] - picked[:, 1])
        gate_pair = jnp.stack([leading, 1.0 - leading], axis=-1)
        gate_rows = jnp.pad(gate_pair.T, ((0, 0), (0, model_width - token_rows)))
        sent = jnp.concatenate(
            [
                norm_two,
                jnp.zeros((padded_rows - 8 - token_rows, model_width), half),
                gate_rows.astype(half),
                jnp.zeros((6, model_width), half),
            ]
        )
        combined, *expert_saved = moe(
            False, 2 * layer, rows=sent, slots=slot_tables[layer], up=up_all[layer],
            down=down_all[layer],
        )
        out_rows = middle + combined[:token_rows]
        saved = (
            inputs, norm_one, qkv_rows, log_totals, attended, middle, norm_two, gate_pair,
            expert_saved,
        )
        return (out_rows, saved)

    def layer_backward(layer, d_out, saved):
        (
            inputs, norm_one, qkv_rows, log_totals, attended, middle, norm_two, gate_pair,
            expert_saved,
        ) = saved
        chosen = chosen_all[layer]
        all_rows, hidden, slope, back_rows, gates = expert_saved
        sent = jnp.pad(d_out.astype(half), ((0, padded_rows - token_rows), (0, 0)))
        combined, up_grad, down_grad = moe(
            True, 2 * layer + 1, rows=sent, slots=slot_tables[layer], up=up_all[layer],
            down=down_all[layer], saved=(gates, hidden, slope, back_rows, all_rows),
        )
        d_gate_rows = combined[padded_rows - 8 :, :token_rows]
        d_gate = jnp.stack([d_gate_rows[0] + d_gate_rows[1], d_gate_rows[2] + d_gate_rows[3]], axis=1)
        d_lead = (d_gate[:, 0] - d_gate[:, 1]) * gate_pair[:, 0] * gate_pair[:, 1]
        d_logits = (d_lead[:, None] * (chosen[:, 0] - chosen[:, 1])).astype(half)
        d_norm_two = combined[:token_rows] + jnp.einsum(
            "te,de->td", d_logits, router_all[layer], preferred_element_type=jnp.float32
        )
        normed_two, unit_two, inverse_two = norm_forward(
            middle, norm_all[layer][1], norm_all[layer][3]
        )
        d_middle_norm, gain_two, shift_two = norm_backward(
            d_norm_two, unit_two, inverse_two, norm_all[layer][1]
        )
        d_middle = d_out + d_middle_norm
        d_middle_half = d_middle.astype(half)
        d_attended = jnp.einsum(
            "te,de->td", d_middle_half, out_all[layer], preferred_element_type=jnp.float32
        ).astype(half)
        if local_images == 1:
            d_qkv = attend_call(qkv_rows, d_attended)
        else:
            d_qkv = attend_backward(qkv_rows, log_totals, d_attended, local_images)
        d_norm_one = jnp.einsum(
            "te,de->td", d_qkv, qkv_all[layer], preferred_element_type=jnp.float32
        )
        normed_one, unit_one, inverse_one = norm_forward(
            inputs, norm_all[layer][0], norm_all[layer][2]
        )
        d_input_norm, gain_one, shift_one = norm_backward(
            d_norm_one, unit_one, inverse_one, norm_all[layer][0]
        )
        d_input = d_middle + d_input_norm
        small = jnp.concatenate(
            [
                jnp.einsum("td,te->de", norm_two, d_logits, preferred_element_type=jnp.float32),
                jnp.stack([gain_one, gain_two, shift_one, shift_two], axis=1),
            ],
            axis=1,
        )
        return (d_input, (norm_one, d_qkv, attended, d_middle_half, small), (up_grad, down_grad))

    qkv_part, out_part = 3 * model_width // 2, model_width // 2
    small_width = round_up(expert_count + 4, 128)

    def dense_gradients(norm_one, d_qkv, attended, d_middle_half, small):
        own = jnp.concatenate([norm_one, d_qkv, attended, d_middle_half], axis=1)
        pair = jnp.concatenate([own, lax.ppermute(own, "section", swapped)], axis=0)
        d_qkv_part = lax.dynamic_slice_in_dim(
            pair, model_width + section_index * qkv_part, qkv_part, axis=1
        )
        d_out_part = lax.dynamic_slice_in_dim(
            pair, 5 * model_width + section_index * out_part, out_part, axis=1
        )
        qkv_grad = jnp.einsum(
            "td,te->de", pair[:, :model_width], d_qkv_part, preferred_element_type=jnp.float32
        )
        out_grad = jnp.einsum(
            "td,te->de", pair[:, 4 * model_width : 5 * model_width], d_out_part,
            preferred_element_type=jnp.float32,
        )
        small = jnp.pad(small, ((0, 0), (0, small_width - expert_count - 4)))
        packed_grad = jnp.concatenate(
            [qkv_grad.astype(half), out_grad.astype(half), small.astype(half)], axis=1
        )
        blocks = packed_grad.reshape(depth, groups, -1, packed_grad.shape[1]).transpose(1, 0, 2, 3)
        blocks = lax.all_to_all(blocks, "expert", split_axis=0, concat_axis=0, tiled=True)
        blocks = jnp.sum(blocks.astype(jnp.float32), axis=0).astype(half)
        blocks = lax.all_to_all(blocks, "dp", split_axis=0, concat_axis=0, tiled=True)
        return jnp.sum(blocks.astype(jnp.float32), axis=0)

    saved_list = []
    for layer in range(2):
        if layer > 0:
            stream = stream.astype(half).astype(jnp.float32)
        stream, saved = layer_forward(layer, stream)
        saved_list.append(saved)
    dense_operands = [None, None]
    expert_grads = [None, None]
    for layer in (1, 0):
        if layer < 1:
            cotangent = cotangent.astype(half).astype(jnp.float32)
        cotangent, operands, expert_grads[layer] = layer_backward(
            layer, cotangent, saved_list[layer]
        )
        dense_operands[layer] = operands

    def mine(first, second):
        return jnp.where(is_first, first, second)

    def both(first, second):
        own, away = mine(first, second), mine(second, first)
        return own, lax.ppermute(away, "section", swapped)

    if model_width % (16 * depth * groups) == 0:
        operands = [
            item[:4] + (jnp.pad(item[4], ((0, 0), (0, small_width - expert_count - 4))),)
            for item in dense_operands
        ]
        shard, other_up, other_down, other_rows = finish_call(
            9, depth, groups, operands[0], operands[1], *expert_grads[0], *expert_grads[1],
            cotangent, stream,
        )
        own_up = mine(expert_grads[0][0], expert_grads[1][0])
        own_down = mine(expert_grads[0][1], expert_grads[1][1])
        own_rows = mine(cotangent, stream)
        qkv_shard = shard[:, : 3 * model_width]
        out_shard = shard[:, 3 * model_width : 4 * model_width]
        small_shard = shard[:, 4 * model_width :]
    else:
        shards = [dense_gradients(*item) for item in dense_operands]
        own_shard, other_shard = both(shards[0], shards[1])
        low, high = mine(own_shard, other_shard), mine(other_shard, own_shard)
        qkv_shard = jnp.concatenate([low[:, :qkv_part], high[:, :qkv_part]], axis=1)
        out_shard = jnp.concatenate(
            [low[:, qkv_part : qkv_part + out_part], high[:, qkv_part : qkv_part + out_part]], axis=1
        )
        small_shard = (low + high)[:, qkv_part + out_part :]
        own_up, other_up = both(expert_grads[0][0], expert_grads[1][0])
        own_down, other_down = both(expert_grads[0][1], expert_grads[1][1])
        own_rows, other_rows = both(cotangent, stream)
    norm_shard = small_shard[:, expert_count : expert_count + 4].T

    def expert_grad(own, other):
        return (own.astype(jnp.float32) + other.astype(jnp.float32))[None]

    boundary_rows = jnp.stack([mine(own_rows, other_rows), mine(other_rows, own_rows)])
    boundary_out = boundary_rows.reshape(1, MB, local_images, boundary_in.shape[3], model_width)
    return (
        boundary_out,
        norm_shard[None, 0:2],
        norm_shard[None, 2:4],
        qkv_shard[None],
        out_shard[None],
        small_shard[None, :, :expert_count],
        expert_grad(own_up, other_up),
        expert_grad(own_down, other_down),
    )


def solution(mesh):
    in_specs = (
        P("section", None, ("dp", "expert"), None, None),
        P("section", None, ("dp", "expert"), None, None),
        P("section", None, ("dp", "expert"), None, None),
        P("section", None, ("dp", "expert")),
        P("section", None, ("dp", "expert")),
        P("section", ("dp", "expert"), None),
        P("section", ("dp", "expert"), None),
        P("section", ("dp", "expert"), None),
        P("section", "expert", None, "dp"),
        P("section", "expert", "dp", None),
    )
    out_specs = (
        P("section", None, ("dp", "expert"), None, None),
        P("section", None, ("dp", "expert")),
        P("section", None, ("dp", "expert")),
        P("section", ("dp", "expert"), None),
        P("section", ("dp", "expert"), None),
        P("section", ("dp", "expert"), None),
        P("section", "expert", None, "dp"),
        P("section", "expert", "dp", None),
    )
    return jax.shard_map(
        on_device, mesh=mesh, in_specs=in_specs, out_specs=out_specs, check_vma=False
    )
```

```python
import functools
import math

import jax
import jax.numpy as jnp
from jax import lax
from jax.experimental import pallas as pl
from jax.experimental.pallas import tpu as pltpu
from jax.sharding import PartitionSpec as P

HEADS = 12
HEAD_DIM = 64
EXP_DEV = 2
MB = 2


EPS = 1e-06
SQRT_HALF = 0.7071067811865476
INV_ROOT_TAU = 0.3989422804014327
MESH = pl.DeviceIdType.MESH


def round_up(value, unit):
    return (value + unit - 1) // unit * unit


def z_order(step, z, depth):
    if depth == 1:
        return z
    direction = 1 - 2 * (z // (depth // 2))
    return lax.rem(z + step * direction + depth, depth)


def f32_dot(a, b, dims):
    return lax.dot_general(a, b, (dims, ((), ())), preferred_element_type=jnp.float32)


def moe_kernel(backward, shape, *refs):
    depth, groups, cap_rows, token_rows, model_width, hidden_width = shape
    if backward:
        (
            rows_ref, slots_ref, gates_ref, up_source, down_source, back_source, slope_source,
            hidden_source, kept_source, out_ref, up_grad_ref, down_grad_ref,
            up_ref, down_ref, back_ref, slope_ref, hidden_ref, kept_ref,
            inbox, d_pre_ref, taken_ref, raw, sent_rows, sent_back, sent_home, home, back, d_gates, *sems,
        ) = refs
    else:
        (
            rows_ref, slots_ref, up_source, down_source,
            out_ref, gates_ref, taken_target, hidden_target, slope_target, back_target,
            up_ref, down_ref, taken_ref, hidden_ref, slope_ref, back,
            inbox, raw, sent_rows, sent_back, sent_home, home, *sems,
        ) = refs
    far_send, far_recv, go_send, go_recv, back_send, back_recv, home_send, home_recv = sems[:8]
    load_sem, store_sem = sems[8:]
    half = jnp.bfloat16
    section, z, column = (
        lax.axis_index("section"), lax.axis_index("dp"), lax.axis_index("expert")
    )
    slot_count = 2 * groups * cap_rows
    tail = token_rows - 16

    def z_peer(distance):
        return (section, lax.rem(z + distance, depth), column)

    def xy_peer(distance):
        return lax.rem(column + distance, groups)

    barrier = pltpu.get_barrier_semaphore()

    def greet_z(distance, carry):
        pl.semaphore_signal(barrier, inc=1, device_id=z_peer(distance), device_id_type=MESH)
        return carry

    def greet_xy(distance, carry):
        pl.semaphore_signal(
            barrier, inc=1, device_id=(section, z, xy_peer(distance)), device_id_type=MESH
        )
        return carry

    lax.fori_loop(1, depth, greet_z, 0)
    lax.fori_loop(1, groups, greet_xy, 0)
    pl.semaphore_wait(barrier, depth - 1 + groups - 1)

    def far_copy(direction, image):
        target = lax.rem(z + 2 * direction - 1 + depth, depth)
        source = raw.at[image]
        return pltpu.make_async_remote_copy(
            src_ref=source, dst_ref=raw.at[image],
            send_sem=far_send.at[direction, image], recv_sem=far_recv.at[image],
            device_id=(section, target, column), device_id_type=MESH,
        )

    def go_copy(image, source, target):
        return pltpu.make_async_remote_copy(
            src_ref=sent_rows.at[image, target], dst_ref=inbox.at[image, source],
            send_sem=go_send.at[image, target], recv_sem=go_recv.at[image, source],
            device_id=(section, z, target), device_id_type=MESH,
        )

    def back_copy(image, source, target):
        return pltpu.make_async_remote_copy(
            src_ref=sent_back.at[image, target], dst_ref=back.at[image, source],
            send_sem=back_send.at[image, target], recv_sem=back_recv.at[image, source],
            device_id=(section, z, target), device_id_type=MESH,
        )

    def home_copy(source, target):
        return pltpu.make_async_remote_copy(
            src_ref=sent_home.at[target], dst_ref=home.at[source],
            send_sem=home_send.at[target], recv_sem=home_recv.at[source],
            device_id=(section, target, column), device_id_type=MESH,
        )

    loads = [(up_source, up_ref), (down_source, down_ref)]
    if backward:
        loads += [
            (back_source, back_ref), (slope_source, slope_ref),
            (hidden_source, hidden_ref), (kept_source, kept_ref),
        ]
    loads = [
        pltpu.make_async_copy(source, target, load_sem.at[index])
        for index, (source, target) in enumerate(loads)
    ]

    def store_copies(image):
        pairs = [
            (taken_ref.at[0, image], taken_target.at[0, image]),
            (taken_ref.at[1, image], taken_target.at[1, image]),
            (hidden_ref.at[0, image], hidden_target.at[0, image]),
            (hidden_ref.at[1, image], hidden_target.at[1, image]),
            (slope_ref.at[0, image], slope_target.at[0, image]),
            (slope_ref.at[1, image], slope_target.at[1, image]),
            (back.at[image], back_target.at[image]),
        ]
        return [
            pltpu.make_async_copy(source, target, store_sem.at[index, image])
            for index, (source, target) in enumerate(pairs)
        ]

    raw[z] = rows_ref[...]

    @pl.when(z < depth - 1)
    def _():
        far_copy(1, z).start()

    @pl.when(z > 0)
    def _():
        far_copy(0, z).start()

    for copy in loads[2:3] + loads[:2] + loads[3:]:
        copy.start()

    def match(image):
        slots = slots_ref[image][:, :token_rows]
        index = lax.broadcasted_iota(jnp.int32, (slot_count, token_rows), 0)
        return index == slots[0:1], index == slots[1:2]

    def gate_table(image):
        first, second = match(image)
        gates = gates_ref[image]
        table = jnp.where(first, gates[0:1], 0.0) + jnp.where(second, gates[1:2], 0.0)
        return table.astype(half)

    def ones_table(image):
        first, second = match(image)
        return jnp.where(first | second, 1.0, 0.0).astype(half)

    def pass_on(step):
        low, high = z - step, z + step

        @pl.when(low >= 0)
        def _():
            far_copy(1, low).wait_recv()

            @pl.when(z < depth - 1)
            def _():
                far_copy(1, low).start()

        @pl.when(high < depth)
        def _():
            far_copy(0, high).wait_recv()

            @pl.when(z > 0)
            def _():
                far_copy(0, high).start()

    def dispatch(image):
        if not backward:
            gates_ref[image] = raw[image, tail:, :token_rows].astype(jnp.float32)[8:16]
        table = gate_table(image) if backward else ones_table(image)
        rows = raw[image]
        blocks = f32_dot(table, rows, ((1,), (0,))).astype(half)
        sent_rows[image] = blocks.reshape(groups, 2 * cap_rows, model_width)

        def send(distance, carry):
            go_copy(image, column, xy_peer(distance)).start()
            return carry

        lax.fori_loop(1, groups, send, 0)
        inbox[image, column] = sent_rows[image, column]
        if backward:

            @pl.when(image == z)
            def _():
                loads[2].wait()

            first, second = match(image)
            returned = back_ref[image].reshape(slot_count, model_width)
            ones = jnp.ones((8, model_width), half)
            row_index = lax.broadcasted_iota(jnp.int32, (8, token_rows), 0)
            packed = jnp.zeros((8, token_rows), jnp.float32)
            for choice, found in enumerate((first, second)):
                table = jnp.where(found, 1.0, 0.0).astype(half)
                selected = f32_dot(table, returned, ((0,), (0,)))
                product = (selected * rows.astype(jnp.float32)).astype(half)
                sums = f32_dot(ones, product, ((1,), (1,)))
                high = sums.astype(half).astype(jnp.float32)
                packed = jnp.where(row_index == 2 * choice, high, packed)
                packed = jnp.where(row_index == 2 * choice + 1, sums - high, packed)
            d_gates[image] = packed

    def experts(image):
        def arrive(distance, carry):
            go_copy(image, xy_peer(distance), column).wait_recv()
            return carry

        lax.fori_loop(1, groups, arrive, 0)
        block = inbox[image].astype(jnp.float32)
        results = []
        for expert in range(2):
            rows = block[:, expert * cap_rows : (expert + 1) * cap_rows]
            rows = rows.reshape(groups * cap_rows, model_width).astype(half)
            taken_ref[expert, image] = rows
            if backward:
                d_hidden = f32_dot(rows, down_ref[expert], ((1,), (1,)))
                d_pre = (d_hidden * slope_ref[expert, image].astype(jnp.float32)).astype(half)
                d_pre_ref[expert, image] = d_pre
                result = f32_dot(d_pre, up_ref[expert], ((1,), (1,)))
            else:
                pre = f32_dot(rows, up_ref[expert], ((1,), (0,)))
                share = 0.5 * (1.0 + lax.erf(pre * SQRT_HALF))
                slope = share + pre * jnp.exp(-0.5 * pre * pre) * INV_ROOT_TAU
                hidden = (pre * share).astype(half)
                hidden_ref[expert, image] = hidden
                slope_ref[expert, image] = slope.astype(half)
                result = f32_dot(hidden, down_ref[expert], ((1,), (0,)))
            results.append(result.reshape(groups, cap_rows, model_width))
        sent_back[image] = jnp.concatenate(results, axis=1).astype(half)

        def send(distance, carry):
            back_copy(image, column, xy_peer(distance)).start()
            return carry

        lax.fori_loop(1, groups, send, 0)
        back[image, column] = sent_back[image, column]
        if not backward:
            for copy in store_copies(image)[:6]:
                copy.start()

    def combine(image):
        def arrive(distance, carry):
            back_copy(image, xy_peer(distance), column).wait_recv()
            return carry

        lax.fori_loop(1, groups, arrive, 0)
        if not backward:
            store_copies(image)[6].start()
        table = ones_table(image) if backward else gate_table(image)
        total = f32_dot(table, back[image].reshape(slot_count, model_width), ((0,), (0,)))
        if backward:
            extra = jnp.concatenate(
                [jnp.zeros((8, token_rows), jnp.float32), d_gates[image]], axis=0
            )

        @pl.when(image == z)
        def _():
            out_ref[...] = total
            if backward:
                out_ref[tail:, :token_rows] = total[tail:, :token_rows] + extra

        @pl.when(image != z)
        def _():
            sent_home[image] = total.astype(half)
            if backward:
                sent_home[image, tail:, :token_rows] = (
                    total[tail:, :token_rows] + extra
                ).astype(half)
            home_copy(z, image).start()

    def stage(step, carry):
        @pl.when(jnp.logical_and(step >= 1, step < depth))
        def _():
            pass_on(step)

        @pl.when(step < depth)
        def _():
            dispatch(z_order(step, z, depth))

        @pl.when(step == 2)
        def _():
            loads[0].wait()
            loads[1].wait()
            if backward:
                loads[3].wait()

        @pl.when(jnp.logical_and(step >= 2, step < depth + 2))
        def _():
            experts(z_order(lax.rem(step - 1, depth), z, depth))

        @pl.when(step >= 3)
        def _():
            combine(z_order(lax.rem(step - 2, depth), z, depth))

        return carry

    lax.fori_loop(0, depth + 3, stage, 0)

    if backward:
        loads[4].wait()
        loads[5].wait()

        def expert_gradients(expert, carry):
            kept = kept_ref[expert].reshape(depth * groups * cap_rows, model_width)
            d_pre = d_pre_ref[expert].reshape(depth * groups * cap_rows, hidden_width)
            up_grad_ref[expert] = f32_dot(kept, d_pre, ((0,), (0,))).astype(half)
            hidden = hidden_ref[expert].reshape(depth * groups * cap_rows, hidden_width)
            grads = taken_ref[expert].reshape(depth * groups * cap_rows, model_width)
            down_grad_ref[expert] = f32_dot(hidden, grads, ((0,), (0,))).astype(half)
            return carry

        lax.fori_loop(0, 2, expert_gradients, 0)

    def finish_home(distance, carry):
        source = lax.rem(z + distance, depth)
        home_copy(source, z).wait_recv()
        out_ref[...] += home[source].astype(jnp.float32)
        return carry

    lax.fori_loop(1, depth, finish_home, 0)

    def drain_home(distance, carry):
        home_copy(z, lax.rem(z + distance, depth)).wait_send()
        return carry

    lax.fori_loop(1, depth, drain_home, 0)

    def drain_image(image, carry):
        if not backward:
            for copy in store_copies(image):
                copy.wait()

        @pl.when(jnp.logical_and(z < depth - 1, image <= z))
        def _():
            far_copy(1, image).wait_send()

        @pl.when(jnp.logical_and(z > 0, image >= z))
        def _():
            far_copy(0, image).wait_send()

        def drain(distance, inner):
            go_copy(image, column, xy_peer(distance)).wait_send()
            back_copy(image, column, xy_peer(distance)).wait_send()
            return inner

        lax.fori_loop(1, groups, drain, 0)
        return carry

    lax.fori_loop(0, depth, drain_image, 0)


def moe_call(backward, call_id, depth, groups, cap_rows, rows, slots, up, down, saved=()):
    token_rows, model_width = rows.shape
    hidden_width = up.shape[2]
    half = jnp.bfloat16
    shape = (depth, groups, cap_rows, token_rows, model_width, hidden_width)
    taken = jax.ShapeDtypeStruct((2, depth, groups * cap_rows, model_width), half)
    hidden = jax.ShapeDtypeStruct((2, depth, groups * cap_rows, hidden_width), half)
    back = jax.ShapeDtypeStruct((depth, groups, 2 * cap_rows, model_width), half)
    out = jax.ShapeDtypeStruct((token_rows, model_width), jnp.float32)
    vmem, anywhere = pl.BlockSpec(memory_space=pltpu.VMEM), pl.BlockSpec(memory_space=pl.ANY)
    if backward:
        operands = (rows, slots, saved[0], up, down) + saved[1:]
        in_specs = [vmem] * 3 + [anywhere] * 6
        out_shape = (
            out, jax.ShapeDtypeStruct(up.shape, half), jax.ShapeDtypeStruct(down.shape, half)
        )
        out_specs = [vmem] * 3
        buffers = (up, down, back, hidden, hidden, taken, back, hidden, taken)
    else:
        operands = (rows, slots, up, down)
        in_specs = [vmem] * 2 + [anywhere] * 2
        gates = jax.ShapeDtypeStruct((depth, 8, token_rows), jnp.float32)
        out_shape = (out, gates, taken, hidden, hidden, back)
        out_specs = [vmem] * 2 + [anywhere] * 4
        buffers = (up, down, taken, hidden, hidden, back, back)
    scratch = [pltpu.VMEM(item.shape, half) for item in buffers]
    scratch += [
        pltpu.VMEM((depth, token_rows, model_width), half),
        pltpu.VMEM(back.shape, half),
        pltpu.VMEM(back.shape, half),
        pltpu.VMEM((depth, token_rows, model_width), half),
        pltpu.VMEM((depth, token_rows, model_width), half),
    ]
    if backward:
        scratch += [
            pltpu.VMEM(back.shape, half),
            pltpu.VMEM((depth, 8, token_rows), jnp.float32),
        ]
    scratch += [
        pltpu.SemaphoreType.DMA((2, depth)),
        pltpu.SemaphoreType.DMA((depth,)),
        pltpu.SemaphoreType.DMA((depth, groups)),
        pltpu.SemaphoreType.DMA((depth, groups)),
        pltpu.SemaphoreType.DMA((depth, groups)),
        pltpu.SemaphoreType.DMA((depth, groups)),
        pltpu.SemaphoreType.DMA((depth,)),
        pltpu.SemaphoreType.DMA((depth,)),
        pltpu.SemaphoreType.DMA((6,)),
        pltpu.SemaphoreType.DMA((7, depth)),
    ]
    return pl.pallas_call(
        functools.partial(moe_kernel, backward, shape),
        out_shape=out_shape,
        in_specs=in_specs,
        out_specs=out_specs,
        scratch_shapes=scratch,
        compiler_params=pltpu.CompilerParams(
            collective_id=call_id, has_side_effects=True, vmem_limit_bytes=50 * 2**20
        ),
        name="moe_backward" if backward else "moe_forward",
    )(*operands)

def start_kernel(shape, *refs):
    depth, groups = shape
    (
        packed_ref, up_ref, down_ref, edge_ref, table_ref,
        dense_first, dense_second, up_first, up_second, down_first, down_second,
        rows_ref, cotangent_ref, table_first, table_second,
        shard_send, shard_recv, core_send, core_recv, table_send, table_recv, own_sem,
    ) = refs
    section, z, column = (
        lax.axis_index("section"), lax.axis_index("dp"), lax.axis_index("expert")
    )
    other = (1 - section, z, column)
    is_first = section == 0

    def z_peer(distance):
        return lax.rem(z + distance, depth)

    def xy_peer(distance):
        return lax.rem(column + distance, groups)

    barrier = pltpu.get_barrier_semaphore()

    def greet_z(distance, carry):
        pl.semaphore_signal(
            barrier, inc=1, device_id=(section, z_peer(distance), column), device_id_type=MESH
        )
        return carry

    def greet_xy(distance, carry):
        pl.semaphore_signal(
            barrier, inc=1, device_id=(section, z, xy_peer(distance)), device_id_type=MESH
        )
        return carry

    pl.semaphore_signal(barrier, inc=1, device_id=other, device_id_type=MESH)
    lax.fori_loop(1, depth, greet_z, 0)
    lax.fori_loop(1, groups, greet_xy, 0)
    pl.semaphore_wait(barrier, depth + groups - 1)

    def remote(source, target, send, recv, device):
        return pltpu.make_async_remote_copy(
            src_ref=source, dst_ref=target, send_sem=send, recv_sem=recv,
            device_id=device, device_id_type=MESH,
        )

    def run(first):
        own, away = (dense_first, dense_second) if first else (dense_second, dense_first)

        def shard_copy(kind, layer, plane, lane, device):
            return remote(
                layer.at[plane, lane], layer.at[plane, lane],
                shard_send.at[kind, plane, lane],
                shard_recv.at[0, plane, lane],
                device,
            )

        def z_copy(direction, plane):
            device = (section, lax.rem(z + 2 * direction - 1 + depth, depth), column)
            return shard_copy(direction, own, plane, column, device)

        def core_copy(layer, plane, lane):
            return remote(
                layer.at[plane, lane], layer.at[plane, lane],
                shard_send.at[2, plane, lane], shard_recv.at[1, plane, lane], other,
            )

        def xy_copy(plane, source, target):
            return shard_copy(3 + target, own, plane, source, (section, z, target))

        def pass_copy(plane, source, target):
            return shard_copy(3 + groups, own, plane, source, (section, z, target))

        def swap(index, source, target):
            return remote(source, target, core_send.at[index], core_recv.at[index], other)

        def local(index, source, target):
            return pltpu.make_async_copy(source, target, own_sem.at[index])

        square = groups == 4
        beside = column + 1 - 2 * lax.rem(column, 2)
        above = lax.rem(column + 2, groups)
        across = groups - 1 - column
        direct = 3 if square else groups

        def near(distance):
            if square:
                return beside + (distance - 1) * (above - beside)
            return xy_peer(distance)

        def spread(plane):
            core_copy(own, plane, column).start()

            def send(distance, carry):
                xy_copy(plane, column, near(distance)).start()
                return carry

            lax.fori_loop(1, direct, send, 0)

        def take(plane):
            def arrive(distance, carry):
                lane = near(distance)
                xy_copy(plane, lane, column).wait_recv()
                core_copy(own, plane, lane).start()
                if square:

                    @pl.when(lax.rem(plane, 2) == distance - 1)
                    def _():
                        pass_copy(plane, lane, near(3 - distance)).start()

                return carry

            lax.fori_loop(1, direct, arrive, 0)

        own_shard = local(0, packed_ref, own.at[z, column])

        def first_copies():
            remote_ones = [
                swap(0, edge_ref.at[1], rows_ref),
                swap(1, table_ref.at[1], table_first.at[z]),
                swap(2, up_ref, up_first),
                swap(3, down_ref, down_first),
            ]
            local_ones = [
                local(1, edge_ref.at[0], rows_ref),
                local(2, table_ref.at[0], table_first.at[z]),
                local(3, up_ref, up_first),
                local(4, down_ref, down_first),
            ]
            return remote_ones, local_ones

        def second_copies():
            remote_ones = [
                swap(0, edge_ref.at[0], cotangent_ref),
                swap(1, table_ref.at[0], table_second.at[z]),
                swap(2, up_ref, up_second),
                swap(3, down_ref, down_second),
            ]
            local_ones = [
                local(1, edge_ref.at[1], cotangent_ref),
                local(2, table_ref.at[1], table_second.at[z]),
                local(3, up_ref, up_second),
                local(4, down_ref, down_second),
            ]
            return remote_ones, local_ones

        own_shard.start()
        own_shard.wait()

        @pl.when(z < depth - 1)
        def _():
            z_copy(1, z).start()

        @pl.when(z > 0)
        def _():
            z_copy(0, z).start()

        spread(z)

        first_remote, first_local = first_copies()
        second_remote, second_local = second_copies()
        out_going, in_coming = (
            (first_remote, second_remote) if first else (second_remote, first_remote)
        )
        local_ones = first_local if first else second_local
        for copy in out_going[:2] + local_ones + out_going[2:]:
            copy.start()

        def step(distance, carry):
            low, high = z - distance, z + distance

            @pl.when(low >= 0)
            def _():
                z_copy(1, low).wait_recv()

                @pl.when(z < depth - 1)
                def _():
                    z_copy(1, low).start()

                spread(low)

            @pl.when(high < depth)
            def _():
                z_copy(0, high).wait_recv()

                @pl.when(z > 0)
                def _():
                    z_copy(0, high).start()

                spread(high)

            take(z_order(distance - 1, z, depth))
            return carry

        lax.fori_loop(1, depth, step, 0)
        take(z_order(depth - 1, z, depth))

        def table_copies(source, target):
            pairs = []
            for layer, table in enumerate((table_first, table_second)):
                pairs.append(
                    remote(
                        table.at[source], table.at[source], table_send.at[layer, target],
                        table_recv.at[layer, source], (section, target, column),
                    )
                )
            return pairs

        local_ones[1].wait()
        in_coming[1].wait_recv()

        def send_tables(distance, carry):
            for copy in table_copies(z, z_peer(distance)):
                copy.start()
            return carry

        lax.fori_loop(1, depth, send_tables, 0)

        if square:

            def last_arrival(index, carry):
                plane = z_order(index, z, depth)
                pass_copy(plane, across, column).wait_recv()
                core_copy(own, plane, across).start()
                return carry

            lax.fori_loop(0, depth, last_arrival, 0)

        def drain(plane, carry):
            @pl.when(jnp.logical_and(z < depth - 1, plane <= z))
            def _():
                z_copy(1, plane).wait_send()

            @pl.when(jnp.logical_and(z > 0, plane >= z))
            def _():
                z_copy(0, plane).wait_send()

            def drain_core(lane, inner):
                core_copy(away, plane, lane).wait_recv()
                core_copy(own, plane, lane).wait_send()
                return inner

            def drain_xy(distance, inner):
                xy_copy(plane, column, near(distance)).wait_send()
                if square:

                    @pl.when(lax.rem(plane, 2) == distance - 1)
                    def _():
                        pass_copy(plane, near(distance), near(3 - distance)).wait_send()

                return inner

            lax.fori_loop(0, groups, drain_core, 0)
            return lax.fori_loop(1, direct, drain_xy, carry)

        lax.fori_loop(0, depth, drain, 0)

        for index in (0, 2, 3):
            in_coming[index].wait_recv()
        for copy in out_going:
            copy.wait_send()
        for copy in local_ones[:1] + local_ones[2:]:
            copy.wait()

        def finish_tables(distance, carry):
            for copy in table_copies(z_peer(distance), z):
                copy.wait_recv()
            for copy in table_copies(z, z_peer(distance)):
                copy.wait_send()
            return carry

        lax.fori_loop(1, depth, finish_tables, 0)

    pl.when(is_first)(functools.partial(run, True))
    pl.when(jnp.logical_not(is_first))(functools.partial(run, False))


def start_call(call_id, depth, groups, packed, up, down, edge, table):
    rows, width = packed.shape
    half = jnp.bfloat16
    out_shape = (
        jax.ShapeDtypeStruct((depth, groups, rows, width), half),
        jax.ShapeDtypeStruct((depth, groups, rows, width), half),
        jax.ShapeDtypeStruct(up.shape, half),
        jax.ShapeDtypeStruct(up.shape, half),
        jax.ShapeDtypeStruct(down.shape, half),
        jax.ShapeDtypeStruct(down.shape, half),
        jax.ShapeDtypeStruct(edge.shape[1:], jnp.float32),
        jax.ShapeDtypeStruct(edge.shape[1:], jnp.float32),
        jax.ShapeDtypeStruct((depth,) + table.shape[1:], jnp.int32),
        jax.ShapeDtypeStruct((depth,) + table.shape[1:], jnp.int32),
    )
    return pl.pallas_call(
        functools.partial(start_kernel, (depth, groups)),
        out_shape=out_shape,
        in_specs=[pl.BlockSpec(memory_space=pltpu.VMEM)] * 5,
        out_specs=[pl.BlockSpec(memory_space=pl.ANY)] * len(out_shape),
        scratch_shapes=[
            pltpu.SemaphoreType.DMA((4 + groups, depth, groups)),
            pltpu.SemaphoreType.DMA((2, depth, groups)),
            pltpu.SemaphoreType.DMA((4,)),
            pltpu.SemaphoreType.DMA((4,)),
            pltpu.SemaphoreType.DMA((2, depth)),
            pltpu.SemaphoreType.DMA((2, depth)),
            pltpu.SemaphoreType.DMA((5,)),
        ],
        compiler_params=pltpu.CompilerParams(
            collective_id=call_id, has_side_effects=True, vmem_limit_bytes=40 * 2**20
        ),
        name="start_exchange",
    )(packed, up, down, edge, table)

def finish_kernel(shape, *refs):
    depth, groups, token_rows, padded_rows, model_width = shape
    first_refs, second_refs, rest = refs[0:5], refs[5:10], refs[10:]
    (
        up_first, down_first, up_second, down_second, rows_first, rows_second,
        shard_ref, up_ref, down_ref, rows_ref,
        pair, away, small_pair, table, inbox, sent_home, home,
        core_send, core_recv, go_send, go_recv, home_send, home_recv,
    ) = rest
    half = jnp.bfloat16
    section, z, column = (
        lax.axis_index("section"), lax.axis_index("dp"), lax.axis_index("expert")
    )
    other = (1 - section, z, column)
    is_first = section == 0
    shard_rows = table.shape[1]

    def z_peer(distance):
        return lax.rem(z + distance, depth)

    def xy_peer(distance):
        return lax.rem(column + distance, groups)

    barrier = pltpu.get_barrier_semaphore()

    def greet_z(distance, carry):
        pl.semaphore_signal(
            barrier, inc=1, device_id=(section, z_peer(distance), column), device_id_type=MESH
        )
        return carry

    def greet_xy(distance, carry):
        pl.semaphore_signal(
            barrier, inc=1, device_id=(section, z, xy_peer(distance)), device_id_type=MESH
        )
        return carry

    pl.semaphore_signal(barrier, inc=1, device_id=other, device_id_type=MESH)
    lax.fori_loop(1, depth, greet_z, 0)
    lax.fori_loop(1, groups, greet_xy, 0)
    pl.semaphore_wait(barrier, depth + groups - 1)

    def swap(index, source, target):
        return pltpu.make_async_remote_copy(
            src_ref=source, dst_ref=target, send_sem=core_send.at[index],
            recv_sem=core_recv.at[index], device_id=other, device_id_type=MESH,
        )

    def pack(target, operands):
        target[padded_rows - 16 :, :] = jnp.zeros((16, target.shape[1]), half)
        offset = 0
        for operand in operands:
            width = operand.shape[1]
            target[:token_rows, offset : offset + width] = operand[...]
            offset += width

    def side_copies(first):
        if first:
            sources = (second_refs[4], up_second, down_second, rows_second)
        else:
            sources = (first_refs[4], up_first, down_first, rows_first)
        targets = (small_pair.at[1], up_ref, down_ref, rows_ref)
        return [
            swap(1 + index, source, target)
            for index, (source, target) in enumerate(zip(sources, targets))
        ]

    operand_copy = swap(0, away, pair.at[1])
    for first in (True, False):

        @pl.when(is_first if first else jnp.logical_not(is_first))
        def _():
            mine, others = (first_refs, second_refs) if first else (second_refs, first_refs)
            pack(away, others[:4])
            operand_copy.start()
            for copy in side_copies(first):
                copy.start()
            pack(pair.at[0], mine[:4])
            small_pair[0] = mine[4][...]

    operand_copy.wait_recv()
    rows = 2 * padded_rows

    def product(left, right, target):
        a = pair[:, :, left : left + model_width].reshape(rows, model_width)
        b = pair[:, :, right : right + model_width].reshape(rows, model_width)
        value = f32_dot(a, b, ((0,), (0,))).astype(half)
        table[:, :, target : target + model_width] = value.reshape(
            depth * groups, shard_rows, model_width
        )

    for index in range(3):
        product(0, (1 + index) * model_width, index * model_width)
    product(4 * model_width, 5 * model_width, 3 * model_width)
    for copy in side_copies(True)[:1]:
        copy.wait_recv()
    small = (small_pair[0] + small_pair[1]).astype(half)
    table[:, :, 4 * model_width :] = small.reshape(depth * groups, shard_rows, small.shape[1])

    def go_copy(plane, source, target):
        return pltpu.make_async_remote_copy(
            src_ref=table.at[plane * groups + target], dst_ref=inbox.at[plane, source],
            send_sem=go_send.at[plane, target], recv_sem=go_recv.at[plane, source],
            device_id=(section, z, target), device_id_type=MESH,
        )

    def home_copy(source, target):
        return pltpu.make_async_remote_copy(
            src_ref=sent_home.at[target], dst_ref=home.at[source],
            send_sem=home_send.at[target], recv_sem=home_recv.at[source],
            device_id=(section, target, column), device_id_type=MESH,
        )

    def send_plane(step, carry):
        plane = z_peer(step)

        def send(distance, inner):
            go_copy(plane, column, xy_peer(distance)).start()
            return inner

        return lax.fori_loop(1, groups, send, carry)

    lax.fori_loop(1, depth + 1, send_plane, 0)

    def sum_plane(step, carry):
        plane = z_peer(step)

        def arrive(distance, total):
            lane = xy_peer(distance)
            go_copy(plane, lane, column).wait_recv()
            return total + inbox[plane, lane].astype(jnp.float32)

        own = table[plane * groups + column].astype(jnp.float32)
        total = lax.fori_loop(1, groups, arrive, own)

        @pl.when(plane == z)
        def _():
            shard_ref[...] = total

        @pl.when(plane != z)
        def _():
            sent_home[plane] = total.astype(half)
            home_copy(z, plane).start()

        return carry

    lax.fori_loop(1, depth + 1, sum_plane, 0)

    def finish_home(distance, carry):
        source = z_peer(distance)
        home_copy(source, z).wait_recv()
        shard_ref[...] += home[source].astype(jnp.float32)
        home_copy(z, source).wait_send()
        return carry

    lax.fori_loop(1, depth, finish_home, 0)

    def drain_plane(plane, carry):
        def drain(distance, inner):
            go_copy(plane, column, xy_peer(distance)).wait_send()
            return inner

        return lax.fori_loop(1, groups, drain, carry)

    lax.fori_loop(0, depth, drain_plane, 0)
    operand_copy.wait_send()
    for index, copy in enumerate(side_copies(True)):
        copy.wait_send()
        if index > 0:
            copy.wait_recv()


def finish_call(call_id, depth, groups, first, second, up_first, down_first, up_second, down_second,
                rows_first, rows_second):
    token_rows, model_width = first[0].shape
    padded_rows = round_up(token_rows, 16)
    small_width = first[4].shape[1]
    width = 4 * model_width + small_width
    shard_rows = model_width // (depth * groups)
    half = jnp.bfloat16
    out_shape = (
        jax.ShapeDtypeStruct((shard_rows, width), jnp.float32),
        jax.ShapeDtypeStruct(up_first.shape, half),
        jax.ShapeDtypeStruct(down_first.shape, half),
        jax.ShapeDtypeStruct(rows_first.shape, jnp.float32),
    )
    home = pltpu.VMEM((depth, shard_rows, width), half)
    return pl.pallas_call(
        functools.partial(
            finish_kernel, (depth, groups, token_rows, padded_rows, model_width)
        ),
        out_shape=out_shape,
        in_specs=[pl.BlockSpec(memory_space=pltpu.VMEM)] * 16,
        out_specs=[pl.BlockSpec(memory_space=pltpu.VMEM)] + [pl.BlockSpec(memory_space=pl.ANY)] * 3,
        scratch_shapes=[
            pltpu.VMEM((2, padded_rows, 6 * model_width), half),
            pltpu.VMEM((padded_rows, 6 * model_width), half),
            pltpu.VMEM((2, model_width, small_width), jnp.float32),
            pltpu.VMEM((depth * groups, shard_rows, width), half),
            pltpu.VMEM((depth, groups, shard_rows, width), half),
            home,
            home,
            pltpu.SemaphoreType.DMA((5,)),
            pltpu.SemaphoreType.DMA((5,)),
            pltpu.SemaphoreType.DMA((depth, groups)),
            pltpu.SemaphoreType.DMA((depth, groups)),
            pltpu.SemaphoreType.DMA((depth,)),
            pltpu.SemaphoreType.DMA((depth,)),
        ],
        compiler_params=pltpu.CompilerParams(
            collective_id=call_id, has_side_effects=True, vmem_limit_bytes=50 * 2**20
        ),
        name="finish_exchange",
    )(*first, *second, up_first, down_first, up_second, down_second, rows_first, rows_second)

def head_mask(head):
    lanes = lax.broadcasted_iota(jnp.int32, (1, 2 * HEAD_DIM), 1)
    return jnp.where(lanes // HEAD_DIM == head, 1.0, 0.0).astype(jnp.bfloat16)


def attend_kernel(width, qkv_ref, out_ref):
    scale_factor = 1.0 / math.sqrt(HEAD_DIM)
    pair_width = 2 * HEAD_DIM

    def pair(index, carry):
        def columns(part):
            start = pl.multiple_of(part * width + index * pair_width, pair_width)
            return qkv_ref[:, pl.ds(start, pair_width)]

        queries, keys, values = columns(0), columns(1), columns(2)
        total = jnp.zeros(queries.shape, jnp.float32)
        for head in range(2):
            mask = head_mask(head)
            scores = f32_dot(queries * mask, keys, ((1,), (1,))) * scale_factor
            log_totals = jnp.log(jnp.sum(jnp.exp(scores), axis=1, keepdims=True))
            probs = jnp.exp(scores - log_totals).astype(jnp.bfloat16)
            total = total + f32_dot(probs, values * mask, ((1,), (0,)))
        start = pl.multiple_of(index * pair_width, pair_width)
        out_ref[:, pl.ds(start, pair_width)] = total.astype(jnp.bfloat16)
        return carry

    lax.fori_loop(0, width // pair_width, pair, 0)


def attend_backward_kernel(width, qkv_ref, d_out_ref, d_qkv_ref):
    scale_factor = 1.0 / math.sqrt(HEAD_DIM)
    pair_width = 2 * HEAD_DIM
    half = jnp.bfloat16

    def pair(index, carry):
        def place(part):
            return pl.ds(pl.multiple_of(part * width + index * pair_width, pair_width), pair_width)

        queries, keys, values = (qkv_ref[:, place(part)] for part in range(3))
        d_out = d_out_ref[:, place(0)]
        d_queries = jnp.zeros(queries.shape, jnp.float32)
        d_keys, d_values = d_queries, d_queries
        for head in range(2):
            mask = head_mask(head)
            own_queries, own_d_out = queries * mask, d_out * mask
            scores = f32_dot(keys, own_queries, ((1,), (1,))) * scale_factor
            log_totals = jnp.log(jnp.sum(jnp.exp(scores), axis=0, keepdims=True))
            probs = jnp.exp(scores - log_totals)
            d_probs = f32_dot(values, own_d_out, ((1,), (1,)))
            row_dot = jnp.sum(probs * d_probs, axis=0, keepdims=True)
            d_scores = (probs * (d_probs - row_dot) * scale_factor).astype(half)
            d_values = d_values + f32_dot(probs.astype(half), own_d_out, ((1,), (0,)))
            d_keys = d_keys + f32_dot(d_scores, own_queries, ((1,), (0,)))
            d_queries = d_queries + f32_dot(d_scores, keys * mask, ((0,), (0,)))
        for part, value in enumerate((d_queries, d_keys, d_values)):
            d_qkv_ref[:, place(part)] = value.astype(half)
        return carry

    lax.fori_loop(0, width // pair_width, pair, 0)


def attend_call(qkv_rows, d_attended=None):
    rows, width = qkv_rows.shape
    width = width // 3
    operands = (qkv_rows,) if d_attended is None else (qkv_rows, d_attended)
    kernel = attend_kernel if d_attended is None else attend_backward_kernel
    out_width = width if d_attended is None else 3 * width
    return pl.pallas_call(
        functools.partial(kernel, width),
        out_shape=jax.ShapeDtypeStruct((rows, out_width), jnp.bfloat16),
        in_specs=[pl.BlockSpec(memory_space=pltpu.VMEM)] * len(operands),
        out_specs=pl.BlockSpec(memory_space=pltpu.VMEM),
        compiler_params=pltpu.CompilerParams(vmem_limit_bytes=24 * 2**20),
        name="attend" if d_attended is None else "attend_backward",
    )(*operands)


def norm_forward(values, gain_row, shift_row):
    centred = values - jnp.mean(values, axis=-1, keepdims=True)
    variance = jnp.mean(centred * centred, axis=-1, keepdims=True)
    inverse = lax.rsqrt(variance + EPS)
    unit_rows = centred * inverse
    return (unit_rows * gain_row + shift_row, unit_rows, inverse)


def norm_backward(d_normed, unit_rows, inverse, gain_row):
    d_gain = jnp.sum(d_normed * unit_rows, axis=0)
    d_shift = jnp.sum(d_normed, axis=0)
    scaled = d_normed * gain_row
    d_values = inverse * (
        scaled
        - jnp.mean(scaled, axis=-1, keepdims=True)
        - unit_rows * jnp.mean(scaled * unit_rows, axis=-1, keepdims=True)
    )
    return (d_values, d_gain, d_shift)


def gelu_slope(pre_act):
    return (
        0.5 * (1.0 + lax.erf(pre_act * SQRT_HALF))
        + pre_act * jnp.exp(-0.5 * pre_act * pre_act) * INV_ROOT_TAU
    )


def split_heads(qkv_rows, image_count):
    feature_count = qkv_rows.shape[1] // 3
    return [
        qkv_rows[:, part_index * feature_count : (part_index + 1) * feature_count].reshape(
            image_count, -1, HEADS, HEAD_DIM
        )
        for part_index in range(3)
    ]


def attend_forward(qkv_rows, image_count):
    queries, key_rows, value_rows = split_heads(qkv_rows, image_count)
    scale_factor = 1.0 / math.sqrt(HEAD_DIM)
    scores = (
        jnp.einsum("bqhd,bkhd->bhqk", queries, key_rows, preferred_element_type=jnp.float32)
        * scale_factor
    )
    log_totals = jnp.log(jnp.sum(jnp.exp(scores), axis=-1))
    probs_half = jnp.exp(scores - log_totals[..., None]).astype(jnp.bfloat16)
    attended = jnp.einsum(
        "bhqk,bkhd->bqhd", probs_half, value_rows, preferred_element_type=jnp.float32
    )
    return (attended.astype(jnp.bfloat16).reshape(-1, HEADS * HEAD_DIM), log_totals)


def attend_backward(qkv_rows, log_totals, d_attended, image_count):
    queries, key_rows, value_rows = split_heads(qkv_rows, image_count)
    scale_factor = 1.0 / math.sqrt(HEAD_DIM)
    scores = (
        jnp.einsum("bqhd,bkhd->bhqk", queries, key_rows, preferred_element_type=jnp.float32)
        * scale_factor
    )
    probs = jnp.exp(scores - log_totals[..., None])
    probs_half = probs.astype(jnp.bfloat16)
    d_heads = d_attended.reshape(image_count, -1, HEADS, HEAD_DIM)
    d_values = jnp.einsum(
        "bhqk,bqhd->bkhd", probs_half, d_heads, preferred_element_type=jnp.float32
    )
    d_probs = jnp.einsum("bqhd,bkhd->bhqk", d_heads, value_rows, preferred_element_type=jnp.float32)
    row_dot = jnp.sum(probs * d_probs, axis=-1, keepdims=True)
    d_scores = (probs * (d_probs - row_dot) * scale_factor).astype(jnp.bfloat16)
    d_queries = jnp.einsum(
        "bhqk,bkhd->bqhd", d_scores, key_rows, preferred_element_type=jnp.float32
    )
    d_keys = jnp.einsum("bhqk,bqhd->bkhd", d_scores, queries, preferred_element_type=jnp.float32)
    feature_count = HEADS * HEAD_DIM
    joined = jnp.concatenate(
        [
            d_queries.reshape(-1, feature_count),
            d_keys.reshape(-1, feature_count),
            d_values.reshape(-1, feature_count),
        ],
        axis=1,
    )
    return joined.astype(jnp.bfloat16)


def on_device(
    boundary_in, routes, capacity_slots, ln_gain, ln_bias, w_qkv, w_out, w_router, w_up, w_down
):
    section_index = lax.axis_index("section")
    is_first = section_index == 0
    depth = lax.axis_size("dp")
    groups = lax.axis_size("expert")
    expert_count = EXP_DEV * groups
    local_images = boundary_in.shape[2]
    token_rows = local_images * boundary_in.shape[3]
    model_width = boundary_in.shape[4]
    capacity = 26 * token_rows // (16 * expert_count)
    cap_rows = round_up(capacity, 8)
    padded_rows = round_up(token_rows + 8, 16)
    half = jnp.bfloat16
    swapped = [(0, 1), (1, 0)]

    edge = boundary_in[0].reshape(MB, token_rows, model_width)
    route_rows = routes[0].reshape(MB, token_rows, 2)
    slot_rows = capacity_slots[0].reshape(MB, token_rows, 2)
    slot_index = jnp.where(slot_rows < capacity, route_rows * cap_rows + slot_rows, -1)
    table = jnp.concatenate([slot_index, route_rows], axis=2).transpose(0, 2, 1)
    table = jnp.pad(
        table, ((0, 0), (0, 4), (0, padded_rows - token_rows)), constant_values=-1
    )

    norm_columns = jnp.concatenate([ln_gain, ln_bias], axis=1).transpose(0, 2, 1)
    used = 4 * model_width + expert_count + 4
    padding = -used % 128
    packed = jnp.concatenate([w_qkv, w_out, w_router, norm_columns], axis=2)
    packed = jnp.pad(packed, ((0, 0), (0, 0), (0, padding)))
    (
        dense_first, dense_second, up_first, up_second, down_first, down_second,
        stream, cotangent, table_first, table_second,
    ) = start_call(8, depth, groups, packed[0], w_up[0], w_down[0], edge, table)
    qkv_all, out_all, router_all, norm_all = [], [], [], []

    def add_dense(item):
        qkv_all.append(item[:, : 3 * model_width])
        out_all.append(item[:, 3 * model_width : 4 * model_width])
        router_all.append(item[:, 4 * model_width : used - 4])
        norm_all.append(item[:, used - 4 : used].T.astype(jnp.float32))

    add_dense(dense_first.reshape(model_width, used + padding))
    add_dense(dense_second.reshape(model_width, used + padding))
    up_all = (up_first, up_second)
    down_all = (down_first, down_second)
    slot_tables = (table_first, table_second)
    z_index = lax.axis_index("dp")
    chosen_all = [
        (
            lax.dynamic_index_in_dim(item, z_index, 0, False)[2:4, :token_rows].T[..., None]
            == jnp.arange(expert_count, dtype=jnp.int32)
        ).astype(jnp.float32)
        for item in slot_tables
    ]
    moe = functools.partial(moe_call, depth=depth, groups=groups, cap_rows=cap_rows)

    def layer_forward(layer, inputs):
        chosen = chosen_all[layer]
        normed_one, unit_one, inverse_one = norm_forward(
            inputs, norm_all[layer][0], norm_all[layer][2]
        )
        norm_one = normed_one.astype(half)
        qkv_rows = jnp.dot(norm_one, qkv_all[layer], preferred_element_type=jnp.float32).astype(half)
        if local_images == 1:
            attended, log_totals = attend_call(qkv_rows), None
        else:
            attended, log_totals = attend_forward(qkv_rows, local_images)
        middle = inputs + jnp.dot(attended, out_all[layer], preferred_element_type=jnp.float32)
        normed_two, unit_two, inverse_two = norm_forward(
            middle, norm_all[layer][1], norm_all[layer][3]
        )
        norm_two = normed_two.astype(half)
        logits = jnp.dot(norm_two, router_all[layer], preferred_element_type=jnp.float32)
        picked = jnp.sum(logits[:, None, :] * chosen, axis=-1)
        leading = jax.nn.sigmoid(picked[:, 0] - picked[:, 1])
        gate_pair = jnp.stack([leading, 1.0 - leading], axis=-1)
        gate_rows = jnp.pad(gate_pair.T, ((0, 0), (0, model_width - token_rows)))
        sent = jnp.concatenate(
            [
                norm_two,
                jnp.zeros((padded_rows - 8 - token_rows, model_width), half),
                gate_rows.astype(half),
                jnp.zeros((6, model_width), half),
            ]
        )
        combined, *expert_saved = moe(
            False, 2 * layer, rows=sent, slots=slot_tables[layer], up=up_all[layer],
            down=down_all[layer],
        )
        out_rows = middle + combined[:token_rows]
        saved = (
            inputs, norm_one, qkv_rows, log_totals, attended, middle, norm_two, gate_pair,
            expert_saved,
        )
        return (out_rows, saved)

    def layer_backward(layer, d_out, saved):
        (
            inputs, norm_one, qkv_rows, log_totals, attended, middle, norm_two, gate_pair,
            expert_saved,
        ) = saved
        chosen = chosen_all[layer]
        gates, all_rows, hidden, slope, back_rows = expert_saved
        sent = jnp.pad(d_out.astype(half), ((0, padded_rows - token_rows), (0, 0)))
        combined, up_grad, down_grad = moe(
            True, 2 * layer + 1, rows=sent, slots=slot_tables[layer], up=up_all[layer],
            down=down_all[layer], saved=(gates, back_rows, slope, hidden, all_rows),
        )
        d_gate_rows = combined[padded_rows - 8 :, :token_rows]
        d_gate = jnp.stack([d_gate_rows[0] + d_gate_rows[1], d_gate_rows[2] + d_gate_rows[3]], axis=1)
        d_lead = (d_gate[:, 0] - d_gate[:, 1]) * gate_pair[:, 0] * gate_pair[:, 1]
        d_logits = (d_lead[:, None] * (chosen[:, 0] - chosen[:, 1])).astype(half)
        d_norm_two = combined[:token_rows] + jnp.einsum(
            "te,de->td", d_logits, router_all[layer], preferred_element_type=jnp.float32
        )
        normed_two, unit_two, inverse_two = norm_forward(
            middle, norm_all[layer][1], norm_all[layer][3]
        )
        d_middle_norm, gain_two, shift_two = norm_backward(
            d_norm_two, unit_two, inverse_two, norm_all[layer][1]
        )
        d_middle = d_out + d_middle_norm
        d_middle_half = d_middle.astype(half)
        d_attended = jnp.einsum(
            "te,de->td", d_middle_half, out_all[layer], preferred_element_type=jnp.float32
        ).astype(half)
        if local_images == 1:
            d_qkv = attend_call(qkv_rows, d_attended)
        else:
            d_qkv = attend_backward(qkv_rows, log_totals, d_attended, local_images)
        d_norm_one = jnp.einsum(
            "te,de->td", d_qkv, qkv_all[layer], preferred_element_type=jnp.float32
        )
        normed_one, unit_one, inverse_one = norm_forward(
            inputs, norm_all[layer][0], norm_all[layer][2]
        )
        d_input_norm, gain_one, shift_one = norm_backward(
            d_norm_one, unit_one, inverse_one, norm_all[layer][0]
        )
        d_input = d_middle + d_input_norm
        small = jnp.concatenate(
            [
                jnp.einsum("td,te->de", norm_two, d_logits, preferred_element_type=jnp.float32),
                jnp.stack([gain_one, gain_two, shift_one, shift_two], axis=1),
            ],
            axis=1,
        )
        return (d_input, (norm_one, d_qkv, attended, d_middle_half, small), (up_grad, down_grad))

    qkv_part, out_part = 3 * model_width // 2, model_width // 2
    small_width = round_up(expert_count + 4, 128)

    def dense_gradients(norm_one, d_qkv, attended, d_middle_half, small):
        own = jnp.concatenate([norm_one, d_qkv, attended, d_middle_half], axis=1)
        pair = jnp.concatenate([own, lax.ppermute(own, "section", swapped)], axis=0)
        d_qkv_part = lax.dynamic_slice_in_dim(
            pair, model_width + section_index * qkv_part, qkv_part, axis=1
        )
        d_out_part = lax.dynamic_slice_in_dim(
            pair, 5 * model_width + section_index * out_part, out_part, axis=1
        )
        qkv_grad = jnp.einsum(
            "td,te->de", pair[:, :model_width], d_qkv_part, preferred_element_type=jnp.float32
        )
        out_grad = jnp.einsum(
            "td,te->de", pair[:, 4 * model_width : 5 * model_width], d_out_part,
            preferred_element_type=jnp.float32,
        )
        small = jnp.pad(small, ((0, 0), (0, small_width - expert_count - 4)))
        packed_grad = jnp.concatenate(
            [qkv_grad.astype(half), out_grad.astype(half), small.astype(half)], axis=1
        )
        blocks = packed_grad.reshape(depth, groups, -1, packed_grad.shape[1]).transpose(1, 0, 2, 3)
        blocks = lax.all_to_all(blocks, "expert", split_axis=0, concat_axis=0, tiled=True)
        blocks = jnp.sum(blocks.astype(jnp.float32), axis=0).astype(half)
        blocks = lax.all_to_all(blocks, "dp", split_axis=0, concat_axis=0, tiled=True)
        return jnp.sum(blocks.astype(jnp.float32), axis=0)

    saved_list = []
    for layer in range(2):
        if layer > 0:
            stream = stream.astype(half).astype(jnp.float32)
        stream, saved = layer_forward(layer, stream)
        saved_list.append(saved)
    dense_operands = [None, None]
    expert_grads = [None, None]
    for layer in (1, 0):
        if layer < 1:
            cotangent = cotangent.astype(half).astype(jnp.float32)
        cotangent, operands, expert_grads[layer] = layer_backward(
            layer, cotangent, saved_list[layer]
        )
        dense_operands[layer] = operands

    def mine(first, second):
        return jnp.where(is_first, first, second)

    def both(first, second):
        own, away = mine(first, second), mine(second, first)
        return own, lax.ppermute(away, "section", swapped)

    if model_width % (16 * depth * groups) == 0:
        operands = [
            item[:4] + (jnp.pad(item[4], ((0, 0), (0, small_width - expert_count - 4))),)
            for item in dense_operands
        ]
        shard, other_up, other_down, other_rows = finish_call(
            9, depth, groups, operands[0], operands[1], *expert_grads[0], *expert_grads[1],
            cotangent, stream,
        )
        own_up = mine(expert_grads[0][0], expert_grads[1][0])
        own_down = mine(expert_grads[0][1], expert_grads[1][1])
        own_rows = mine(cotangent, stream)
        qkv_shard = shard[:, : 3 * model_width]
        out_shard = shard[:, 3 * model_width : 4 * model_width]
        small_shard = shard[:, 4 * model_width :]
    else:
        shards = [dense_gradients(*item) for item in dense_operands]
        own_shard, other_shard = both(shards[0], shards[1])
        low, high = mine(own_shard, other_shard), mine(other_shard, own_shard)
        qkv_shard = jnp.concatenate([low[:, :qkv_part], high[:, :qkv_part]], axis=1)
        out_shard = jnp.concatenate(
            [low[:, qkv_part : qkv_part + out_part], high[:, qkv_part : qkv_part + out_part]], axis=1
        )
        small_shard = (low + high)[:, qkv_part + out_part :]
        own_up, other_up = both(expert_grads[0][0], expert_grads[1][0])
        own_down, other_down = both(expert_grads[0][1], expert_grads[1][1])
        own_rows, other_rows = both(cotangent, stream)
    norm_shard = small_shard[:, expert_count : expert_count + 4].T

    def expert_grad(own, other):
        return (own.astype(jnp.float32) + other.astype(jnp.float32))[None]

    boundary_rows = jnp.stack([mine(own_rows, other_rows), mine(other_rows, own_rows)])
    boundary_out = boundary_rows.reshape(1, MB, local_images, boundary_in.shape[3], model_width)
    return (
        boundary_out,
        norm_shard[None, 0:2],
        norm_shard[None, 2:4],
        qkv_shard[None],
        out_shard[None],
        small_shard[None, :, :expert_count],
        expert_grad(own_up, other_up),
        expert_grad(own_down, other_down),
    )


def solution(mesh):
    in_specs = (
        P("section", None, ("dp", "expert"), None, None),
        P("section", None, ("dp", "expert"), None, None),
        P("section", None, ("dp", "expert"), None, None),
        P("section", None, ("dp", "expert")),
        P("section", None, ("dp", "expert")),
        P("section", ("dp", "expert"), None),
        P("section", ("dp", "expert"), None),
        P("section", ("dp", "expert"), None),
        P("section", "expert", None, "dp"),
        P("section", "expert", "dp", None),
    )
    out_specs = (
        P("section", None, ("dp", "expert"), None, None),
        P("section", None, ("dp", "expert")),
        P("section", None, ("dp", "expert")),
        P("section", ("dp", "expert"), None),
        P("section", ("dp", "expert"), None),
        P("section", ("dp", "expert"), None),
        P("section", "expert", None, "dp"),
        P("section", "expert", "dp", None),
    )
    return jax.shard_map(
        on_device, mesh=mesh, in_specs=in_specs, out_specs=out_specs, check_vma=False
    )
```

```python
import functools
import math

import jax
import jax.numpy as jnp
from jax import lax
from jax.experimental import pallas as pl
from jax.experimental.pallas import tpu as pltpu
from jax.sharding import PartitionSpec as P

HEADS = 12
HEAD_DIM = 64
EXP_DEV = 2
MB = 2


EPS = 1e-06
SQRT_HALF = 0.7071067811865476
INV_ROOT_TAU = 0.3989422804014327
MESH = pl.DeviceIdType.MESH


def round_up(value, unit):
    return (value + unit - 1) // unit * unit


def z_order(step, z, depth):
    if depth == 1:
        return z
    direction = 1 - 2 * (z // (depth // 2))
    return lax.rem(z + step * direction + depth, depth)


def f32_dot(a, b, dims):
    return lax.dot_general(a, b, (dims, ((), ())), preferred_element_type=jnp.float32)


def moe_kernel(backward, shape, *refs):
    depth, groups, cap_rows, token_rows, model_width, hidden_width = shape
    if backward:
        (
            rows_ref, slots_ref, gates_ref, up_source, down_source, back_source, slope_source,
            hidden_source, kept_source, out_ref, up_grad_ref, down_grad_ref,
            up_ref, down_ref, back_ref, slope_ref, hidden_ref, kept_ref,
            inbox, d_pre_ref, taken_ref, raw, sent_rows, sent_back, sent_home, home, back, d_gates, *sems,
        ) = refs
    else:
        (
            rows_ref, slots_ref, up_source, down_source,
            out_ref, gates_ref, taken_target, hidden_target, slope_target, back_target,
            up_ref, down_ref, taken_ref, hidden_ref, slope_ref, back,
            inbox, raw, sent_rows, sent_back, sent_home, home, *sems,
        ) = refs
    far_send, far_recv, go_send, go_recv, back_send, back_recv, home_send, home_recv = sems[:8]
    load_sem, store_sem = sems[8:]
    half = jnp.bfloat16
    section, z, column = (
        lax.axis_index("section"), lax.axis_index("dp"), lax.axis_index("expert")
    )
    slot_count = 2 * groups * cap_rows
    tail = token_rows - 16

    def z_peer(distance):
        return (section, lax.rem(z + distance, depth), column)

    def xy_peer(distance):
        return lax.rem(column + distance, groups)

    barrier = pltpu.get_barrier_semaphore()

    def greet_z(distance, carry):
        pl.semaphore_signal(barrier, inc=1, device_id=z_peer(distance), device_id_type=MESH)
        return carry

    def greet_xy(distance, carry):
        pl.semaphore_signal(
            barrier, inc=1, device_id=(section, z, xy_peer(distance)), device_id_type=MESH
        )
        return carry

    lax.fori_loop(1, depth, greet_z, 0)
    lax.fori_loop(1, groups, greet_xy, 0)
    pl.semaphore_wait(barrier, depth - 1 + groups - 1)

    def far_copy(direction, image):
        target = lax.rem(z + 2 * direction - 1 + depth, depth)
        source = raw.at[image]
        return pltpu.make_async_remote_copy(
            src_ref=source, dst_ref=raw.at[image],
            send_sem=far_send.at[direction, image], recv_sem=far_recv.at[image],
            device_id=(section, target, column), device_id_type=MESH,
        )

    def go_copy(image, source, target):
        return pltpu.make_async_remote_copy(
            src_ref=sent_rows.at[image, target], dst_ref=inbox.at[image, source],
            send_sem=go_send.at[image, target], recv_sem=go_recv.at[image, source],
            device_id=(section, z, target), device_id_type=MESH,
        )

    def back_copy(image, source, target):
        return pltpu.make_async_remote_copy(
            src_ref=sent_back.at[image, target], dst_ref=back.at[image, source],
            send_sem=back_send.at[image, target], recv_sem=back_recv.at[image, source],
            device_id=(section, z, target), device_id_type=MESH,
        )

    def home_copy(source, target):
        return pltpu.make_async_remote_copy(
            src_ref=sent_home.at[target], dst_ref=home.at[source],
            send_sem=home_send.at[target], recv_sem=home_recv.at[source],
            device_id=(section, target, column), device_id_type=MESH,
        )

    loads = [(up_source, up_ref), (down_source, down_ref)]
    if backward:
        loads += [
            (back_source, back_ref), (slope_source, slope_ref),
            (hidden_source, hidden_ref), (kept_source, kept_ref),
        ]
    loads = [
        pltpu.make_async_copy(source, target, load_sem.at[index])
        for index, (source, target) in enumerate(loads)
    ]

    def store_copies(image):
        pairs = [
            (taken_ref.at[0, image], taken_target.at[0, image]),
            (taken_ref.at[1, image], taken_target.at[1, image]),
            (hidden_ref.at[0, image], hidden_target.at[0, image]),
            (hidden_ref.at[1, image], hidden_target.at[1, image]),
            (slope_ref.at[0, image], slope_target.at[0, image]),
            (slope_ref.at[1, image], slope_target.at[1, image]),
            (back.at[image], back_target.at[image]),
        ]
        return [
            pltpu.make_async_copy(source, target, store_sem.at[index, image])
            for index, (source, target) in enumerate(pairs)
        ]

    raw[z] = rows_ref[...]

    @pl.when(z < depth - 1)
    def _():
        far_copy(1, z).start()

    @pl.when(z > 0)
    def _():
        far_copy(0, z).start()

    for copy in loads[2:3] + loads[:2] + loads[3:]:
        copy.start()

    def match(image):
        slots = slots_ref[image][:, :token_rows]
        index = lax.broadcasted_iota(jnp.int32, (slot_count, token_rows), 0)
        return index == slots[0:1], index == slots[1:2]

    def gate_table(image):
        first, second = match(image)
        gates = gates_ref[image]
        table = jnp.where(first, gates[0:1], 0.0) + jnp.where(second, gates[1:2], 0.0)
        return table.astype(half)

    def ones_table(image):
        first, second = match(image)
        return jnp.where(first | second, 1.0, 0.0).astype(half)

    def pass_on(step):
        low, high = z - step, z + step

        @pl.when(low >= 0)
        def _():
            far_copy(1, low).wait_recv()

            @pl.when(z < depth - 1)
            def _():
                far_copy(1, low).start()

        @pl.when(high < depth)
        def _():
            far_copy(0, high).wait_recv()

            @pl.when(z > 0)
            def _():
                far_copy(0, high).start()

    def dispatch(image):
        if not backward:
            gates_ref[image] = raw[image, tail:, :token_rows].astype(jnp.float32)[8:16]
        table = gate_table(image) if backward else ones_table(image)
        rows = raw[image]
        blocks = f32_dot(table, rows, ((1,), (0,))).astype(half)
        sent_rows[image] = blocks.reshape(groups, 2 * cap_rows, model_width)

        def send(distance, carry):
            go_copy(image, column, xy_peer(distance)).start()
            return carry

        lax.fori_loop(1, groups, send, 0)
        inbox[image, column] = sent_rows[image, column]
        if backward:

            @pl.when(image == z)
            def _():
                loads[2].wait()

            first, second = match(image)
            returned = back_ref[image].reshape(slot_count, model_width)
            ones = jnp.ones((8, model_width), half)
            row_index = lax.broadcasted_iota(jnp.int32, (8, token_rows), 0)
            packed = jnp.zeros((8, token_rows), jnp.float32)
            for choice, found in enumerate((first, second)):
                table = jnp.where(found, 1.0, 0.0).astype(half)
                selected = f32_dot(table, returned, ((0,), (0,)))
                product = (selected * rows.astype(jnp.float32)).astype(half)
                sums = f32_dot(ones, product, ((1,), (1,)))
                high = sums.astype(half).astype(jnp.float32)
                packed = jnp.where(row_index == 2 * choice, high, packed)
                packed = jnp.where(row_index == 2 * choice + 1, sums - high, packed)
            d_gates[image] = packed

    def experts(image):
        def arrive(distance, carry):
            go_copy(image, xy_peer(distance), column).wait_recv()
            return carry

        lax.fori_loop(1, groups, arrive, 0)
        block = inbox[image].astype(jnp.float32)
        results = []
        for expert in range(2):
            rows = block[:, expert * cap_rows : (expert + 1) * cap_rows]
            rows = rows.reshape(groups * cap_rows, model_width).astype(half)
            taken_ref[expert, image] = rows
            if backward:
                d_hidden = f32_dot(rows, down_ref[expert], ((1,), (1,)))
                d_pre = (d_hidden * slope_ref[expert, image].astype(jnp.float32)).astype(half)
                d_pre_ref[expert, image] = d_pre
                result = f32_dot(d_pre, up_ref[expert], ((1,), (1,)))
            else:
                pre = f32_dot(rows, up_ref[expert], ((1,), (0,)))
                share = 0.5 * (1.0 + lax.erf(pre * SQRT_HALF))
                slope = share + pre * jnp.exp(-0.5 * pre * pre) * INV_ROOT_TAU
                hidden = (pre * share).astype(half)
                hidden_ref[expert, image] = hidden
                slope_ref[expert, image] = slope.astype(half)
                result = f32_dot(hidden, down_ref[expert], ((1,), (0,)))
            results.append(result.reshape(groups, cap_rows, model_width))
        sent_back[image] = jnp.concatenate(results, axis=1).astype(half)

        def send(distance, carry):
            back_copy(image, column, xy_peer(distance)).start()
            return carry

        lax.fori_loop(1, groups, send, 0)
        back[image, column] = sent_back[image, column]
        if not backward:
            for copy in store_copies(image)[:6]:
                copy.start()

    def combine(image):
        def arrive(distance, carry):
            back_copy(image, xy_peer(distance), column).wait_recv()
            return carry

        lax.fori_loop(1, groups, arrive, 0)
        if not backward:
            store_copies(image)[6].start()
        table = ones_table(image) if backward else gate_table(image)
        total = f32_dot(table, back[image].reshape(slot_count, model_width), ((0,), (0,)))
        if backward:
            extra = jnp.concatenate(
                [jnp.zeros((8, token_rows), jnp.float32), d_gates[image]], axis=0
            )

        @pl.when(image == z)
        def _():
            out_ref[...] = total
            if backward:
                out_ref[tail:, :token_rows] = total[tail:, :token_rows] + extra

        @pl.when(image != z)
        def _():
            sent_home[image] = total.astype(half)
            if backward:
                sent_home[image, tail:, :token_rows] = (
                    total[tail:, :token_rows] + extra
                ).astype(half)
            home_copy(z, image).start()

    def stage(step, carry):
        @pl.when(jnp.logical_and(step >= 1, step < depth))
        def _():
            pass_on(step)

        @pl.when(step < depth)
        def _():
            dispatch(z_order(step, z, depth))

        @pl.when(step == 2)
        def _():
            loads[0].wait()
            loads[1].wait()
            if backward:
                loads[3].wait()

        @pl.when(jnp.logical_and(step >= 2, step < depth + 2))
        def _():
            experts(z_order(lax.rem(step - 1, depth), z, depth))

        @pl.when(step >= 3)
        def _():
            combine(z_order(lax.rem(step - 2, depth), z, depth))

        return carry

    lax.fori_loop(0, depth + 3, stage, 0)

    if backward:
        loads[4].wait()
        loads[5].wait()

        def expert_gradients(expert, carry):
            kept = kept_ref[expert].reshape(depth * groups * cap_rows, model_width)
            d_pre = d_pre_ref[expert].reshape(depth * groups * cap_rows, hidden_width)
            up_grad_ref[expert] = f32_dot(kept, d_pre, ((0,), (0,))).astype(half)
            hidden = hidden_ref[expert].reshape(depth * groups * cap_rows, hidden_width)
            grads = taken_ref[expert].reshape(depth * groups * cap_rows, model_width)
            down_grad_ref[expert] = f32_dot(hidden, grads, ((0,), (0,))).astype(half)
            return carry

        lax.fori_loop(0, 2, expert_gradients, 0)

    def finish_home(distance, carry):
        source = lax.rem(z + distance, depth)
        home_copy(source, z).wait_recv()
        out_ref[...] += home[source].astype(jnp.float32)
        return carry

    lax.fori_loop(1, depth, finish_home, 0)

    def drain_home(distance, carry):
        home_copy(z, lax.rem(z + distance, depth)).wait_send()
        return carry

    lax.fori_loop(1, depth, drain_home, 0)

    def drain_image(image, carry):
        if not backward:
            for copy in store_copies(image):
                copy.wait()

        @pl.when(jnp.logical_and(z < depth - 1, image <= z))
        def _():
            far_copy(1, image).wait_send()

        @pl.when(jnp.logical_and(z > 0, image >= z))
        def _():
            far_copy(0, image).wait_send()

        def drain(distance, inner):
            go_copy(image, column, xy_peer(distance)).wait_send()
            back_copy(image, column, xy_peer(distance)).wait_send()
            return inner

        lax.fori_loop(1, groups, drain, 0)
        return carry

    lax.fori_loop(0, depth, drain_image, 0)


def moe_call(backward, call_id, depth, groups, cap_rows, rows, slots, up, down, saved=()):
    token_rows, model_width = rows.shape
    hidden_width = up.shape[2]
    half = jnp.bfloat16
    shape = (depth, groups, cap_rows, token_rows, model_width, hidden_width)
    taken = jax.ShapeDtypeStruct((2, depth, groups * cap_rows, model_width), half)
    hidden = jax.ShapeDtypeStruct((2, depth, groups * cap_rows, hidden_width), half)
    back = jax.ShapeDtypeStruct((depth, groups, 2 * cap_rows, model_width), half)
    out = jax.ShapeDtypeStruct((token_rows, model_width), jnp.float32)
    vmem, anywhere = pl.BlockSpec(memory_space=pltpu.VMEM), pl.BlockSpec(memory_space=pl.ANY)
    if backward:
        operands = (rows, slots, saved[0], up, down) + saved[1:]
        in_specs = [vmem] * 3 + [anywhere] * 6
        out_shape = (
            out, jax.ShapeDtypeStruct(up.shape, half), jax.ShapeDtypeStruct(down.shape, half)
        )
        out_specs = [vmem] * 3
        buffers = (up, down, back, hidden, hidden, taken, back, hidden, taken)
    else:
        operands = (rows, slots, up, down)
        in_specs = [vmem] * 2 + [anywhere] * 2
        gates = jax.ShapeDtypeStruct((depth, 8, token_rows), jnp.float32)
        out_shape = (out, gates, taken, hidden, hidden, back)
        out_specs = [vmem] * 2 + [anywhere] * 4
        buffers = (up, down, taken, hidden, hidden, back, back)
    scratch = [pltpu.VMEM(item.shape, half) for item in buffers]
    scratch += [
        pltpu.VMEM((depth, token_rows, model_width), half),
        pltpu.VMEM(back.shape, half),
        pltpu.VMEM(back.shape, half),
        pltpu.VMEM((depth, token_rows, model_width), half),
        pltpu.VMEM((depth, token_rows, model_width), half),
    ]
    if backward:
        scratch += [
            pltpu.VMEM(back.shape, half),
            pltpu.VMEM((depth, 8, token_rows), jnp.float32),
        ]
    scratch += [
        pltpu.SemaphoreType.DMA((2, depth)),
        pltpu.SemaphoreType.DMA((depth,)),
        pltpu.SemaphoreType.DMA((depth, groups)),
        pltpu.SemaphoreType.DMA((depth, groups)),
        pltpu.SemaphoreType.DMA((depth, groups)),
        pltpu.SemaphoreType.DMA((depth, groups)),
        pltpu.SemaphoreType.DMA((depth,)),
        pltpu.SemaphoreType.DMA((depth,)),
        pltpu.SemaphoreType.DMA((6,)),
        pltpu.SemaphoreType.DMA((7, depth)),
    ]
    return pl.pallas_call(
        functools.partial(moe_kernel, backward, shape),
        out_shape=out_shape,
        in_specs=in_specs,
        out_specs=out_specs,
        scratch_shapes=scratch,
        compiler_params=pltpu.CompilerParams(
            collective_id=call_id, has_side_effects=True, vmem_limit_bytes=60 * 2**20
        ),
        name="moe_backward" if backward else "moe_forward",
    )(*operands)

def start_kernel(shape, *refs):
    depth, groups = shape
    (
        packed_ref, up_ref, down_ref, edge_ref, table_ref,
        dense_first, dense_second, up_first, up_second, down_first, down_second,
        rows_ref, cotangent_ref, table_first, table_second,
        shard_send, shard_recv, core_send, core_recv, table_send, table_recv, own_sem,
    ) = refs
    section, z, column = (
        lax.axis_index("section"), lax.axis_index("dp"), lax.axis_index("expert")
    )
    other = (1 - section, z, column)
    is_first = section == 0

    def z_peer(distance):
        return lax.rem(z + distance, depth)

    def xy_peer(distance):
        return lax.rem(column + distance, groups)

    barrier = pltpu.get_barrier_semaphore()

    def greet_z(distance, carry):
        pl.semaphore_signal(
            barrier, inc=1, device_id=(section, z_peer(distance), column), device_id_type=MESH
        )
        return carry

    def greet_xy(distance, carry):
        pl.semaphore_signal(
            barrier, inc=1, device_id=(section, z, xy_peer(distance)), device_id_type=MESH
        )
        return carry

    pl.semaphore_signal(barrier, inc=1, device_id=other, device_id_type=MESH)
    lax.fori_loop(1, depth, greet_z, 0)
    lax.fori_loop(1, groups, greet_xy, 0)
    pl.semaphore_wait(barrier, depth + groups - 1)

    def remote(source, target, send, recv, device):
        return pltpu.make_async_remote_copy(
            src_ref=source, dst_ref=target, send_sem=send, recv_sem=recv,
            device_id=device, device_id_type=MESH,
        )

    def run(first):
        own, away = (dense_first, dense_second) if first else (dense_second, dense_first)

        def shard_copy(kind, layer, plane, lane, device):
            return remote(
                layer.at[plane, lane], layer.at[plane, lane],
                shard_send.at[kind, plane, lane],
                shard_recv.at[0, plane, lane],
                device,
            )

        def z_copy(direction, plane):
            device = (section, lax.rem(z + 2 * direction - 1 + depth, depth), column)
            return shard_copy(direction, own, plane, column, device)

        def core_copy(layer, plane, lane):
            return remote(
                layer.at[plane, lane], layer.at[plane, lane],
                shard_send.at[2, plane, lane], shard_recv.at[1, plane, lane], other,
            )

        def xy_copy(plane, source, target):
            return shard_copy(3 + target, own, plane, source, (section, z, target))

        def pass_copy(plane, source, target):
            return shard_copy(3 + groups, own, plane, source, (section, z, target))

        def swap(index, source, target):
            return remote(source, target, core_send.at[index], core_recv.at[index], other)

        def local(index, source, target):
            return pltpu.make_async_copy(source, target, own_sem.at[index])

        square = groups == 4
        beside = column + 1 - 2 * lax.rem(column, 2)
        above = lax.rem(column + 2, groups)
        across = groups - 1 - column
        direct = 3 if square else groups

        def near(distance):
            if square:
                return beside + (distance - 1) * (above - beside)
            return xy_peer(distance)

        def spread(plane):
            core_copy(own, plane, column).start()

            def send(distance, carry):
                xy_copy(plane, column, near(distance)).start()
                return carry

            lax.fori_loop(1, direct, send, 0)

        def take(plane):
            def arrive(distance, carry):
                lane = near(distance)
                xy_copy(plane, lane, column).wait_recv()
                core_copy(own, plane, lane).start()
                if square:

                    @pl.when(lax.rem(plane, 2) == distance - 1)
                    def _():
                        pass_copy(plane, lane, near(3 - distance)).start()

                return carry

            lax.fori_loop(1, direct, arrive, 0)

        own_shard = local(0, packed_ref, own.at[z, column])

        def first_copies():
            remote_ones = [
                swap(0, edge_ref.at[1], rows_ref),
                swap(1, table_ref.at[1], table_first.at[z]),
                swap(2, up_ref, up_first),
                swap(3, down_ref, down_first),
            ]
            local_ones = [
                local(1, edge_ref.at[0], rows_ref),
                local(2, table_ref.at[0], table_first.at[z]),
                local(3, up_ref, up_first),
                local(4, down_ref, down_first),
            ]
            return remote_ones, local_ones

        def second_copies():
            remote_ones = [
                swap(0, edge_ref.at[0], cotangent_ref),
                swap(1, table_ref.at[0], table_second.at[z]),
                swap(2, up_ref, up_second),
                swap(3, down_ref, down_second),
            ]
            local_ones = [
                local(1, edge_ref.at[1], cotangent_ref),
                local(2, table_ref.at[1], table_second.at[z]),
                local(3, up_ref, up_second),
                local(4, down_ref, down_second),
            ]
            return remote_ones, local_ones

        own_shard.start()
        own_shard.wait()

        @pl.when(z < depth - 1)
        def _():
            z_copy(1, z).start()

        @pl.when(z > 0)
        def _():
            z_copy(0, z).start()

        spread(z)

        first_remote, first_local = first_copies()
        second_remote, second_local = second_copies()
        out_going, in_coming = (
            (first_remote, second_remote) if first else (second_remote, first_remote)
        )
        local_ones = first_local if first else second_local
        for copy in out_going[:2] + local_ones + out_going[2:]:
            copy.start()

        def step(distance, carry):
            low, high = z - distance, z + distance

            @pl.when(low >= 0)
            def _():
                z_copy(1, low).wait_recv()

                @pl.when(z < depth - 1)
                def _():
                    z_copy(1, low).start()

                spread(low)

            @pl.when(high < depth)
            def _():
                z_copy(0, high).wait_recv()

                @pl.when(z > 0)
                def _():
                    z_copy(0, high).start()

                spread(high)

            take(z_order(distance - 1, z, depth))
            return carry

        lax.fori_loop(1, depth, step, 0)
        take(z_order(depth - 1, z, depth))

        def table_copies(source, target):
            pairs = []
            for layer, table in enumerate((table_first, table_second)):
                pairs.append(
                    remote(
                        table.at[source], table.at[source], table_send.at[layer, target],
                        table_recv.at[layer, source], (section, target, column),
                    )
                )
            return pairs

        local_ones[1].wait()
        in_coming[1].wait_recv()

        def send_tables(distance, carry):
            for copy in table_copies(z, z_peer(distance)):
                copy.start()
            return carry

        lax.fori_loop(1, depth, send_tables, 0)

        if square:

            def last_arrival(index, carry):
                plane = z_order(index, z, depth)
                pass_copy(plane, across, column).wait_recv()
                core_copy(own, plane, across).start()
                return carry

            lax.fori_loop(0, depth, last_arrival, 0)

        def drain(plane, carry):
            @pl.when(jnp.logical_and(z < depth - 1, plane <= z))
            def _():
                z_copy(1, plane).wait_send()

            @pl.when(jnp.logical_and(z > 0, plane >= z))
            def _():
                z_copy(0, plane).wait_send()

            def drain_core(lane, inner):
                core_copy(away, plane, lane).wait_recv()
                core_copy(own, plane, lane).wait_send()
                return inner

            def drain_xy(distance, inner):
                xy_copy(plane, column, near(distance)).wait_send()
                if square:

                    @pl.when(lax.rem(plane, 2) == distance - 1)
                    def _():
                        pass_copy(plane, near(distance), near(3 - distance)).wait_send()

                return inner

            lax.fori_loop(0, groups, drain_core, 0)
            return lax.fori_loop(1, direct, drain_xy, carry)

        lax.fori_loop(0, depth, drain, 0)

        for index in (0, 2, 3):
            in_coming[index].wait_recv()
        for copy in out_going:
            copy.wait_send()
        for copy in local_ones[:1] + local_ones[2:]:
            copy.wait()

        def finish_tables(distance, carry):
            for copy in table_copies(z_peer(distance), z):
                copy.wait_recv()
            for copy in table_copies(z, z_peer(distance)):
                copy.wait_send()
            return carry

        lax.fori_loop(1, depth, finish_tables, 0)

    pl.when(is_first)(functools.partial(run, True))
    pl.when(jnp.logical_not(is_first))(functools.partial(run, False))


def start_call(call_id, depth, groups, packed, up, down, edge, table):
    rows, width = packed.shape
    half = jnp.bfloat16
    out_shape = (
        jax.ShapeDtypeStruct((depth, groups, rows, width), half),
        jax.ShapeDtypeStruct((depth, groups, rows, width), half),
        jax.ShapeDtypeStruct(up.shape, half),
        jax.ShapeDtypeStruct(up.shape, half),
        jax.ShapeDtypeStruct(down.shape, half),
        jax.ShapeDtypeStruct(down.shape, half),
        jax.ShapeDtypeStruct(edge.shape[1:], jnp.float32),
        jax.ShapeDtypeStruct(edge.shape[1:], jnp.float32),
        jax.ShapeDtypeStruct((depth,) + table.shape[1:], jnp.int32),
        jax.ShapeDtypeStruct((depth,) + table.shape[1:], jnp.int32),
    )
    return pl.pallas_call(
        functools.partial(start_kernel, (depth, groups)),
        out_shape=out_shape,
        in_specs=[pl.BlockSpec(memory_space=pltpu.VMEM)] * 5,
        out_specs=[pl.BlockSpec(memory_space=pl.ANY)] * len(out_shape),
        scratch_shapes=[
            pltpu.SemaphoreType.DMA((4 + groups, depth, groups)),
            pltpu.SemaphoreType.DMA((2, depth, groups)),
            pltpu.SemaphoreType.DMA((4,)),
            pltpu.SemaphoreType.DMA((4,)),
            pltpu.SemaphoreType.DMA((2, depth)),
            pltpu.SemaphoreType.DMA((2, depth)),
            pltpu.SemaphoreType.DMA((5,)),
        ],
        compiler_params=pltpu.CompilerParams(
            collective_id=call_id, has_side_effects=True, vmem_limit_bytes=60 * 2**20
        ),
        name="start_exchange",
    )(packed, up, down, edge, table)

def finish_kernel(shape, *refs):
    depth, groups, token_rows, padded_rows, model_width = shape
    first_refs, second_refs, rest = refs[0:5], refs[5:10], refs[10:]
    (
        up_first, down_first, up_second, down_second, rows_first, rows_second,
        shard_ref, up_ref, down_ref, rows_ref,
        pair, away, small_pair, table, inbox, middle, sent_home, home,
        core_send, core_recv, go_send, go_recv, home_send, home_recv,
    ) = rest
    half = jnp.bfloat16
    section, z, column = (
        lax.axis_index("section"), lax.axis_index("dp"), lax.axis_index("expert")
    )
    other = (1 - section, z, column)
    is_first = section == 0
    shard_rows = table.shape[1]

    def z_peer(distance):
        return lax.rem(z + distance, depth)

    def xy_peer(distance):
        return lax.rem(column + distance, groups)

    barrier = pltpu.get_barrier_semaphore()

    def greet_z(distance, carry):
        pl.semaphore_signal(
            barrier, inc=1, device_id=(section, z_peer(distance), column), device_id_type=MESH
        )
        return carry

    def greet_xy(distance, carry):
        pl.semaphore_signal(
            barrier, inc=1, device_id=(section, z, xy_peer(distance)), device_id_type=MESH
        )
        return carry

    pl.semaphore_signal(barrier, inc=1, device_id=other, device_id_type=MESH)
    lax.fori_loop(1, depth, greet_z, 0)
    lax.fori_loop(1, groups, greet_xy, 0)
    pl.semaphore_wait(barrier, depth + groups - 1)

    def swap(index, source, target):
        return pltpu.make_async_remote_copy(
            src_ref=source, dst_ref=target, send_sem=core_send.at[index],
            recv_sem=core_recv.at[index], device_id=other, device_id_type=MESH,
        )

    def pack(target, operands):
        target[padded_rows - 16 :, :] = jnp.zeros((16, target.shape[1]), half)
        offset = 0
        for operand in operands:
            width = operand.shape[1]
            target[:token_rows, offset : offset + width] = operand[...]
            offset += width

    def side_copies(first):
        if first:
            sources = (second_refs[4], up_second, down_second, rows_second)
        else:
            sources = (first_refs[4], up_first, down_first, rows_first)
        targets = (small_pair.at[1], up_ref, down_ref, rows_ref)
        return [
            swap(1 + index, source, target)
            for index, (source, target) in enumerate(zip(sources, targets))
        ]

    operand_copy = swap(0, away, pair.at[1])
    for first in (True, False):

        @pl.when(is_first if first else jnp.logical_not(is_first))
        def _():
            mine, others = (first_refs, second_refs) if first else (second_refs, first_refs)
            pack(away, others[:4])
            operand_copy.start()
            for copy in side_copies(first):
                copy.start()
            pack(pair.at[0], mine[:4])
            small_pair[0] = mine[4][...]

    operand_copy.wait_recv()
    rows = 2 * padded_rows

    def product(left, right, target):
        a = pair[:, :, left : left + model_width].reshape(rows, model_width)
        b = pair[:, :, right : right + model_width].reshape(rows, model_width)
        value = f32_dot(a, b, ((0,), (0,))).astype(half)
        table[:, :, target : target + model_width] = value.reshape(
            depth * groups, shard_rows, model_width
        )

    for index in range(3):
        product(0, (1 + index) * model_width, index * model_width)
    product(4 * model_width, 5 * model_width, 3 * model_width)
    for copy in side_copies(True)[:1]:
        copy.wait_recv()
    small = (small_pair[0] + small_pair[1]).astype(half)
    table[:, :, 4 * model_width :] = small.reshape(depth * groups, shard_rows, small.shape[1])

    beside = column + 1 - 2 * lax.rem(column, 2)
    above = lax.rem(column + 2, groups)
    across = groups - 1 - column

    def first_hop(plane):
        return beside + lax.rem(plane, 2) * (above - beside)

    def second_hop(plane):
        return above + lax.rem(plane, 2) * (beside - above)

    def go_copy(plane, kind):
        if kind == 2:
            source, target = middle.at[plane], second_hop(plane)
        else:
            target = first_hop(plane)
            source = table.at[plane * groups + (across if kind == 1 else target)]
        return pltpu.make_async_remote_copy(
            src_ref=source, dst_ref=inbox.at[plane, kind],
            send_sem=go_send.at[plane, kind], recv_sem=go_recv.at[plane, kind],
            device_id=(section, z, target), device_id_type=MESH,
        )

    def home_copy(source, target):
        return pltpu.make_async_remote_copy(
            src_ref=sent_home.at[target], dst_ref=home.at[source],
            send_sem=home_send.at[target], recv_sem=home_recv.at[source],
            device_id=(section, target, column), device_id_type=MESH,
        )

    def send_plane(step, carry):
        go_copy(z_peer(step), 1).start()
        go_copy(z_peer(step), 0).start()
        return carry

    lax.fori_loop(1, depth + 1, send_plane, 0)

    def sum_plane(step, carry):
        @pl.when(step <= depth)
        def _():
            plane = z_peer(step)
            go_copy(plane, 1).wait_recv()
            own = table[plane * groups + second_hop(plane)].astype(jnp.float32)
            middle[plane] = (own + inbox[plane, 1].astype(jnp.float32)).astype(half)
            go_copy(plane, 2).start()

        @pl.when(step >= 2)
        def _():
            plane = z_peer(step - 1)
            go_copy(plane, 0).wait_recv()
            total = table[plane * groups + column].astype(jnp.float32)
            total = total + inbox[plane, 0].astype(jnp.float32)
            go_copy(plane, 2).wait_recv()
            total = total + inbox[plane, 2].astype(jnp.float32)

            @pl.when(plane == z)
            def _():
                shard_ref[...] = total

            @pl.when(plane != z)
            def _():
                sent_home[plane] = total.astype(half)
                home_copy(z, plane).start()

        return carry

    lax.fori_loop(1, depth + 2, sum_plane, 0)

    def finish_home(distance, carry):
        source = z_peer(distance)
        home_copy(source, z).wait_recv()
        shard_ref[...] += home[source].astype(jnp.float32)
        home_copy(z, source).wait_send()
        return carry

    lax.fori_loop(1, depth, finish_home, 0)

    def drain_plane(plane, carry):
        for kind in range(3):
            go_copy(plane, kind).wait_send()
        return carry

    lax.fori_loop(0, depth, drain_plane, 0)
    operand_copy.wait_send()
    for index, copy in enumerate(side_copies(True)):
        copy.wait_send()
        if index > 0:
            copy.wait_recv()


def finish_call(call_id, depth, groups, first, second, up_first, down_first, up_second, down_second,
                rows_first, rows_second):
    token_rows, model_width = first[0].shape
    padded_rows = round_up(token_rows, 16)
    small_width = first[4].shape[1]
    width = 4 * model_width + small_width
    shard_rows = model_width // (depth * groups)
    half = jnp.bfloat16
    out_shape = (
        jax.ShapeDtypeStruct((shard_rows, width), jnp.float32),
        jax.ShapeDtypeStruct(up_first.shape, half),
        jax.ShapeDtypeStruct(down_first.shape, half),
        jax.ShapeDtypeStruct(rows_first.shape, jnp.float32),
    )
    home = pltpu.VMEM((depth, shard_rows, width), half)
    return pl.pallas_call(
        functools.partial(
            finish_kernel, (depth, groups, token_rows, padded_rows, model_width)
        ),
        out_shape=out_shape,
        in_specs=[pl.BlockSpec(memory_space=pltpu.VMEM)] * 16,
        out_specs=[pl.BlockSpec(memory_space=pltpu.VMEM)] + [pl.BlockSpec(memory_space=pl.ANY)] * 3,
        scratch_shapes=[
            pltpu.VMEM((2, padded_rows, 6 * model_width), half),
            pltpu.VMEM((padded_rows, 6 * model_width), half),
            pltpu.VMEM((2, model_width, small_width), jnp.float32),
            pltpu.VMEM((depth * groups, shard_rows, width), half),
            pltpu.VMEM((depth, 3, shard_rows, width), half),
            home,
            home,
            home,
            pltpu.SemaphoreType.DMA((5,)),
            pltpu.SemaphoreType.DMA((5,)),
            pltpu.SemaphoreType.DMA((depth, 3)),
            pltpu.SemaphoreType.DMA((depth, 3)),
            pltpu.SemaphoreType.DMA((depth,)),
            pltpu.SemaphoreType.DMA((depth,)),
        ],
        compiler_params=pltpu.CompilerParams(
            collective_id=call_id, has_side_effects=True, vmem_limit_bytes=60 * 2**20
        ),
        name="finish_exchange",
    )(*first, *second, up_first, down_first, up_second, down_second, rows_first, rows_second)

def head_mask(head):
    lanes = lax.broadcasted_iota(jnp.int32, (1, 2 * HEAD_DIM), 1)
    return jnp.where(lanes // HEAD_DIM == head, 1.0, 0.0).astype(jnp.bfloat16)


def attend_kernel(width, qkv_ref, out_ref):
    scale_factor = 1.0 / math.sqrt(HEAD_DIM)
    pair_width = 2 * HEAD_DIM

    def pair(index, carry):
        def columns(part):
            start = pl.multiple_of(part * width + index * pair_width, pair_width)
            return qkv_ref[:, pl.ds(start, pair_width)]

        queries, keys, values = columns(0), columns(1), columns(2)
        total = jnp.zeros(queries.shape, jnp.float32)
        for head in range(2):
            mask = head_mask(head)
            scores = f32_dot(queries * mask, keys, ((1,), (1,))) * scale_factor
            log_totals = jnp.log(jnp.sum(jnp.exp(scores), axis=1, keepdims=True))
            probs = jnp.exp(scores - log_totals).astype(jnp.bfloat16)
            total = total + f32_dot(probs, values * mask, ((1,), (0,)))
        start = pl.multiple_of(index * pair_width, pair_width)
        out_ref[:, pl.ds(start, pair_width)] = total.astype(jnp.bfloat16)
        return carry

    lax.fori_loop(0, width // pair_width, pair, 0)


def attend_backward_kernel(width, qkv_ref, d_out_ref, d_qkv_ref):
    scale_factor = 1.0 / math.sqrt(HEAD_DIM)
    pair_width = 2 * HEAD_DIM
    half = jnp.bfloat16

    def pair(index, carry):
        def place(part):
            return pl.ds(pl.multiple_of(part * width + index * pair_width, pair_width), pair_width)

        queries, keys, values = (qkv_ref[:, place(part)] for part in range(3))
        d_out = d_out_ref[:, place(0)]
        d_queries = jnp.zeros(queries.shape, jnp.float32)
        d_keys, d_values = d_queries, d_queries
        for head in range(2):
            mask = head_mask(head)
            own_queries, own_d_out = queries * mask, d_out * mask
            scores = f32_dot(keys, own_queries, ((1,), (1,))) * scale_factor
            log_totals = jnp.log(jnp.sum(jnp.exp(scores), axis=0, keepdims=True))
            probs = jnp.exp(scores - log_totals)
            d_probs = f32_dot(values, own_d_out, ((1,), (1,)))
            row_dot = jnp.sum(probs * d_probs, axis=0, keepdims=True)
            d_scores = (probs * (d_probs - row_dot) * scale_factor).astype(half)
            d_values = d_values + f32_dot(probs.astype(half), own_d_out, ((1,), (0,)))
            d_keys = d_keys + f32_dot(d_scores, own_queries, ((1,), (0,)))
            d_queries = d_queries + f32_dot(d_scores, keys * mask, ((0,), (0,)))
        for part, value in enumerate((d_queries, d_keys, d_values)):
            d_qkv_ref[:, place(part)] = value.astype(half)
        return carry

    lax.fori_loop(0, width // pair_width, pair, 0)


def attend_call(qkv_rows, d_attended=None):
    rows, width = qkv_rows.shape
    width = width // 3
    operands = (qkv_rows,) if d_attended is None else (qkv_rows, d_attended)
    kernel = attend_kernel if d_attended is None else attend_backward_kernel
    out_width = width if d_attended is None else 3 * width
    return pl.pallas_call(
        functools.partial(kernel, width),
        out_shape=jax.ShapeDtypeStruct((rows, out_width), jnp.bfloat16),
        in_specs=[pl.BlockSpec(memory_space=pltpu.VMEM)] * len(operands),
        out_specs=pl.BlockSpec(memory_space=pltpu.VMEM),
        compiler_params=pltpu.CompilerParams(vmem_limit_bytes=24 * 2**20),
        name="attend" if d_attended is None else "attend_backward",
    )(*operands)


def norm_forward(values, gain_row, shift_row):
    centred = values - jnp.mean(values, axis=-1, keepdims=True)
    variance = jnp.mean(centred * centred, axis=-1, keepdims=True)
    inverse = lax.rsqrt(variance + EPS)
    unit_rows = centred * inverse
    return (unit_rows * gain_row + shift_row, unit_rows, inverse)


def norm_backward(d_normed, unit_rows, inverse, gain_row):
    d_gain = jnp.sum(d_normed * unit_rows, axis=0)
    d_shift = jnp.sum(d_normed, axis=0)
    scaled = d_normed * gain_row
    d_values = inverse * (
        scaled
        - jnp.mean(scaled, axis=-1, keepdims=True)
        - unit_rows * jnp.mean(scaled * unit_rows, axis=-1, keepdims=True)
    )
    return (d_values, d_gain, d_shift)


def gelu_slope(pre_act):
    return (
        0.5 * (1.0 + lax.erf(pre_act * SQRT_HALF))
        + pre_act * jnp.exp(-0.5 * pre_act * pre_act) * INV_ROOT_TAU
    )


def split_heads(qkv_rows, image_count):
    feature_count = qkv_rows.shape[1] // 3
    return [
        qkv_rows[:, part_index * feature_count : (part_index + 1) * feature_count].reshape(
            image_count, -1, HEADS, HEAD_DIM
        )
        for part_index in range(3)
    ]


def attend_forward(qkv_rows, image_count):
    queries, key_rows, value_rows = split_heads(qkv_rows, image_count)
    scale_factor = 1.0 / math.sqrt(HEAD_DIM)
    scores = (
        jnp.einsum("bqhd,bkhd->bhqk", queries, key_rows, preferred_element_type=jnp.float32)
        * scale_factor
    )
    log_totals = jnp.log(jnp.sum(jnp.exp(scores), axis=-1))
    probs_half = jnp.exp(scores - log_totals[..., None]).astype(jnp.bfloat16)
    attended = jnp.einsum(
        "bhqk,bkhd->bqhd", probs_half, value_rows, preferred_element_type=jnp.float32
    )
    return (attended.astype(jnp.bfloat16).reshape(-1, HEADS * HEAD_DIM), log_totals)


def attend_backward(qkv_rows, log_totals, d_attended, image_count):
    queries, key_rows, value_rows = split_heads(qkv_rows, image_count)
    scale_factor = 1.0 / math.sqrt(HEAD_DIM)
    scores = (
        jnp.einsum("bqhd,bkhd->bhqk", queries, key_rows, preferred_element_type=jnp.float32)
        * scale_factor
    )
    probs = jnp.exp(scores - log_totals[..., None])
    probs_half = probs.astype(jnp.bfloat16)
    d_heads = d_attended.reshape(image_count, -1, HEADS, HEAD_DIM)
    d_values = jnp.einsum(
        "bhqk,bqhd->bkhd", probs_half, d_heads, preferred_element_type=jnp.float32
    )
    d_probs = jnp.einsum("bqhd,bkhd->bhqk", d_heads, value_rows, preferred_element_type=jnp.float32)
    row_dot = jnp.sum(probs * d_probs, axis=-1, keepdims=True)
    d_scores = (probs * (d_probs - row_dot) * scale_factor).astype(jnp.bfloat16)
    d_queries = jnp.einsum(
        "bhqk,bkhd->bqhd", d_scores, key_rows, preferred_element_type=jnp.float32
    )
    d_keys = jnp.einsum("bhqk,bqhd->bkhd", d_scores, queries, preferred_element_type=jnp.float32)
    feature_count = HEADS * HEAD_DIM
    joined = jnp.concatenate(
        [
            d_queries.reshape(-1, feature_count),
            d_keys.reshape(-1, feature_count),
            d_values.reshape(-1, feature_count),
        ],
        axis=1,
    )
    return joined.astype(jnp.bfloat16)


def on_device(
    boundary_in, routes, capacity_slots, ln_gain, ln_bias, w_qkv, w_out, w_router, w_up, w_down
):
    section_index = lax.axis_index("section")
    is_first = section_index == 0
    depth = lax.axis_size("dp")
    groups = lax.axis_size("expert")
    expert_count = EXP_DEV * groups
    local_images = boundary_in.shape[2]
    token_rows = local_images * boundary_in.shape[3]
    model_width = boundary_in.shape[4]
    capacity = 26 * token_rows // (16 * expert_count)
    cap_rows = round_up(capacity, 8)
    padded_rows = round_up(token_rows + 8, 16)
    half = jnp.bfloat16
    swapped = [(0, 1), (1, 0)]

    edge = boundary_in[0].reshape(MB, token_rows, model_width)
    route_rows = routes[0].reshape(MB, token_rows, 2)
    slot_rows = capacity_slots[0].reshape(MB, token_rows, 2)
    slot_index = jnp.where(slot_rows < capacity, route_rows * cap_rows + slot_rows, -1)
    table = jnp.concatenate([slot_index, route_rows], axis=2).transpose(0, 2, 1)
    table = jnp.pad(
        table, ((0, 0), (0, 4), (0, padded_rows - token_rows)), constant_values=-1
    )

    norm_columns = jnp.concatenate([ln_gain, ln_bias], axis=1).transpose(0, 2, 1)
    used = 4 * model_width + expert_count + 4
    padding = -used % 128
    packed = jnp.concatenate([w_qkv, w_out, w_router, norm_columns], axis=2)
    packed = jnp.pad(packed, ((0, 0), (0, 0), (0, padding)))
    (
        dense_first, dense_second, up_first, up_second, down_first, down_second,
        stream, cotangent, table_first, table_second,
    ) = start_call(8, depth, groups, packed[0], w_up[0], w_down[0], edge, table)
    qkv_all, out_all, router_all, norm_all = [], [], [], []

    def add_dense(item):
        qkv_all.append(item[:, : 3 * model_width])
        out_all.append(item[:, 3 * model_width : 4 * model_width])
        router_all.append(item[:, 4 * model_width : used - 4])
        norm_all.append(item[:, used - 4 : used].T.astype(jnp.float32))

    add_dense(dense_first.reshape(model_width, used + padding))
    add_dense(dense_second.reshape(model_width, used + padding))
    up_all = (up_first, up_second)
    down_all = (down_first, down_second)
    slot_tables = (table_first, table_second)
    z_index = lax.axis_index("dp")
    chosen_all = [
        (
            lax.dynamic_index_in_dim(item, z_index, 0, False)[2:4, :token_rows].T[..., None]
            == jnp.arange(expert_count, dtype=jnp.int32)
        ).astype(jnp.float32)
        for item in slot_tables
    ]
    moe = functools.partial(moe_call, depth=depth, groups=groups, cap_rows=cap_rows)

    def layer_forward(layer, inputs):
        chosen = chosen_all[layer]
        normed_one, unit_one, inverse_one = norm_forward(
            inputs, norm_all[layer][0], norm_all[layer][2]
        )
        norm_one = normed_one.astype(half)
        qkv_rows = jnp.dot(norm_one, qkv_all[layer], preferred_element_type=jnp.float32).astype(half)
        if local_images == 1:
            attended, log_totals = attend_call(qkv_rows), None
        else:
            attended, log_totals = attend_forward(qkv_rows, local_images)
        middle = inputs + jnp.dot(attended, out_all[layer], preferred_element_type=jnp.float32)
        normed_two, unit_two, inverse_two = norm_forward(
            middle, norm_all[layer][1], norm_all[layer][3]
        )
        norm_two = normed_two.astype(half)
        logits = jnp.dot(norm_two, router_all[layer], preferred_element_type=jnp.float32)
        picked = jnp.sum(logits[:, None, :] * chosen, axis=-1)
        leading = jax.nn.sigmoid(picked[:, 0] - picked[:, 1])
        gate_pair = jnp.stack([leading, 1.0 - leading], axis=-1)
        gate_rows = jnp.pad(gate_pair.T, ((0, 0), (0, model_width - token_rows)))
        sent = jnp.concatenate(
            [
                norm_two,
                jnp.zeros((padded_rows - 8 - token_rows, model_width), half),
                gate_rows.astype(half),
                jnp.zeros((6, model_width), half),
            ]
        )
        combined, *expert_saved = moe(
            False, 2 * layer, rows=sent, slots=slot_tables[layer], up=up_all[layer],
            down=down_all[layer],
        )
        out_rows = middle + combined[:token_rows]
        saved = (
            inputs, norm_one, qkv_rows, log_totals, attended, middle, norm_two, gate_pair,
            expert_saved,
        )
        return (out_rows, saved)

    def layer_backward(layer, d_out, saved):
        (
            inputs, norm_one, qkv_rows, log_totals, attended, middle, norm_two, gate_pair,
            expert_saved,
        ) = saved
        chosen = chosen_all[layer]
        gates, all_rows, hidden, slope, back_rows = expert_saved
        sent = jnp.pad(d_out.astype(half), ((0, padded_rows - token_rows), (0, 0)))
        combined, up_grad, down_grad = moe(
            True, 2 * layer + 1, rows=sent, slots=slot_tables[layer], up=up_all[layer],
            down=down_all[layer], saved=(gates, back_rows, slope, hidden, all_rows),
        )
        d_gate_rows = combined[padded_rows - 8 :, :token_rows]
        d_gate = jnp.stack([d_gate_rows[0] + d_gate_rows[1], d_gate_rows[2] + d_gate_rows[3]], axis=1)
        d_lead = (d_gate[:, 0] - d_gate[:, 1]) * gate_pair[:, 0] * gate_pair[:, 1]
        d_logits = (d_lead[:, None] * (chosen[:, 0] - chosen[:, 1])).astype(half)
        d_norm_two = combined[:token_rows] + jnp.einsum(
            "te,de->td", d_logits, router_all[layer], preferred_element_type=jnp.float32
        )
        normed_two, unit_two, inverse_two = norm_forward(
            middle, norm_all[layer][1], norm_all[layer][3]
        )
        d_middle_norm, gain_two, shift_two = norm_backward(
            d_norm_two, unit_two, inverse_two, norm_all[layer][1]
        )
        d_middle = d_out + d_middle_norm
        d_middle_half = d_middle.astype(half)
        d_attended = jnp.einsum(
            "te,de->td", d_middle_half, out_all[layer], preferred_element_type=jnp.float32
        ).astype(half)
        if local_images == 1:
            d_qkv = attend_call(qkv_rows, d_attended)
        else:
            d_qkv = attend_backward(qkv_rows, log_totals, d_attended, local_images)
        d_norm_one = jnp.einsum(
            "te,de->td", d_qkv, qkv_all[layer], preferred_element_type=jnp.float32
        )
        normed_one, unit_one, inverse_one = norm_forward(
            inputs, norm_all[layer][0], norm_all[layer][2]
        )
        d_input_norm, gain_one, shift_one = norm_backward(
            d_norm_one, unit_one, inverse_one, norm_all[layer][0]
        )
        d_input = d_middle + d_input_norm
        small = jnp.concatenate(
            [
                jnp.einsum("td,te->de", norm_two, d_logits, preferred_element_type=jnp.float32),
                jnp.stack([gain_one, gain_two, shift_one, shift_two], axis=1),
            ],
            axis=1,
        )
        return (d_input, (norm_one, d_qkv, attended, d_middle_half, small), (up_grad, down_grad))

    qkv_part, out_part = 3 * model_width // 2, model_width // 2
    small_width = round_up(expert_count + 4, 128)

    def dense_gradients(norm_one, d_qkv, attended, d_middle_half, small):
        own = jnp.concatenate([norm_one, d_qkv, attended, d_middle_half], axis=1)
        pair = jnp.concatenate([own, lax.ppermute(own, "section", swapped)], axis=0)
        d_qkv_part = lax.dynamic_slice_in_dim(
            pair, model_width + section_index * qkv_part, qkv_part, axis=1
        )
        d_out_part = lax.dynamic_slice_in_dim(
            pair, 5 * model_width + section_index * out_part, out_part, axis=1
        )
        qkv_grad = jnp.einsum(
            "td,te->de", pair[:, :model_width], d_qkv_part, preferred_element_type=jnp.float32
        )
        out_grad = jnp.einsum(
            "td,te->de", pair[:, 4 * model_width : 5 * model_width], d_out_part,
            preferred_element_type=jnp.float32,
        )
        small = jnp.pad(small, ((0, 0), (0, small_width - expert_count - 4)))
        packed_grad = jnp.concatenate(
            [qkv_grad.astype(half), out_grad.astype(half), small.astype(half)], axis=1
        )
        blocks = packed_grad.reshape(depth, groups, -1, packed_grad.shape[1]).transpose(1, 0, 2, 3)
        blocks = lax.all_to_all(blocks, "expert", split_axis=0, concat_axis=0, tiled=True)
        blocks = jnp.sum(blocks.astype(jnp.float32), axis=0).astype(half)
        blocks = lax.all_to_all(blocks, "dp", split_axis=0, concat_axis=0, tiled=True)
        return jnp.sum(blocks.astype(jnp.float32), axis=0)

    saved_list = []
    for layer in range(2):
        if layer > 0:
            stream = stream.astype(half).astype(jnp.float32)
        stream, saved = layer_forward(layer, stream)
        saved_list.append(saved)
    dense_operands = [None, None]
    expert_grads = [None, None]
    for layer in (1, 0):
        if layer < 1:
            cotangent = cotangent.astype(half).astype(jnp.float32)
        cotangent, operands, expert_grads[layer] = layer_backward(
            layer, cotangent, saved_list[layer]
        )
        dense_operands[layer] = operands

    def mine(first, second):
        return jnp.where(is_first, first, second)

    def both(first, second):
        own, away = mine(first, second), mine(second, first)
        return own, lax.ppermute(away, "section", swapped)

    if groups == 4 and model_width % (16 * depth * groups) == 0:
        operands = [
            item[:4] + (jnp.pad(item[4], ((0, 0), (0, small_width - expert_count - 4))),)
            for item in dense_operands
        ]
        shard, other_up, other_down, other_rows = finish_call(
            9, depth, groups, operands[0], operands[1], *expert_grads[0], *expert_grads[1],
            cotangent, stream,
        )
        own_up = mine(expert_grads[0][0], expert_grads[1][0])
        own_down = mine(expert_grads[0][1], expert_grads[1][1])
        own_rows = mine(cotangent, stream)
        qkv_shard = shard[:, : 3 * model_width]
        out_shard = shard[:, 3 * model_width : 4 * model_width]
        small_shard = shard[:, 4 * model_width :]
    else:
        shards = [dense_gradients(*item) for item in dense_operands]
        own_shard, other_shard = both(shards[0], shards[1])
        low, high = mine(own_shard, other_shard), mine(other_shard, own_shard)
        qkv_shard = jnp.concatenate([low[:, :qkv_part], high[:, :qkv_part]], axis=1)
        out_shard = jnp.concatenate(
            [low[:, qkv_part : qkv_part + out_part], high[:, qkv_part : qkv_part + out_part]], axis=1
        )
        small_shard = (low + high)[:, qkv_part + out_part :]
        own_up, other_up = both(expert_grads[0][0], expert_grads[1][0])
        own_down, other_down = both(expert_grads[0][1], expert_grads[1][1])
        own_rows, other_rows = both(cotangent, stream)
    norm_shard = small_shard[:, expert_count : expert_count + 4].T

    def expert_grad(own, other):
        return (own.astype(jnp.float32) + other.astype(jnp.float32))[None]

    boundary_rows = jnp.stack([mine(own_rows, other_rows), mine(other_rows, own_rows)])
    boundary_out = boundary_rows.reshape(1, MB, local_images, boundary_in.shape[3], model_width)
    return (
        boundary_out,
        norm_shard[None, 0:2],
        norm_shard[None, 2:4],
        qkv_shard[None],
        out_shard[None],
        small_shard[None, :, :expert_count],
        expert_grad(own_up, other_up),
        expert_grad(own_down, other_down),
    )


def solution(mesh):
    in_specs = (
        P("section", None, ("dp", "expert"), None, None),
        P("section", None, ("dp", "expert"), None, None),
        P("section", None, ("dp", "expert"), None, None),
        P("section", None, ("dp", "expert")),
        P("section", None, ("dp", "expert")),
        P("section", ("dp", "expert"), None),
        P("section", ("dp", "expert"), None),
        P("section", ("dp", "expert"), None),
        P("section", "expert", None, "dp"),
        P("section", "expert", "dp", None),
    )
    out_specs = (
        P("section", None, ("dp", "expert"), None, None),
        P("section", None, ("dp", "expert")),
        P("section", None, ("dp", "expert")),
        P("section", ("dp", "expert"), None),
        P("section", ("dp", "expert"), None),
        P("section", ("dp", "expert"), None),
        P("section", "expert", None, "dp"),
        P("section", "expert", "dp", None),
    )
    return jax.shard_map(
        on_device, mesh=mesh, in_specs=in_specs, out_specs=out_specs, check_vma=False
    )
```

```python
import functools
import math

import jax
import jax.numpy as jnp
from jax import lax
from jax.experimental import pallas as pl
from jax.experimental.pallas import tpu as pltpu
from jax.sharding import PartitionSpec as P

HEADS = 12
HEAD_DIM = 64
EXP_DEV = 2
MB = 2


EPS = 1e-06
SQRT_HALF = 0.7071067811865476
INV_ROOT_TAU = 0.3989422804014327
MESH = pl.DeviceIdType.MESH


def round_up(value, unit):
    return (value + unit - 1) // unit * unit


def z_order(step, z, depth):
    if depth == 1:
        return z
    direction = 1 - 2 * (z // (depth // 2))
    return lax.rem(z + step * direction + depth, depth)


def f32_dot(a, b, dims):
    return lax.dot_general(a, b, (dims, ((), ())), preferred_element_type=jnp.float32)


def moe_kernel(backward, shape, *refs):
    depth, groups, cap_rows, token_rows, model_width, hidden_width = shape
    if backward:
        (
            rows_ref, slots_ref, gates_ref, up_source, down_source, back_source, slope_source,
            hidden_source, kept_source, out_ref, up_grad_ref, down_grad_ref,
            up_ref, down_ref, back_ref, slope_ref, hidden_ref, kept_ref,
            inbox, d_pre_ref, taken_ref, raw, sent_rows, sent_back, sent_home, home, back, d_gates, *sems,
        ) = refs
    else:
        (
            rows_ref, slots_ref, up_source, down_source,
            out_ref, gates_ref, taken_target, hidden_target, slope_target, back_target,
            up_ref, down_ref, taken_ref, hidden_ref, slope_ref, back,
            inbox, raw, sent_rows, sent_back, sent_home, home, *sems,
        ) = refs
    far_send, far_recv, go_send, go_recv, back_send, back_recv, home_send, home_recv = sems[:8]
    load_sem, store_sem = sems[8:]
    half = jnp.bfloat16
    section, z, column = (
        lax.axis_index("section"), lax.axis_index("dp"), lax.axis_index("expert")
    )
    slot_count = 2 * groups * cap_rows
    tail = token_rows - 16

    def z_peer(distance):
        return (section, lax.rem(z + distance, depth), column)

    def xy_peer(distance):
        return lax.rem(column + distance, groups)

    barrier = pltpu.get_barrier_semaphore()

    def greet_z(distance, carry):
        pl.semaphore_signal(barrier, inc=1, device_id=z_peer(distance), device_id_type=MESH)
        return carry

    def greet_xy(distance, carry):
        pl.semaphore_signal(
            barrier, inc=1, device_id=(section, z, xy_peer(distance)), device_id_type=MESH
        )
        return carry

    lax.fori_loop(1, depth, greet_z, 0)
    lax.fori_loop(1, groups, greet_xy, 0)
    pl.semaphore_wait(barrier, depth - 1 + groups - 1)

    def far_copy(direction, image):
        target = lax.rem(z + 2 * direction - 1 + depth, depth)
        source = raw.at[image]
        return pltpu.make_async_remote_copy(
            src_ref=source, dst_ref=raw.at[image],
            send_sem=far_send.at[direction, image], recv_sem=far_recv.at[image],
            device_id=(section, target, column), device_id_type=MESH,
        )

    def go_copy(image, source, target):
        return pltpu.make_async_remote_copy(
            src_ref=sent_rows.at[image, target], dst_ref=inbox.at[image, source],
            send_sem=go_send.at[image, target], recv_sem=go_recv.at[image, source],
            device_id=(section, z, target), device_id_type=MESH,
        )

    def back_copy(image, source, target):
        return pltpu.make_async_remote_copy(
            src_ref=sent_back.at[image, target], dst_ref=back.at[image, source],
            send_sem=back_send.at[image, target], recv_sem=back_recv.at[image, source],
            device_id=(section, z, target), device_id_type=MESH,
        )

    def home_copy(source, target):
        return pltpu.make_async_remote_copy(
            src_ref=sent_home.at[target], dst_ref=home.at[source],
            send_sem=home_send.at[target], recv_sem=home_recv.at[source],
            device_id=(section, target, column), device_id_type=MESH,
        )

    loads = [(up_source, up_ref), (down_source, down_ref)]
    if backward:
        loads += [
            (back_source, back_ref), (slope_source, slope_ref),
            (hidden_source, hidden_ref), (kept_source, kept_ref),
        ]
    loads = [
        pltpu.make_async_copy(source, target, load_sem.at[index])
        for index, (source, target) in enumerate(loads)
    ]

    def store_copies(image):
        pairs = [
            (taken_ref.at[0, image], taken_target.at[0, image]),
            (taken_ref.at[1, image], taken_target.at[1, image]),
            (hidden_ref.at[0, image], hidden_target.at[0, image]),
            (hidden_ref.at[1, image], hidden_target.at[1, image]),
            (slope_ref.at[0, image], slope_target.at[0, image]),
            (slope_ref.at[1, image], slope_target.at[1, image]),
            (back.at[image], back_target.at[image]),
        ]
        return [
            pltpu.make_async_copy(source, target, store_sem.at[index, image])
            for index, (source, target) in enumerate(pairs)
        ]

    raw[z] = rows_ref[...]

    @pl.when(z < depth - 1)
    def _():
        far_copy(1, z).start()

    @pl.when(z > 0)
    def _():
        far_copy(0, z).start()

    for copy in loads[2:3] + loads[:2] + loads[3:]:
        copy.start()

    def match(image):
        slots = slots_ref[image][:, :token_rows]
        index = lax.broadcasted_iota(jnp.int32, (slot_count, token_rows), 0)
        return index == slots[0:1], index == slots[1:2]

    def gate_table(image):
        first, second = match(image)
        gates = gates_ref[image]
        table = jnp.where(first, gates[0:1], 0.0) + jnp.where(second, gates[1:2], 0.0)
        return table.astype(half)

    def ones_table(image):
        first, second = match(image)
        return jnp.where(first | second, 1.0, 0.0).astype(half)

    def pass_on(step):
        low, high = z - step, z + step

        @pl.when(low >= 0)
        def _():
            far_copy(1, low).wait_recv()

            @pl.when(z < depth - 1)
            def _():
                far_copy(1, low).start()

        @pl.when(high < depth)
        def _():
            far_copy(0, high).wait_recv()

            @pl.when(z > 0)
            def _():
                far_copy(0, high).start()

    def dispatch(image):
        if not backward:
            gates_ref[image] = raw[image, tail:, :token_rows].astype(jnp.float32)[8:16]
        table = gate_table(image) if backward else ones_table(image)
        rows = raw[image]
        blocks = f32_dot(table, rows, ((1,), (0,))).astype(half)
        sent_rows[image] = blocks.reshape(groups, 2 * cap_rows, model_width)

        def send(distance, carry):
            go_copy(image, column, xy_peer(distance)).start()
            return carry

        lax.fori_loop(1, groups, send, 0)
        inbox[image, column] = sent_rows[image, column]
        if backward:

            @pl.when(image == z)
            def _():
                loads[2].wait()

            first, second = match(image)
            returned = back_ref[image].reshape(slot_count, model_width)
            ones = jnp.ones((8, model_width), half)
            row_index = lax.broadcasted_iota(jnp.int32, (8, token_rows), 0)
            packed = jnp.zeros((8, token_rows), jnp.float32)
            for choice, found in enumerate((first, second)):
                table = jnp.where(found, 1.0, 0.0).astype(half)
                selected = f32_dot(table, returned, ((0,), (0,)))
                product = (selected * rows.astype(jnp.float32)).astype(half)
                sums = f32_dot(ones, product, ((1,), (1,)))
                high = sums.astype(half).astype(jnp.float32)
                packed = jnp.where(row_index == 2 * choice, high, packed)
                packed = jnp.where(row_index == 2 * choice + 1, sums - high, packed)
            d_gates[image] = packed

    def experts(image):
        def arrive(distance, carry):
            go_copy(image, xy_peer(distance), column).wait_recv()
            return carry

        lax.fori_loop(1, groups, arrive, 0)
        block = inbox[image].astype(jnp.float32)
        results = []
        for expert in range(2):
            rows = block[:, expert * cap_rows : (expert + 1) * cap_rows]
            rows = rows.reshape(groups * cap_rows, model_width).astype(half)
            taken_ref[expert, image] = rows
            if backward:
                d_hidden = f32_dot(rows, down_ref[expert], ((1,), (1,)))
                d_pre = (d_hidden * slope_ref[expert, image].astype(jnp.float32)).astype(half)
                d_pre_ref[expert, image] = d_pre
                result = f32_dot(d_pre, up_ref[expert], ((1,), (1,)))
            else:
                pre = f32_dot(rows, up_ref[expert], ((1,), (0,)))
                share = 0.5 * (1.0 + lax.erf(pre * SQRT_HALF))
                slope = share + pre * jnp.exp(-0.5 * pre * pre) * INV_ROOT_TAU
                hidden = (pre * share).astype(half)
                hidden_ref[expert, image] = hidden
                slope_ref[expert, image] = slope.astype(half)
                result = f32_dot(hidden, down_ref[expert], ((1,), (0,)))
            results.append(result.reshape(groups, cap_rows, model_width))
        sent_back[image] = jnp.concatenate(results, axis=1).astype(half)

        def send(distance, carry):
            back_copy(image, column, xy_peer(distance)).start()
            return carry

        lax.fori_loop(1, groups, send, 0)
        back[image, column] = sent_back[image, column]
        if not backward:
            for copy in store_copies(image)[:6]:
                copy.start()

    def combine(image):
        def arrive(distance, carry):
            back_copy(image, xy_peer(distance), column).wait_recv()
            return carry

        lax.fori_loop(1, groups, arrive, 0)
        if not backward:
            store_copies(image)[6].start()
        table = ones_table(image) if backward else gate_table(image)
        total = f32_dot(table, back[image].reshape(slot_count, model_width), ((0,), (0,)))
        if backward:
            extra = jnp.concatenate(
                [jnp.zeros((8, token_rows), jnp.float32), d_gates[image]], axis=0
            )

        @pl.when(image == z)
        def _():
            out_ref[...] = total
            if backward:
                out_ref[tail:, :token_rows] = total[tail:, :token_rows] + extra

        @pl.when(image != z)
        def _():
            sent_home[image] = total.astype(half)
            if backward:
                sent_home[image, tail:, :token_rows] = (
                    total[tail:, :token_rows] + extra
                ).astype(half)
            home_copy(z, image).start()

    def stage(step, carry):
        @pl.when(jnp.logical_and(step >= 1, step < depth))
        def _():
            pass_on(step)

        @pl.when(step < depth)
        def _():
            dispatch(z_order(step, z, depth))

        @pl.when(step == 2)
        def _():
            loads[0].wait()
            loads[1].wait()
            if backward:
                loads[3].wait()

        @pl.when(jnp.logical_and(step >= 2, step < depth + 2))
        def _():
            experts(z_order(lax.rem(step - 1, depth), z, depth))

        @pl.when(step >= 3)
        def _():
            combine(z_order(lax.rem(step - 2, depth), z, depth))

        return carry

    lax.fori_loop(0, depth + 3, stage, 0)

    if backward:
        loads[4].wait()
        loads[5].wait()

        def expert_gradients(expert, carry):
            kept = kept_ref[expert].reshape(depth * groups * cap_rows, model_width)
            d_pre = d_pre_ref[expert].reshape(depth * groups * cap_rows, hidden_width)
            up_grad_ref[expert] = f32_dot(kept, d_pre, ((0,), (0,))).astype(half)
            hidden = hidden_ref[expert].reshape(depth * groups * cap_rows, hidden_width)
            grads = taken_ref[expert].reshape(depth * groups * cap_rows, model_width)
            down_grad_ref[expert] = f32_dot(hidden, grads, ((0,), (0,))).astype(half)
            return carry

        lax.fori_loop(0, 2, expert_gradients, 0)

    def finish_home(distance, carry):
        source = lax.rem(z + distance, depth)
        home_copy(source, z).wait_recv()
        out_ref[...] += home[source].astype(jnp.float32)
        return carry

    lax.fori_loop(1, depth, finish_home, 0)

    def drain_home(distance, carry):
        home_copy(z, lax.rem(z + distance, depth)).wait_send()
        return carry

    lax.fori_loop(1, depth, drain_home, 0)

    def drain_image(image, carry):
        if not backward:
            for copy in store_copies(image):
                copy.wait()

        @pl.when(jnp.logical_and(z < depth - 1, image <= z))
        def _():
            far_copy(1, image).wait_send()

        @pl.when(jnp.logical_and(z > 0, image >= z))
        def _():
            far_copy(0, image).wait_send()

        def drain(distance, inner):
            go_copy(image, column, xy_peer(distance)).wait_send()
            back_copy(image, column, xy_peer(distance)).wait_send()
            return inner

        lax.fori_loop(1, groups, drain, 0)
        return carry

    lax.fori_loop(0, depth, drain_image, 0)


def moe_call(backward, call_id, depth, groups, cap_rows, rows, slots, up, down, saved=()):
    token_rows, model_width = rows.shape
    hidden_width = up.shape[2]
    half = jnp.bfloat16
    shape = (depth, groups, cap_rows, token_rows, model_width, hidden_width)
    taken = jax.ShapeDtypeStruct((2, depth, groups * cap_rows, model_width), half)
    hidden = jax.ShapeDtypeStruct((2, depth, groups * cap_rows, hidden_width), half)
    back = jax.ShapeDtypeStruct((depth, groups, 2 * cap_rows, model_width), half)
    out = jax.ShapeDtypeStruct((token_rows, model_width), jnp.float32)
    vmem, anywhere = pl.BlockSpec(memory_space=pltpu.VMEM), pl.BlockSpec(memory_space=pl.ANY)
    if backward:
        operands = (rows, slots, saved[0], up, down) + saved[1:]
        in_specs = [vmem] * 3 + [anywhere] * 6
        out_shape = (
            out, jax.ShapeDtypeStruct(up.shape, half), jax.ShapeDtypeStruct(down.shape, half)
        )
        out_specs = [vmem] * 3
        buffers = (up, down, back, hidden, hidden, taken, back, hidden, taken)
    else:
        operands = (rows, slots, up, down)
        in_specs = [vmem] * 2 + [anywhere] * 2
        gates = jax.ShapeDtypeStruct((depth, 8, token_rows), jnp.float32)
        out_shape = (out, gates, taken, hidden, hidden, back)
        out_specs = [vmem] * 2 + [anywhere] * 4
        buffers = (up, down, taken, hidden, hidden, back, back)
    scratch = [pltpu.VMEM(item.shape, half) for item in buffers]
    scratch += [
        pltpu.VMEM((depth, token_rows, model_width), half),
        pltpu.VMEM(back.shape, half),
        pltpu.VMEM(back.shape, half),
        pltpu.VMEM((depth, token_rows, model_width), half),
        pltpu.VMEM((depth, token_rows, model_width), half),
    ]
    if backward:
        scratch += [
            pltpu.VMEM(back.shape, half),
            pltpu.VMEM((depth, 8, token_rows), jnp.float32),
        ]
    scratch += [
        pltpu.SemaphoreType.DMA((2, depth)),
        pltpu.SemaphoreType.DMA((depth,)),
        pltpu.SemaphoreType.DMA((depth, groups)),
        pltpu.SemaphoreType.DMA((depth, groups)),
        pltpu.SemaphoreType.DMA((depth, groups)),
        pltpu.SemaphoreType.DMA((depth, groups)),
        pltpu.SemaphoreType.DMA((depth,)),
        pltpu.SemaphoreType.DMA((depth,)),
        pltpu.SemaphoreType.DMA((6,)),
        pltpu.SemaphoreType.DMA((7, depth)),
    ]
    return pl.pallas_call(
        functools.partial(moe_kernel, backward, shape),
        out_shape=out_shape,
        in_specs=in_specs,
        out_specs=out_specs,
        scratch_shapes=scratch,
        compiler_params=pltpu.CompilerParams(
            collective_id=call_id, has_side_effects=True, vmem_limit_bytes=50 * 2**20
        ),
        name="moe_backward" if backward else "moe_forward",
    )(*operands)

def start_kernel(shape, *refs):
    depth, groups = shape
    (
        packed_ref, up_ref, down_ref, edge_ref, table_ref,
        dense_first, dense_second, up_first, up_second, down_first, down_second,
        rows_ref, cotangent_ref, table_first, table_second,
        shard_send, shard_recv, core_send, core_recv, table_send, table_recv, own_sem,
    ) = refs
    section, z, column = (
        lax.axis_index("section"), lax.axis_index("dp"), lax.axis_index("expert")
    )
    other = (1 - section, z, column)
    is_first = section == 0

    def z_peer(distance):
        return lax.rem(z + distance, depth)

    def xy_peer(distance):
        return lax.rem(column + distance, groups)

    barrier = pltpu.get_barrier_semaphore()

    def greet_z(distance, carry):
        pl.semaphore_signal(
            barrier, inc=1, device_id=(section, z_peer(distance), column), device_id_type=MESH
        )
        return carry

    def greet_xy(distance, carry):
        pl.semaphore_signal(
            barrier, inc=1, device_id=(section, z, xy_peer(distance)), device_id_type=MESH
        )
        return carry

    pl.semaphore_signal(barrier, inc=1, device_id=other, device_id_type=MESH)
    lax.fori_loop(1, depth, greet_z, 0)
    lax.fori_loop(1, groups, greet_xy, 0)
    pl.semaphore_wait(barrier, depth + groups - 1)

    def remote(source, target, send, recv, device):
        return pltpu.make_async_remote_copy(
            src_ref=source, dst_ref=target, send_sem=send, recv_sem=recv,
            device_id=device, device_id_type=MESH,
        )

    def run(first):
        own, away = (dense_first, dense_second) if first else (dense_second, dense_first)

        def shard_copy(kind, layer, plane, lane, device):
            return remote(
                layer.at[plane, lane], layer.at[plane, lane],
                shard_send.at[kind, plane, lane],
                shard_recv.at[0, plane, lane],
                device,
            )

        def z_copy(direction, plane):
            device = (section, lax.rem(z + 2 * direction - 1 + depth, depth), column)
            return shard_copy(direction, own, plane, column, device)

        def core_copy(layer, plane, lane):
            return remote(
                layer.at[plane, lane], layer.at[plane, lane],
                shard_send.at[2, plane, lane], shard_recv.at[1, plane, lane], other,
            )

        def xy_copy(plane, source, target):
            return shard_copy(3 + target, own, plane, source, (section, z, target))

        def pass_copy(plane, source, target):
            return shard_copy(3 + groups, own, plane, source, (section, z, target))

        def swap(index, source, target):
            return remote(source, target, core_send.at[index], core_recv.at[index], other)

        def local(index, source, target):
            return pltpu.make_async_copy(source, target, own_sem.at[index])

        square = groups == 4
        beside = column + 1 - 2 * lax.rem(column, 2)
        above = lax.rem(column + 2, groups)
        across = groups - 1 - column
        direct = 3 if square else groups

        def near(distance):
            if square:
                return beside + (distance - 1) * (above - beside)
            return xy_peer(distance)

        def spread(plane):
            core_copy(own, plane, column).start()

            def send(distance, carry):
                xy_copy(plane, column, near(distance)).start()
                return carry

            lax.fori_loop(1, direct, send, 0)

        def take(plane):
            def arrive(distance, carry):
                lane = near(distance)
                xy_copy(plane, lane, column).wait_recv()
                core_copy(own, plane, lane).start()
                if square:

                    @pl.when(lax.rem(plane, 2) == distance - 1)
                    def _():
                        pass_copy(plane, lane, near(3 - distance)).start()

                return carry

            lax.fori_loop(1, direct, arrive, 0)

        own_shard = local(0, packed_ref, own.at[z, column])

        def first_copies():
            remote_ones = [
                swap(0, edge_ref.at[1], rows_ref),
                swap(1, table_ref.at[1], table_first.at[z]),
                swap(2, up_ref, up_first),
                swap(3, down_ref, down_first),
            ]
            local_ones = [
                local(1, edge_ref.at[0], rows_ref),
                local(2, table_ref.at[0], table_first.at[z]),
                local(3, up_ref, up_first),
                local(4, down_ref, down_first),
            ]
            return remote_ones, local_ones

        def second_copies():
            remote_ones = [
                swap(0, edge_ref.at[0], cotangent_ref),
                swap(1, table_ref.at[0], table_second.at[z]),
                swap(2, up_ref, up_second),
                swap(3, down_ref, down_second),
            ]
            local_ones = [
                local(1, edge_ref.at[1], cotangent_ref),
                local(2, table_ref.at[1], table_second.at[z]),
                local(3, up_ref, up_second),
                local(4, down_ref, down_second),
            ]
            return remote_ones, local_ones

        own_shard.start()
        own_shard.wait()

        @pl.when(z < depth - 1)
        def _():
            z_copy(1, z).start()

        @pl.when(z > 0)
        def _():
            z_copy(0, z).start()

        spread(z)

        first_remote, first_local = first_copies()
        second_remote, second_local = second_copies()
        out_going, in_coming = (
            (first_remote, second_remote) if first else (second_remote, first_remote)
        )
        local_ones = first_local if first else second_local
        for copy in out_going[:2] + local_ones + out_going[2:]:
            copy.start()

        def step(distance, carry):
            low, high = z - distance, z + distance

            @pl.when(low >= 0)
            def _():
                z_copy(1, low).wait_recv()

                @pl.when(z < depth - 1)
                def _():
                    z_copy(1, low).start()

                spread(low)

            @pl.when(high < depth)
            def _():
                z_copy(0, high).wait_recv()

                @pl.when(z > 0)
                def _():
                    z_copy(0, high).start()

                spread(high)

            take(z_order(distance - 1, z, depth))
            return carry

        lax.fori_loop(1, depth, step, 0)
        take(z_order(depth - 1, z, depth))

        def table_copies(source, target):
            pairs = []
            for layer, table in enumerate((table_first, table_second)):
                pairs.append(
                    remote(
                        table.at[source], table.at[source], table_send.at[layer, target],
                        table_recv.at[layer, source], (section, target, column),
                    )
                )
            return pairs

        local_ones[1].wait()
        in_coming[1].wait_recv()

        def send_tables(distance, carry):
            for copy in table_copies(z, z_peer(distance)):
                copy.start()
            return carry

        lax.fori_loop(1, depth, send_tables, 0)

        if square:

            def last_arrival(index, carry):
                plane = z_order(index, z, depth)
                pass_copy(plane, across, column).wait_recv()
                core_copy(own, plane, across).start()
                return carry

            lax.fori_loop(0, depth, last_arrival, 0)

        def drain(plane, carry):
            @pl.when(jnp.logical_and(z < depth - 1, plane <= z))
            def _():
                z_copy(1, plane).wait_send()

            @pl.when(jnp.logical_and(z > 0, plane >= z))
            def _():
                z_copy(0, plane).wait_send()

            def drain_core(lane, inner):
                core_copy(away, plane, lane).wait_recv()
                core_copy(own, plane, lane).wait_send()
                return inner

            def drain_xy(distance, inner):
                xy_copy(plane, column, near(distance)).wait_send()
                if square:

                    @pl.when(lax.rem(plane, 2) == distance - 1)
                    def _():
                        pass_copy(plane, near(distance), near(3 - distance)).wait_send()

                return inner

            lax.fori_loop(0, groups, drain_core, 0)
            return lax.fori_loop(1, direct, drain_xy, carry)

        lax.fori_loop(0, depth, drain, 0)

        for index in (0, 2, 3):
            in_coming[index].wait_recv()
        for copy in out_going:
            copy.wait_send()
        for copy in local_ones[:1] + local_ones[2:]:
            copy.wait()

        def finish_tables(distance, carry):
            for copy in table_copies(z_peer(distance), z):
                copy.wait_recv()
            for copy in table_copies(z, z_peer(distance)):
                copy.wait_send()
            return carry

        lax.fori_loop(1, depth, finish_tables, 0)

    pl.when(is_first)(functools.partial(run, True))
    pl.when(jnp.logical_not(is_first))(functools.partial(run, False))


def start_call(call_id, depth, groups, packed, up, down, edge, table):
    rows, width = packed.shape
    half = jnp.bfloat16
    out_shape = (
        jax.ShapeDtypeStruct((depth, groups, rows, width), half),
        jax.ShapeDtypeStruct((depth, groups, rows, width), half),
        jax.ShapeDtypeStruct(up.shape, half),
        jax.ShapeDtypeStruct(up.shape, half),
        jax.ShapeDtypeStruct(down.shape, half),
        jax.ShapeDtypeStruct(down.shape, half),
        jax.ShapeDtypeStruct(edge.shape[1:], jnp.float32),
        jax.ShapeDtypeStruct(edge.shape[1:], jnp.float32),
        jax.ShapeDtypeStruct((depth,) + table.shape[1:], jnp.int32),
        jax.ShapeDtypeStruct((depth,) + table.shape[1:], jnp.int32),
    )
    return pl.pallas_call(
        functools.partial(start_kernel, (depth, groups)),
        out_shape=out_shape,
        in_specs=[pl.BlockSpec(memory_space=pltpu.VMEM)] * 5,
        out_specs=[pl.BlockSpec(memory_space=pl.ANY)] * len(out_shape),
        scratch_shapes=[
            pltpu.SemaphoreType.DMA((4 + groups, depth, groups)),
            pltpu.SemaphoreType.DMA((2, depth, groups)),
            pltpu.SemaphoreType.DMA((4,)),
            pltpu.SemaphoreType.DMA((4,)),
            pltpu.SemaphoreType.DMA((2, depth)),
            pltpu.SemaphoreType.DMA((2, depth)),
            pltpu.SemaphoreType.DMA((5,)),
        ],
        compiler_params=pltpu.CompilerParams(
            collective_id=call_id, has_side_effects=True, vmem_limit_bytes=60 * 2**20
        ),
        name="start_exchange",
    )(packed, up, down, edge, table)

def finish_kernel(shape, *refs):
    depth, groups, token_rows, padded_rows, model_width = shape
    first_refs, second_refs, rest = refs[0:5], refs[5:10], refs[10:]
    (
        up_first, down_first, up_second, down_second, rows_first, rows_second,
        shard_ref, up_ref, down_ref, rows_ref,
        pair, away, small_pair, table, inbox, sent_home, home,
        core_send, core_recv, go_send, go_recv, home_send, home_recv,
    ) = rest
    half = jnp.bfloat16
    section, z, column = (
        lax.axis_index("section"), lax.axis_index("dp"), lax.axis_index("expert")
    )
    other = (1 - section, z, column)
    is_first = section == 0
    shard_rows = table.shape[1]

    def z_peer(distance):
        return lax.rem(z + distance, depth)

    def xy_peer(distance):
        return lax.rem(column + distance, groups)

    barrier = pltpu.get_barrier_semaphore()

    def greet_z(distance, carry):
        pl.semaphore_signal(
            barrier, inc=1, device_id=(section, z_peer(distance), column), device_id_type=MESH
        )
        return carry

    def greet_xy(distance, carry):
        pl.semaphore_signal(
            barrier, inc=1, device_id=(section, z, xy_peer(distance)), device_id_type=MESH
        )
        return carry

    pl.semaphore_signal(barrier, inc=1, device_id=other, device_id_type=MESH)
    lax.fori_loop(1, depth, greet_z, 0)
    lax.fori_loop(1, groups, greet_xy, 0)
    pl.semaphore_wait(barrier, depth + groups - 1)

    def swap(index, source, target):
        return pltpu.make_async_remote_copy(
            src_ref=source, dst_ref=target, send_sem=core_send.at[index],
            recv_sem=core_recv.at[index], device_id=other, device_id_type=MESH,
        )

    def pack(target, operands):
        target[padded_rows - 16 :, :] = jnp.zeros((16, target.shape[1]), half)
        offset = 0
        for operand in operands:
            width = operand.shape[1]
            target[:token_rows, offset : offset + width] = operand[...]
            offset += width

    def side_copies(first):
        if first:
            sources = (second_refs[4], up_second, down_second, rows_second)
        else:
            sources = (first_refs[4], up_first, down_first, rows_first)
        targets = (small_pair.at[1], up_ref, down_ref, rows_ref)
        return [
            swap(1 + index, source, target)
            for index, (source, target) in enumerate(zip(sources, targets))
        ]

    operand_copy = swap(0, away, pair.at[1])
    for first in (True, False):

        @pl.when(is_first if first else jnp.logical_not(is_first))
        def _():
            mine, others = (first_refs, second_refs) if first else (second_refs, first_refs)
            pack(away, others[:4])
            operand_copy.start()
            side_copies(first)[0].start()
            pack(pair.at[0], mine[:4])
            small_pair[0] = mine[4][...]

    operand_copy.wait_recv()
    rows = 2 * padded_rows

    def product(left, right, target):
        a = pair[:, :, left : left + model_width].reshape(rows, model_width)
        b = pair[:, :, right : right + model_width].reshape(rows, model_width)
        value = f32_dot(a, b, ((0,), (0,))).astype(half)
        table[:, :, target : target + model_width] = value.reshape(
            depth * groups, shard_rows, model_width
        )

    for index in range(3):
        product(0, (1 + index) * model_width, index * model_width)
    product(4 * model_width, 5 * model_width, 3 * model_width)
    for copy in side_copies(True)[:1]:
        copy.wait_recv()
    small = (small_pair[0] + small_pair[1]).astype(half)
    table[:, :, 4 * model_width :] = small.reshape(depth * groups, shard_rows, small.shape[1])

    def go_copy(plane, source, target):
        return pltpu.make_async_remote_copy(
            src_ref=table.at[plane * groups + target], dst_ref=inbox.at[plane, source],
            send_sem=go_send.at[plane, target], recv_sem=go_recv.at[plane, source],
            device_id=(section, z, target), device_id_type=MESH,
        )

    def home_copy(source, target):
        return pltpu.make_async_remote_copy(
            src_ref=sent_home.at[target], dst_ref=home.at[source],
            send_sem=home_send.at[target], recv_sem=home_recv.at[source],
            device_id=(section, target, column), device_id_type=MESH,
        )

    def send_plane(step, carry):
        plane = z_peer(step)

        def send(distance, inner):
            go_copy(plane, column, xy_peer(distance)).start()
            return inner

        return lax.fori_loop(1, groups, send, carry)

    lax.fori_loop(1, 2 + 1, send_plane, 0)

    for first in (True, False):

        @pl.when(is_first if first else jnp.logical_not(is_first))
        def _():
            for copy in side_copies(first)[1:]:
                copy.start()

    def sum_plane(step, carry):
        plane = z_peer(step)

        def arrive(distance, total):
            lane = xy_peer(distance)
            go_copy(plane, lane, column).wait_recv()
            return total + inbox[plane, lane].astype(jnp.float32)

        own = table[plane * groups + column].astype(jnp.float32)
        total = lax.fori_loop(1, groups, arrive, own)

        @pl.when(step + 2 <= depth)
        def _():
            send_plane(step + 2, 0)

        @pl.when(plane == z)
        def _():
            shard_ref[...] = total

        @pl.when(plane != z)
        def _():
            sent_home[plane] = total.astype(half)
            home_copy(z, plane).start()

        return carry

    lax.fori_loop(1, depth + 1, sum_plane, 0)

    def finish_home(distance, carry):
        source = z_peer(distance)
        home_copy(source, z).wait_recv()
        shard_ref[...] += home[source].astype(jnp.float32)
        home_copy(z, source).wait_send()
        return carry

    lax.fori_loop(1, depth, finish_home, 0)

    def drain_plane(plane, carry):
        def drain(distance, inner):
            go_copy(plane, column, xy_peer(distance)).wait_send()
            return inner

        return lax.fori_loop(1, groups, drain, carry)

    lax.fori_loop(0, depth, drain_plane, 0)
    operand_copy.wait_send()
    for index, copy in enumerate(side_copies(True)):
        copy.wait_send()
        if index > 0:
            copy.wait_recv()


def finish_call(call_id, depth, groups, first, second, up_first, down_first, up_second, down_second,
                rows_first, rows_second):
    token_rows, model_width = first[0].shape
    padded_rows = round_up(token_rows, 16)
    small_width = first[4].shape[1]
    width = 4 * model_width + small_width
    shard_rows = model_width // (depth * groups)
    half = jnp.bfloat16
    out_shape = (
        jax.ShapeDtypeStruct((shard_rows, width), jnp.float32),
        jax.ShapeDtypeStruct(up_first.shape, half),
        jax.ShapeDtypeStruct(down_first.shape, half),
        jax.ShapeDtypeStruct(rows_first.shape, jnp.float32),
    )
    home = pltpu.VMEM((depth, shard_rows, width), half)
    return pl.pallas_call(
        functools.partial(
            finish_kernel, (depth, groups, token_rows, padded_rows, model_width)
        ),
        out_shape=out_shape,
        in_specs=[pl.BlockSpec(memory_space=pltpu.VMEM)] * 16,
        out_specs=[pl.BlockSpec(memory_space=pltpu.VMEM)] + [pl.BlockSpec(memory_space=pl.ANY)] * 3,
        scratch_shapes=[
            pltpu.VMEM((2, padded_rows, 6 * model_width), half),
            pltpu.VMEM((padded_rows, 6 * model_width), half),
            pltpu.VMEM((2, model_width, small_width), jnp.float32),
            pltpu.VMEM((depth * groups, shard_rows, width), half),
            pltpu.VMEM((depth, groups, shard_rows, width), half),
            home,
            home,
            pltpu.SemaphoreType.DMA((5,)),
            pltpu.SemaphoreType.DMA((5,)),
            pltpu.SemaphoreType.DMA((depth, groups)),
            pltpu.SemaphoreType.DMA((depth, groups)),
            pltpu.SemaphoreType.DMA((depth,)),
            pltpu.SemaphoreType.DMA((depth,)),
        ],
        compiler_params=pltpu.CompilerParams(
            collective_id=call_id, has_side_effects=True, vmem_limit_bytes=50 * 2**20
        ),
        name="finish_exchange",
    )(*first, *second, up_first, down_first, up_second, down_second, rows_first, rows_second)

def head_mask(head):
    lanes = lax.broadcasted_iota(jnp.int32, (1, 2 * HEAD_DIM), 1)
    return jnp.where(lanes // HEAD_DIM == head, 1.0, 0.0).astype(jnp.bfloat16)


def attend_kernel(width, qkv_ref, out_ref):
    scale_factor = 1.0 / math.sqrt(HEAD_DIM)
    pair_width = 2 * HEAD_DIM

    def pair(index, carry):
        def columns(part):
            start = pl.multiple_of(part * width + index * pair_width, pair_width)
            return qkv_ref[:, pl.ds(start, pair_width)]

        queries, keys, values = columns(0), columns(1), columns(2)
        total = jnp.zeros(queries.shape, jnp.float32)
        for head in range(2):
            mask = head_mask(head)
            scores = f32_dot(queries * mask, keys, ((1,), (1,))) * scale_factor
            log_totals = jnp.log(jnp.sum(jnp.exp(scores), axis=1, keepdims=True))
            probs = jnp.exp(scores - log_totals).astype(jnp.bfloat16)
            total = total + f32_dot(probs, values * mask, ((1,), (0,)))
        start = pl.multiple_of(index * pair_width, pair_width)
        out_ref[:, pl.ds(start, pair_width)] = total.astype(jnp.bfloat16)
        return carry

    lax.fori_loop(0, width // pair_width, pair, 0)


def attend_backward_kernel(width, qkv_ref, d_out_ref, d_qkv_ref):
    scale_factor = 1.0 / math.sqrt(HEAD_DIM)
    pair_width = 2 * HEAD_DIM
    half = jnp.bfloat16

    def pair(index, carry):
        def place(part):
            return pl.ds(pl.multiple_of(part * width + index * pair_width, pair_width), pair_width)

        queries, keys, values = (qkv_ref[:, place(part)] for part in range(3))
        d_out = d_out_ref[:, place(0)]
        d_queries = jnp.zeros(queries.shape, jnp.float32)
        d_keys, d_values = d_queries, d_queries
        for head in range(2):
            mask = head_mask(head)
            own_queries, own_d_out = queries * mask, d_out * mask
            scores = f32_dot(keys, own_queries, ((1,), (1,))) * scale_factor
            log_totals = jnp.log(jnp.sum(jnp.exp(scores), axis=0, keepdims=True))
            probs = jnp.exp(scores - log_totals)
            d_probs = f32_dot(values, own_d_out, ((1,), (1,)))
            row_dot = jnp.sum(probs * d_probs, axis=0, keepdims=True)
            d_scores = (probs * (d_probs - row_dot) * scale_factor).astype(half)
            d_values = d_values + f32_dot(probs.astype(half), own_d_out, ((1,), (0,)))
            d_keys = d_keys + f32_dot(d_scores, own_queries, ((1,), (0,)))
            d_queries = d_queries + f32_dot(d_scores, keys * mask, ((0,), (0,)))
        for part, value in enumerate((d_queries, d_keys, d_values)):
            d_qkv_ref[:, place(part)] = value.astype(half)
        return carry

    lax.fori_loop(0, width // pair_width, pair, 0)


def attend_call(qkv_rows, d_attended=None):
    rows, width = qkv_rows.shape
    width = width // 3
    operands = (qkv_rows,) if d_attended is None else (qkv_rows, d_attended)
    kernel = attend_kernel if d_attended is None else attend_backward_kernel
    out_width = width if d_attended is None else 3 * width
    return pl.pallas_call(
        functools.partial(kernel, width),
        out_shape=jax.ShapeDtypeStruct((rows, out_width), jnp.bfloat16),
        in_specs=[pl.BlockSpec(memory_space=pltpu.VMEM)] * len(operands),
        out_specs=pl.BlockSpec(memory_space=pltpu.VMEM),
        compiler_params=pltpu.CompilerParams(vmem_limit_bytes=24 * 2**20),
        name="attend" if d_attended is None else "attend_backward",
    )(*operands)


def norm_forward(values, gain_row, shift_row):
    centred = values - jnp.mean(values, axis=-1, keepdims=True)
    variance = jnp.mean(centred * centred, axis=-1, keepdims=True)
    inverse = lax.rsqrt(variance + EPS)
    unit_rows = centred * inverse
    return (unit_rows * gain_row + shift_row, unit_rows, inverse)


def norm_backward(d_normed, unit_rows, inverse, gain_row):
    d_gain = jnp.sum(d_normed * unit_rows, axis=0)
    d_shift = jnp.sum(d_normed, axis=0)
    scaled = d_normed * gain_row
    d_values = inverse * (
        scaled
        - jnp.mean(scaled, axis=-1, keepdims=True)
        - unit_rows * jnp.mean(scaled * unit_rows, axis=-1, keepdims=True)
    )
    return (d_values, d_gain, d_shift)


def gelu_slope(pre_act):
    return (
        0.5 * (1.0 + lax.erf(pre_act * SQRT_HALF))
        + pre_act * jnp.exp(-0.5 * pre_act * pre_act) * INV_ROOT_TAU
    )


def split_heads(qkv_rows, image_count):
    feature_count = qkv_rows.shape[1] // 3
    return [
        qkv_rows[:, part_index * feature_count : (part_index + 1) * feature_count].reshape(
            image_count, -1, HEADS, HEAD_DIM
        )
        for part_index in range(3)
    ]


def attend_forward(qkv_rows, image_count):
    queries, key_rows, value_rows = split_heads(qkv_rows, image_count)
    scale_factor = 1.0 / math.sqrt(HEAD_DIM)
    scores = (
        jnp.einsum("bqhd,bkhd->bhqk", queries, key_rows, preferred_element_type=jnp.float32)
        * scale_factor
    )
    log_totals = jnp.log(jnp.sum(jnp.exp(scores), axis=-1))
    probs_half = jnp.exp(scores - log_totals[..., None]).astype(jnp.bfloat16)
    attended = jnp.einsum(
        "bhqk,bkhd->bqhd", probs_half, value_rows, preferred_element_type=jnp.float32
    )
    return (attended.astype(jnp.bfloat16).reshape(-1, HEADS * HEAD_DIM), log_totals)


def attend_backward(qkv_rows, log_totals, d_attended, image_count):
    queries, key_rows, value_rows = split_heads(qkv_rows, image_count)
    scale_factor = 1.0 / math.sqrt(HEAD_DIM)
    scores = (
        jnp.einsum("bqhd,bkhd->bhqk", queries, key_rows, preferred_element_type=jnp.float32)
        * scale_factor
    )
    probs = jnp.exp(scores - log_totals[..., None])
    probs_half = probs.astype(jnp.bfloat16)
    d_heads = d_attended.reshape(image_count, -1, HEADS, HEAD_DIM)
    d_values = jnp.einsum(
        "bhqk,bqhd->bkhd", probs_half, d_heads, preferred_element_type=jnp.float32
    )
    d_probs = jnp.einsum("bqhd,bkhd->bhqk", d_heads, value_rows, preferred_element_type=jnp.float32)
    row_dot = jnp.sum(probs * d_probs, axis=-1, keepdims=True)
    d_scores = (probs * (d_probs - row_dot) * scale_factor).astype(jnp.bfloat16)
    d_queries = jnp.einsum(
        "bhqk,bkhd->bqhd", d_scores, key_rows, preferred_element_type=jnp.float32
    )
    d_keys = jnp.einsum("bhqk,bqhd->bkhd", d_scores, queries, preferred_element_type=jnp.float32)
    feature_count = HEADS * HEAD_DIM
    joined = jnp.concatenate(
        [
            d_queries.reshape(-1, feature_count),
            d_keys.reshape(-1, feature_count),
            d_values.reshape(-1, feature_count),
        ],
        axis=1,
    )
    return joined.astype(jnp.bfloat16)


def on_device(
    boundary_in, routes, capacity_slots, ln_gain, ln_bias, w_qkv, w_out, w_router, w_up, w_down
):
    section_index = lax.axis_index("section")
    is_first = section_index == 0
    depth = lax.axis_size("dp")
    groups = lax.axis_size("expert")
    expert_count = EXP_DEV * groups
    local_images = boundary_in.shape[2]
    token_rows = local_images * boundary_in.shape[3]
    model_width = boundary_in.shape[4]
    capacity = 26 * token_rows // (16 * expert_count)
    cap_rows = round_up(capacity, 8)
    padded_rows = round_up(token_rows + 8, 16)
    half = jnp.bfloat16
    swapped = [(0, 1), (1, 0)]

    edge = boundary_in[0].reshape(MB, token_rows, model_width)
    route_rows = routes[0].reshape(MB, token_rows, 2)
    slot_rows = capacity_slots[0].reshape(MB, token_rows, 2)
    slot_index = jnp.where(slot_rows < capacity, route_rows * cap_rows + slot_rows, -1)
    table = jnp.concatenate([slot_index, route_rows], axis=2).transpose(0, 2, 1)
    table = jnp.pad(
        table, ((0, 0), (0, 4), (0, padded_rows - token_rows)), constant_values=-1
    )

    norm_columns = jnp.concatenate([ln_gain, ln_bias], axis=1).transpose(0, 2, 1)
    used = 4 * model_width + expert_count + 4
    padding = -used % 128
    packed = jnp.concatenate([w_qkv, w_out, w_router, norm_columns], axis=2)
    packed = jnp.pad(packed, ((0, 0), (0, 0), (0, padding)))
    (
        dense_first, dense_second, up_first, up_second, down_first, down_second,
        stream, cotangent, table_first, table_second,
    ) = start_call(8, depth, groups, packed[0], w_up[0], w_down[0], edge, table)
    qkv_all, out_all, router_all, norm_all = [], [], [], []

    def add_dense(item):
        qkv_all.append(item[:, : 3 * model_width])
        out_all.append(item[:, 3 * model_width : 4 * model_width])
        router_all.append(item[:, 4 * model_width : used - 4])
        norm_all.append(item[:, used - 4 : used].T.astype(jnp.float32))

    add_dense(dense_first.reshape(model_width, used + padding))
    add_dense(dense_second.reshape(model_width, used + padding))
    up_all = (up_first, up_second)
    down_all = (down_first, down_second)
    slot_tables = (table_first, table_second)
    z_index = lax.axis_index("dp")
    chosen_all = [
        (
            lax.dynamic_index_in_dim(item, z_index, 0, False)[2:4, :token_rows].T[..., None]
            == jnp.arange(expert_count, dtype=jnp.int32)
        ).astype(jnp.float32)
        for item in slot_tables
    ]
    moe = functools.partial(moe_call, depth=depth, groups=groups, cap_rows=cap_rows)

    def layer_forward(layer, inputs):
        chosen = chosen_all[layer]
        normed_one, unit_one, inverse_one = norm_forward(
            inputs, norm_all[layer][0], norm_all[layer][2]
        )
        norm_one = normed_one.astype(half)
        qkv_rows = jnp.dot(norm_one, qkv_all[layer], preferred_element_type=jnp.float32).astype(half)
        if local_images == 1:
            attended, log_totals = attend_call(qkv_rows), None
        else:
            attended, log_totals = attend_forward(qkv_rows, local_images)
        middle = inputs + jnp.dot(attended, out_all[layer], preferred_element_type=jnp.float32)
        normed_two, unit_two, inverse_two = norm_forward(
            middle, norm_all[layer][1], norm_all[layer][3]
        )
        norm_two = normed_two.astype(half)
        logits = jnp.dot(norm_two, router_all[layer], preferred_element_type=jnp.float32)
        picked = jnp.sum(logits[:, None, :] * chosen, axis=-1)
        leading = jax.nn.sigmoid(picked[:, 0] - picked[:, 1])
        gate_pair = jnp.stack([leading, 1.0 - leading], axis=-1)
        gate_rows = jnp.pad(gate_pair.T, ((0, 0), (0, model_width - token_rows)))
        sent = jnp.concatenate(
            [
                norm_two,
                jnp.zeros((padded_rows - 8 - token_rows, model_width), half),
                gate_rows.astype(half),
                jnp.zeros((6, model_width), half),
            ]
        )
        combined, *expert_saved = moe(
            False, 2 * layer, rows=sent, slots=slot_tables[layer], up=up_all[layer],
            down=down_all[layer],
        )
        out_rows = middle + combined[:token_rows]
        saved = (
            inputs, norm_one, qkv_rows, log_totals, attended, middle, norm_two, gate_pair,
            expert_saved,
        )
        return (out_rows, saved)

    def layer_backward(layer, d_out, saved):
        (
            inputs, norm_one, qkv_rows, log_totals, attended, middle, norm_two, gate_pair,
            expert_saved,
        ) = saved
        chosen = chosen_all[layer]
        gates, all_rows, hidden, slope, back_rows = expert_saved
        sent = jnp.pad(d_out.astype(half), ((0, padded_rows - token_rows), (0, 0)))
        combined, up_grad, down_grad = moe(
            True, 2 * layer + 1, rows=sent, slots=slot_tables[layer], up=up_all[layer],
            down=down_all[layer], saved=(gates, back_rows, slope, hidden, all_rows),
        )
        d_gate_rows = combined[padded_rows - 8 :, :token_rows]
        d_gate = jnp.stack([d_gate_rows[0] + d_gate_rows[1], d_gate_rows[2] + d_gate_rows[3]], axis=1)
        d_lead = (d_gate[:, 0] - d_gate[:, 1]) * gate_pair[:, 0] * gate_pair[:, 1]
        d_logits = (d_lead[:, None] * (chosen[:, 0] - chosen[:, 1])).astype(half)
        d_norm_two = combined[:token_rows] + jnp.einsum(
            "te,de->td", d_logits, router_all[layer], preferred_element_type=jnp.float32
        )
        normed_two, unit_two, inverse_two = norm_forward(
            middle, norm_all[layer][1], norm_all[layer][3]
        )
        d_middle_norm, gain_two, shift_two = norm_backward(
            d_norm_two, unit_two, inverse_two, norm_all[layer][1]
        )
        d_middle = d_out + d_middle_norm
        d_middle_half = d_middle.astype(half)
        d_attended = jnp.einsum(
            "te,de->td", d_middle_half, out_all[layer], preferred_element_type=jnp.float32
        ).astype(half)
        if local_images == 1:
            d_qkv = attend_call(qkv_rows, d_attended)
        else:
            d_qkv = attend_backward(qkv_rows, log_totals, d_attended, local_images)
        d_norm_one = jnp.einsum(
            "te,de->td", d_qkv, qkv_all[layer], preferred_element_type=jnp.float32
        )
        normed_one, unit_one, inverse_one = norm_forward(
            inputs, norm_all[layer][0], norm_all[layer][2]
        )
        d_input_norm, gain_one, shift_one = norm_backward(
            d_norm_one, unit_one, inverse_one, norm_all[layer][0]
        )
        d_input = d_middle + d_input_norm
        small = jnp.concatenate(
            [
                jnp.einsum("td,te->de", norm_two, d_logits, preferred_element_type=jnp.float32),
                jnp.stack([gain_one, gain_two, shift_one, shift_two], axis=1),
            ],
            axis=1,
        )
        return (d_input, (norm_one, d_qkv, attended, d_middle_half, small), (up_grad, down_grad))

    qkv_part, out_part = 3 * model_width // 2, model_width // 2
    small_width = round_up(expert_count + 4, 128)

    def dense_gradients(norm_one, d_qkv, attended, d_middle_half, small):
        own = jnp.concatenate([norm_one, d_qkv, attended, d_middle_half], axis=1)
        pair = jnp.concatenate([own, lax.ppermute(own, "section", swapped)], axis=0)
        d_qkv_part = lax.dynamic_slice_in_dim(
            pair, model_width + section_index * qkv_part, qkv_part, axis=1
        )
        d_out_part = lax.dynamic_slice_in_dim(
            pair, 5 * model_width + section_index * out_part, out_part, axis=1
        )
        qkv_grad = jnp.einsum(
            "td,te->de", pair[:, :model_width], d_qkv_part, preferred_element_type=jnp.float32
        )
        out_grad = jnp.einsum(
            "td,te->de", pair[:, 4 * model_width : 5 * model_width], d_out_part,
            preferred_element_type=jnp.float32,
        )
        small = jnp.pad(small, ((0, 0), (0, small_width - expert_count - 4)))
        packed_grad = jnp.concatenate(
            [qkv_grad.astype(half), out_grad.astype(half), small.astype(half)], axis=1
        )
        blocks = packed_grad.reshape(depth, groups, -1, packed_grad.shape[1]).transpose(1, 0, 2, 3)
        blocks = lax.all_to_all(blocks, "expert", split_axis=0, concat_axis=0, tiled=True)
        blocks = jnp.sum(blocks.astype(jnp.float32), axis=0).astype(half)
        blocks = lax.all_to_all(blocks, "dp", split_axis=0, concat_axis=0, tiled=True)
        return jnp.sum(blocks.astype(jnp.float32), axis=0)

    saved_list = []
    for layer in range(2):
        if layer > 0:
            stream = stream.astype(half).astype(jnp.float32)
        stream, saved = layer_forward(layer, stream)
        saved_list.append(saved)
    dense_operands = [None, None]
    expert_grads = [None, None]
    for layer in (1, 0):
        if layer < 1:
            cotangent = cotangent.astype(half).astype(jnp.float32)
        cotangent, operands, expert_grads[layer] = layer_backward(
            layer, cotangent, saved_list[layer]
        )
        dense_operands[layer] = operands

    def mine(first, second):
        return jnp.where(is_first, first, second)

    def both(first, second):
        own, away = mine(first, second), mine(second, first)
        return own, lax.ppermute(away, "section", swapped)

    if model_width % (16 * depth * groups) == 0:
        operands = [
            item[:4] + (jnp.pad(item[4], ((0, 0), (0, small_width - expert_count - 4))),)
            for item in dense_operands
        ]
        shard, other_up, other_down, other_rows = finish_call(
            9, depth, groups, operands[0], operands[1], *expert_grads[0], *expert_grads[1],
            cotangent, stream,
        )
        own_up = mine(expert_grads[0][0], expert_grads[1][0])
        own_down = mine(expert_grads[0][1], expert_grads[1][1])
        own_rows = mine(cotangent, stream)
        qkv_shard = shard[:, : 3 * model_width]
        out_shard = shard[:, 3 * model_width : 4 * model_width]
        small_shard = shard[:, 4 * model_width :]
    else:
        shards = [dense_gradients(*item) for item in dense_operands]
        own_shard, other_shard = both(shards[0], shards[1])
        low, high = mine(own_shard, other_shard), mine(other_shard, own_shard)
        qkv_shard = jnp.concatenate([low[:, :qkv_part], high[:, :qkv_part]], axis=1)
        out_shard = jnp.concatenate(
            [low[:, qkv_part : qkv_part + out_part], high[:, qkv_part : qkv_part + out_part]], axis=1
        )
        small_shard = (low + high)[:, qkv_part + out_part :]
        own_up, other_up = both(expert_grads[0][0], expert_grads[1][0])
        own_down, other_down = both(expert_grads[0][1], expert_grads[1][1])
        own_rows, other_rows = both(cotangent, stream)
    norm_shard = small_shard[:, expert_count : expert_count + 4].T

    def expert_grad(own, other):
        return (own.astype(jnp.float32) + other.astype(jnp.float32))[None]

    boundary_rows = jnp.stack([mine(own_rows, other_rows), mine(other_rows, own_rows)])
    boundary_out = boundary_rows.reshape(1, MB, local_images, boundary_in.shape[3], model_width)
    return (
        boundary_out,
        norm_shard[None, 0:2],
        norm_shard[None, 2:4],
        qkv_shard[None],
        out_shard[None],
        small_shard[None, :, :expert_count],
        expert_grad(own_up, other_up),
        expert_grad(own_down, other_down),
    )


def solution(mesh):
    in_specs = (
        P("section", None, ("dp", "expert"), None, None),
        P("section", None, ("dp", "expert"), None, None),
        P("section", None, ("dp", "expert"), None, None),
        P("section", None, ("dp", "expert")),
        P("section", None, ("dp", "expert")),
        P("section", ("dp", "expert"), None),
        P("section", ("dp", "expert"), None),
        P("section", ("dp", "expert"), None),
        P("section", "expert", None, "dp"),
        P("section", "expert", "dp", None),
    )
    out_specs = (
        P("section", None, ("dp", "expert"), None, None),
        P("section", None, ("dp", "expert")),
        P("section", None, ("dp", "expert")),
        P("section", ("dp", "expert"), None),
        P("section", ("dp", "expert"), None),
        P("section", ("dp", "expert"), None),
        P("section", "expert", None, "dp"),
        P("section", "expert", "dp", None),
    )
    return jax.shard_map(
        on_device, mesh=mesh, in_specs=in_specs, out_specs=out_specs, check_vma=False
    )
```

```python
import functools
import math

import jax
import jax.numpy as jnp
from jax import lax
from jax.experimental import pallas as pl
from jax.experimental.pallas import tpu as pltpu
from jax.sharding import PartitionSpec as P

HEADS = 12
HEAD_DIM = 64
EXP_DEV = 2
MB = 2


EPS = 1e-06
SQRT_HALF = 0.7071067811865476
INV_ROOT_TAU = 0.3989422804014327
MESH = pl.DeviceIdType.MESH


def round_up(value, unit):
    return (value + unit - 1) // unit * unit


def z_order(step, z, depth):
    if depth == 1:
        return z
    direction = 1 - 2 * (z // (depth // 2))
    return lax.rem(z + step * direction + depth, depth)


def f32_dot(a, b, dims):
    return lax.dot_general(a, b, (dims, ((), ())), preferred_element_type=jnp.float32)


def moe_kernel(backward, shape, *refs):
    depth, groups, cap_rows, token_rows, model_width, hidden_width = shape
    if backward:
        (
            rows_ref, slots_ref, gates_ref, up_source, down_source, back_source, slope_source,
            hidden_source, kept_source, out_ref, up_grad_ref, down_grad_ref,
            up_ref, down_ref, back_ref, slope_ref, hidden_ref, kept_ref,
            inbox, d_pre_ref, taken_ref, raw, sent_rows, sent_back, sent_home, home, back, d_gates, *sems,
        ) = refs
    else:
        (
            rows_ref, slots_ref, up_source, down_source,
            out_ref, gates_ref, taken_target, hidden_target, slope_target, back_target,
            up_ref, down_ref, taken_ref, hidden_ref, slope_ref, back,
            inbox, raw, sent_rows, sent_back, sent_home, home, *sems,
        ) = refs
    far_send, far_recv, go_send, go_recv, back_send, back_recv, home_send, home_recv = sems[:8]
    load_sem, store_sem = sems[8:]
    half = jnp.bfloat16
    section, z, column = (
        lax.axis_index("section"), lax.axis_index("dp"), lax.axis_index("expert")
    )
    slot_count = 2 * groups * cap_rows
    tail = token_rows - 16

    def z_peer(distance):
        return (section, lax.rem(z + distance, depth), column)

    def xy_peer(distance):
        if groups == 4 and not backward:
            across = 3 - column
            beside = column + 1 - 2 * lax.rem(column, 2)
            above = lax.rem(column + 2, 4)
            last = (distance - 1) * (distance - 2) // 2
            middle = (distance - 1) * (3 - distance)
            first = (2 - distance) * (3 - distance) // 2
            return first * across + middle * beside + last * above
        return lax.rem(column + distance, groups)

    barrier = pltpu.get_barrier_semaphore()

    def greet_z(distance, carry):
        pl.semaphore_signal(barrier, inc=1, device_id=z_peer(distance), device_id_type=MESH)
        return carry

    def greet_xy(distance, carry):
        pl.semaphore_signal(
            barrier, inc=1, device_id=(section, z, xy_peer(distance)), device_id_type=MESH
        )
        return carry

    lax.fori_loop(1, depth, greet_z, 0)
    lax.fori_loop(1, groups, greet_xy, 0)
    pl.semaphore_wait(barrier, depth - 1 + groups - 1)

    def far_copy(direction, image):
        target = lax.rem(z + 2 * direction - 1 + depth, depth)
        source = raw.at[image]
        return pltpu.make_async_remote_copy(
            src_ref=source, dst_ref=raw.at[image],
            send_sem=far_send.at[direction, image], recv_sem=far_recv.at[image],
            device_id=(section, target, column), device_id_type=MESH,
        )

    def go_copy(image, source, target):
        return pltpu.make_async_remote_copy(
            src_ref=sent_rows.at[image, target], dst_ref=inbox.at[image, source],
            send_sem=go_send.at[image, target], recv_sem=go_recv.at[image, source],
            device_id=(section, z, target), device_id_type=MESH,
        )

    def back_copy(image, source, target):
        return pltpu.make_async_remote_copy(
            src_ref=sent_back.at[image, target], dst_ref=back.at[image, source],
            send_sem=back_send.at[image, target], recv_sem=back_recv.at[image, source],
            device_id=(section, z, target), device_id_type=MESH,
        )

    def home_copy(source, target):
        return pltpu.make_async_remote_copy(
            src_ref=sent_home.at[target], dst_ref=home.at[source],
            send_sem=home_send.at[target], recv_sem=home_recv.at[source],
            device_id=(section, target, column), device_id_type=MESH,
        )

    loads = [(up_source, up_ref), (down_source, down_ref)]
    if backward:
        loads += [
            (back_source, back_ref), (slope_source, slope_ref),
            (hidden_source, hidden_ref), (kept_source, kept_ref),
        ]
    loads = [
        pltpu.make_async_copy(source, target, load_sem.at[index])
        for index, (source, target) in enumerate(loads)
    ]

    def store_copies(image):
        pairs = [
            (taken_ref.at[0, image], taken_target.at[0, image]),
            (taken_ref.at[1, image], taken_target.at[1, image]),
            (hidden_ref.at[0, image], hidden_target.at[0, image]),
            (hidden_ref.at[1, image], hidden_target.at[1, image]),
            (slope_ref.at[0, image], slope_target.at[0, image]),
            (slope_ref.at[1, image], slope_target.at[1, image]),
            (back.at[image], back_target.at[image]),
        ]
        return [
            pltpu.make_async_copy(source, target, store_sem.at[index, image])
            for index, (source, target) in enumerate(pairs)
        ]

    if backward:
        raw[z, tail:] = jnp.zeros((16, model_width), half)
        raw[z, : rows_ref.shape[0]] = rows_ref[...]
    else:
        raw[z] = rows_ref[...]

    @pl.when(z < depth - 1)
    def _():
        far_copy(1, z).start()

    @pl.when(z > 0)
    def _():
        far_copy(0, z).start()

    for copy in loads[2:3] + loads[:2] + loads[3:]:
        copy.start()

    def match(image):
        slots = slots_ref[image][:, :token_rows]
        index = lax.broadcasted_iota(jnp.int32, (slot_count, token_rows), 0)
        return index == slots[0:1], index == slots[1:2]

    def gate_table(image):
        first, second = match(image)
        gates = gates_ref[image]
        table = jnp.where(first, gates[0:1], 0.0) + jnp.where(second, gates[1:2], 0.0)
        return table.astype(half)

    def ones_table(image):
        first, second = match(image)
        return jnp.where(first | second, 1.0, 0.0).astype(half)

    def pass_on(step):
        low, high = z - step, z + step

        @pl.when(low >= 0)
        def _():
            far_copy(1, low).wait_recv()

            @pl.when(z < depth - 1)
            def _():
                far_copy(1, low).start()

        @pl.when(high < depth)
        def _():
            far_copy(0, high).wait_recv()

            @pl.when(z > 0)
            def _():
                far_copy(0, high).start()

    def dispatch(image):
        if not backward:
            gates_ref[image] = raw[image, tail:, :token_rows].astype(jnp.float32)[8:16]
        table = gate_table(image) if backward else ones_table(image)
        rows = raw[image]
        blocks = f32_dot(table, rows, ((1,), (0,))).astype(half)
        sent_rows[image] = blocks.reshape(groups, 2 * cap_rows, model_width)

        def send(distance, carry):
            go_copy(image, column, xy_peer(distance)).start()
            return carry

        lax.fori_loop(1, groups, send, 0)
        inbox[image, column] = sent_rows[image, column]
        if backward:

            @pl.when(image == z)
            def _():
                loads[2].wait()

            first, second = match(image)
            returned = back_ref[image].reshape(slot_count, model_width)
            ones = jnp.ones((8, model_width), half)
            row_index = lax.broadcasted_iota(jnp.int32, (8, token_rows), 0)
            packed = jnp.zeros((8, token_rows), jnp.float32)
            for choice, found in enumerate((first, second)):
                table = jnp.where(found, 1.0, 0.0).astype(half)
                selected = f32_dot(table, returned, ((0,), (0,)))
                product = (selected * rows.astype(jnp.float32)).astype(half)
                sums = f32_dot(ones, product, ((1,), (1,)))
                high = sums.astype(half).astype(jnp.float32)
                packed = jnp.where(row_index == 2 * choice, high, packed)
                packed = jnp.where(row_index == 2 * choice + 1, sums - high, packed)
            d_gates[image] = packed

    def experts(image):
        def arrive(distance, carry):
            go_copy(image, xy_peer(distance), column).wait_recv()
            return carry

        lax.fori_loop(1, groups, arrive, 0)
        block = inbox[image].astype(jnp.float32)
        results = []
        for expert in range(2):
            rows = block[:, expert * cap_rows : (expert + 1) * cap_rows]
            rows = rows.reshape(groups * cap_rows, model_width).astype(half)
            taken_ref[expert, image] = rows
            if backward:
                d_hidden = f32_dot(rows, down_ref[expert], ((1,), (1,)))
                d_pre = (d_hidden * slope_ref[expert, image].astype(jnp.float32)).astype(half)
                d_pre_ref[expert, image] = d_pre
                result = f32_dot(d_pre, up_ref[expert], ((1,), (1,)))
            else:
                pre = f32_dot(rows, up_ref[expert], ((1,), (0,)))
                share = 0.5 * (1.0 + lax.erf(pre * SQRT_HALF))
                slope = share + pre * jnp.exp(-0.5 * pre * pre) * INV_ROOT_TAU
                hidden = (pre * share).astype(half)
                hidden_ref[expert, image] = hidden
                slope_ref[expert, image] = slope.astype(half)
                result = f32_dot(hidden, down_ref[expert], ((1,), (0,)))
            results.append(result.reshape(groups, cap_rows, model_width))
        sent_back[image] = jnp.concatenate(results, axis=1).astype(half)

        def send(distance, carry):
            back_copy(image, column, xy_peer(distance)).start()
            return carry

        lax.fori_loop(1, groups, send, 0)
        back[image, column] = sent_back[image, column]
        if not backward:
            for copy in store_copies(image)[:6]:
                copy.start()

    def combine(image):
        def arrive(distance, carry):
            back_copy(image, xy_peer(distance), column).wait_recv()
            return carry

        lax.fori_loop(1, groups, arrive, 0)
        if not backward:
            store_copies(image)[6].start()
        table = ones_table(image) if backward else gate_table(image)
        total = f32_dot(table, back[image].reshape(slot_count, model_width), ((0,), (0,)))
        if backward:
            extra = jnp.concatenate(
                [jnp.zeros((8, token_rows), jnp.float32), d_gates[image]], axis=0
            )

        @pl.when(image == z)
        def _():
            out_ref[...] = total
            if backward:
                out_ref[tail:, :token_rows] = total[tail:, :token_rows] + extra

        @pl.when(image != z)
        def _():
            sent_home[image] = total.astype(half)
            if backward:
                sent_home[image, tail:, :token_rows] = (
                    total[tail:, :token_rows] + extra
                ).astype(half)
            home_copy(z, image).start()

    def stage(step, carry):
        @pl.when(jnp.logical_and(step >= 1, step < depth))
        def _():
            pass_on(step)

        @pl.when(step < depth)
        def _():
            dispatch(z_order(step, z, depth))

        @pl.when(step == 2)
        def _():
            loads[0].wait()
            loads[1].wait()
            if backward:
                loads[3].wait()

        @pl.when(jnp.logical_and(step >= 2, step < depth + 2))
        def _():
            experts(z_order(lax.rem(step - 1, depth), z, depth))

        @pl.when(step >= 3)
        def _():
            combine(z_order(lax.rem(step - 2, depth), z, depth))

        return carry

    lax.fori_loop(0, depth + 3, stage, 0)

    if backward:
        loads[4].wait()
        loads[5].wait()

        def expert_gradients(expert, carry):
            kept = kept_ref[expert].reshape(depth * groups * cap_rows, model_width)
            d_pre = d_pre_ref[expert].reshape(depth * groups * cap_rows, hidden_width)
            up_grad_ref[expert] = f32_dot(kept, d_pre, ((0,), (0,))).astype(half)
            hidden = hidden_ref[expert].reshape(depth * groups * cap_rows, hidden_width)
            grads = taken_ref[expert].reshape(depth * groups * cap_rows, model_width)
            down_grad_ref[expert] = f32_dot(hidden, grads, ((0,), (0,))).astype(half)
            return carry

        lax.fori_loop(0, 2, expert_gradients, 0)

    def finish_home(distance, carry):
        source = lax.rem(z + distance, depth)
        home_copy(source, z).wait_recv()
        out_ref[...] += home[source].astype(jnp.float32)
        return carry

    lax.fori_loop(1, depth, finish_home, 0)

    def drain_home(distance, carry):
        home_copy(z, lax.rem(z + distance, depth)).wait_send()
        return carry

    lax.fori_loop(1, depth, drain_home, 0)

    def drain_image(image, carry):
        if not backward:
            for copy in store_copies(image):
                copy.wait()

        @pl.when(jnp.logical_and(z < depth - 1, image <= z))
        def _():
            far_copy(1, image).wait_send()

        @pl.when(jnp.logical_and(z > 0, image >= z))
        def _():
            far_copy(0, image).wait_send()

        def drain(distance, inner):
            go_copy(image, column, xy_peer(distance)).wait_send()
            back_copy(image, column, xy_peer(distance)).wait_send()
            return inner

        lax.fori_loop(1, groups, drain, 0)
        return carry

    lax.fori_loop(0, depth, drain_image, 0)


def moe_call(backward, call_id, depth, groups, cap_rows, rows, slots, up, down, saved=()):
    model_width = rows.shape[1]
    token_rows = saved[0].shape[2] if backward else rows.shape[0]
    hidden_width = up.shape[2]
    half = jnp.bfloat16
    shape = (depth, groups, cap_rows, token_rows, model_width, hidden_width)
    taken = jax.ShapeDtypeStruct((2, depth, groups * cap_rows, model_width), half)
    hidden = jax.ShapeDtypeStruct((2, depth, groups * cap_rows, hidden_width), half)
    back = jax.ShapeDtypeStruct((depth, groups, 2 * cap_rows, model_width), half)
    out = jax.ShapeDtypeStruct((token_rows, model_width), jnp.float32)
    vmem, anywhere = pl.BlockSpec(memory_space=pltpu.VMEM), pl.BlockSpec(memory_space=pl.ANY)
    if backward:
        operands = (rows, slots, saved[0], up, down) + saved[1:]
        in_specs = [vmem] * 3 + [anywhere] * 6
        out_shape = (
            out, jax.ShapeDtypeStruct(up.shape, half), jax.ShapeDtypeStruct(down.shape, half)
        )
        out_specs = [vmem] * 3
        buffers = (up, down, back, hidden, hidden, taken, back, hidden, taken)
    else:
        operands = (rows, slots, up, down)
        in_specs = [vmem] * 2 + [anywhere] * 2
        gates = jax.ShapeDtypeStruct((depth, 8, token_rows), jnp.float32)
        out_shape = (out, gates, taken, hidden, hidden, back)
        out_specs = [vmem] * 2 + [anywhere] * 4
        buffers = (up, down, taken, hidden, hidden, back, back)
    scratch = [pltpu.VMEM(item.shape, half) for item in buffers]
    scratch += [
        pltpu.VMEM((depth, token_rows, model_width), half),
        pltpu.VMEM(back.shape, half),
        pltpu.VMEM(back.shape, half),
        pltpu.VMEM((depth, token_rows, model_width), half),
        pltpu.VMEM((depth, token_rows, model_width), half),
    ]
    if backward:
        scratch += [
            pltpu.VMEM(back.shape, half),
            pltpu.VMEM((depth, 8, token_rows), jnp.float32),
        ]
    scratch += [
        pltpu.SemaphoreType.DMA((2, depth)),
        pltpu.SemaphoreType.DMA((depth,)),
        pltpu.SemaphoreType.DMA((depth, groups)),
        pltpu.SemaphoreType.DMA((depth, groups)),
        pltpu.SemaphoreType.DMA((depth, groups)),
        pltpu.SemaphoreType.DMA((depth, groups)),
        pltpu.SemaphoreType.DMA((depth,)),
        pltpu.SemaphoreType.DMA((depth,)),
        pltpu.SemaphoreType.DMA((6,)),
        pltpu.SemaphoreType.DMA((7, depth)),
    ]
    return pl.pallas_call(
        functools.partial(moe_kernel, backward, shape),
        out_shape=out_shape,
        in_specs=in_specs,
        out_specs=out_specs,
        scratch_shapes=scratch,
        compiler_params=pltpu.CompilerParams(
            collective_id=call_id, has_side_effects=True, vmem_limit_bytes=50 * 2**20
        ),
        name=("mb_" if backward else "mf_")+"wD",
    )(*operands)

def start_kernel(shape, *refs):
    depth, groups = shape
    (
        packed_ref, up_ref, down_ref, edge_ref, table_ref,
        dense_first, dense_second, up_first, up_second, down_first, down_second,
        rows_ref, cotangent_ref, table_first, table_second,
        shard_send, shard_recv, core_send, core_recv, table_send, table_recv, own_sem,
    ) = refs
    section, z, column = (
        lax.axis_index("section"), lax.axis_index("dp"), lax.axis_index("expert")
    )
    other = (1 - section, z, column)
    is_first = section == 0

    def z_peer(distance):
        return lax.rem(z + distance, depth)

    def xy_peer(distance):
        return lax.rem(column + distance, groups)

    barrier = pltpu.get_barrier_semaphore()

    def greet_z(distance, carry):
        pl.semaphore_signal(
            barrier, inc=1, device_id=(section, z_peer(distance), column), device_id_type=MESH
        )
        return carry

    def greet_xy(distance, carry):
        pl.semaphore_signal(
            barrier, inc=1, device_id=(section, z, xy_peer(distance)), device_id_type=MESH
        )
        return carry

    pl.semaphore_signal(barrier, inc=1, device_id=other, device_id_type=MESH)
    lax.fori_loop(1, depth, greet_z, 0)
    lax.fori_loop(1, groups, greet_xy, 0)
    pl.semaphore_wait(barrier, depth + groups - 1)

    def remote(source, target, send, recv, device):
        return pltpu.make_async_remote_copy(
            src_ref=source, dst_ref=target, send_sem=send, recv_sem=recv,
            device_id=device, device_id_type=MESH,
        )

    def run(first):
        own, away = (dense_first, dense_second) if first else (dense_second, dense_first)

        def shard_copy(kind, layer, plane, lane, device):
            return remote(
                layer.at[plane, lane], layer.at[plane, lane],
                shard_send.at[kind, plane, lane],
                shard_recv.at[0, plane, lane],
                device,
            )

        def z_copy(direction, plane):
            device = (section, lax.rem(z + 2 * direction - 1 + depth, depth), column)
            return shard_copy(direction, own, plane, column, device)

        def core_copy(layer, plane, lane):
            return remote(
                layer.at[plane, lane], layer.at[plane, lane],
                shard_send.at[2, plane, lane], shard_recv.at[1, plane, lane], other,
            )

        def xy_copy(plane, source, target):
            return shard_copy(3 + target, own, plane, source, (section, z, target))

        def pass_copy(plane, source, target):
            return shard_copy(3 + groups, own, plane, source, (section, z, target))

        def swap(index, source, target):
            return remote(source, target, core_send.at[index], core_recv.at[index], other)

        def local(index, source, target):
            return pltpu.make_async_copy(source, target, own_sem.at[index])

        square = groups == 4
        beside = column + 1 - 2 * lax.rem(column, 2)
        above = lax.rem(column + 2, groups)
        across = groups - 1 - column
        direct = 3 if square else groups

        def near(distance):
            if square:
                return beside + (distance - 1) * (above - beside)
            return xy_peer(distance)

        def spread(plane):
            core_copy(own, plane, column).start()

            def send(distance, carry):
                xy_copy(plane, column, near(distance)).start()
                return carry

            lax.fori_loop(1, direct, send, 0)

        def take(plane):
            def arrive(distance, carry):
                lane = near(distance)
                xy_copy(plane, lane, column).wait_recv()
                core_copy(own, plane, lane).start()
                if square:

                    @pl.when(lax.rem(plane, 2) == distance - 1)
                    def _():
                        pass_copy(plane, lane, near(3 - distance)).start()

                return carry

            lax.fori_loop(1, direct, arrive, 0)

        own_shard = local(0, packed_ref, own.at[z, column])

        def first_copies():
            remote_ones = [
                swap(0, edge_ref.at[1], rows_ref),
                swap(1, table_ref.at[1], table_first.at[z]),
                swap(2, up_ref, up_first),
                swap(3, down_ref, down_first),
            ]
            local_ones = [
                local(1, edge_ref.at[0], rows_ref),
                local(2, table_ref.at[0], table_first.at[z]),
                local(3, up_ref, up_first),
                local(4, down_ref, down_first),
            ]
            return remote_ones, local_ones

        def second_copies():
            remote_ones = [
                swap(0, edge_ref.at[0], cotangent_ref),
                swap(1, table_ref.at[0], table_second.at[z]),
                swap(2, up_ref, up_second),
                swap(3, down_ref, down_second),
            ]
            local_ones = [
                local(1, edge_ref.at[1], cotangent_ref),
                local(2, table_ref.at[1], table_second.at[z]),
                local(3, up_ref, up_second),
                local(4, down_ref, down_second),
            ]
            return remote_ones, local_ones

        own_shard.start()
        own_shard.wait()

        @pl.when(z < depth - 1)
        def _():
            z_copy(1, z).start()

        @pl.when(z > 0)
        def _():
            z_copy(0, z).start()

        spread(z)

        first_remote, first_local = first_copies()
        second_remote, second_local = second_copies()
        out_going, in_coming = (
            (first_remote, second_remote) if first else (second_remote, first_remote)
        )
        local_ones = first_local if first else second_local
        for copy in out_going[:2] + local_ones + out_going[2:]:
            copy.start()

        def step(distance, carry):
            low, high = z - distance, z + distance

            @pl.when(low >= 0)
            def _():
                z_copy(1, low).wait_recv()

                @pl.when(z < depth - 1)
                def _():
                    z_copy(1, low).start()

                spread(low)

            @pl.when(high < depth)
            def _():
                z_copy(0, high).wait_recv()

                @pl.when(z > 0)
                def _():
                    z_copy(0, high).start()

                spread(high)

            take(z_order(distance - 1, z, depth))
            return carry

        lax.fori_loop(1, depth, step, 0)
        take(z_order(depth - 1, z, depth))

        def table_copies(source, target):
            pairs = []
            for layer, table in enumerate((table_first, table_second)):
                pairs.append(
                    remote(
                        table.at[source], table.at[source], table_send.at[layer, target],
                        table_recv.at[layer, source], (section, target, column),
                    )
                )
            return pairs

        local_ones[1].wait()
        in_coming[1].wait_recv()

        def send_tables(distance, carry):
            for copy in table_copies(z, z_peer(distance)):
                copy.start()
            return carry

        lax.fori_loop(1, depth, send_tables, 0)

        if square:

            def last_arrival(index, carry):
                plane = z_order(index, z, depth)
                pass_copy(plane, across, column).wait_recv()
                core_copy(own, plane, across).start()
                return carry

            lax.fori_loop(0, depth, last_arrival, 0)

        def drain(plane, carry):
            @pl.when(jnp.logical_and(z < depth - 1, plane <= z))
            def _():
                z_copy(1, plane).wait_send()

            @pl.when(jnp.logical_and(z > 0, plane >= z))
            def _():
                z_copy(0, plane).wait_send()

            def drain_core(lane, inner):
                core_copy(away, plane, lane).wait_recv()
                core_copy(own, plane, lane).wait_send()
                return inner

            def drain_xy(distance, inner):
                xy_copy(plane, column, near(distance)).wait_send()
                if square:

                    @pl.when(lax.rem(plane, 2) == distance - 1)
                    def _():
                        pass_copy(plane, near(distance), near(3 - distance)).wait_send()

                return inner

            lax.fori_loop(0, groups, drain_core, 0)
            return lax.fori_loop(1, direct, drain_xy, carry)

        lax.fori_loop(0, depth, drain, 0)

        for index in (0, 2, 3):
            in_coming[index].wait_recv()
        for copy in out_going:
            copy.wait_send()
        for copy in local_ones[:1] + local_ones[2:]:
            copy.wait()

        def finish_tables(distance, carry):
            for copy in table_copies(z_peer(distance), z):
                copy.wait_recv()
            for copy in table_copies(z, z_peer(distance)):
                copy.wait_send()
            return carry

        lax.fori_loop(1, depth, finish_tables, 0)

    pl.when(is_first)(functools.partial(run, True))
    pl.when(jnp.logical_not(is_first))(functools.partial(run, False))


def start_call(call_id, depth, groups, packed, up, down, edge, table):
    rows, width = packed.shape
    half = jnp.bfloat16
    out_shape = (
        jax.ShapeDtypeStruct((depth, groups, rows, width), half),
        jax.ShapeDtypeStruct((depth, groups, rows, width), half),
        jax.ShapeDtypeStruct(up.shape, half),
        jax.ShapeDtypeStruct(up.shape, half),
        jax.ShapeDtypeStruct(down.shape, half),
        jax.ShapeDtypeStruct(down.shape, half),
        jax.ShapeDtypeStruct(edge.shape[1:], jnp.float32),
        jax.ShapeDtypeStruct(edge.shape[1:], jnp.float32),
        jax.ShapeDtypeStruct((depth,) + table.shape[1:], jnp.int32),
        jax.ShapeDtypeStruct((depth,) + table.shape[1:], jnp.int32),
    )
    return pl.pallas_call(
        functools.partial(start_kernel, (depth, groups)),
        out_shape=out_shape,
        in_specs=[pl.BlockSpec(memory_space=pltpu.VMEM)] * 5,
        out_specs=[pl.BlockSpec(memory_space=pl.ANY)] * len(out_shape),
        scratch_shapes=[
            pltpu.SemaphoreType.DMA((4 + groups, depth, groups)),
            pltpu.SemaphoreType.DMA((2, depth, groups)),
            pltpu.SemaphoreType.DMA((4,)),
            pltpu.SemaphoreType.DMA((4,)),
            pltpu.SemaphoreType.DMA((2, depth)),
            pltpu.SemaphoreType.DMA((2, depth)),
            pltpu.SemaphoreType.DMA((5,)),
        ],
        compiler_params=pltpu.CompilerParams(
            collective_id=call_id, has_side_effects=True, vmem_limit_bytes=60 * 2**20
        ),
        name="start_exchange",
    )(packed, up, down, edge, table)

def finish_kernel(shape, *refs):
    depth, groups, token_rows, padded_rows, model_width = shape
    first_refs, second_refs, rest = refs[0:5], refs[5:10], refs[10:]
    (
        up_first, down_first, up_second, down_second, rows_first, rows_second,
        shard_ref, up_ref, down_ref, rows_ref,
        pair, away, small_pair, table, inbox, sent_home, home,
        core_send, core_recv, go_send, go_recv, home_send, home_recv,
    ) = rest
    half = jnp.bfloat16
    section, z, column = (
        lax.axis_index("section"), lax.axis_index("dp"), lax.axis_index("expert")
    )
    other = (1 - section, z, column)
    is_first = section == 0
    shard_rows = table.shape[1]

    def z_peer(distance):
        return lax.rem(z + distance, depth)

    def xy_peer(distance):
        return lax.rem(column + distance, groups)

    barrier = pltpu.get_barrier_semaphore()

    def greet_z(distance, carry):
        pl.semaphore_signal(
            barrier, inc=1, device_id=(section, z_peer(distance), column), device_id_type=MESH
        )
        return carry

    def greet_xy(distance, carry):
        pl.semaphore_signal(
            barrier, inc=1, device_id=(section, z, xy_peer(distance)), device_id_type=MESH
        )
        return carry

    pl.semaphore_signal(barrier, inc=1, device_id=other, device_id_type=MESH)
    lax.fori_loop(1, depth, greet_z, 0)
    lax.fori_loop(1, groups, greet_xy, 0)
    pl.semaphore_wait(barrier, depth + groups - 1)

    def swap(index, source, target):
        return pltpu.make_async_remote_copy(
            src_ref=source, dst_ref=target, send_sem=core_send.at[index],
            recv_sem=core_recv.at[index], device_id=other, device_id_type=MESH,
        )

    def pack(target, operands):
        target[padded_rows - 16 :, :] = jnp.zeros((16, target.shape[1]), half)
        offset = 0
        for operand in operands:
            width = operand.shape[1]
            target[:token_rows, offset : offset + width] = operand[...]
            offset += width

    def side_copies(first):
        if first:
            sources = (second_refs[4], up_second, down_second, rows_second)
        else:
            sources = (first_refs[4], up_first, down_first, rows_first)
        targets = (small_pair.at[1], up_ref, down_ref, rows_ref)
        return [
            swap(1 + index, source, target)
            for index, (source, target) in enumerate(zip(sources, targets))
        ]

    operand_copy = swap(0, away, pair.at[1])
    for first in (True, False):

        @pl.when(is_first if first else jnp.logical_not(is_first))
        def _():
            mine, others = (first_refs, second_refs) if first else (second_refs, first_refs)
            pack(away, others[:4])
            operand_copy.start()
            side_copies(first)[0].start()
            pack(pair.at[0], mine[:4])
            small_pair[0] = mine[4][...]

    operand_copy.wait_recv()
    rows = 2 * padded_rows

    def product(left, right, target):
        a = pair[:, :, left : left + model_width].reshape(rows, model_width)
        b = pair[:, :, right : right + model_width].reshape(rows, model_width)
        value = f32_dot(a, b, ((0,), (0,))).astype(half)
        table[:, :, target : target + model_width] = value.reshape(
            depth * groups, shard_rows, model_width
        )

    for index in range(3):
        product(0, (1 + index) * model_width, index * model_width)
    product(4 * model_width, 5 * model_width, 3 * model_width)
    for copy in side_copies(True)[:1]:
        copy.wait_recv()
    small = (small_pair[0] + small_pair[1]).astype(half)
    table[:, :, 4 * model_width :] = small.reshape(depth * groups, shard_rows, small.shape[1])

    def go_copy(plane, source, target):
        return pltpu.make_async_remote_copy(
            src_ref=table.at[plane * groups + target], dst_ref=inbox.at[plane, source],
            send_sem=go_send.at[plane, target], recv_sem=go_recv.at[plane, source],
            device_id=(section, z, target), device_id_type=MESH,
        )

    def home_copy(source, target):
        return pltpu.make_async_remote_copy(
            src_ref=sent_home.at[target], dst_ref=home.at[source],
            send_sem=home_send.at[target], recv_sem=home_recv.at[source],
            device_id=(section, target, column), device_id_type=MESH,
        )

    def send_plane(step, carry):
        plane = z_peer(step)

        def send(distance, inner):
            go_copy(plane, column, xy_peer(distance)).start()
            return inner

        return lax.fori_loop(1, groups, send, carry)

    lax.fori_loop(1, 2 + 1, send_plane, 0)

    for first in (True, False):

        @pl.when(is_first if first else jnp.logical_not(is_first))
        def _():
            for copy in side_copies(first)[1:]:
                copy.start()

    def sum_plane(step, carry):
        plane = z_peer(step)

        def arrive(distance, total):
            lane = xy_peer(distance)
            go_copy(plane, lane, column).wait_recv()
            return total + inbox[plane, lane].astype(jnp.float32)

        own = table[plane * groups + column].astype(jnp.float32)
        total = lax.fori_loop(1, groups, arrive, own)

        @pl.when(step + 2 <= depth)
        def _():
            send_plane(step + 2, 0)

        @pl.when(plane == z)
        def _():
            shard_ref[...] = total

        @pl.when(plane != z)
        def _():
            sent_home[plane] = total.astype(half)
            home_copy(z, plane).start()

        return carry

    lax.fori_loop(1, depth + 1, sum_plane, 0)

    def finish_home(distance, carry):
        source = z_peer(distance)
        home_copy(source, z).wait_recv()
        shard_ref[...] += home[source].astype(jnp.float32)
        home_copy(z, source).wait_send()
        return carry

    lax.fori_loop(1, depth, finish_home, 0)

    def drain_plane(plane, carry):
        def drain(distance, inner):
            go_copy(plane, column, xy_peer(distance)).wait_send()
            return inner

        return lax.fori_loop(1, groups, drain, carry)

    lax.fori_loop(0, depth, drain_plane, 0)
    operand_copy.wait_send()
    for index, copy in enumerate(side_copies(True)):
        copy.wait_send()
        if index > 0:
            copy.wait_recv()


def finish_call(call_id, depth, groups, first, second, up_first, down_first, up_second, down_second,
                rows_first, rows_second):
    token_rows, model_width = first[0].shape
    padded_rows = round_up(token_rows, 16)
    small_width = first[4].shape[1]
    width = 4 * model_width + small_width
    shard_rows = model_width // (depth * groups)
    half = jnp.bfloat16
    out_shape = (
        jax.ShapeDtypeStruct((shard_rows, width), jnp.float32),
        jax.ShapeDtypeStruct(up_first.shape, half),
        jax.ShapeDtypeStruct(down_first.shape, half),
        jax.ShapeDtypeStruct(rows_first.shape, jnp.float32),
    )
    home = pltpu.VMEM((depth, shard_rows, width), half)
    return pl.pallas_call(
        functools.partial(
            finish_kernel, (depth, groups, token_rows, padded_rows, model_width)
        ),
        out_shape=out_shape,
        in_specs=[pl.BlockSpec(memory_space=pltpu.VMEM)] * 16,
        out_specs=[pl.BlockSpec(memory_space=pltpu.VMEM)] + [pl.BlockSpec(memory_space=pl.ANY)] * 3,
        scratch_shapes=[
            pltpu.VMEM((2, padded_rows, 6 * model_width), half),
            pltpu.VMEM((padded_rows, 6 * model_width), half),
            pltpu.VMEM((2, model_width, small_width), jnp.float32),
            pltpu.VMEM((depth * groups, shard_rows, width), half),
            pltpu.VMEM((depth, groups, shard_rows, width), half),
            home,
            home,
            pltpu.SemaphoreType.DMA((5,)),
            pltpu.SemaphoreType.DMA((5,)),
            pltpu.SemaphoreType.DMA((depth, groups)),
            pltpu.SemaphoreType.DMA((depth, groups)),
            pltpu.SemaphoreType.DMA((depth,)),
            pltpu.SemaphoreType.DMA((depth,)),
        ],
        compiler_params=pltpu.CompilerParams(
            collective_id=call_id, has_side_effects=True, vmem_limit_bytes=50 * 2**20
        ),
        name="finish_exchange",
    )(*first, *second, up_first, down_first, up_second, down_second, rows_first, rows_second)

def head_mask(head):
    lanes = lax.broadcasted_iota(jnp.int32, (1, 2 * HEAD_DIM), 1)
    return jnp.where(lanes // HEAD_DIM == head, 1.0, 0.0).astype(jnp.bfloat16)


def attend_kernel(width, qkv_ref, out_ref):
    scale_factor = 1.0 / math.sqrt(HEAD_DIM)
    pair_width = 2 * HEAD_DIM

    def pair(index, carry):
        def columns(part):
            start = pl.multiple_of(part * width + index * pair_width, pair_width)
            return qkv_ref[:, pl.ds(start, pair_width)]

        queries, keys, values = columns(0), columns(1), columns(2)
        total = jnp.zeros(queries.shape, jnp.float32)
        for head in range(2):
            mask = head_mask(head)
            scores = f32_dot(queries * mask, keys, ((1,), (1,))) * scale_factor
            log_totals = jnp.log(jnp.sum(jnp.exp(scores), axis=1, keepdims=True))
            probs = jnp.exp(scores - log_totals).astype(jnp.bfloat16)
            total = total + f32_dot(probs, values * mask, ((1,), (0,)))
        start = pl.multiple_of(index * pair_width, pair_width)
        out_ref[:, pl.ds(start, pair_width)] = total.astype(jnp.bfloat16)
        return carry

    lax.fori_loop(0, width // pair_width, pair, 0)


def attend_backward_kernel(width, qkv_ref, d_out_ref, d_qkv_ref):
    scale_factor = 1.0 / math.sqrt(HEAD_DIM)
    pair_width = 2 * HEAD_DIM
    half = jnp.bfloat16

    def pair(index, carry):
        def place(part):
            return pl.ds(pl.multiple_of(part * width + index * pair_width, pair_width), pair_width)

        queries, keys, values = (qkv_ref[:, place(part)] for part in range(3))
        d_out = d_out_ref[:, place(0)]
        d_queries = jnp.zeros(queries.shape, jnp.float32)
        d_keys, d_values = d_queries, d_queries
        for head in range(2):
            mask = head_mask(head)
            own_queries, own_d_out = queries * mask, d_out * mask
            scores = f32_dot(keys, own_queries, ((1,), (1,))) * scale_factor
            log_totals = jnp.log(jnp.sum(jnp.exp(scores), axis=0, keepdims=True))
            probs = jnp.exp(scores - log_totals)
            d_probs = f32_dot(values, own_d_out, ((1,), (1,)))
            row_dot = jnp.sum(probs * d_probs, axis=0, keepdims=True)
            d_scores = (probs * (d_probs - row_dot) * scale_factor).astype(half)
            d_values = d_values + f32_dot(probs.astype(half), own_d_out, ((1,), (0,)))
            d_keys = d_keys + f32_dot(d_scores, own_queries, ((1,), (0,)))
            d_queries = d_queries + f32_dot(d_scores, keys * mask, ((0,), (0,)))
        for part, value in enumerate((d_queries, d_keys, d_values)):
            d_qkv_ref[:, place(part)] = value.astype(half)
        return carry

    lax.fori_loop(0, width // pair_width, pair, 0)


def attend_call(qkv_rows, d_attended=None):
    rows, width = qkv_rows.shape
    width = width // 3
    operands = (qkv_rows,) if d_attended is None else (qkv_rows, d_attended)
    kernel = attend_kernel if d_attended is None else attend_backward_kernel
    out_width = width if d_attended is None else 3 * width
    return pl.pallas_call(
        functools.partial(kernel, width),
        out_shape=jax.ShapeDtypeStruct((rows, out_width), jnp.bfloat16),
        in_specs=[pl.BlockSpec(memory_space=pltpu.VMEM)] * len(operands),
        out_specs=pl.BlockSpec(memory_space=pltpu.VMEM),
        compiler_params=pltpu.CompilerParams(vmem_limit_bytes=24 * 2**20),
        name="attend" if d_attended is None else "attend_backward",
    )(*operands)


def norm_forward(values, gain_row, shift_row):
    centred = values - jnp.mean(values, axis=-1, keepdims=True)
    variance = jnp.mean(centred * centred, axis=-1, keepdims=True)
    inverse = lax.rsqrt(variance + EPS)
    unit_rows = centred * inverse
    return (unit_rows * gain_row + shift_row, unit_rows, inverse)


def norm_backward(d_normed, unit_rows, inverse, gain_row):
    d_gain = jnp.sum(d_normed * unit_rows, axis=0)
    d_shift = jnp.sum(d_normed, axis=0)
    scaled = d_normed * gain_row
    d_values = inverse * (
        scaled
        - jnp.mean(scaled, axis=-1, keepdims=True)
        - unit_rows * jnp.mean(scaled * unit_rows, axis=-1, keepdims=True)
    )
    return (d_values, d_gain, d_shift)


def gelu_slope(pre_act):
    return (
        0.5 * (1.0 + lax.erf(pre_act * SQRT_HALF))
        + pre_act * jnp.exp(-0.5 * pre_act * pre_act) * INV_ROOT_TAU
    )


def split_heads(qkv_rows, image_count):
    feature_count = qkv_rows.shape[1] // 3
    return [
        qkv_rows[:, part_index * feature_count : (part_index + 1) * feature_count].reshape(
            image_count, -1, HEADS, HEAD_DIM
        )
        for part_index in range(3)
    ]


def attend_forward(qkv_rows, image_count):
    queries, key_rows, value_rows = split_heads(qkv_rows, image_count)
    scale_factor = 1.0 / math.sqrt(HEAD_DIM)
    scores = (
        jnp.einsum("bqhd,bkhd->bhqk", queries, key_rows, preferred_element_type=jnp.float32)
        * scale_factor
    )
    log_totals = jnp.log(jnp.sum(jnp.exp(scores), axis=-1))
    probs_half = jnp.exp(scores - log_totals[..., None]).astype(jnp.bfloat16)
    attended = jnp.einsum(
        "bhqk,bkhd->bqhd", probs_half, value_rows, preferred_element_type=jnp.float32
    )
    return (attended.astype(jnp.bfloat16).reshape(-1, HEADS * HEAD_DIM), log_totals)


def attend_backward(qkv_rows, log_totals, d_attended, image_count):
    queries, key_rows, value_rows = split_heads(qkv_rows, image_count)
    scale_factor = 1.0 / math.sqrt(HEAD_DIM)
    scores = (
        jnp.einsum("bqhd,bkhd->bhqk", queries, key_rows, preferred_element_type=jnp.float32)
        * scale_factor
    )
    probs = jnp.exp(scores - log_totals[..., None])
    probs_half = probs.astype(jnp.bfloat16)
    d_heads = d_attended.reshape(image_count, -1, HEADS, HEAD_DIM)
    d_values = jnp.einsum(
        "bhqk,bqhd->bkhd", probs_half, d_heads, preferred_element_type=jnp.float32
    )
    d_probs = jnp.einsum("bqhd,bkhd->bhqk", d_heads, value_rows, preferred_element_type=jnp.float32)
    row_dot = jnp.sum(probs * d_probs, axis=-1, keepdims=True)
    d_scores = (probs * (d_probs - row_dot) * scale_factor).astype(jnp.bfloat16)
    d_queries = jnp.einsum(
        "bhqk,bkhd->bqhd", d_scores, key_rows, preferred_element_type=jnp.float32
    )
    d_keys = jnp.einsum("bhqk,bqhd->bkhd", d_scores, queries, preferred_element_type=jnp.float32)
    feature_count = HEADS * HEAD_DIM
    joined = jnp.concatenate(
        [
            d_queries.reshape(-1, feature_count),
            d_keys.reshape(-1, feature_count),
            d_values.reshape(-1, feature_count),
        ],
        axis=1,
    )
    return joined.astype(jnp.bfloat16)


def on_device(
    boundary_in, routes, capacity_slots, ln_gain, ln_bias, w_qkv, w_out, w_router, w_up, w_down
):
    section_index = lax.axis_index("section")
    is_first = section_index == 0
    depth = lax.axis_size("dp")
    groups = lax.axis_size("expert")
    expert_count = EXP_DEV * groups
    local_images = boundary_in.shape[2]
    token_rows = local_images * boundary_in.shape[3]
    model_width = boundary_in.shape[4]
    capacity = 26 * token_rows // (16 * expert_count)
    cap_rows = round_up(capacity, 8)
    padded_rows = round_up(token_rows + 8, 16)
    half = jnp.bfloat16
    swapped = [(0, 1), (1, 0)]

    edge = boundary_in[0].reshape(MB, token_rows, model_width)
    route_rows = routes[0].reshape(MB, token_rows, 2)
    slot_rows = capacity_slots[0].reshape(MB, token_rows, 2)
    slot_index = jnp.where(slot_rows < capacity, route_rows * cap_rows + slot_rows, -1)
    table = jnp.concatenate([slot_index, route_rows], axis=2).transpose(0, 2, 1)
    table = jnp.pad(
        table, ((0, 0), (0, 4), (0, padded_rows - token_rows)), constant_values=-1
    )

    norm_columns = jnp.concatenate([ln_gain, ln_bias], axis=1).transpose(0, 2, 1)
    used = 4 * model_width + expert_count + 4
    padding = -used % 128
    packed = jnp.concatenate([w_qkv, w_out, w_router, norm_columns], axis=2)
    packed = jnp.pad(packed, ((0, 0), (0, 0), (0, padding)))
    (
        dense_first, dense_second, up_first, up_second, down_first, down_second,
        stream, cotangent, table_first, table_second,
    ) = start_call(8, depth, groups, packed[0], w_up[0], w_down[0], edge, table)
    qkv_all, out_all, router_all, norm_all = [], [], [], []

    def add_dense(item):
        qkv_all.append(item[:, : 3 * model_width])
        out_all.append(item[:, 3 * model_width : 4 * model_width])
        router_all.append(item[:, 4 * model_width : used - 4])
        norm_all.append(item[:, used - 4 : used].T.astype(jnp.float32))

    add_dense(dense_first.reshape(model_width, used + padding))
    add_dense(dense_second.reshape(model_width, used + padding))
    up_all = (up_first, up_second)
    down_all = (down_first, down_second)
    slot_tables = (table_first, table_second)
    z_index = lax.axis_index("dp")
    chosen_all = [
        (
            lax.dynamic_index_in_dim(item, z_index, 0, False)[2:4, :token_rows].T[..., None]
            == jnp.arange(expert_count, dtype=jnp.int32)
        ).astype(jnp.float32)
        for item in slot_tables
    ]
    moe = functools.partial(moe_call, depth=depth, groups=groups, cap_rows=cap_rows)

    def layer_forward(layer, inputs):
        chosen = chosen_all[layer]
        normed_one, unit_one, inverse_one = norm_forward(
            inputs, norm_all[layer][0], norm_all[layer][2]
        )
        norm_one = normed_one.astype(half)
        qkv_rows = jnp.dot(norm_one, qkv_all[layer], preferred_element_type=jnp.float32).astype(half)
        if local_images == 1:
            attended, log_totals = attend_call(qkv_rows), None
        else:
            attended, log_totals = attend_forward(qkv_rows, local_images)
        middle = inputs + jnp.dot(attended, out_all[layer], preferred_element_type=jnp.float32)
        normed_two, unit_two, inverse_two = norm_forward(
            middle, norm_all[layer][1], norm_all[layer][3]
        )
        norm_two = normed_two.astype(half)
        logits = jnp.dot(norm_two, router_all[layer], preferred_element_type=jnp.float32)
        picked = jnp.sum(logits[:, None, :] * chosen, axis=-1)
        leading = jax.nn.sigmoid(picked[:, 0] - picked[:, 1])
        gate_pair = jnp.stack([leading, 1.0 - leading], axis=-1)
        gate_rows = jnp.pad(gate_pair.T, ((0, 0), (0, model_width - token_rows)))
        sent = jnp.concatenate(
            [
                norm_two,
                jnp.zeros((padded_rows - 8 - token_rows, model_width), half),
                gate_rows.astype(half),
                jnp.zeros((6, model_width), half),
            ]
        )
        combined, *expert_saved = moe(
            False, 2 * layer, rows=sent, slots=slot_tables[layer], up=up_all[layer],
            down=down_all[layer],
        )
        out_rows = middle + combined[:token_rows]
        saved = (
            inputs, norm_one, qkv_rows, log_totals, attended, middle, norm_two, gate_pair,
            expert_saved,
        )
        return (out_rows, saved)

    def layer_backward(layer, d_out, saved):
        (
            inputs, norm_one, qkv_rows, log_totals, attended, middle, norm_two, gate_pair,
            expert_saved,
        ) = saved
        chosen = chosen_all[layer]
        gates, all_rows, hidden, slope, back_rows = expert_saved
        sent = d_out.astype(half)
        combined, up_grad, down_grad = moe(
            True, 2 * layer + 1, rows=sent, slots=slot_tables[layer], up=up_all[layer],
            down=down_all[layer], saved=(gates, back_rows, slope, hidden, all_rows),
        )
        d_gate_rows = combined[padded_rows - 8 :, :token_rows]
        d_gate = jnp.stack([d_gate_rows[0] + d_gate_rows[1], d_gate_rows[2] + d_gate_rows[3]], axis=1)
        d_lead = (d_gate[:, 0] - d_gate[:, 1]) * gate_pair[:, 0] * gate_pair[:, 1]
        d_logits = (d_lead[:, None] * (chosen[:, 0] - chosen[:, 1])).astype(half)
        d_norm_two = combined[:token_rows] + jnp.einsum(
            "te,de->td", d_logits, router_all[layer], preferred_element_type=jnp.float32
        )
        normed_two, unit_two, inverse_two = norm_forward(
            middle, norm_all[layer][1], norm_all[layer][3]
        )
        d_middle_norm, gain_two, shift_two = norm_backward(
            d_norm_two, unit_two, inverse_two, norm_all[layer][1]
        )
        d_middle = d_out + d_middle_norm
        d_middle_half = d_middle.astype(half)
        d_attended = jnp.einsum(
            "te,de->td", d_middle_half, out_all[layer], preferred_element_type=jnp.float32
        ).astype(half)
        if local_images == 1:
            d_qkv = attend_call(qkv_rows, d_attended)
        else:
            d_qkv = attend_backward(qkv_rows, log_totals, d_attended, local_images)
        d_norm_one = jnp.einsum(
            "te,de->td", d_qkv, qkv_all[layer], preferred_element_type=jnp.float32
        )
        normed_one, unit_one, inverse_one = norm_forward(
            inputs, norm_all[layer][0], norm_all[layer][2]
        )
        d_input_norm, gain_one, shift_one = norm_backward(
            d_norm_one, unit_one, inverse_one, norm_all[layer][0]
        )
        d_input = d_middle + d_input_norm
        small = jnp.concatenate(
            [
                jnp.einsum("td,te->de", norm_two, d_logits, preferred_element_type=jnp.float32),
                jnp.stack([gain_one, gain_two, shift_one, shift_two], axis=1),
            ],
            axis=1,
        )
        return (d_input, (norm_one, d_qkv, attended, d_middle_half, small), (up_grad, down_grad))

    qkv_part, out_part = 3 * model_width // 2, model_width // 2
    small_width = round_up(expert_count + 4, 128)

    def dense_gradients(norm_one, d_qkv, attended, d_middle_half, small):
        own = jnp.concatenate([norm_one, d_qkv, attended, d_middle_half], axis=1)
        pair = jnp.concatenate([own, lax.ppermute(own, "section", swapped)], axis=0)
        d_qkv_part = lax.dynamic_slice_in_dim(
            pair, model_width + section_index * qkv_part, qkv_part, axis=1
        )
        d_out_part = lax.dynamic_slice_in_dim(
            pair, 5 * model_width + section_index * out_part, out_part, axis=1
        )
        qkv_grad = jnp.einsum(
            "td,te->de", pair[:, :model_width], d_qkv_part, preferred_element_type=jnp.float32
        )
        out_grad = jnp.einsum(
            "td,te->de", pair[:, 4 * model_width : 5 * model_width], d_out_part,
            preferred_element_type=jnp.float32,
        )
        small = jnp.pad(small, ((0, 0), (0, small_width - expert_count - 4)))
        packed_grad = jnp.concatenate(
            [qkv_grad.astype(half), out_grad.astype(half), small.astype(half)], axis=1
        )
        blocks = packed_grad.reshape(depth, groups, -1, packed_grad.shape[1]).transpose(1, 0, 2, 3)
        blocks = lax.all_to_all(blocks, "expert", split_axis=0, concat_axis=0, tiled=True)
        blocks = jnp.sum(blocks.astype(jnp.float32), axis=0).astype(half)
        blocks = lax.all_to_all(blocks, "dp", split_axis=0, concat_axis=0, tiled=True)
        return jnp.sum(blocks.astype(jnp.float32), axis=0)

    saved_list = []
    for layer in range(2):
        if layer > 0:
            stream = stream.astype(half).astype(jnp.float32)
        stream, saved = layer_forward(layer, stream)
        saved_list.append(saved)
    dense_operands = [None, None]
    expert_grads = [None, None]
    for layer in (1, 0):
        if layer < 1:
            cotangent = cotangent.astype(half).astype(jnp.float32)
        cotangent, operands, expert_grads[layer] = layer_backward(
            layer, cotangent, saved_list[layer]
        )
        dense_operands[layer] = operands

    def mine(first, second):
        return jnp.where(is_first, first, second)

    def both(first, second):
        own, away = mine(first, second), mine(second, first)
        return own, lax.ppermute(away, "section", swapped)

    if model_width % (16 * depth * groups) == 0:
        operands = [
            item[:4] + (jnp.pad(item[4], ((0, 0), (0, small_width - expert_count - 4))),)
            for item in dense_operands
        ]
        shard, other_up, other_down, other_rows = finish_call(
            9, depth, groups, operands[0], operands[1], *expert_grads[0], *expert_grads[1],
            cotangent, stream,
        )
        own_up = mine(expert_grads[0][0], expert_grads[1][0])
        own_down = mine(expert_grads[0][1], expert_grads[1][1])
        own_rows = mine(cotangent, stream)
        qkv_shard = shard[:, : 3 * model_width]
        out_shard = shard[:, 3 * model_width : 4 * model_width]
        small_shard = shard[:, 4 * model_width :]
    else:
        shards = [dense_gradients(*item) for item in dense_operands]
        own_shard, other_shard = both(shards[0], shards[1])
        low, high = mine(own_shard, other_shard), mine(other_shard, own_shard)
        qkv_shard = jnp.concatenate([low[:, :qkv_part], high[:, :qkv_part]], axis=1)
        out_shard = jnp.concatenate(
            [low[:, qkv_part : qkv_part + out_part], high[:, qkv_part : qkv_part + out_part]], axis=1
        )
        small_shard = (low + high)[:, qkv_part + out_part :]
        own_up, other_up = both(expert_grads[0][0], expert_grads[1][0])
        own_down, other_down = both(expert_grads[0][1], expert_grads[1][1])
        own_rows, other_rows = both(cotangent, stream)
    norm_shard = small_shard[:, expert_count : expert_count + 4].T

    def expert_grad(own, other):
        return (own.astype(jnp.float32) + other.astype(jnp.float32))[None]

    boundary_rows = jnp.stack([mine(own_rows, other_rows), mine(other_rows, own_rows)])
    boundary_out = boundary_rows.reshape(1, MB, local_images, boundary_in.shape[3], model_width)
    return (
        boundary_out,
        norm_shard[None, 0:2],
        norm_shard[None, 2:4],
        qkv_shard[None],
        out_shard[None],
        small_shard[None, :, :expert_count],
        expert_grad(own_up, other_up),
        expert_grad(own_down, other_down),
    )


def solution(mesh):
    in_specs = (
        P("section", None, ("dp", "expert"), None, None),
        P("section", None, ("dp", "expert"), None, None),
        P("section", None, ("dp", "expert"), None, None),
        P("section", None, ("dp", "expert")),
        P("section", None, ("dp", "expert")),
        P("section", ("dp", "expert"), None),
        P("section", ("dp", "expert"), None),
        P("section", ("dp", "expert"), None),
        P("section", "expert", None, "dp"),
        P("section", "expert", "dp", None),
    )
    out_specs = (
        P("section", None, ("dp", "expert"), None, None),
        P("section", None, ("dp", "expert")),
        P("section", None, ("dp", "expert")),
        P("section", ("dp", "expert"), None),
        P("section", ("dp", "expert"), None),
        P("section", ("dp", "expert"), None),
        P("section", "expert", None, "dp"),
        P("section", "expert", "dp", None),
    )
    return jax.shard_map(
        on_device, mesh=mesh, in_specs=in_specs, out_specs=out_specs, check_vma=False
    )
```

```python
import functools
import math

import jax
import jax.numpy as jnp
from jax import lax
from jax.experimental import pallas as pl
from jax.experimental.pallas import tpu as pltpu
from jax.sharding import PartitionSpec as P

HEADS = 12
HEAD_DIM = 64
EXP_DEV = 2
MB = 2


EPS = 1e-06
SQRT_HALF = 0.7071067811865476
INV_ROOT_TAU = 0.3989422804014327
MESH = pl.DeviceIdType.MESH


def round_up(value, unit):
    return (value + unit - 1) // unit * unit


def z_order(step, z, depth):
    if depth == 1:
        return z
    direction = 1 - 2 * (z // (depth // 2))
    return lax.rem(z + step * direction + depth, depth)


def f32_dot(a, b, dims):
    return lax.dot_general(a, b, (dims, ((), ())), preferred_element_type=jnp.float32)


def moe_kernel(backward, shape, *refs):
    depth, groups, cap_rows, token_rows, model_width, hidden_width = shape
    if backward:
        (
            rows_ref, slots_ref, gates_ref, up_source, down_source, back_source, slope_source,
            hidden_source, kept_source, out_ref, up_grad_ref, down_grad_ref,
            up_ref, down_ref, back_ref, slope_ref, hidden_ref, kept_ref,
            inbox, d_pre_ref, taken_ref, raw, sent_rows, sent_back, sent_home, home, back, d_gates, *sems,
        ) = refs
    else:
        (
            rows_ref, slots_ref, up_source, down_source,
            out_ref, gates_ref, taken_target, hidden_target, slope_target, back_target,
            up_ref, down_ref, taken_ref, hidden_ref, slope_ref, back,
            inbox, raw, sent_rows, sent_back, sent_home, home, *sems,
        ) = refs
    far_send, far_recv, go_send, go_recv, back_send, back_recv, home_send, home_recv = sems[:8]
    load_sem, store_sem = sems[8:]
    half = jnp.bfloat16
    section, z, column = (
        lax.axis_index("section"), lax.axis_index("dp"), lax.axis_index("expert")
    )
    slot_count = 2 * groups * cap_rows
    tail = token_rows - 16

    def z_peer(distance):
        return (section, lax.rem(z + distance, depth), column)

    def xy_peer(distance):
        if groups == 4 and not backward:
            across = 3 - column
            beside = column + 1 - 2 * lax.rem(column, 2)
            above = lax.rem(column + 2, 4)
            last = (distance - 1) * (distance - 2) // 2
            middle = (distance - 1) * (3 - distance)
            first = (2 - distance) * (3 - distance) // 2
            return first * across + middle * beside + last * above
        return lax.rem(column + distance, groups)

    barrier = pltpu.get_barrier_semaphore()

    def greet_z(distance, carry):
        pl.semaphore_signal(barrier, inc=1, device_id=z_peer(distance), device_id_type=MESH)
        return carry

    def greet_xy(distance, carry):
        pl.semaphore_signal(
            barrier, inc=1, device_id=(section, z, xy_peer(distance)), device_id_type=MESH
        )
        return carry

    lax.fori_loop(1, depth, greet_z, 0)
    lax.fori_loop(1, groups, greet_xy, 0)
    pl.semaphore_wait(barrier, depth - 1 + groups - 1)

    def far_copy(direction, image):
        target = lax.rem(z + 2 * direction - 1 + depth, depth)
        source = raw.at[image]
        return pltpu.make_async_remote_copy(
            src_ref=source, dst_ref=raw.at[image],
            send_sem=far_send.at[direction, image], recv_sem=far_recv.at[image],
            device_id=(section, target, column), device_id_type=MESH,
        )

    def go_copy(image, source, target):
        return pltpu.make_async_remote_copy(
            src_ref=sent_rows.at[image, target], dst_ref=inbox.at[image, source],
            send_sem=go_send.at[image, target], recv_sem=go_recv.at[image, source],
            device_id=(section, z, target), device_id_type=MESH,
        )

    def back_copy(image, source, target):
        return pltpu.make_async_remote_copy(
            src_ref=sent_back.at[image, target], dst_ref=back.at[image, source],
            send_sem=back_send.at[image, target], recv_sem=back_recv.at[image, source],
            device_id=(section, z, target), device_id_type=MESH,
        )

    def home_copy(source, target):
        return pltpu.make_async_remote_copy(
            src_ref=sent_home.at[target], dst_ref=home.at[source],
            send_sem=home_send.at[target], recv_sem=home_recv.at[source],
            device_id=(section, target, column), device_id_type=MESH,
        )

    loads = [(up_source, up_ref), (down_source, down_ref)]
    if backward:
        loads += [
            (back_source, back_ref), (slope_source, slope_ref),
            (hidden_source, hidden_ref), (kept_source, kept_ref),
        ]
    loads = [
        pltpu.make_async_copy(source, target, load_sem.at[index])
        for index, (source, target) in enumerate(loads)
    ]

    def store_copies(image):
        pairs = [
            (taken_ref.at[0, image], taken_target.at[0, image]),
            (taken_ref.at[1, image], taken_target.at[1, image]),
            (hidden_ref.at[0, image], hidden_target.at[0, image]),
            (hidden_ref.at[1, image], hidden_target.at[1, image]),
            (slope_ref.at[0, image], slope_target.at[0, image]),
            (slope_ref.at[1, image], slope_target.at[1, image]),
            (back.at[image], back_target.at[image]),
        ]
        return [
            pltpu.make_async_copy(source, target, store_sem.at[index, image])
            for index, (source, target) in enumerate(pairs)
        ]

    if backward:
        raw[z, tail:] = jnp.zeros((16, model_width), half)
        raw[z, : rows_ref.shape[0]] = rows_ref[...]
    else:
        raw[z] = rows_ref[...]

    @pl.when(z < depth - 1)
    def _():
        far_copy(1, z).start()

    @pl.when(z > 0)
    def _():
        far_copy(0, z).start()

    for copy in loads[2:3] + loads[:2] + loads[3:]:
        copy.start()

    def match(image):
        slots = slots_ref[image][:, :token_rows]
        index = lax.broadcasted_iota(jnp.int32, (slot_count, token_rows), 0)
        return index == slots[0:1], index == slots[1:2]

    def gate_table(image):
        first, second = match(image)
        gates = gates_ref[image]
        table = jnp.where(first, gates[0:1], 0.0) + jnp.where(second, gates[1:2], 0.0)
        return table.astype(half)

    def ones_table(image):
        first, second = match(image)
        return jnp.where(first | second, 1.0, 0.0).astype(half)

    def pass_on(step):
        low, high = z - step, z + step

        @pl.when(low >= 0)
        def _():
            far_copy(1, low).wait_recv()

            @pl.when(z < depth - 1)
            def _():
                far_copy(1, low).start()

        @pl.when(high < depth)
        def _():
            far_copy(0, high).wait_recv()

            @pl.when(z > 0)
            def _():
                far_copy(0, high).start()

    def dispatch(image):
        if not backward:
            gates_ref[image] = raw[image, tail:, :token_rows].astype(jnp.float32)[8:16]
        table = gate_table(image) if backward else ones_table(image)
        rows = raw[image]
        blocks = f32_dot(table, rows, ((1,), (0,))).astype(half)
        sent_rows[image] = blocks.reshape(groups, 2 * cap_rows, model_width)

        def send(distance, carry):
            go_copy(image, column, xy_peer(distance)).start()
            return carry

        lax.fori_loop(1, groups, send, 0)
        inbox[image, column] = sent_rows[image, column]
        if backward:

            @pl.when(image == z)
            def _():
                loads[2].wait()

            first, second = match(image)
            returned = back_ref[image].reshape(slot_count, model_width)
            ones = jnp.ones((8, model_width), half)
            row_index = lax.broadcasted_iota(jnp.int32, (8, token_rows), 0)
            packed = jnp.zeros((8, token_rows), jnp.float32)
            for choice, found in enumerate((first, second)):
                table = jnp.where(found, 1.0, 0.0).astype(half)
                selected = f32_dot(table, returned, ((0,), (0,)))
                product = (selected * rows.astype(jnp.float32)).astype(half)
                sums = f32_dot(ones, product, ((1,), (1,)))
                high = sums.astype(half).astype(jnp.float32)
                packed = jnp.where(row_index == 2 * choice, high, packed)
                packed = jnp.where(row_index == 2 * choice + 1, sums - high, packed)
            d_gates[image] = packed

    def experts(image):
        def arrive(distance, carry):
            go_copy(image, xy_peer(distance), column).wait_recv()
            return carry

        lax.fori_loop(1, groups, arrive, 0)
        block = inbox[image].astype(jnp.float32)
        results = []
        for expert in range(2):
            rows = block[:, expert * cap_rows : (expert + 1) * cap_rows]
            rows = rows.reshape(groups * cap_rows, model_width).astype(half)
            taken_ref[expert, image] = rows
            if backward:
                d_hidden = f32_dot(rows, down_ref[expert], ((1,), (1,)))
                d_pre = (d_hidden * slope_ref[expert, image].astype(jnp.float32)).astype(half)
                d_pre_ref[expert, image] = d_pre
                result = f32_dot(d_pre, up_ref[expert], ((1,), (1,)))
            else:
                pre = f32_dot(rows, up_ref[expert], ((1,), (0,)))
                share = 0.5 * (1.0 + lax.erf(pre * SQRT_HALF))
                slope = share + pre * jnp.exp(-0.5 * pre * pre) * INV_ROOT_TAU
                hidden = (pre * share).astype(half)
                hidden_ref[expert, image] = hidden
                slope_ref[expert, image] = slope.astype(half)
                result = f32_dot(hidden, down_ref[expert], ((1,), (0,)))
            results.append(result.reshape(groups, cap_rows, model_width))
        sent_back[image] = jnp.concatenate(results, axis=1).astype(half)

        def send(distance, carry):
            back_copy(image, column, xy_peer(distance)).start()
            return carry

        lax.fori_loop(1, groups, send, 0)
        back[image, column] = sent_back[image, column]
        if not backward:
            for copy in store_copies(image)[:6]:
                copy.start()

    def combine(image):
        def arrive(distance, carry):
            back_copy(image, xy_peer(distance), column).wait_recv()
            return carry

        lax.fori_loop(1, groups, arrive, 0)
        if not backward:
            store_copies(image)[6].start()
        table = ones_table(image) if backward else gate_table(image)
        total = f32_dot(table, back[image].reshape(slot_count, model_width), ((0,), (0,)))
        if backward:
            extra = jnp.concatenate(
                [jnp.zeros((8, token_rows), jnp.float32), d_gates[image]], axis=0
            )

        @pl.when(image == z)
        def _():
            out_ref[...] = total
            if backward:
                out_ref[tail:, :token_rows] = total[tail:, :token_rows] + extra

        @pl.when(image != z)
        def _():
            sent_home[image] = total.astype(half)
            if backward:
                sent_home[image, tail:, :token_rows] = (
                    total[tail:, :token_rows] + extra
                ).astype(half)
            home_copy(z, image).start()

    def stage(step, carry):
        @pl.when(jnp.logical_and(step >= 1, step < depth))
        def _():
            pass_on(step)

        @pl.when(step < depth)
        def _():
            dispatch(z_order(step, z, depth))

        @pl.when(step == 2)
        def _():
            loads[0].wait()
            loads[1].wait()
            if backward:
                loads[3].wait()

        @pl.when(jnp.logical_and(step >= 2, step < depth + 2))
        def _():
            experts(z_order(lax.rem(step - 1, depth), z, depth))

        @pl.when(step >= 3)
        def _():
            combine(z_order(lax.rem(step - 2, depth), z, depth))

        return carry

    lax.fori_loop(0, depth + 3, stage, 0)

    if backward:
        loads[4].wait()
        loads[5].wait()

        def expert_gradients(expert, carry):
            kept = kept_ref[expert].reshape(depth * groups * cap_rows, model_width)
            d_pre = d_pre_ref[expert].reshape(depth * groups * cap_rows, hidden_width)
            up_grad_ref[expert] = f32_dot(kept, d_pre, ((0,), (0,))).astype(half)
            hidden = hidden_ref[expert].reshape(depth * groups * cap_rows, hidden_width)
            grads = taken_ref[expert].reshape(depth * groups * cap_rows, model_width)
            down_grad_ref[expert] = f32_dot(hidden, grads, ((0,), (0,))).astype(half)
            return carry

        lax.fori_loop(0, 2, expert_gradients, 0)

    def finish_home(distance, carry):
        source = lax.rem(z + distance, depth)
        home_copy(source, z).wait_recv()
        out_ref[...] += home[source].astype(jnp.float32)
        return carry

    lax.fori_loop(1, depth, finish_home, 0)

    def drain_home(distance, carry):
        home_copy(z, lax.rem(z + distance, depth)).wait_send()
        return carry

    lax.fori_loop(1, depth, drain_home, 0)

    def drain_image(image, carry):
        if not backward:
            for copy in store_copies(image):
                copy.wait()

        @pl.when(jnp.logical_and(z < depth - 1, image <= z))
        def _():
            far_copy(1, image).wait_send()

        @pl.when(jnp.logical_and(z > 0, image >= z))
        def _():
            far_copy(0, image).wait_send()

        def drain(distance, inner):
            go_copy(image, column, xy_peer(distance)).wait_send()
            back_copy(image, column, xy_peer(distance)).wait_send()
            return inner

        lax.fori_loop(1, groups, drain, 0)
        return carry

    lax.fori_loop(0, depth, drain_image, 0)


def moe_call(backward, call_id, depth, groups, cap_rows, rows, slots, up, down, saved=()):
    model_width = rows.shape[1]
    token_rows = saved[0].shape[2] if backward else rows.shape[0]
    hidden_width = up.shape[2]
    half = jnp.bfloat16
    shape = (depth, groups, cap_rows, token_rows, model_width, hidden_width)
    taken = jax.ShapeDtypeStruct((2, depth, groups * cap_rows, model_width), half)
    hidden = jax.ShapeDtypeStruct((2, depth, groups * cap_rows, hidden_width), half)
    back = jax.ShapeDtypeStruct((depth, groups, 2 * cap_rows, model_width), half)
    out = jax.ShapeDtypeStruct((token_rows, model_width), jnp.float32)
    vmem, anywhere = pl.BlockSpec(memory_space=pltpu.VMEM), pl.BlockSpec(memory_space=pl.ANY)
    if backward:
        operands = (rows, slots, saved[0], up, down) + saved[1:]
        in_specs = [vmem] * 3 + [anywhere] * 6
        out_shape = (
            out, jax.ShapeDtypeStruct(up.shape, half), jax.ShapeDtypeStruct(down.shape, half)
        )
        out_specs = [vmem] * 3
        buffers = (up, down, back, hidden, hidden, taken, back, hidden, taken)
    else:
        operands = (rows, slots, up, down)
        in_specs = [vmem] * 2 + [anywhere] * 2
        gates = jax.ShapeDtypeStruct((depth, 8, token_rows), jnp.float32)
        out_shape = (out, gates, taken, hidden, hidden, back)
        out_specs = [vmem] * 2 + [anywhere] * 4
        buffers = (up, down, taken, hidden, hidden, back, back)
    scratch = [pltpu.VMEM(item.shape, half) for item in buffers]
    scratch += [
        pltpu.VMEM((depth, token_rows, model_width), half),
        pltpu.VMEM(back.shape, half),
        pltpu.VMEM(back.shape, half),
        pltpu.VMEM((depth, token_rows, model_width), half),
        pltpu.VMEM((depth, token_rows, model_width), half),
    ]
    if backward:
        scratch += [
            pltpu.VMEM(back.shape, half),
            pltpu.VMEM((depth, 8, token_rows), jnp.float32),
        ]
    scratch += [
        pltpu.SemaphoreType.DMA((2, depth)),
        pltpu.SemaphoreType.DMA((depth,)),
        pltpu.SemaphoreType.DMA((depth, groups)),
        pltpu.SemaphoreType.DMA((depth, groups)),
        pltpu.SemaphoreType.DMA((depth, groups)),
        pltpu.SemaphoreType.DMA((depth, groups)),
        pltpu.SemaphoreType.DMA((depth,)),
        pltpu.SemaphoreType.DMA((depth,)),
        pltpu.SemaphoreType.DMA((6,)),
        pltpu.SemaphoreType.DMA((7, depth)),
    ]
    return pl.pallas_call(
        functools.partial(moe_kernel, backward, shape),
        out_shape=out_shape,
        in_specs=in_specs,
        out_specs=out_specs,
        scratch_shapes=scratch,
        compiler_params=pltpu.CompilerParams(
            collective_id=call_id, has_side_effects=True, vmem_limit_bytes=54 * 2**20
        ),
        name="moe_backward" if backward else "moe_forward",
    )(*operands)

def start_kernel(shape, *refs):
    depth, groups = shape
    (
        packed_ref, up_ref, down_ref, edge_ref, table_ref,
        dense_first, dense_second, up_first, up_second, down_first, down_second,
        rows_ref, cotangent_ref, table_first, table_second,
        shard_send, shard_recv, core_send, core_recv, table_send, table_recv, own_sem,
    ) = refs
    section, z, column = (
        lax.axis_index("section"), lax.axis_index("dp"), lax.axis_index("expert")
    )
    other = (1 - section, z, column)
    is_first = section == 0

    def z_peer(distance):
        return lax.rem(z + distance, depth)

    def xy_peer(distance):
        return lax.rem(column + distance, groups)

    barrier = pltpu.get_barrier_semaphore()

    def greet_z(distance, carry):
        pl.semaphore_signal(
            barrier, inc=1, device_id=(section, z_peer(distance), column), device_id_type=MESH
        )
        return carry

    def greet_xy(distance, carry):
        pl.semaphore_signal(
            barrier, inc=1, device_id=(section, z, xy_peer(distance)), device_id_type=MESH
        )
        return carry

    pl.semaphore_signal(barrier, inc=1, device_id=other, device_id_type=MESH)
    lax.fori_loop(1, depth, greet_z, 0)
    lax.fori_loop(1, groups, greet_xy, 0)
    pl.semaphore_wait(barrier, depth + groups - 1)

    def remote(source, target, send, recv, device):
        return pltpu.make_async_remote_copy(
            src_ref=source, dst_ref=target, send_sem=send, recv_sem=recv,
            device_id=device, device_id_type=MESH,
        )

    def run(first):
        own, away = (dense_first, dense_second) if first else (dense_second, dense_first)

        def shard_copy(kind, layer, plane, lane, device):
            return remote(
                layer.at[plane, lane], layer.at[plane, lane],
                shard_send.at[kind, plane, lane],
                shard_recv.at[0, plane, lane],
                device,
            )

        def z_copy(direction, plane):
            device = (section, lax.rem(z + 2 * direction - 1 + depth, depth), column)
            return shard_copy(direction, own, plane, column, device)

        def core_copy(layer, plane, lane):
            return remote(
                layer.at[plane, lane], layer.at[plane, lane],
                shard_send.at[2, plane, lane], shard_recv.at[1, plane, lane], other,
            )

        def xy_copy(plane, source, target):
            return shard_copy(3 + target, own, plane, source, (section, z, target))

        def pass_copy(plane, source, target):
            return shard_copy(3 + groups, own, plane, source, (section, z, target))

        def swap(index, source, target):
            return remote(source, target, core_send.at[index], core_recv.at[index], other)

        def local(index, source, target):
            return pltpu.make_async_copy(source, target, own_sem.at[index])

        square = groups == 4
        beside = column + 1 - 2 * lax.rem(column, 2)
        above = lax.rem(column + 2, groups)
        across = groups - 1 - column
        direct = 3 if square else groups

        def near(distance):
            if square:
                return beside + (distance - 1) * (above - beside)
            return xy_peer(distance)

        def spread(plane):
            core_copy(own, plane, column).start()

            def send(distance, carry):
                xy_copy(plane, column, near(distance)).start()
                return carry

            lax.fori_loop(1, direct, send, 0)

        def take(plane):
            def arrive(distance, carry):
                lane = near(distance)
                xy_copy(plane, lane, column).wait_recv()
                core_copy(own, plane, lane).start()
                if square:

                    @pl.when(lax.rem(plane, 2) == distance - 1)
                    def _():
                        pass_copy(plane, lane, near(3 - distance)).start()

                return carry

            lax.fori_loop(1, direct, arrive, 0)

        own_shard = local(0, packed_ref, own.at[z, column])

        def first_copies():
            remote_ones = [
                swap(0, edge_ref.at[1], rows_ref),
                swap(1, table_ref.at[1], table_first.at[z]),
                swap(2, up_ref, up_first),
                swap(3, down_ref, down_first),
            ]
            local_ones = [
                local(1, edge_ref.at[0], rows_ref),
                local(2, table_ref.at[0], table_first.at[z]),
                local(3, up_ref, up_first),
                local(4, down_ref, down_first),
            ]
            return remote_ones, local_ones

        def second_copies():
            remote_ones = [
                swap(0, edge_ref.at[0], cotangent_ref),
                swap(1, table_ref.at[0], table_second.at[z]),
                swap(2, up_ref, up_second),
                swap(3, down_ref, down_second),
            ]
            local_ones = [
                local(1, edge_ref.at[1], cotangent_ref),
                local(2, table_ref.at[1], table_second.at[z]),
                local(3, up_ref, up_second),
                local(4, down_ref, down_second),
            ]
            return remote_ones, local_ones

        own_shard.start()
        own_shard.wait()

        @pl.when(z < depth - 1)
        def _():
            z_copy(1, z).start()

        @pl.when(z > 0)
        def _():
            z_copy(0, z).start()

        spread(z)

        first_remote, first_local = first_copies()
        second_remote, second_local = second_copies()
        out_going, in_coming = (
            (first_remote, second_remote) if first else (second_remote, first_remote)
        )
        local_ones = first_local if first else second_local
        for copy in out_going[:2] + local_ones + out_going[2:]:
            copy.start()

        def step(distance, carry):
            low, high = z - distance, z + distance

            @pl.when(low >= 0)
            def _():
                z_copy(1, low).wait_recv()

                @pl.when(z < depth - 1)
                def _():
                    z_copy(1, low).start()

                spread(low)

            @pl.when(high < depth)
            def _():
                z_copy(0, high).wait_recv()

                @pl.when(z > 0)
                def _():
                    z_copy(0, high).start()

                spread(high)

            take(z_order(distance - 1, z, depth))
            return carry

        lax.fori_loop(1, depth, step, 0)
        take(z_order(depth - 1, z, depth))

        def table_copies(source, target):
            pairs = []
            for layer, table in enumerate((table_first, table_second)):
                pairs.append(
                    remote(
                        table.at[source], table.at[source], table_send.at[layer, target],
                        table_recv.at[layer, source], (section, target, column),
                    )
                )
            return pairs

        local_ones[1].wait()
        in_coming[1].wait_recv()

        def send_tables(distance, carry):
            for copy in table_copies(z, z_peer(distance)):
                copy.start()
            return carry

        lax.fori_loop(1, depth, send_tables, 0)

        if square:

            def last_arrival(index, carry):
                plane = z_order(index, z, depth)
                pass_copy(plane, across, column).wait_recv()
                core_copy(own, plane, across).start()
                return carry

            lax.fori_loop(0, depth, last_arrival, 0)

        def drain(plane, carry):
            @pl.when(jnp.logical_and(z < depth - 1, plane <= z))
            def _():
                z_copy(1, plane).wait_send()

            @pl.when(jnp.logical_and(z > 0, plane >= z))
            def _():
                z_copy(0, plane).wait_send()

            def drain_core(lane, inner):
                core_copy(away, plane, lane).wait_recv()
                core_copy(own, plane, lane).wait_send()
                return inner

            def drain_xy(distance, inner):
                xy_copy(plane, column, near(distance)).wait_send()
                if square:

                    @pl.when(lax.rem(plane, 2) == distance - 1)
                    def _():
                        pass_copy(plane, near(distance), near(3 - distance)).wait_send()

                return inner

            lax.fori_loop(0, groups, drain_core, 0)
            return lax.fori_loop(1, direct, drain_xy, carry)

        lax.fori_loop(0, depth, drain, 0)

        for index in (0, 2, 3):
            in_coming[index].wait_recv()
        for copy in out_going:
            copy.wait_send()
        for copy in local_ones[:1] + local_ones[2:]:
            copy.wait()

        def finish_tables(distance, carry):
            for copy in table_copies(z_peer(distance), z):
                copy.wait_recv()
            for copy in table_copies(z, z_peer(distance)):
                copy.wait_send()
            return carry

        lax.fori_loop(1, depth, finish_tables, 0)

    pl.when(is_first)(functools.partial(run, True))
    pl.when(jnp.logical_not(is_first))(functools.partial(run, False))


def start_call(call_id, depth, groups, packed, up, down, edge, table):
    rows, width = packed.shape
    half = jnp.bfloat16
    out_shape = (
        jax.ShapeDtypeStruct((depth, groups, rows, width), half),
        jax.ShapeDtypeStruct((depth, groups, rows, width), half),
        jax.ShapeDtypeStruct(up.shape, half),
        jax.ShapeDtypeStruct(up.shape, half),
        jax.ShapeDtypeStruct(down.shape, half),
        jax.ShapeDtypeStruct(down.shape, half),
        jax.ShapeDtypeStruct(edge.shape[1:], jnp.float32),
        jax.ShapeDtypeStruct(edge.shape[1:], jnp.float32),
        jax.ShapeDtypeStruct((depth,) + table.shape[1:], jnp.int32),
        jax.ShapeDtypeStruct((depth,) + table.shape[1:], jnp.int32),
    )
    return pl.pallas_call(
        functools.partial(start_kernel, (depth, groups)),
        out_shape=out_shape,
        in_specs=[pl.BlockSpec(memory_space=pltpu.VMEM)] * 5,
        out_specs=[pl.BlockSpec(memory_space=pl.ANY)] * len(out_shape),
        scratch_shapes=[
            pltpu.SemaphoreType.DMA((4 + groups, depth, groups)),
            pltpu.SemaphoreType.DMA((2, depth, groups)),
            pltpu.SemaphoreType.DMA((4,)),
            pltpu.SemaphoreType.DMA((4,)),
            pltpu.SemaphoreType.DMA((2, depth)),
            pltpu.SemaphoreType.DMA((2, depth)),
            pltpu.SemaphoreType.DMA((5,)),
        ],
        compiler_params=pltpu.CompilerParams(
            collective_id=call_id, has_side_effects=True, vmem_limit_bytes=60 * 2**20
        ),
        name="start_exchange",
    )(packed, up, down, edge, table)

def finish_kernel(shape, *refs):
    depth, groups, token_rows, padded_rows, model_width = shape
    first_refs, second_refs, rest = refs[0:5], refs[5:10], refs[10:]
    (
        up_first, down_first, up_second, down_second, rows_first, rows_second,
        shard_ref, up_ref, down_ref, rows_ref,
        pair, away, small_pair, table, inbox, sent_home, home,
        core_send, core_recv, go_send, go_recv, home_send, home_recv,
    ) = rest
    half = jnp.bfloat16
    section, z, column = (
        lax.axis_index("section"), lax.axis_index("dp"), lax.axis_index("expert")
    )
    other = (1 - section, z, column)
    is_first = section == 0
    shard_rows = table.shape[1]

    def z_peer(distance):
        return lax.rem(z + distance, depth)

    def xy_peer(distance):
        return lax.rem(column + distance, groups)

    barrier = pltpu.get_barrier_semaphore()

    def greet_z(distance, carry):
        pl.semaphore_signal(
            barrier, inc=1, device_id=(section, z_peer(distance), column), device_id_type=MESH
        )
        return carry

    def greet_xy(distance, carry):
        pl.semaphore_signal(
            barrier, inc=1, device_id=(section, z, xy_peer(distance)), device_id_type=MESH
        )
        return carry

    pl.semaphore_signal(barrier, inc=1, device_id=other, device_id_type=MESH)
    lax.fori_loop(1, depth, greet_z, 0)
    lax.fori_loop(1, groups, greet_xy, 0)
    pl.semaphore_wait(barrier, depth + groups - 1)

    def swap(index, source, target):
        return pltpu.make_async_remote_copy(
            src_ref=source, dst_ref=target, send_sem=core_send.at[index],
            recv_sem=core_recv.at[index], device_id=other, device_id_type=MESH,
        )

    def pack(target, operands):
        target[padded_rows - 16 :, :] = jnp.zeros((16, target.shape[1]), half)
        offset = 0
        for operand in operands:
            width = operand.shape[1]
            target[:token_rows, offset : offset + width] = operand[...]
            offset += width

    def side_copies(first):
        if first:
            sources = (second_refs[4], up_second, down_second, rows_second)
        else:
            sources = (first_refs[4], up_first, down_first, rows_first)
        targets = (small_pair.at[1], up_ref, down_ref, rows_ref)
        return [
            swap(1 + index, source, target)
            for index, (source, target) in enumerate(zip(sources, targets))
        ]

    operand_copy = swap(0, away, pair.at[1])
    for first in (True, False):

        @pl.when(is_first if first else jnp.logical_not(is_first))
        def _():
            mine, others = (first_refs, second_refs) if first else (second_refs, first_refs)
            pack(away, others[:4])
            operand_copy.start()
            side_copies(first)[0].start()
            pack(pair.at[0], mine[:4])
            small_pair[0] = mine[4][...]

    operand_copy.wait_recv()
    rows = 2 * padded_rows

    def product(left, right, target):
        a = pair[:, :, left : left + model_width].reshape(rows, model_width)
        b = pair[:, :, right : right + model_width].reshape(rows, model_width)
        value = f32_dot(a, b, ((0,), (0,))).astype(half)
        table[:, :, target : target + model_width] = value.reshape(
            depth * groups, shard_rows, model_width
        )

    for index in range(3):
        product(0, (1 + index) * model_width, index * model_width)
    product(4 * model_width, 5 * model_width, 3 * model_width)
    for copy in side_copies(True)[:1]:
        copy.wait_recv()
    small = (small_pair[0] + small_pair[1]).astype(half)
    table[:, :, 4 * model_width :] = small.reshape(depth * groups, shard_rows, small.shape[1])

    def go_copy(plane, source, target):
        return pltpu.make_async_remote_copy(
            src_ref=table.at[plane * groups + target], dst_ref=inbox.at[plane, source],
            send_sem=go_send.at[plane, target], recv_sem=go_recv.at[plane, source],
            device_id=(section, z, target), device_id_type=MESH,
        )

    def home_copy(source, target):
        return pltpu.make_async_remote_copy(
            src_ref=sent_home.at[target], dst_ref=home.at[source],
            send_sem=home_send.at[target], recv_sem=home_recv.at[source],
            device_id=(section, target, column), device_id_type=MESH,
        )

    def send_plane(step, carry):
        plane = z_peer(step)

        def send(distance, inner):
            go_copy(plane, column, xy_peer(distance)).start()
            return inner

        return lax.fori_loop(1, groups, send, carry)

    lax.fori_loop(1, 2 + 1, send_plane, 0)

    for first in (True, False):

        @pl.when(is_first if first else jnp.logical_not(is_first))
        def _():
            for copy in side_copies(first)[1:]:
                copy.start()

    def sum_plane(step, carry):
        plane = z_peer(step)

        def arrive(distance, total):
            lane = xy_peer(distance)
            go_copy(plane, lane, column).wait_recv()
            return total + inbox[plane, lane].astype(jnp.float32)

        own = table[plane * groups + column].astype(jnp.float32)
        total = lax.fori_loop(1, groups, arrive, own)

        @pl.when(step + 2 <= depth)
        def _():
            send_plane(step + 2, 0)

        @pl.when(plane == z)
        def _():
            shard_ref[...] = total

        @pl.when(plane != z)
        def _():
            sent_home[plane] = total.astype(half)
            home_copy(z, plane).start()

        return carry

    lax.fori_loop(1, depth + 1, sum_plane, 0)

    def finish_home(distance, carry):
        source = z_peer(distance)
        home_copy(source, z).wait_recv()
        shard_ref[...] += home[source].astype(jnp.float32)
        home_copy(z, source).wait_send()
        return carry

    lax.fori_loop(1, depth, finish_home, 0)

    def drain_plane(plane, carry):
        def drain(distance, inner):
            go_copy(plane, column, xy_peer(distance)).wait_send()
            return inner

        return lax.fori_loop(1, groups, drain, carry)

    lax.fori_loop(0, depth, drain_plane, 0)
    operand_copy.wait_send()
    for index, copy in enumerate(side_copies(True)):
        copy.wait_send()
        if index > 0:
            copy.wait_recv()


def finish_call(call_id, depth, groups, first, second, up_first, down_first, up_second, down_second,
                rows_first, rows_second):
    token_rows, model_width = first[0].shape
    padded_rows = round_up(token_rows, 16)
    small_width = first[4].shape[1]
    width = 4 * model_width + small_width
    shard_rows = model_width // (depth * groups)
    half = jnp.bfloat16
    out_shape = (
        jax.ShapeDtypeStruct((shard_rows, width), jnp.float32),
        jax.ShapeDtypeStruct(up_first.shape, half),
        jax.ShapeDtypeStruct(down_first.shape, half),
        jax.ShapeDtypeStruct(rows_first.shape, jnp.float32),
    )
    home = pltpu.VMEM((depth, shard_rows, width), half)
    return pl.pallas_call(
        functools.partial(
            finish_kernel, (depth, groups, token_rows, padded_rows, model_width)
        ),
        out_shape=out_shape,
        in_specs=[pl.BlockSpec(memory_space=pltpu.VMEM)] * 16,
        out_specs=[pl.BlockSpec(memory_space=pltpu.VMEM)] + [pl.BlockSpec(memory_space=pl.ANY)] * 3,
        scratch_shapes=[
            pltpu.VMEM((2, padded_rows, 6 * model_width), half),
            pltpu.VMEM((padded_rows, 6 * model_width), half),
            pltpu.VMEM((2, model_width, small_width), jnp.float32),
            pltpu.VMEM((depth * groups, shard_rows, width), half),
            pltpu.VMEM((depth, groups, shard_rows, width), half),
            home,
            home,
            pltpu.SemaphoreType.DMA((5,)),
            pltpu.SemaphoreType.DMA((5,)),
            pltpu.SemaphoreType.DMA((depth, groups)),
            pltpu.SemaphoreType.DMA((depth, groups)),
            pltpu.SemaphoreType.DMA((depth,)),
            pltpu.SemaphoreType.DMA((depth,)),
        ],
        compiler_params=pltpu.CompilerParams(
            collective_id=call_id, has_side_effects=True, vmem_limit_bytes=54 * 2**20
        ),
        name="finish_exchange",
    )(*first, *second, up_first, down_first, up_second, down_second, rows_first, rows_second)

def head_mask(head):
    lanes = lax.broadcasted_iota(jnp.int32, (1, 2 * HEAD_DIM), 1)
    return jnp.where(lanes // HEAD_DIM == head, 1.0, 0.0).astype(jnp.bfloat16)


def attend_kernel(width, qkv_ref, out_ref):
    scale_factor = 1.0 / math.sqrt(HEAD_DIM)
    pair_width = 2 * HEAD_DIM

    def pair(index, carry):
        def columns(part):
            start = pl.multiple_of(part * width + index * pair_width, pair_width)
            return qkv_ref[:, pl.ds(start, pair_width)]

        queries, keys, values = columns(0), columns(1), columns(2)
        total = jnp.zeros(queries.shape, jnp.float32)
        for head in range(2):
            mask = head_mask(head)
            scores = f32_dot(queries * mask, keys, ((1,), (1,))) * scale_factor
            log_totals = jnp.log(jnp.sum(jnp.exp(scores), axis=1, keepdims=True))
            probs = jnp.exp(scores - log_totals).astype(jnp.bfloat16)
            total = total + f32_dot(probs, values * mask, ((1,), (0,)))
        start = pl.multiple_of(index * pair_width, pair_width)
        out_ref[:, pl.ds(start, pair_width)] = total.astype(jnp.bfloat16)
        return carry

    lax.fori_loop(0, width // pair_width, pair, 0)


def attend_backward_kernel(width, qkv_ref, d_out_ref, d_qkv_ref):
    scale_factor = 1.0 / math.sqrt(HEAD_DIM)
    pair_width = 2 * HEAD_DIM
    half = jnp.bfloat16

    def pair(index, carry):
        def place(part):
            return pl.ds(pl.multiple_of(part * width + index * pair_width, pair_width), pair_width)

        queries, keys, values = (qkv_ref[:, place(part)] for part in range(3))
        d_out = d_out_ref[:, place(0)]
        d_queries = jnp.zeros(queries.shape, jnp.float32)
        d_keys, d_values = d_queries, d_queries
        for head in range(2):
            mask = head_mask(head)
            own_queries, own_d_out = queries * mask, d_out * mask
            scores = f32_dot(keys, own_queries, ((1,), (1,))) * scale_factor
            log_totals = jnp.log(jnp.sum(jnp.exp(scores), axis=0, keepdims=True))
            probs = jnp.exp(scores - log_totals)
            d_probs = f32_dot(values, own_d_out, ((1,), (1,)))
            row_dot = jnp.sum(probs * d_probs, axis=0, keepdims=True)
            d_scores = (probs * (d_probs - row_dot) * scale_factor).astype(half)
            d_values = d_values + f32_dot(probs.astype(half), own_d_out, ((1,), (0,)))
            d_keys = d_keys + f32_dot(d_scores, own_queries, ((1,), (0,)))
            d_queries = d_queries + f32_dot(d_scores, keys * mask, ((0,), (0,)))
        for part, value in enumerate((d_queries, d_keys, d_values)):
            d_qkv_ref[:, place(part)] = value.astype(half)
        return carry

    lax.fori_loop(0, width // pair_width, pair, 0)


def attend_call(qkv_rows, d_attended=None):
    rows, width = qkv_rows.shape
    width = width // 3
    operands = (qkv_rows,) if d_attended is None else (qkv_rows, d_attended)
    kernel = attend_kernel if d_attended is None else attend_backward_kernel
    out_width = width if d_attended is None else 3 * width
    return pl.pallas_call(
        functools.partial(kernel, width),
        out_shape=jax.ShapeDtypeStruct((rows, out_width), jnp.bfloat16),
        in_specs=[pl.BlockSpec(memory_space=pltpu.VMEM)] * len(operands),
        out_specs=pl.BlockSpec(memory_space=pltpu.VMEM),
        compiler_params=pltpu.CompilerParams(vmem_limit_bytes=24 * 2**20),
        name="attend" if d_attended is None else "attend_backward",
    )(*operands)


def norm_forward(values, gain_row, shift_row):
    centred = values - jnp.mean(values, axis=-1, keepdims=True)
    variance = jnp.mean(centred * centred, axis=-1, keepdims=True)
    inverse = lax.rsqrt(variance + EPS)
    unit_rows = centred * inverse
    return (unit_rows * gain_row + shift_row, unit_rows, inverse)


def norm_backward(d_normed, unit_rows, inverse, gain_row):
    d_gain = jnp.sum(d_normed * unit_rows, axis=0)
    d_shift = jnp.sum(d_normed, axis=0)
    scaled = d_normed * gain_row
    d_values = inverse * (
        scaled
        - jnp.mean(scaled, axis=-1, keepdims=True)
        - unit_rows * jnp.mean(scaled * unit_rows, axis=-1, keepdims=True)
    )
    return (d_values, d_gain, d_shift)


def gelu_slope(pre_act):
    return (
        0.5 * (1.0 + lax.erf(pre_act * SQRT_HALF))
        + pre_act * jnp.exp(-0.5 * pre_act * pre_act) * INV_ROOT_TAU
    )


def split_heads(qkv_rows, image_count):
    feature_count = qkv_rows.shape[1] // 3
    return [
        qkv_rows[:, part_index * feature_count : (part_index + 1) * feature_count].reshape(
            image_count, -1, HEADS, HEAD_DIM
        )
        for part_index in range(3)
    ]


def attend_forward(qkv_rows, image_count):
    queries, key_rows, value_rows = split_heads(qkv_rows, image_count)
    scale_factor = 1.0 / math.sqrt(HEAD_DIM)
    scores = (
        jnp.einsum("bqhd,bkhd->bhqk", queries, key_rows, preferred_element_type=jnp.float32)
        * scale_factor
    )
    log_totals = jnp.log(jnp.sum(jnp.exp(scores), axis=-1))
    probs_half = jnp.exp(scores - log_totals[..., None]).astype(jnp.bfloat16)
    attended = jnp.einsum(
        "bhqk,bkhd->bqhd", probs_half, value_rows, preferred_element_type=jnp.float32
    )
    return (attended.astype(jnp.bfloat16).reshape(-1, HEADS * HEAD_DIM), log_totals)


def attend_backward(qkv_rows, log_totals, d_attended, image_count):
    queries, key_rows, value_rows = split_heads(qkv_rows, image_count)
    scale_factor = 1.0 / math.sqrt(HEAD_DIM)
    scores = (
        jnp.einsum("bqhd,bkhd->bhqk", queries, key_rows, preferred_element_type=jnp.float32)
        * scale_factor
    )
    probs = jnp.exp(scores - log_totals[..., None])
    probs_half = probs.astype(jnp.bfloat16)
    d_heads = d_attended.reshape(image_count, -1, HEADS, HEAD_DIM)
    d_values = jnp.einsum(
        "bhqk,bqhd->bkhd", probs_half, d_heads, preferred_element_type=jnp.float32
    )
    d_probs = jnp.einsum("bqhd,bkhd->bhqk", d_heads, value_rows, preferred_element_type=jnp.float32)
    row_dot = jnp.sum(probs * d_probs, axis=-1, keepdims=True)
    d_scores = (probs * (d_probs - row_dot) * scale_factor).astype(jnp.bfloat16)
    d_queries = jnp.einsum(
        "bhqk,bkhd->bqhd", d_scores, key_rows, preferred_element_type=jnp.float32
    )
    d_keys = jnp.einsum("bhqk,bqhd->bkhd", d_scores, queries, preferred_element_type=jnp.float32)
    feature_count = HEADS * HEAD_DIM
    joined = jnp.concatenate(
        [
            d_queries.reshape(-1, feature_count),
            d_keys.reshape(-1, feature_count),
            d_values.reshape(-1, feature_count),
        ],
        axis=1,
    )
    return joined.astype(jnp.bfloat16)


def on_device(
    boundary_in, routes, capacity_slots, ln_gain, ln_bias, w_qkv, w_out, w_router, w_up, w_down
):
    section_index = lax.axis_index("section")
    is_first = section_index == 0
    depth = lax.axis_size("dp")
    groups = lax.axis_size("expert")
    expert_count = EXP_DEV * groups
    local_images = boundary_in.shape[2]
    token_rows = local_images * boundary_in.shape[3]
    model_width = boundary_in.shape[4]
    capacity = 26 * token_rows // (16 * expert_count)
    cap_rows = round_up(capacity, 8)
    padded_rows = round_up(token_rows + 8, 16)
    half = jnp.bfloat16
    swapped = [(0, 1), (1, 0)]

    edge = boundary_in[0].reshape(MB, token_rows, model_width)
    route_rows = routes[0].reshape(MB, token_rows, 2)
    slot_rows = capacity_slots[0].reshape(MB, token_rows, 2)
    slot_index = jnp.where(slot_rows < capacity, route_rows * cap_rows + slot_rows, -1)
    table = jnp.concatenate([slot_index, route_rows], axis=2).transpose(0, 2, 1)
    table = jnp.pad(
        table, ((0, 0), (0, 4), (0, padded_rows - token_rows)), constant_values=-1
    )

    norm_columns = jnp.concatenate([ln_gain, ln_bias], axis=1).transpose(0, 2, 1)
    used = 4 * model_width + expert_count + 4
    padding = -used % 128
    packed = jnp.concatenate([w_qkv, w_out, w_router, norm_columns], axis=2)
    packed = jnp.pad(packed, ((0, 0), (0, 0), (0, padding)))
    (
        dense_first, dense_second, up_first, up_second, down_first, down_second,
        stream, cotangent, table_first, table_second,
    ) = start_call(8, depth, groups, packed[0], w_up[0], w_down[0], edge, table)
    qkv_all, out_all, router_all, norm_all = [], [], [], []

    def add_dense(item):
        qkv_all.append(item[:, : 3 * model_width])
        out_all.append(item[:, 3 * model_width : 4 * model_width])
        router_all.append(item[:, 4 * model_width : used - 4])
        norm_all.append(item[:, used - 4 : used].T.astype(jnp.float32))

    add_dense(dense_first.reshape(model_width, used + padding))
    add_dense(dense_second.reshape(model_width, used + padding))
    up_all = (up_first, up_second)
    down_all = (down_first, down_second)
    slot_tables = (table_first, table_second)
    z_index = lax.axis_index("dp")
    chosen_all = [
        (
            lax.dynamic_index_in_dim(item, z_index, 0, False)[2:4, :token_rows].T[..., None]
            == jnp.arange(expert_count, dtype=jnp.int32)
        ).astype(jnp.float32)
        for item in slot_tables
    ]
    moe = functools.partial(moe_call, depth=depth, groups=groups, cap_rows=cap_rows)

    def layer_forward(layer, inputs):
        chosen = chosen_all[layer]
        normed_one, unit_one, inverse_one = norm_forward(
            inputs, norm_all[layer][0], norm_all[layer][2]
        )
        norm_one = normed_one.astype(half)
        qkv_rows = jnp.dot(norm_one, qkv_all[layer], preferred_element_type=jnp.float32).astype(half)
        if local_images == 1:
            attended, log_totals = attend_call(qkv_rows), None
        else:
            attended, log_totals = attend_forward(qkv_rows, local_images)
        middle = inputs + jnp.dot(attended, out_all[layer], preferred_element_type=jnp.float32)
        normed_two, unit_two, inverse_two = norm_forward(
            middle, norm_all[layer][1], norm_all[layer][3]
        )
        norm_two = normed_two.astype(half)
        logits = jnp.dot(norm_two, router_all[layer], preferred_element_type=jnp.float32)
        picked = jnp.sum(logits[:, None, :] * chosen, axis=-1)
        leading = jax.nn.sigmoid(picked[:, 0] - picked[:, 1])
        gate_pair = jnp.stack([leading, 1.0 - leading], axis=-1)
        gate_rows = jnp.pad(gate_pair.T, ((0, 0), (0, model_width - token_rows)))
        sent = jnp.concatenate(
            [
                norm_two,
                jnp.zeros((padded_rows - 8 - token_rows, model_width), half),
                gate_rows.astype(half),
                jnp.zeros((6, model_width), half),
            ]
        )
        combined, *expert_saved = moe(
            False, 2 * layer, rows=sent, slots=slot_tables[layer], up=up_all[layer],
            down=down_all[layer],
        )
        out_rows = middle + combined[:token_rows]
        saved = (
            inputs, norm_one, qkv_rows, log_totals, attended, middle, norm_two, gate_pair,
            expert_saved,
        )
        return (out_rows, saved)

    def layer_backward(layer, d_out, saved):
        (
            inputs, norm_one, qkv_rows, log_totals, attended, middle, norm_two, gate_pair,
            expert_saved,
        ) = saved
        chosen = chosen_all[layer]
        gates, all_rows, hidden, slope, back_rows = expert_saved
        sent = d_out.astype(half)
        combined, up_grad, down_grad = moe(
            True, 2 * layer + 1, rows=sent, slots=slot_tables[layer], up=up_all[layer],
            down=down_all[layer], saved=(gates, back_rows, slope, hidden, all_rows),
        )
        d_gate_rows = combined[padded_rows - 8 :, :token_rows]
        d_gate = jnp.stack([d_gate_rows[0] + d_gate_rows[1], d_gate_rows[2] + d_gate_rows[3]], axis=1)
        d_lead = (d_gate[:, 0] - d_gate[:, 1]) * gate_pair[:, 0] * gate_pair[:, 1]
        d_logits = (d_lead[:, None] * (chosen[:, 0] - chosen[:, 1])).astype(half)
        d_norm_two = combined[:token_rows] + jnp.einsum(
            "te,de->td", d_logits, router_all[layer], preferred_element_type=jnp.float32
        )
        normed_two, unit_two, inverse_two = norm_forward(
            middle, norm_all[layer][1], norm_all[layer][3]
        )
        d_middle_norm, gain_two, shift_two = norm_backward(
            d_norm_two, unit_two, inverse_two, norm_all[layer][1]
        )
        d_middle = d_out + d_middle_norm
        d_middle_half = d_middle.astype(half)
        d_attended = jnp.einsum(
            "te,de->td", d_middle_half, out_all[layer], preferred_element_type=jnp.float32
        ).astype(half)
        if local_images == 1:
            d_qkv = attend_call(qkv_rows, d_attended)
        else:
            d_qkv = attend_backward(qkv_rows, log_totals, d_attended, local_images)
        d_norm_one = jnp.einsum(
            "te,de->td", d_qkv, qkv_all[layer], preferred_element_type=jnp.float32
        )
        normed_one, unit_one, inverse_one = norm_forward(
            inputs, norm_all[layer][0], norm_all[layer][2]
        )
        d_input_norm, gain_one, shift_one = norm_backward(
            d_norm_one, unit_one, inverse_one, norm_all[layer][0]
        )
        d_input = d_middle + d_input_norm
        small = jnp.concatenate(
            [
                jnp.einsum("td,te->de", norm_two, d_logits, preferred_element_type=jnp.float32),
                jnp.stack([gain_one, gain_two, shift_one, shift_two], axis=1),
            ],
            axis=1,
        )
        return (d_input, (norm_one, d_qkv, attended, d_middle_half, small), (up_grad, down_grad))

    qkv_part, out_part = 3 * model_width // 2, model_width // 2
    small_width = round_up(expert_count + 4, 128)

    def dense_gradients(norm_one, d_qkv, attended, d_middle_half, small):
        own = jnp.concatenate([norm_one, d_qkv, attended, d_middle_half], axis=1)
        pair = jnp.concatenate([own, lax.ppermute(own, "section", swapped)], axis=0)
        d_qkv_part = lax.dynamic_slice_in_dim(
            pair, model_width + section_index * qkv_part, qkv_part, axis=1
        )
        d_out_part = lax.dynamic_slice_in_dim(
            pair, 5 * model_width + section_index * out_part, out_part, axis=1
        )
        qkv_grad = jnp.einsum(
            "td,te->de", pair[:, :model_width], d_qkv_part, preferred_element_type=jnp.float32
        )
        out_grad = jnp.einsum(
            "td,te->de", pair[:, 4 * model_width : 5 * model_width], d_out_part,
            preferred_element_type=jnp.float32,
        )
        small = jnp.pad(small, ((0, 0), (0, small_width - expert_count - 4)))
        packed_grad = jnp.concatenate(
            [qkv_grad.astype(half), out_grad.astype(half), small.astype(half)], axis=1
        )
        blocks = packed_grad.reshape(depth, groups, -1, packed_grad.shape[1]).transpose(1, 0, 2, 3)
        blocks = lax.all_to_all(blocks, "expert", split_axis=0, concat_axis=0, tiled=True)
        blocks = jnp.sum(blocks.astype(jnp.float32), axis=0).astype(half)
        blocks = lax.all_to_all(blocks, "dp", split_axis=0, concat_axis=0, tiled=True)
        return jnp.sum(blocks.astype(jnp.float32), axis=0)

    saved_list = []
    for layer in range(2):
        if layer > 0:
            stream = stream.astype(half).astype(jnp.float32)
        stream, saved = layer_forward(layer, stream)
        saved_list.append(saved)
    dense_operands = [None, None]
    expert_grads = [None, None]
    for layer in (1, 0):
        if layer < 1:
            cotangent = cotangent.astype(half).astype(jnp.float32)
        cotangent, operands, expert_grads[layer] = layer_backward(
            layer, cotangent, saved_list[layer]
        )
        dense_operands[layer] = operands

    def mine(first, second):
        return jnp.where(is_first, first, second)

    def both(first, second):
        own, away = mine(first, second), mine(second, first)
        return own, lax.ppermute(away, "section", swapped)

    if model_width % (16 * depth * groups) == 0:
        operands = [
            item[:4] + (jnp.pad(item[4], ((0, 0), (0, small_width - expert_count - 4))),)
            for item in dense_operands
        ]
        shard, other_up, other_down, other_rows = finish_call(
            9, depth, groups, operands[0], operands[1], *expert_grads[0], *expert_grads[1],
            cotangent, stream,
        )
        own_up = mine(expert_grads[0][0], expert_grads[1][0])
        own_down = mine(expert_grads[0][1], expert_grads[1][1])
        own_rows = mine(cotangent, stream)
        qkv_shard = shard[:, : 3 * model_width]
        out_shard = shard[:, 3 * model_width : 4 * model_width]
        small_shard = shard[:, 4 * model_width :]
    else:
        shards = [dense_gradients(*item) for item in dense_operands]
        own_shard, other_shard = both(shards[0], shards[1])
        low, high = mine(own_shard, other_shard), mine(other_shard, own_shard)
        qkv_shard = jnp.concatenate([low[:, :qkv_part], high[:, :qkv_part]], axis=1)
        out_shard = jnp.concatenate(
            [low[:, qkv_part : qkv_part + out_part], high[:, qkv_part : qkv_part + out_part]], axis=1
        )
        small_shard = (low + high)[:, qkv_part + out_part :]
        own_up, other_up = both(expert_grads[0][0], expert_grads[1][0])
        own_down, other_down = both(expert_grads[0][1], expert_grads[1][1])
        own_rows, other_rows = both(cotangent, stream)
    norm_shard = small_shard[:, expert_count : expert_count + 4].T

    def expert_grad(own, other):
        return (own.astype(jnp.float32) + other.astype(jnp.float32))[None]

    boundary_rows = jnp.stack([mine(own_rows, other_rows), mine(other_rows, own_rows)])
    boundary_out = boundary_rows.reshape(1, MB, local_images, boundary_in.shape[3], model_width)
    return (
        boundary_out,
        norm_shard[None, 0:2],
        norm_shard[None, 2:4],
        qkv_shard[None],
        out_shard[None],
        small_shard[None, :, :expert_count],
        expert_grad(own_up, other_up),
        expert_grad(own_down, other_down),
    )


def solution(mesh):
    in_specs = (
        P("section", None, ("dp", "expert"), None, None),
        P("section", None, ("dp", "expert"), None, None),
        P("section", None, ("dp", "expert"), None, None),
        P("section", None, ("dp", "expert")),
        P("section", None, ("dp", "expert")),
        P("section", ("dp", "expert"), None),
        P("section", ("dp", "expert"), None),
        P("section", ("dp", "expert"), None),
        P("section", "expert", None, "dp"),
        P("section", "expert", "dp", None),
    )
    out_specs = (
        P("section", None, ("dp", "expert"), None, None),
        P("section", None, ("dp", "expert")),
        P("section", None, ("dp", "expert")),
        P("section", ("dp", "expert"), None),
        P("section", ("dp", "expert"), None),
        P("section", ("dp", "expert"), None),
        P("section", "expert", None, "dp"),
        P("section", "expert", "dp", None),
    )
    return jax.shard_map(
        on_device, mesh=mesh, in_specs=in_specs, out_specs=out_specs, check_vma=False
    )
```
